256 devices in a mesh: shot: 8 (over y, x_lo), tile: 32 (over x_hi, z, core).
Axes of the slice: x: 4 (x_hi: 2, x_lo: 2; x = x_hi * 2 + x_lo), y: 4, z: 8, core: 2. Of those that a mesh axis runs over, the one named last changes fastest.
Arguments:
- p_now: float32 [8, 4096, 16, 128], P('shot', 'tile'), may hold values from -6 to 6
- p_prev: float32 [8, 4096, 16, 128], P('shot', 'tile'), may hold values from -6 to 6
- adj_now: float32 [8, 4096, 16, 128], P('shot', 'tile'), may hold values from -60 to 60
- adj_next: float32 [8, 4096, 16, 128], P('shot', 'tile'), may hold values from -60 to 60
- coef_old: float32 [2048, 512], P('tile'), may hold values from 0.14 to 0.28
- signs: int32 [8, 2048], P('shot', 'tile'), may hold values from 0 to 1
- elem_index: int32 [2048], P('tile'), may hold values from 0 to 262143
- wavelet: float32 [5], replicated, may hold values from -4 to 4
Outputs:
- direction: float32 [2048, 512], P('tile')
- p_last: float32 [8, 4096, 16, 128], P('shot', 'tile')
The draws below stay inside these ranges and needn't reach their ends.
All inputs are finite; a program needn't handle non-finite values.
Results may differ from the reference program's by a relative error of at most 0.0003.
Values sent between devices are 32-bit elements; how exact they have to be, the bound alone decides.
No kernel may reach another device: no remote copies, remote signals or barrier semaphores. Data moves between devices by JAX's collectives and lax.ppermute only.
A program may use at most 64 MiB of HBM per device.

```python
import jax
import jax.numpy as jnp
from jax import lax

CX = 128
CZ = 128
CY = 16
OV = 8
STEPS = 4
ELEM_DEV = 64
CXC = 64
CYC = 8
CZC = 64
NX = 4096
NXC = 2048
GROUPS = 8
ELEMS = 2048
N_TILE = 32


def adjoint_field(key):
    position = jnp.arange(NX, dtype=jnp.float32) / max(NX - 1, 1)
    shape = (GROUPS, NX, CY, CZ)
    base = jnp.clip(jax.random.normal(key, shape, jnp.float32), -4.0, 4.0)
    scale = jnp.exp(jnp.log(4.0) * position)[:, None, None] * jnp.ones((1, 1, CZ), jnp.float32)
    return base * scale[None]


def draw_adj_now(key, part):
    return adjoint_field(jax.random.fold_in(key, 11))


def draw_adj_next(key, part):
    return adjoint_field(jax.random.fold_in(key, 12))


def plant(values, rng, least, high):
    place = [jax.random.randint(jax.random.fold_in(rng, axis), (), 0, length) for axis, length in enumerate(values.shape)]
    main_axis = values.shape.index(max(values.shape))
    beside = place[:main_axis] + [(place[main_axis] + 1) % values.shape[main_axis]] + place[main_axis + 1:]
    return values.at[tuple(place)].set(least).at[tuple(beside)].set(high)


def shard_levels(key, dims, shards, smallest, largest):
    def one(dim, blocks):
        steps = jax.random.uniform(jax.random.fold_in(jax.random.fold_in(key, 6), dim), (blocks,), jnp.float32, smallest / len(shards), largest / len(shards))
        return jnp.repeat(jnp.exp(steps), dims[dim] // blocks).reshape((-1,) + (1,) * (len(dims) - dim - 1))

    loudness = one(*shards[0])
    for cut in shards[1:]:
        loudness = loudness * one(*cut)
    return loudness


def bell_draw(stream_key, dims, spread, bound, split=(), kind=jnp.bfloat16):
    array = jax.random.normal(stream_key, dims, jnp.float32) * spread
    if len(split) > 0:
        array = shard_levels(stream_key, dims, split, -0.22, 0.18) * array
    return jnp.clip(array, min=-bound, max=bound).astype(kind)


def setup_inputs(seed: int = 0) -> dict:
    key_of = jax.random.split(jax.random.key(seed), 9)
    return {
        "p_now": bell_draw(key_of[0], (GROUPS, NX, CY, CZ), 1.0, 6.0, ((0, 8), (1, 32)), jnp.float32),
        "p_prev": bell_draw(key_of[1], (GROUPS, NX, CY, CZ), 1.0, 6.0, ((0, 8), (1, 32)), jnp.float32),
        "adj_now": draw_adj_now(jax.random.fold_in(key_of[8], 71), 0),
        "adj_next": draw_adj_next(jax.random.fold_in(key_of[8], 71), 0),
        "coef_old": jnp.clip(0.14 + 0.14 * jax.random.uniform(key_of[4], (NXC, CYC * CZC), jnp.float32) ** shard_levels(key_of[4], (NXC, CYC * CZC), ((0, 32),), -0.2, 0.2), 0.14, 0.28),
        "signs": plant(jax.random.randint(key_of[5], (GROUPS, ELEMS), 0, 2), jax.random.fold_in(key_of[5], 1), 0, 1).astype(jnp.int32),
        "elem_index": plant(jax.random.randint(key_of[6], (ELEMS,), 0, CX * CY * CZ), jax.random.fold_in(key_of[6], 1), 0, (CX * CY * CZ) - 1).astype(jnp.int32),
        "wavelet": bell_draw(key_of[7], (STEPS + 1,), 1.0, 4.0, (), jnp.float32),
    }


HIGH = lax.Precision.HIGHEST
LEARN = 0.02
EPSILON = 1e-06

def spectral_second(length):
    index = jnp.arange(length, dtype=jnp.int32)
    phase = index[:, None] * index[None, :] % length
    angle = 2.0 * jnp.pi / length * phase.astype(jnp.float32)
    number = jnp.minimum(index, length - index).astype(jnp.float32) * (2.0 * jnp.pi / length)
    weight = -(number * number) / length
    cosine = jnp.cos(angle)
    sine = jnp.sin(angle)
    first = jnp.dot(cosine * weight[None, :], cosine, precision=HIGH, preferred_element_type=jnp.float32)
    second = jnp.dot(sine * weight[None, :], sine, precision=HIGH, preferred_element_type=jnp.float32)
    return first + second

def taper_bell(inner, margin):
    ramp = jnp.sin(0.5 * jnp.pi * (jnp.arange(margin, dtype=jnp.float32) + 0.5) / margin) ** 2
    return jnp.concatenate([ramp, jnp.ones((inner,), jnp.float32), ramp[::-1]])

def spline_weight(offset):
    mag = jnp.abs(offset)
    inner = 2.0 / 3.0 - mag * mag + 0.5 * mag * mag * mag
    outer = (2.0 - mag) ** 3 / 6.0
    return jnp.where(mag < 1.0, inner, jnp.where(mag < 2.0, outer, 0.0))

def spline_expand_x(fine, coarse):
    rows = jnp.arange(fine, dtype=jnp.int32)[:, None]
    cols = jnp.arange(coarse + 4, dtype=jnp.int32)[None, :] - 2
    return spline_weight(((rows - 2 * cols).astype(jnp.float32) - 0.5) * 0.5)

def spline_project_x(fine, coarse):
    rows = jnp.arange(coarse, dtype=jnp.int32)[:, None]
    cols = jnp.arange(fine + 8, dtype=jnp.int32)[None, :] - 4
    return spline_weight(((cols - 2 * rows).astype(jnp.float32) - 0.5) * 0.5)

def periodic_spline(fine, coarse):
    rows = jnp.arange(fine, dtype=jnp.int32)[:, None]
    cols = jnp.arange(coarse, dtype=jnp.int32)[None, :]
    summed = jnp.zeros((fine, coarse), jnp.float32)
    for image in range(-2, 3):
        summed = summed + spline_weight(((rows - 2 * cols + image * fine).astype(jnp.float32) - 0.5) * 0.5)
    return summed

def laplacian(rimmed, field, second_x, second_z, bell):
    window = rimmed * bell[:, None, None]
    along_x = jnp.einsum('iw,wyz->iyz', second_x, window, precision=HIGH)
    along_z = jnp.einsum('xyz,zk->xyk', field, second_z, precision=HIGH)
    along_y = jnp.roll(field, 1, 1) + jnp.roll(field, -1, 1) - 2.0 * field
    return along_x + along_y + along_z

def expand_local(coef_rim):
    expander = spline_expand_x(CX, CXC)
    wide = jnp.dot(expander, coef_rim, precision=HIGH, preferred_element_type=jnp.float32).reshape(CX, CYC, CZC)
    wide = jnp.einsum('xjk,yj->xyk', wide, periodic_spline(CY, CYC), precision=HIGH)
    return jnp.einsum('xyk,zk->xyz', wide, periodic_spline(CZ, CZC), precision=HIGH)

def project_fine(rimmed):
    projector = spline_project_x(CX, CXC)
    narrow = jnp.dot(projector, rimmed.reshape(CX + 8, CY * CZ), precision=HIGH, preferred_element_type=jnp.float32)
    narrow = narrow.reshape(CXC, CY, CZ)
    narrow = jnp.einsum('xyz,yj->xjz', narrow, periodic_spline(CY, CYC), precision=HIGH)
    narrow = jnp.einsum('xjz,zk->xjk', narrow, periodic_spline(CZ, CZC), precision=HIGH)
    return narrow.reshape(CXC, CYC * CZC)

def reference(p_now, p_prev, adj_now, adj_next, coef_old, signs, elem_index, wavelet):
    second_x = spectral_second(CX + 2 * OV)[OV:OV + CX]
    second_z = spectral_second(CZ)
    bell = taper_bell(CX, OV)
    tiles = jnp.arange(N_TILE, dtype=jnp.int32)
    offsets = (tiles[:, None] * (CX * CY * CZ) + elem_index.reshape(N_TILE, ELEM_DEV)).reshape(-1).astype(jnp.int32)

    def laplace_all(field):
        padded = jnp.pad(field, ((OV, OV), (0, 0), (0, 0)))

        def one_tile(tile):
            rimmed = lax.dynamic_slice_in_dim(padded, tile * CX, CX + 2 * OV, 0)
            core = lax.dynamic_slice_in_dim(field, tile * CX, CX, 0)
            return laplacian(rimmed, core, second_x, second_z, bell)
        return lax.map(one_tile, tiles).reshape(field.shape)

    def expand_all(coef):
        padded = jnp.pad(coef, ((2, 2), (0, 0)))

        def one_tile(tile):
            return expand_local(lax.dynamic_slice_in_dim(padded, tile * CXC, CXC + 4, 0))
        return lax.map(one_tile, tiles).reshape(NX, CY, CZ)

    def project_all(image):
        padded = jnp.pad(image, ((4, 4), (0, 0), (0, 0)))

        def one_tile(tile):
            return project_fine(lax.dynamic_slice_in_dim(padded, tile * CX, CX + 8, 0))
        return lax.map(one_tile, tiles).reshape(NXC, CYC * CZC)

    def inject(field, step, amounts):
        flat = field.reshape(-1).at[offsets].add(wavelet[step] * amounts)
        return flat.reshape(field.shape)
    speed_old = expand_all(coef_old)
    squared_old = speed_old * speed_old

    def one_group(inputs):
        field_now, field_prev, adjoint_now, adjoint_next, sign_row = inputs
        amounts = (2 * sign_row - 1).astype(jnp.float32)
        forward = [field_prev, field_now]
        curvatures = []
        for step in range(STEPS):
            lap_p = laplace_all(forward[-1])
            curvatures.append(lap_p)
            following = 2.0 * forward[-1] - forward[-2] + squared_old * lap_p
            forward.append(inject(following, step, amounts))
        adjoint = [adjoint_next, adjoint_now]
        for step in range(STEPS):
            lap_q = laplace_all(adjoint[-1])
            adjoint.append(2.0 * adjoint[-1] - adjoint[-2] + squared_old * lap_q)
        summed = jnp.zeros_like(field_now)
        for step in range(STEPS):
            summed = summed + adjoint[STEPS + 1 - step] * curvatures[step]
        image = 2.0 * speed_old * summed
        return (project_all(image), forward[-2], forward[-1])
    partials, third, fourth = lax.map(one_group, (p_now, p_prev, adj_now, adj_next, signs))
    total = lax.optimization_barrier(jnp.sum(partials, axis=0))
    scale = jnp.sqrt(jnp.sum(total * total) / (NXC * CYC * CZC) + EPSILON)
    direction = total / scale
    coef_new = coef_old - LEARN * direction
    speed_new = expand_all(coef_new)
    squared_new = speed_new * speed_new

    def last_step(inputs):
        before, latest, sign_row = inputs
        amounts = (2 * sign_row - 1).astype(jnp.float32)
        following = 2.0 * latest - before + squared_new * laplace_all(latest)
        return inject(following, STEPS, amounts)
    p_last = lax.map(last_step, (third, fourth, signs))
    return (direction, p_last)
```

```python
import functools

import jax
import jax.numpy as jnp
import ml_dtypes
import numpy as np
from jax import lax
from jax.experimental import pallas as pl
from jax.experimental.pallas import tpu as pltpu
from jax.sharding import Mesh
from jax.sharding import PartitionSpec as P

CX = 128
CZ = 128
CY = 16
OV = 8
STEPS = 4
ELEMS = 64
CXC = 64
CYC = 8
CZC = 64
ROWS = 72
LEARN = 0.02
EPSILON = 1e-06
BF = jnp.bfloat16
F32 = jnp.float32
SHOT = ("y", "xl")
TILE = ("xh", "z", "core")


def spectral_second(length):
    index = np.arange(length)
    number = np.minimum(index, length - index) * (2.0 * np.pi / length)
    phase = (index[:, None, None] - index[None, :, None]) * index[None, None, :] % length
    return -np.sum(number**2 * np.cos(2.0 * np.pi / length * phase), axis=2) / length


def spline_units(offset):
    mag = np.abs(offset)
    inner = 2.0 / 3.0 - mag**2 + 0.5 * mag**3
    outer = (2.0 - mag) ** 3 / 6.0
    return np.round(384.0 * np.where(mag < 1.0, inner, np.where(mag < 2.0, outer, 0.0)))


def halves(matrix):
    high = matrix.astype(np.float32).astype(ml_dtypes.bfloat16)
    low = (matrix - high.astype(np.float64)).astype(np.float32).astype(ml_dtypes.bfloat16)
    return high, low


@functools.cache
def constants():
    out = {}
    second_x = spectral_second(CX + 2 * OV)[OV : OV + CX]
    ramp = np.sin(0.5 * np.pi * (np.arange(OV) + 0.5) / OV) ** 2
    left = second_x[:, :OV] * ramp[None, :]
    right = second_x[:, OV + CX :] * ramp[None, ::-1]
    high, low = halves(second_x[:, OV : OV + CX])
    out["own_x"] = np.block([[high, high], [low, np.zeros_like(low)]])
    sides = []
    for pair in ((right, left), (left, right)):
        high, low = halves(np.concatenate(pair, axis=1))
        sides.append(np.concatenate([high, high, low], axis=1))
    out["halo_x"] = np.stack(sides)
    high, low = halves(spectral_second(CZ) - 2.0 * np.eye(CZ))
    out["own_z"] = np.block([[high, low], [high, np.zeros_like(low)]])

    fine_z = np.arange(CZ)[:, None]
    coarse_z = np.arange(CZC)[None, :]
    weight_z = sum(
        spline_units((fine_z - 2 * coarse_z + image * CZ - 0.5) * 0.5) for image in range(-2, 3)
    )
    zero = np.zeros_like(weight_z.T)
    pair = np.block([[weight_z.T, zero], [zero, weight_z.T]])
    out["grow_z"] = np.concatenate([pair, pair], axis=0)
    zero = np.zeros_like(weight_z)
    out["shrink_z"] = np.block(
        [[weight_z, zero], [weight_z, zero], [zero, weight_z], [zero, weight_z]]
    )

    def column(coarse):
        return spline_units((np.arange(CX) - 2 * coarse - 0.5) * 0.5)

    own = np.stack([column(j) for j in range(CXC)], axis=1)
    lower = {j: column(j) for j in (-2, -1, 0, 1)}
    upper = {j: column(j) for j in (62, 63, 64, 65)}
    stack = lambda d: np.stack([d[j] for j in sorted(d)], axis=1)
    grow_old, grow_new, shrink = [], [], []
    inner = own.copy()
    inner[:, [0, 1, 62, 63]] = 0.0
    for core in range(2):
        near, far = (upper, lower) if core == 0 else (lower, upper)
        outside = lambda d: np.stack([d[j] for j in sorted(d) if j < 0 or j > 63], axis=1)
        old = np.concatenate([own, outside(near), outside(far), np.zeros((CX, 4))], axis=1)
        new = np.concatenate([inner, stack(near), stack(far)], axis=1)
        every = np.concatenate([own, stack(near), stack(far)], axis=1)
        grow_old.append(np.concatenate([old, old], axis=1))
        grow_new.append(np.concatenate([new, new], axis=1))
        shrink.append(np.concatenate([every.T, every.T], axis=1))
    out["grow_old"] = np.stack(grow_old)
    out["grow_new"] = np.stack(grow_new)
    out["shrink_x"] = np.stack(shrink)
    return {name: np.asarray(value).astype(ml_dtypes.bfloat16) for name, value in out.items()}


def taps():
    return [
        [
            (j, float(w))
            for j in range(CYC)
            for w in [
                sum(
                    spline_units(np.float64((i - 2 * j + image * CY - 0.5) * 0.5))
                    for image in range(-2, 3)
                )
            ]
            if w
        ]
        for i in range(CY)
    ]


def split(value):
    high = value.astype(BF)
    return high, (value - high.astype(F32)).astype(BF)


def dot(left, right):
    return jnp.dot(left, right, preferred_element_type=F32)


def cat(parts, axis):
    return jnp.concatenate(parts, axis=axis)


def interior(v, own_x, own_z, out):
    for j in range(CY // 2):
        one, two = 2 * j, 2 * j + 1
        high1, low1 = split(v[one])
        high2, low2 = split(v[two])
        x = dot(own_x[...], cat([cat([high1, high2], 1), cat([low1, low2], 1)], 0))
        z = dot(cat([cat([high1, low1], 1), cat([high2, low2], 1)], 0), own_z[...])
        x = x[:CX] + x[CX:]
        z = z[:, :CZ] + z[:, CZ:]
        beside = v[(one - 1) % CY] + v[two]
        out[one] = x[:, :CZ] + z[:CX] + beside
        beside = v[one] + v[(two + 1) % CY]
        out[two] = x[:, CZ:] + z[CX:] + beside


def halo_part(near, far, field, halo_x, pair):
    parts = []
    for y in (2 * pair, 2 * pair + 1):
        start = (field * CY + y) * OV
        high, low = split(cat([near[start : start + OV], far[start : start + OV]], 0))
        parts.append(cat([high, low, high], 0))
    return dot(halo_x, cat(parts, 1))


def edge_rows(v, core, near, far, field):
    near_row = pl.multiple_of((1 - core) * (CX - OV), OV)
    far_row = pl.multiple_of(core * (CX - OV), OV)
    for y in range(CY):
        start = (field * CY + y) * OV
        near[start : start + OV] = v[y, pl.ds(near_row, OV), :]
        far[start : start + OV] = v[y, pl.ds(far_row, OV), :]


def first_edges(p_lo, p_hi, q_lo, q_hi, coef, near, far):
    core = lax.axis_index("core")

    def fill(low, high, field):
        for y in range(CY):
            start = (field * CY + y) * OV
            rows = pl.ds(y, OV, stride=CY)
            first, last = low[rows, :], high[rows, :]
            near[start : start + OV] = jnp.where(core == 0, last, first)
            far[start : start + OV] = jnp.where(core == 0, first, last)

    fill(p_lo, p_hi, 0)
    fill(q_lo, q_hi, 1)
    base = 2 * CY * OV
    for row in range(2):
        for part in range(4):
            lanes = slice(part * 128, part * 128 + 128)
            first = coef[row : row + 1, lanes]
            last = coef[CXC - 2 + row : CXC - 1 + row, lanes]
            spot = base + row * 4 + part
            near[spot : spot + 1] = jnp.where(core == 0, last, first)
            far[spot : spot + 1] = jnp.where(core == 0, first, last)


def reorder(source, target):
    for y in range(CY):
        target[y] = source[pl.ds(y, CX, stride=CY), :]


def prepare(
    signs, index, wavelet, p_now, p_prev, q_now, q_prev, own_x, own_z,
    p0, p1, q0, q1, lap_p, lap_q, source, amounts,
):
    reorder(p_now, p0)
    reorder(q_now, q0)
    interior(p0, own_x, own_z, lap_p)
    interior(q0, own_x, own_z, lap_q)
    reorder(p_prev, p1)
    reorder(q_prev, q1)
    source[...] = jnp.zeros_like(source)
    lane = lax.broadcasted_iota(jnp.int32, (1, CZ), 1)

    def add(e, carry):
        spot = index[e]
        x, rest = spot // (CY * CZ), spot % (CY * CZ)
        y, z = rest // CZ, rest % CZ
        amount = (2 * signs[e] - 1).astype(F32)
        row = source[y, pl.ds(x, 1), :]
        source[y, pl.ds(x, 1), :] = row + jnp.where(lane == z, amount, 0.0)
        return carry

    lax.fori_loop(0, ELEMS, add, 0)
    for step in range(STEPS + 1):
        amounts[step] = jnp.full((8, CZ), wavelet[step], F32)


def grow(coef, grow_z, grow_x, write):
    wide = []
    for pair in range(CYC // 2):
        high, low = split(coef[:, pair * 128 : pair * 128 + 128])
        both = dot(cat([high, low], 1), grow_z[...])
        wide += [both[:, :CZ], both[:, CZ:]]
    weights = taps()
    for pair in range(CY // 2):
        parts = []
        for y in (2 * pair, 2 * pair + 1):
            mixed = None
            for j, w in weights[y]:
                term = wide[j] * w
                mixed = term if mixed is None else mixed + term
            parts.append(mixed)
        high, low = split(cat(parts, 1))
        fine = dot(grow_x, cat([high, low], 0))
        write(2 * pair, fine[:, :CZ])
        write(2 * pair + 1, fine[:, CZ:])


UNIT = 1.0 / 384.0**3


def speed(coef, near, far, grow_z, grow_old, sigma, squared, held):
    core = lax.axis_index("core")
    held[:CXC] = coef[...]
    held[CXC:] = jnp.zeros((ROWS - CXC, CYC * CZC), F32)
    base = 2 * CY * OV
    for row in range(2):
        for part in range(4):
            lanes = slice(part * 128, part * 128 + 128)
            spot = base + row * 4 + part
            held[CXC + row : CXC + row + 1, lanes] = near[spot : spot + 1]
            held[CXC + 2 + row : CXC + 3 + row, lanes] = far[spot : spot + 1]

    def write(y, fine):
        fine = fine * UNIT
        sigma[y] = fine
        squared[y] = fine * fine

    grow(held[...], grow_z, grow_old[core], write)


def advance(step, *refs):
    (near, far, p, p_before, q, q_before, lap_p, lap_q, squared, source, amounts, halo_x) = refs[:12]
    refs = refs[12:]
    core = lax.axis_index("core")
    columns = halo_x[core]
    weight = amounts[step, :1, :]
    if step == 2:
        old_lap, refs = refs[0], refs[1:]
    if step == 3:
        (old_lap, older_q, gathered, sigma), refs = refs[:4], refs[4:]
    if step < 3:
        p_new, q_new, near_out, far_out = refs[:4]
    else:
        p_new, near_out, far_out, image = refs[:4]
    refs = refs[4:]
    if step < 2:
        lap_out = refs[0]
    if step == 2:
        gathered = refs[0]
    for pair in range(CY // 2):
        extra_p = halo_part(near, far, 0, columns, pair)
        extra_q = halo_part(near, far, 1, columns, pair)
        for side in range(2):
            y = 2 * pair + side
            lanes = slice(side * CZ, side * CZ + CZ)
            lap = lap_p[y] + extra_p[:, lanes]
            lap_adj = lap_q[y] + extra_q[:, lanes]
            sq = squared[y]
            p_new[y] = 2.0 * p[y] - p_before[y] + sq * lap + source[y] * weight
            new_q = 2.0 * q[y] - q_before[y] + sq * lap_adj
            if step < 3:
                q_new[y] = new_q
            if step < 2:
                lap_out[y] = lap
            if step == 2:
                gathered[y] = q[y] * lap + new_q * old_lap[y]
            if step == 3:
                total = gathered[y] + older_q[y] * lap + new_q * old_lap[y]
                image[y] = 2.0 * sigma[y] * total
    edge_rows(p_new, core, near_out, far_out, 0)
    if step < 3:
        edge_rows(q_new, core, near_out, far_out, 1)


def inside(p, q, own_x, own_z, lap_p, lap_q):
    interior(p, own_x, own_z, lap_p)
    interior(q, own_x, own_z, lap_q)


def inside_one(p, own_x, own_z, lap_p):
    interior(p, own_x, own_z, lap_p)


def shrink(image, near_in, far_in, shrink_x, shrink_z, own, near, far):
    core = lax.axis_index("core")
    rows_x = shrink_x[core]
    narrow = [None] * CYC
    weights = taps()
    for pair in range(CY // 2):
        high, low = split(cat([image[2 * pair], image[2 * pair + 1]], 1))
        both = dot(rows_x, cat([high, low], 0))
        for side in range(2):
            part = both[:, side * CZ : side * CZ + CZ]
            for j, w in weights[2 * pair + side]:
                term = part * w
                narrow[j] = term if narrow[j] is None else narrow[j] + term
    pieces = []
    for pair in range(CYC // 2):
        parts = []
        for j in (2 * pair, 2 * pair + 1):
            parts += list(split(narrow[j]))
        pieces.append(dot(cat(parts, 1), shrink_z[...]) * UNIT)
    own[...] = cat(pieces, 1)
    field = CY * OV
    near[:field] = near_in[...]
    far[:field] = far_in[...]
    for row in range(4):
        for part in range(4):
            lanes = slice(part * 128, part * 128 + 128)
            spot = field + row * 4 + part
            near[spot : spot + 1] = own[CXC + row : CXC + row + 1, lanes]
            far[spot : spot + 1] = own[CXC + 4 + row : CXC + 5 + row, lanes]


def merge(own, near, far, out):
    out[...] = own[...]
    field = CY * OV
    for row in range(4):
        for part in range(4):
            lanes = slice(part * 128, part * 128 + 128)
            spot = field + row * 4 + part
            a, b = CXC + row, CXC + 4 + row
            out[a : a + 1, lanes] = own[a : a + 1, lanes] + near[spot : spot + 1]
            out[b : b + 1, lanes] = own[b : b + 1, lanes] + far[spot : spot + 1]


def squares(a, b, total, squared):
    core = lax.axis_index("core")
    total[...] = a[...] + b[...]
    chip = lax.axis_index("xh") * lax.axis_size("z") + lax.axis_index("z")
    chips = lax.axis_size("xh") * lax.axis_size("z")
    first = (core == 0) & (chip == 0)
    last = (core == 1) & (chip == chips - 1)
    total[CXC + 4 : CXC + 6] = jnp.where(first, 0.0, total[CXC + 4 : CXC + 6])
    total[CXC + 6 : CXC + 8] = jnp.where(last, 0.0, total[CXC + 6 : CXC + 8])
    total[0:2] = jnp.where(core == 0, total[CXC + 6 : CXC + 8], total[CXC + 2 : CXC + 4])
    total[CXC - 2 : CXC] = jnp.where(core == 0, total[CXC : CXC + 2], total[CXC + 4 : CXC + 6])
    value = total[:CXC]
    value = value * value
    rows = value[0:8]
    for r in range(1, CXC // 8):
        rows = rows + value[8 * r : 8 * r + 8]
    folded = rows[:, :128]
    for c in range(1, 4):
        folded = folded + rows[:, 128 * c : 128 * c + 128]
    squared[...] = folded


def last_terms(
    total, near, far, p, p_before, lap_p, source, amounts, halo_x, grow_z, grow_new,
    lap_out, base, change,
):
    core = lax.axis_index("core")
    columns = halo_x[core]
    weight = amounts[STEPS, :1, :]
    for pair in range(CY // 2):
        extra = halo_part(near, far, 0, columns, pair)
        for side in range(2):
            y = 2 * pair + side
            lap_out[y] = lap_p[y] + extra[:, side * CZ : side * CZ + CZ]
            base[y] = 2.0 * p[y] - p_before[y] + source[y] * weight

    def write(y, fine):
        change[y] = fine * UNIT

    grow(total[...], grow_z, grow_new[core], write)


def finish(count, parts, total, sigma, lap, base, change, direction, p_last):
    value = parts[0]
    for k in range(1, parts.shape[0]):
        value = value + parts[k]
    value = jnp.sum(jnp.sum(value, axis=0, keepdims=True), axis=1, keepdims=True)
    scale = jnp.sqrt(value * (1.0 / count) + EPSILON)
    inverse = 1.0 / scale
    direction[...] = total[:CXC] * inverse
    rate = LEARN * inverse
    for y in range(CY):
        new = sigma[y] - rate * change[y]
        p_last[pl.ds(y, CX, stride=CY), :] = base[y] + new * new * lap[y]


VM = pl.BlockSpec(memory_space=pltpu.VMEM)
SM = pl.BlockSpec(memory_space=pltpu.SMEM)
FIELD = jax.ShapeDtypeStruct((CY, CX, CZ), F32)
PARAMS = pltpu.CompilerParams(vmem_limit_bytes=16 * 2**20)


def rows_of(count, lanes=128):
    return jax.ShapeDtypeStruct((count, lanes), F32)


def call(body, outs, *args, smem=0, scratch=(), flops=0, name=None):
    size = sum(int(np.prod(a.shape)) * a.dtype.itemsize for a in args)
    return pl.pallas_call(
        body,
        out_shape=outs,
        in_specs=[SM] * smem + [VM] * (len(args) - smem),
        out_specs=jax.tree.map(lambda _: VM, outs),
        scratch_shapes=list(scratch),
        compiler_params=PARAMS,
        cost_estimate=pl.CostEstimate(flops=flops, bytes_accessed=size, transcendentals=0),
        name=name,
    )(*args)


def xor_swap(x, axis, mask):
    count = lax.axis_size(axis)
    if mask >= count:
        return jnp.zeros_like(x)
    return lax.ppermute(x, axis, [(i, i ^ mask) for i in range(count)])


def far_swap(x):
    count = lax.axis_size(TILE)
    pairs = [(i, i + 1) for i in range(1, count - 1, 2)]
    return lax.ppermute(x, TILE, pairs + [(b, a) for a, b in pairs])


def exchange(near, far):
    far = far_swap(far)
    near = xor_swap(near, "core", 1)
    return near, far


def on_device(p_now, p_prev, adj_now, adj_next, coef_old, signs, elem_index, wavelet):
    const = {name: jnp.asarray(value) for name, value in constants().items()}
    own_x, own_z, halo_x = const["own_x"], const["own_z"], const["halo_x"]
    flat = lambda a: a.reshape(CX * CY, CZ)
    p_now, p_prev, adj_now, adj_next = map(flat, (p_now, p_prev, adj_now, adj_next))

    edge = rows_of(2 * CY * OV)
    with_coef = rows_of(2 * CY * OV + 8)
    low = pl.BlockSpec((OV * CY, CZ), lambda i: (0, 0))
    high = pl.BlockSpec((OV * CY, CZ), lambda i: (CX // OV - 1, 0))
    near, far = pl.pallas_call(
        first_edges,
        grid=(1,),
        out_shape=(with_coef, with_coef),
        in_specs=[low, high, low, high, pl.BlockSpec((CXC, CYC * CZC), lambda i: (0, 0))],
        out_specs=(pl.BlockSpec(with_coef.shape, lambda i: (0, 0)),) * 2,
        name="first_edges",
    )(p_now, p_now, adj_now, adj_now, coef_old)
    near, far = exchange(near, far)

    p, p_before, q, q_before, lap_p, lap_q, source, amounts = call(
        prepare,
        (FIELD,) * 7 + (jax.ShapeDtypeStruct((STEPS + 1, 8, CZ), F32),),
        signs[0], elem_index, wavelet, p_now, p_prev, adj_now, adj_next, own_x, own_z,
        smem=3, flops=10**9, name="prepare",
    )
    sigma, squared = call(
        speed, (FIELD, FIELD), coef_old, near, far, const["grow_z"], const["grow_old"],
        scratch=[pltpu.VMEM((ROWS, CYC * CZC), F32)], flops=10**8, name="speed",
    )

    laps, qs = [], [q]
    gathered = None
    for step in range(STEPS):
        args = [near, far, p, p_before, q, q_before, lap_p, lap_q, squared, source, amounts, halo_x]
        body = functools.partial(advance, step)
        name = f"advance_{step}"
        if step < 2:
            outs = (FIELD, FIELD, edge, edge, FIELD)
        elif step == 2:
            args.append(laps[1])
            outs = (FIELD, FIELD, edge, edge, FIELD)
        else:
            args += [laps[0], qs[1], gathered, sigma]
            outs = (FIELD, rows_of(CY * OV), rows_of(CY * OV), FIELD)
        result = call(body, outs, *args, flops=10**8, name=name)
        if step < 3:
            p_new, q_new, near, far, other = result
            if step < 2:
                laps.append(other)
            else:
                gathered = other
            p, p_before = p_new, p
            q, q_before = q_new, q
            qs.append(q)
            near, far = exchange(near, far)
            lap_p, lap_q = call(
                inside, (FIELD, FIELD), p, q, own_x, own_z, flops=10**9, name=f"inside_{step}"
            )
        else:
            p_new, near, far, image = result
            p, p_before = p_new, p

    ends = rows_of(CY * OV + 16)
    own, near, far = call(
        shrink,
        (rows_of(ROWS, CYC * CZC), ends, ends),
        image, near, far, const["shrink_x"], const["shrink_z"], flops=10**8, name="shrink",
    )
    near, far = exchange(near, far)
    lap_p = call(inside_one, FIELD, p, own_x, own_z, flops=5 * 10**8, name="inside_last")
    partial = call(merge, rows_of(ROWS, CYC * CZC), own, near, far, name="merge")

    two, one, three = (xor_swap(partial, "y", m) for m in (2, 1, 3))
    partial = (partial + one) + (two + three)
    other = xor_swap(partial, "xl", 1)
    total, squared_sum = call(
        squares, (rows_of(ROWS, CYC * CZC), rows_of(8)), partial, other, name="squares"
    )
    squared_sum = squared_sum + xor_swap(squared_sum, "core", 1)
    squared_sum = squared_sum + xor_swap(squared_sum, "xh", 1)
    deep = lax.axis_size("z")
    parts = lax.all_to_all(
        jnp.broadcast_to(squared_sum, (deep, 8, 128)), "z", split_axis=0, concat_axis=0, tiled=True
    )
    lap_p, base, change = call(
        last_terms,
        (FIELD, FIELD, FIELD),
        total, near, far, p, p_before, lap_p, source, amounts, halo_x,
        const["grow_z"], const["grow_new"], flops=10**8, name="last_terms",
    )
    count = float(lax.axis_size(TILE) * CXC * CYC * CZC)
    direction, p_last = call(
        functools.partial(finish, count),
        (rows_of(CXC, CYC * CZC), rows_of(CX * CY)),
        parts, total, sigma, lap_p, base, change, name="finish",
    )
    return direction, p_last.reshape(1, CX, CY, CZ)


def solution(mesh):
    shots, tiles = mesh.shape["shot"], mesh.shape["tile"]
    fine = Mesh(
        mesh.devices.reshape(shots // 2, 2, 2, tiles // 4, 2), ("y", "xl", "xh", "z", "core")
    )
    placed = (
        P(SHOT, TILE, None, None),
        P(SHOT, TILE, None, None),
        P(SHOT, TILE, None, None),
        P(SHOT, TILE, None, None),
        P(TILE, None),
        P(SHOT, TILE),
        P(TILE),
        P(),
    )
    return jax.shard_map(
        on_device,
        mesh=fine,
        in_specs=placed,
        out_specs=(P(TILE, None), P(SHOT, TILE, None, None)),
        check_vma=False,
    )
```

```python
import functools

import jax
import jax.numpy as jnp
import ml_dtypes
import numpy as np
from jax import lax
from jax.experimental import pallas as pl
from jax.experimental.pallas import tpu as pltpu
from jax.sharding import Mesh
from jax.sharding import PartitionSpec as P

CX = 128
CZ = 128
CY = 16
OV = 8
STEPS = 4
ELEMS = 64
CXC = 64
CYC = 8
CZC = 64
ROWS = 72
LEARN = 0.02
EPSILON = 1e-06
BF = jnp.bfloat16
F32 = jnp.float32
SHOT = ("y", "xl")
TILE = ("xh", "z", "core")


def spectral_second(length):
    index = np.arange(length)
    number = np.minimum(index, length - index) * (2.0 * np.pi / length)
    phase = (index[:, None, None] - index[None, :, None]) * index[None, None, :] % length
    return -np.sum(number**2 * np.cos(2.0 * np.pi / length * phase), axis=2) / length


def spline_units(offset):
    mag = np.abs(offset)
    inner = 2.0 / 3.0 - mag**2 + 0.5 * mag**3
    outer = (2.0 - mag) ** 3 / 6.0
    return np.round(384.0 * np.where(mag < 1.0, inner, np.where(mag < 2.0, outer, 0.0)))


def halves(matrix):
    high = matrix.astype(np.float32).astype(ml_dtypes.bfloat16)
    low = (matrix - high.astype(np.float64)).astype(np.float32).astype(ml_dtypes.bfloat16)
    return high, low


@functools.cache
def constants():
    out = {}
    second_x = spectral_second(CX + 2 * OV)[OV : OV + CX]
    ramp = np.sin(0.5 * np.pi * (np.arange(OV) + 0.5) / OV) ** 2
    left = second_x[:, :OV] * ramp[None, :]
    right = second_x[:, OV + CX :] * ramp[None, ::-1]
    high, low = halves(second_x[:, OV : OV + CX])
    out["own_x"] = np.block([[high, high], [low, np.zeros_like(low)]])
    sides = []
    for pair in ((right, left), (left, right)):
        high, low = halves(np.concatenate(pair, axis=1))
        sides.append(np.concatenate([high, high, low], axis=1))
    out["halo_x"] = np.stack(sides)
    high, low = halves(spectral_second(CZ) - 2.0 * np.eye(CZ))
    out["own_z"] = np.block([[high, low], [high, np.zeros_like(low)]])

    fine_z = np.arange(CZ)[:, None]
    coarse_z = np.arange(CZC)[None, :]
    weight_z = sum(
        spline_units((fine_z - 2 * coarse_z + image * CZ - 0.5) * 0.5) for image in range(-2, 3)
    )
    zero = np.zeros_like(weight_z.T)
    pair = np.block([[weight_z.T, zero], [zero, weight_z.T]])
    out["grow_z"] = np.concatenate([pair, pair], axis=0)
    zero = np.zeros_like(weight_z)
    out["shrink_z"] = np.block(
        [[weight_z, zero], [weight_z, zero], [zero, weight_z], [zero, weight_z]]
    )

    def column(coarse):
        return spline_units((np.arange(CX) - 2 * coarse - 0.5) * 0.5)

    own = np.stack([column(j) for j in range(CXC)], axis=1)
    lower = {j: column(j) for j in (-2, -1, 0, 1)}
    upper = {j: column(j) for j in (62, 63, 64, 65)}
    stack = lambda d: np.stack([d[j] for j in sorted(d)], axis=1)
    grow_old, grow_new, shrink = [], [], []
    inner = own.copy()
    inner[:, [0, 1, 62, 63]] = 0.0
    for core in range(2):
        near, far = (upper, lower) if core == 0 else (lower, upper)
        outside = lambda d: np.stack([d[j] for j in sorted(d) if j < 0 or j > 63], axis=1)
        old = np.concatenate([own, outside(near), outside(far), np.zeros((CX, 4))], axis=1)
        new = np.concatenate([inner, stack(near), stack(far)], axis=1)
        every = np.concatenate([own, stack(near), stack(far)], axis=1)
        grow_old.append(np.concatenate([old, old], axis=1))
        grow_new.append(np.concatenate([new, new], axis=1))
        shrink.append(np.concatenate([every.T, every.T], axis=1))
    out["grow_old"] = np.stack(grow_old)
    out["grow_new"] = np.stack(grow_new)
    out["shrink_x"] = np.stack(shrink)
    return {name: np.asarray(value).astype(ml_dtypes.bfloat16) for name, value in out.items()}


def taps():
    return [
        [
            (j, float(w))
            for j in range(CYC)
            for w in [
                sum(
                    spline_units(np.float64((i - 2 * j + image * CY - 0.5) * 0.5))
                    for image in range(-2, 3)
                )
            ]
            if w
        ]
        for i in range(CY)
    ]


def split(value):
    high = value.astype(BF)
    return high, (value - high.astype(F32)).astype(BF)


def dot(left, right):
    return jnp.dot(left, right, preferred_element_type=F32)


def cat(parts, axis):
    return jnp.concatenate(parts, axis=axis)


def interior(v, own_x, own_z, out):
    for j in range(CY // 2):
        one, two = 2 * j, 2 * j + 1
        high1, low1 = split(v[one])
        high2, low2 = split(v[two])
        x = dot(own_x[...], cat([cat([high1, high2], 1), cat([low1, low2], 1)], 0))
        z = dot(cat([cat([high1, low1], 1), cat([high2, low2], 1)], 0), own_z[...])
        x = x[:CX] + x[CX:]
        z = z[:, :CZ] + z[:, CZ:]
        beside = v[(one - 1) % CY] + v[two]
        out[one] = x[:, :CZ] + z[:CX] + beside
        beside = v[one] + v[(two + 1) % CY]
        out[two] = x[:, CZ:] + z[CX:] + beside


def halo_part(near, far, field, halo_x, pair):
    parts = []
    for y in (2 * pair, 2 * pair + 1):
        start = (field * CY + y) * OV
        high, low = split(cat([near[start : start + OV], far[start : start + OV]], 0))
        parts.append(cat([high, low, high], 0))
    return dot(halo_x, cat(parts, 1))


def edge_rows(v, core, near, far, field):
    near_row = pl.multiple_of((1 - core) * (CX - OV), OV)
    far_row = pl.multiple_of(core * (CX - OV), OV)
    for y in range(CY):
        start = (field * CY + y) * OV
        near[start : start + OV] = v[y, pl.ds(near_row, OV), :]
        far[start : start + OV] = v[y, pl.ds(far_row, OV), :]


def first_edges(p, q, coef, near, far, p_lo, p_hi, q_lo, q_hi, c_lo, c_hi, sems):
    core = lax.axis_index("core")
    block = OV * CY
    copies = [
        pltpu.make_async_copy(source.at[pl.ds(start, size)], target, sems.at[k])
        for k, (source, start, size, target) in enumerate(
            (
                (p, 0, block, p_lo),
                (p, CX * CY - block, block, p_hi),
                (q, 0, block, q_lo),
                (q, CX * CY - block, block, q_hi),
                (coef, 0, 8, c_lo),
                (coef, CXC - 8, 8, c_hi),
            )
        )
    ]
    for copy in copies:
        copy.start()

    def fill(low, high, field):
        for y in range(CY):
            start = (field * CY + y) * OV
            rows = pl.ds(y, OV, stride=CY)
            first, last = low[rows, :], high[rows, :]
            near[start : start + OV] = jnp.where(core == 0, last, first)
            far[start : start + OV] = jnp.where(core == 0, first, last)

    copies[0].wait()
    copies[1].wait()
    fill(p_lo, p_hi, 0)
    copies[2].wait()
    copies[3].wait()
    fill(q_lo, q_hi, 1)
    copies[4].wait()
    copies[5].wait()
    base = 2 * CY * OV
    for row in range(2):
        for part in range(4):
            lanes = slice(part * 128, part * 128 + 128)
            first = c_lo[row : row + 1, lanes]
            last = c_hi[6 + row : 7 + row, lanes]
            spot = base + row * 4 + part
            near[spot : spot + 1] = jnp.where(core == 0, last, first)
            far[spot : spot + 1] = jnp.where(core == 0, first, last)


def reorder(source, target):
    for y in range(CY):
        target[y] = source[pl.ds(y, CX, stride=CY), :]


def prepare(
    signs, index, wavelet, p_now, q_now, own_x, own_z,
    p0, q0, lap_p, lap_q, source, amounts,
):
    reorder(p_now, p0)
    reorder(q_now, q0)
    interior(p0, own_x, own_z, lap_p)
    interior(q0, own_x, own_z, lap_q)
    source[...] = jnp.zeros_like(source)
    lane = lax.broadcasted_iota(jnp.int32, (1, CZ), 1)

    def add(e, carry):
        spot = index[e]
        x, rest = spot // (CY * CZ), spot % (CY * CZ)
        y, z = rest // CZ, rest % CZ
        amount = (2 * signs[e] - 1).astype(F32)
        row = source[y, pl.ds(x, 1), :]
        source[y, pl.ds(x, 1), :] = row + jnp.where(lane == z, amount, 0.0)
        return carry

    lax.fori_loop(0, ELEMS, add, 0)
    for step in range(STEPS + 1):
        amounts[step] = jnp.full((8, CZ), wavelet[step], F32)


def grow(coef, grow_z, grow_x, write):
    wide = []
    for pair in range(CYC // 2):
        high, low = split(coef[:, pair * 128 : pair * 128 + 128])
        both = dot(cat([high, low], 1), grow_z[...])
        wide += [both[:, :CZ], both[:, CZ:]]
    weights = taps()
    for pair in range(CY // 2):
        parts = []
        for y in (2 * pair, 2 * pair + 1):
            mixed = None
            for j, w in weights[y]:
                term = wide[j] * w
                mixed = term if mixed is None else mixed + term
            parts.append(mixed)
        high, low = split(cat(parts, 1))
        fine = dot(grow_x, cat([high, low], 0))
        write(2 * pair, fine[:, :CZ])
        write(2 * pair + 1, fine[:, CZ:])


UNIT = 1.0 / 384.0**3


def speed(coef, near, far, grow_z, grow_old, sigma, squared, held):
    core = lax.axis_index("core")
    held[:CXC] = coef[...]
    held[CXC:] = jnp.zeros((ROWS - CXC, CYC * CZC), F32)
    base = 2 * CY * OV
    for row in range(2):
        for part in range(4):
            lanes = slice(part * 128, part * 128 + 128)
            spot = base + row * 4 + part
            held[CXC + row : CXC + row + 1, lanes] = near[spot : spot + 1]
            held[CXC + 2 + row : CXC + 3 + row, lanes] = far[spot : spot + 1]

    def write(y, fine):
        fine = fine * UNIT
        sigma[y] = fine
        squared[y] = fine * fine

    grow(held[...], grow_z, grow_old[core], write)


def advance(step, *refs):
    (near, far, p, p_before, q, q_before, lap_p, lap_q, squared, source, amounts, halo_x) = refs[:12]
    refs = refs[12:]
    core = lax.axis_index("core")
    columns = halo_x[core]
    weight = amounts[step, :1, :]
    if step == 2:
        old_lap, refs = refs[0], refs[1:]
    if step == 3:
        (old_lap, older_q, gathered, sigma), refs = refs[:4], refs[4:]
    if step < 3:
        p_new, q_new, near_out, far_out = refs[:4]
    else:
        p_new, near_out, far_out, image = refs[:4]
    refs = refs[4:]
    if step < 2:
        lap_out = refs[0]
    if step == 2:
        gathered = refs[0]
    for pair in range(CY // 2):
        extra_p = halo_part(near, far, 0, columns, pair)
        extra_q = halo_part(near, far, 1, columns, pair)
        for side in range(2):
            y = 2 * pair + side
            lanes = slice(side * CZ, side * CZ + CZ)
            lap = lap_p[y] + extra_p[:, lanes]
            lap_adj = lap_q[y] + extra_q[:, lanes]
            sq = squared[y]
            if step == 0:
                rows = pl.ds(y, CX, stride=CY)
                old_p, old_q = p_before[rows, :], q_before[rows, :]
            else:
                old_p, old_q = p_before[y], q_before[y]
            p_new[y] = 2.0 * p[y] - old_p + sq * lap + source[y] * weight
            new_q = 2.0 * q[y] - old_q + sq * lap_adj
            if step < 3:
                q_new[y] = new_q
            if step < 2:
                lap_out[y] = lap
            if step == 2:
                gathered[y] = q[y] * lap + new_q * old_lap[y]
            if step == 3:
                total = gathered[y] + older_q[y] * lap + new_q * old_lap[y]
                image[y] = 2.0 * sigma[y] * total
    edge_rows(p_new, core, near_out, far_out, 0)
    if step < 3:
        edge_rows(q_new, core, near_out, far_out, 1)


def inside(p, q, own_x, own_z, lap_p, lap_q):
    interior(p, own_x, own_z, lap_p)
    interior(q, own_x, own_z, lap_q)


def inside_one(p, own_x, own_z, lap_p):
    interior(p, own_x, own_z, lap_p)


def shrink(image, near_in, far_in, shrink_x, shrink_z, own, near, far):
    core = lax.axis_index("core")
    rows_x = shrink_x[core]
    narrow = [None] * CYC
    weights = taps()
    for pair in range(CY // 2):
        high, low = split(cat([image[2 * pair], image[2 * pair + 1]], 1))
        both = dot(rows_x, cat([high, low], 0))
        for side in range(2):
            part = both[:, side * CZ : side * CZ + CZ]
            for j, w in weights[2 * pair + side]:
                term = part * w
                narrow[j] = term if narrow[j] is None else narrow[j] + term
    pieces = []
    for pair in range(CYC // 2):
        parts = []
        for j in (2 * pair, 2 * pair + 1):
            parts += list(split(narrow[j]))
        pieces.append(dot(cat(parts, 1), shrink_z[...]) * UNIT)
    own[...] = cat(pieces, 1)
    field = CY * OV
    near[:field] = near_in[...]
    far[:field] = far_in[...]
    for row in range(4):
        for part in range(4):
            lanes = slice(part * 128, part * 128 + 128)
            spot = field + row * 4 + part
            near[spot : spot + 1] = own[CXC + row : CXC + row + 1, lanes]
            far[spot : spot + 1] = own[CXC + 4 + row : CXC + 5 + row, lanes]


def merge(own, near, far, out):
    out[...] = own[...]
    field = CY * OV
    for row in range(4):
        for part in range(4):
            lanes = slice(part * 128, part * 128 + 128)
            spot = field + row * 4 + part
            a, b = CXC + row, CXC + 4 + row
            out[a : a + 1, lanes] = own[a : a + 1, lanes] + near[spot : spot + 1]
            out[b : b + 1, lanes] = own[b : b + 1, lanes] + far[spot : spot + 1]


def squares(a, b, total, squared):
    core = lax.axis_index("core")
    total[...] = a[...] + b[...]
    chip = lax.axis_index("xh") * lax.axis_size("z") + lax.axis_index("z")
    chips = lax.axis_size("xh") * lax.axis_size("z")
    first = (core == 0) & (chip == 0)
    last = (core == 1) & (chip == chips - 1)
    total[CXC + 4 : CXC + 6] = jnp.where(first, 0.0, total[CXC + 4 : CXC + 6])
    total[CXC + 6 : CXC + 8] = jnp.where(last, 0.0, total[CXC + 6 : CXC + 8])
    total[0:2] = jnp.where(core == 0, total[CXC + 6 : CXC + 8], total[CXC + 2 : CXC + 4])
    total[CXC - 2 : CXC] = jnp.where(core == 0, total[CXC : CXC + 2], total[CXC + 4 : CXC + 6])
    value = total[:CXC]
    value = value * value
    rows = value[0:8]
    for r in range(1, CXC // 8):
        rows = rows + value[8 * r : 8 * r + 8]
    folded = rows[:, :128]
    for c in range(1, 4):
        folded = folded + rows[:, 128 * c : 128 * c + 128]
    squared[...] = folded


def last_fields(near, far, p, p_before, lap_p, source, amounts, halo_x, lap_out, base):
    core = lax.axis_index("core")
    columns = halo_x[core]
    weight = amounts[STEPS, :1, :]
    for pair in range(CY // 2):
        extra = halo_part(near, far, 0, columns, pair)
        for side in range(2):
            y = 2 * pair + side
            lap_out[y] = lap_p[y] + extra[:, side * CZ : side * CZ + CZ]
            base[y] = 2.0 * p[y] - p_before[y] + source[y] * weight


def add_four(own, one, two, three, out):
    out[...] = (own[...] + one[...]) + (two[...] + three[...])


def spread(total, sigma, lap, base, grow_z, grow_new, zeroth, first, second):
    core = lax.axis_index("core")

    def write(y, fine):
        change = fine * UNIT
        old, curve = sigma[y], lap[y]
        scaled = change * curve
        zeroth[y] = base[y] + old * old * curve
        first[y] = -2.0 * old * scaled
        second[y] = change * scaled

    grow(total[...], grow_z, grow_new[core], write)


def widen(a, b, out):
    value = a[...] + b[...]
    for k in range(out.shape[0]):
        out[k] = value


def finish(count, parts, total, zeroth, first, second, direction, p_last):
    value = parts[0]
    for k in range(1, parts.shape[0]):
        value = value + parts[k]
    value = jnp.sum(jnp.sum(value, axis=0, keepdims=True), axis=1, keepdims=True)
    scale = jnp.sqrt(value * (1.0 / count) + EPSILON)
    inverse = 1.0 / scale
    direction[...] = total[:CXC] * inverse
    rate = LEARN * inverse
    for y in range(CY):
        value = zeroth[y] + rate * (first[y] + rate * second[y])
        p_last[pl.ds(y, CX, stride=CY), :] = value


VM = pl.BlockSpec(memory_space=pltpu.VMEM)
SM = pl.BlockSpec(memory_space=pltpu.SMEM)
FIELD = jax.ShapeDtypeStruct((CY, CX, CZ), F32)
PARAMS = pltpu.CompilerParams(vmem_limit_bytes=4 * 2**20)


def rows_of(count, lanes=128):
    return jax.ShapeDtypeStruct((count, lanes), F32)


def call(body, outs, *args, smem=0, scratch=(), flops=0, name=None, held=()):
    size = sum(int(np.prod(a.shape)) * a.dtype.itemsize for a in args)
    count = len(args)

    def run(*refs):
        body(*refs[:count], *refs[count + len(held) :])

    return pl.pallas_call(
        run,
        out_shape=outs,
        in_specs=[SM] * smem
        + [VM] * (count - smem)
        + [pl.BlockSpec(memory_space=pl.ANY)] * len(held),
        out_specs=jax.tree.map(lambda _: VM, outs),
        scratch_shapes=list(scratch),
        compiler_params=PARAMS,
        cost_estimate=pl.CostEstimate(flops=flops, bytes_accessed=size, transcendentals=0),
        name=name,
    )(*args, *held)


def xor_swap(x, axis, mask):
    count = lax.axis_size(axis)
    if mask >= count:
        return jnp.zeros_like(x)
    return lax.ppermute(x, axis, [(i, i ^ mask) for i in range(count)])


def far_swap(x):
    count = lax.axis_size(TILE)
    pairs = [(i, i + 1) for i in range(1, count - 1, 2)]
    return lax.ppermute(x, TILE, pairs + [(b, a) for a, b in pairs])


def exchange(near, far):
    far = far_swap(far)
    near = xor_swap(near, "core", 1)
    return near, far


def on_device(p_now, p_prev, adj_now, adj_next, coef_old, signs, elem_index, wavelet):
    const = {name: jnp.asarray(value) for name, value in constants().items()}
    own_x, own_z, halo_x = const["own_x"], const["own_z"], const["halo_x"]
    flat = lambda a: a.reshape(CX * CY, CZ)
    p_now, p_prev, adj_now, adj_next = map(flat, (p_now, p_prev, adj_now, adj_next))

    edge = rows_of(2 * CY * OV)
    with_coef = rows_of(2 * CY * OV + 8)
    block = pltpu.VMEM((OV * CY, CZ), F32)
    few = pltpu.VMEM((8, CYC * CZC), F32)
    near, far = pl.pallas_call(
        first_edges,
        out_shape=(with_coef, with_coef),
        in_specs=[pl.BlockSpec(memory_space=pltpu.HBM)] * 3,
        out_specs=(VM, VM),
        scratch_shapes=[block] * 4 + [few] * 2 + [pltpu.SemaphoreType.DMA((6,))],
        compiler_params=PARAMS,
        name="first_edges",
    )(*(pltpu.with_memory_space_constraint(a, pltpu.HBM) for a in (p_now, adj_now, coef_old)))
    near, far = exchange(near, far)

    p, q, lap_p, lap_q, source, amounts = call(
        prepare,
        (FIELD,) * 5 + (jax.ShapeDtypeStruct((STEPS + 1, 8, CZ), F32),),
        signs[0], elem_index, wavelet, p_now, adj_now, own_x, own_z,
        smem=3, flops=10**9, name="prepare",
    )
    sigma, squared = call(
        speed, (FIELD, FIELD), coef_old, near, far, const["grow_z"], const["grow_old"],
        scratch=[pltpu.VMEM((ROWS, CYC * CZC), F32)], flops=10**8, name="speed",
    )

    p_before, q_before = p_prev, adj_next
    laps, qs = [], [q]
    gathered = None
    for step in range(STEPS):
        args = [near, far, p, p_before, q, q_before, lap_p, lap_q, squared, source, amounts, halo_x]
        body = functools.partial(advance, step)
        name = f"advance_{step}"
        if step < 2:
            outs = (FIELD, FIELD, edge, edge, FIELD)
        elif step == 2:
            args.append(laps[1])
            outs = (FIELD, FIELD, edge, edge, FIELD)
        else:
            args += [laps[0], qs[1], gathered, sigma]
            outs = (FIELD, rows_of(CY * OV), rows_of(CY * OV), FIELD)
        result = call(body, outs, *args, flops=10**8, name=name)
        if step < 3:
            p_new, q_new, near, far, other = result
            if step < 2:
                laps.append(other)
            else:
                gathered = other
            p, p_before = p_new, p
            q, q_before = q_new, q
            qs.append(q)
            near, far = exchange(near, far)
            lap_p, lap_q = call(
                inside, (FIELD, FIELD), p, q, own_x, own_z, flops=10**9, name=f"inside_{step}"
            )
        else:
            p_new, near, far, image = result
            p, p_before = p_new, p

    ends = rows_of(CY * OV + 16)
    own, near, far = call(
        shrink,
        (rows_of(ROWS, CYC * CZC), ends, ends),
        image, near, far, const["shrink_x"], const["shrink_z"], flops=10**8, name="shrink",
    )
    near, far = exchange(near, far)
    lap_p = call(inside_one, FIELD, p, own_x, own_z, flops=5 * 10**8, name="inside_last")
    partial = call(merge, rows_of(ROWS, CYC * CZC), own, near, far, name="merge")

    two, one, three = (xor_swap(partial, "y", m) for m in (2, 1, 3))
    lap_p, base = call(
        last_fields, (FIELD, FIELD), near, far, p, p_before, lap_p, source, amounts, halo_x,
        flops=10**8, name="last_fields",
    )
    held = (lap_p, base)
    partial = call(
        add_four, rows_of(ROWS, CYC * CZC), partial, one, two, three, name="add_four", held=held
    )
    other = xor_swap(partial, "xl", 1)
    total, squared_sum = call(
        squares, (rows_of(ROWS, CYC * CZC), rows_of(8)), partial, other, name="squares",
        held=held,
    )
    squared_sum = squared_sum + xor_swap(squared_sum, "core", 1)
    terms = call(
        spread, (FIELD,) * 3, total, sigma, lap_p, base, const["grow_z"], const["grow_new"],
        flops=10**8, name="spread",
    )
    deep = lax.axis_size("z")
    copies = call(
        widen, jax.ShapeDtypeStruct((deep, 8, 128), F32),
        squared_sum, xor_swap(squared_sum, "xh", 1), name="widen", held=terms,
    )
    parts = lax.all_to_all(copies, "z", split_axis=0, concat_axis=0, tiled=True)
    count = float(lax.axis_size(TILE) * CXC * CYC * CZC)
    direction, p_last = call(
        functools.partial(finish, count),
        (rows_of(CXC, CYC * CZC), rows_of(CX * CY)),
        parts, total, *terms, name="finish",
    )
    return direction, p_last.reshape(1, CX, CY, CZ)


def solution(mesh):
    shots, tiles = mesh.shape["shot"], mesh.shape["tile"]
    fine = Mesh(
        mesh.devices.reshape(shots // 2, 2, 2, tiles // 4, 2), ("y", "xl", "xh", "z", "core")
    )
    placed = (
        P(SHOT, TILE, None, None),
        P(SHOT, TILE, None, None),
        P(SHOT, TILE, None, None),
        P(SHOT, TILE, None, None),
        P(TILE, None),
        P(SHOT, TILE),
        P(TILE),
        P(),
    )
    return jax.shard_map(
        on_device,
        mesh=fine,
        in_specs=placed,
        out_specs=(P(TILE, None), P(SHOT, TILE, None, None)),
        check_vma=False,
    )
```

```python
import functools

import jax
import jax.numpy as jnp
import ml_dtypes
import numpy as np
from jax import lax
from jax.experimental import pallas as pl
from jax.experimental.pallas import tpu as pltpu
from jax.sharding import Mesh
from jax.sharding import PartitionSpec as P

CX = 128
CZ = 128
CY = 16
OV = 8
STEPS = 4
ELEMS = 64
CXC = 64
CYC = 8
CZC = 64
ROWS = 72
LEARN = 0.02
EPSILON = 1e-06
BF = jnp.bfloat16
F32 = jnp.float32
SHOT = ("y", "xl")
TILE = ("xh", "z", "core")


def spectral_second(length):
    index = np.arange(length)
    number = np.minimum(index, length - index) * (2.0 * np.pi / length)
    phase = (index[:, None, None] - index[None, :, None]) * index[None, None, :] % length
    return -np.sum(number**2 * np.cos(2.0 * np.pi / length * phase), axis=2) / length


def spline_units(offset):
    mag = np.abs(offset)
    inner = 2.0 / 3.0 - mag**2 + 0.5 * mag**3
    outer = (2.0 - mag) ** 3 / 6.0
    return np.round(384.0 * np.where(mag < 1.0, inner, np.where(mag < 2.0, outer, 0.0)))


def halves(matrix):
    high = matrix.astype(np.float32).astype(ml_dtypes.bfloat16)
    low = (matrix - high.astype(np.float64)).astype(np.float32).astype(ml_dtypes.bfloat16)
    return high, low


def narrow_band(matrix):
    high, low = halves(np.pad(matrix, ((0, OV), (0, OV))))
    return np.concatenate([high, high, low], axis=1)


@functools.cache
def constants():
    out = {}
    second_x = spectral_second(CX + 2 * OV)[OV : OV + CX]
    ramp = np.sin(0.5 * np.pi * (np.arange(OV) + 0.5) / OV) ** 2
    left = second_x[:, :OV] * ramp[None, :]
    right = second_x[:, OV + CX :] * ramp[None, ::-1]
    high, low = halves(second_x[:, OV : OV + CX])
    out["own_x"] = np.block([[high, high], [low, np.zeros_like(low)]])
    sides = []
    for pair in ((right, left), (left, right)):
        high, low = halves(np.concatenate(pair, axis=1))
        sides.append(np.concatenate([high, high, low], axis=1))
    out["halo_x"] = np.stack(sides)
    near_part, cross_part = [], []
    for core in range(2):
        rows = slice(0, OV) if core == 0 else slice(CX - OV, CX)
        near_part.append(narrow_band((right if core == 0 else left)[rows]))
        rows = slice(CX - OV, CX) if core == 0 else slice(0, OV)
        cross_part.append(narrow_band((right if core == 0 else left)[rows]))
    out["near_x"] = np.stack(near_part)
    out["cross_x"] = np.stack(cross_part)
    high, low = halves(spectral_second(CZ) - 2.0 * np.eye(CZ))
    out["own_z"] = np.block([[high, low], [high, np.zeros_like(low)]])

    fine_z = np.arange(CZ)[:, None]
    coarse_z = np.arange(CZC)[None, :]
    weight_z = sum(
        spline_units((fine_z - 2 * coarse_z + image * CZ - 0.5) * 0.5) for image in range(-2, 3)
    )
    zero = np.zeros_like(weight_z.T)
    pair = np.block([[weight_z.T, zero], [zero, weight_z.T]])
    out["grow_z"] = np.concatenate([pair, pair], axis=0)
    zero = np.zeros_like(weight_z)
    out["shrink_z"] = np.block(
        [[weight_z, zero], [weight_z, zero], [zero, weight_z], [zero, weight_z]]
    )

    def column(coarse, start=0, count=CX):
        return spline_units((np.arange(start, start + count) - 2 * coarse - 0.5) * 0.5)

    own = np.stack([column(j) for j in range(CXC)], axis=1)
    lower = {j: column(j) for j in (-2, -1, 0, 1)}
    upper = {j: column(j) for j in (62, 63, 64, 65)}
    stack = lambda d: np.stack([d[j] for j in sorted(d)], axis=1)
    grow_old, grow_new, shrink = [], [], []
    inner = own.copy()
    inner[:, [0, 1, 62, 63]] = 0.0
    for core in range(2):
        near, far = (upper, lower) if core == 0 else (lower, upper)
        near_two, far_six = ((64, 65), range(-6, 0)) if core == 0 else ((-2, -1), range(64, 70))
        beyond = -OV if core == 0 else CX
        old = np.stack(
            [
                np.concatenate([column(j), column(j, beyond, OV)])
                for j in (*range(CXC), *near_two, *far_six)
            ],
            axis=1,
        )
        new = np.concatenate([inner, stack(near), stack(far)], axis=1)
        every = np.concatenate([own, stack(near), stack(far)], axis=1)
        grow_old.append(np.concatenate([old, old], axis=1))
        grow_new.append(np.concatenate([new, new], axis=1))
        shrink.append(np.concatenate([every.T, every.T], axis=1))
    out["grow_old"] = np.stack(grow_old)
    out["grow_new"] = np.stack(grow_new)
    out["shrink_x"] = np.stack(shrink)
    return {name: np.asarray(value).astype(ml_dtypes.bfloat16) for name, value in out.items()}


def taps():
    return [
        [
            (j, float(w))
            for j in range(CYC)
            for w in [
                sum(
                    spline_units(np.float64((i - 2 * j + image * CY - 0.5) * 0.5))
                    for image in range(-2, 3)
                )
            ]
            if w
        ]
        for i in range(CY)
    ]


def split(value):
    high = value.astype(BF)
    return high, (value - high.astype(F32)).astype(BF)


def dot(left, right):
    return jnp.dot(left, right, preferred_element_type=F32)


def cat(parts, axis):
    return jnp.concatenate(parts, axis=axis)


def interior(v, own_x, own_z, out):
    for j in range(CY // 2):
        one, two = 2 * j, 2 * j + 1
        high1, low1 = split(v[one])
        high2, low2 = split(v[two])
        x = dot(own_x[...], cat([cat([high1, high2], 1), cat([low1, low2], 1)], 0))
        z = dot(cat([cat([high1, low1], 1), cat([high2, low2], 1)], 0), own_z[...])
        x = x[:CX] + x[CX:]
        z = z[:, :CZ] + z[:, CZ:]
        beside = v[(one - 1) % CY] + v[two]
        out[one] = x[:, :CZ] + z[:CX] + beside
        beside = v[one] + v[(two + 1) % CY]
        out[two] = x[:, CZ:] + z[CX:] + beside


def halo_part(near, far, field, halo_x, pair):
    parts = []
    for y in (2 * pair, 2 * pair + 1):
        start = (field * CY + y) * OV
        high, low = split(cat([near[start : start + OV], far[start : start + OV]], 0))
        parts.append(cat([high, low, high], 0))
    return dot(halo_x, cat(parts, 1))


def edge_rows(v, core, near, far, field):
    near_row = pl.multiple_of((1 - core) * (CX - OV), OV)
    far_row = pl.multiple_of(core * (CX - OV), OV)
    for y in range(CY):
        start = (field * CY + y) * OV
        near[start : start + OV] = v[y, pl.ds(near_row, OV), :]
        if far is not None:
            far[start : start + OV] = v[y, pl.ds(far_row, OV), :]


def first_edges(p, q, coef, near, far, p_lo, p_hi, q_lo, q_hi, c_lo, c_hi, sems):
    core = lax.axis_index("core")
    block = OV * CY
    copies = [
        pltpu.make_async_copy(source.at[pl.ds(start, size)], target, sems.at[k])
        for k, (source, start, size, target) in enumerate(
            (
                (p, 0, block, p_lo),
                (p, CX * CY - block, block, p_hi),
                (q, 0, block, q_lo),
                (q, CX * CY - block, block, q_hi),
                (coef, 0, 8, c_lo),
                (coef, CXC - 8, 8, c_hi),
            )
        )
    ]
    for copy in copies:
        copy.start()

    def fill(low, high, field):
        for y in range(CY):
            start = (field * CY + y) * OV
            rows = pl.ds(y, OV, stride=CY)
            first, last = low[rows, :], high[rows, :]
            near[start : start + OV] = jnp.where(core == 0, last, first)
            far[start : start + OV] = jnp.where(core == 0, first, last)

    copies[0].wait()
    copies[1].wait()
    fill(p_lo, p_hi, 0)
    copies[2].wait()
    copies[3].wait()
    fill(q_lo, q_hi, 1)
    copies[4].wait()
    copies[5].wait()
    base = 2 * CY * OV
    for row in range(6):
        for part in range(4):
            lanes = slice(part * 128, part * 128 + 128)
            spot = base + row * 4 + part
            if row < 2:
                first = c_lo[row : row + 1, lanes]
                last = c_hi[6 + row : 7 + row, lanes]
                near[spot : spot + 1] = jnp.where(core == 0, last, first)
            first = c_lo[row : row + 1, lanes]
            last = c_hi[2 + row : 3 + row, lanes]
            far[spot : spot + 1] = jnp.where(core == 0, first, last)


def reorder(source, target):
    for y in range(CY):
        target[y] = source[pl.ds(y, CX, stride=CY), :]


def prepare(
    signs, index, wavelet, p_now, q_now, own_x, own_z,
    p0, q0, lap_p, lap_q, source, amounts,
):
    reorder(p_now, p0)
    reorder(q_now, q0)
    interior(p0, own_x, own_z, lap_p)
    interior(q0, own_x, own_z, lap_q)
    source[...] = jnp.zeros_like(source)
    lane = lax.broadcasted_iota(jnp.int32, (1, CZ), 1)

    def add(e, carry):
        spot = index[e]
        x, rest = spot // (CY * CZ), spot % (CY * CZ)
        y, z = rest // CZ, rest % CZ
        amount = (2 * signs[e] - 1).astype(F32)
        row = source[y, pl.ds(x, 1), :]
        source[y, pl.ds(x, 1), :] = row + jnp.where(lane == z, amount, 0.0)
        return carry

    lax.fori_loop(0, ELEMS, add, 0)
    for step in range(STEPS + 1):
        amounts[step] = jnp.full((8, CZ), wavelet[step], F32)


def grow(coef, grow_z, grow_x, write):
    wide = []
    for pair in range(CYC // 2):
        high, low = split(coef[:, pair * 128 : pair * 128 + 128])
        both = dot(cat([high, low], 1), grow_z[...])
        wide += [both[:, :CZ], both[:, CZ:]]
    weights = taps()
    for pair in range(CY // 2):
        parts = []
        for y in (2 * pair, 2 * pair + 1):
            mixed = None
            for j, w in weights[y]:
                term = wide[j] * w
                mixed = term if mixed is None else mixed + term
            parts.append(mixed)
        high, low = split(cat(parts, 1))
        fine = dot(grow_x, cat([high, low], 0))
        write(2 * pair, fine[:, :CZ])
        write(2 * pair + 1, fine[:, CZ:])


UNIT = 1.0 / 384.0**3


def grid_ends():
    core = lax.axis_index("core")
    chip = lax.axis_index("xh") * lax.axis_size("z") + lax.axis_index("z")
    chips = lax.axis_size("xh") * lax.axis_size("z")
    return (core == 0) & (chip == 0), (core == 1) & (chip == chips - 1)


def speed(coef, near, far, grow_z, grow_old, sigma, squared, beyond, held):
    core = lax.axis_index("core")
    held[:CXC] = coef[...]
    base = 2 * CY * OV
    for row in range(6):
        for part in range(4):
            lanes = slice(part * 128, part * 128 + 128)
            spot = base + row * 4 + part
            if row < 2:
                held[CXC + row : CXC + row + 1, lanes] = near[spot : spot + 1]
            held[CXC + 2 + row : CXC + 3 + row, lanes] = far[spot : spot + 1]
    first, last = grid_ends()

    def write(y, fine):
        fine = fine * UNIT
        square = fine * fine
        sigma[y] = fine[:CX]
        squared[y] = square[:CX]
        beyond[y * OV : y * OV + OV] = jnp.where(first | last, 0.0, square[CX:])

    grow(held[...], grow_z, grow_old[core], write)


def advance(step, *refs):
    (near, far, p, p_before, q, q_before, lap_p, lap_q, squared, source, amounts, halo_x) = refs[:12]
    refs = refs[12:]
    core = lax.axis_index("core")
    columns = halo_x[core]
    weight = amounts[step, :1, :]
    if step == 1:
        (sent, beyond, cross_x), refs = refs[:3], refs[3:]
        cross = cross_x[core]
    if step == 2:
        old_lap, refs = refs[0], refs[1:]
    if step == 3:
        (old_lap, older_q, gathered, sigma), refs = refs[:4], refs[4:]
    if step == 0:
        (p_new, q_new, near_out), refs = refs[:3], refs[3:]
    elif step < 3:
        (p_new, q_new, near_out, far_out), refs = refs[:4], refs[4:]
    else:
        p_new, near_out, far_out, image = refs[:4]
    if step < 2:
        lap_out = refs[0]
    if step == 2:
        gathered = refs[0]
    for pair in range(CY // 2):
        extra_p = halo_part(near, far, 0, columns, pair)
        extra_q = halo_part(near, far, 1, columns, pair)
        for side in range(2):
            y = 2 * pair + side
            lanes = slice(side * CZ, side * CZ + CZ)
            lap = lap_p[y] + extra_p[:, lanes]
            lap_adj = lap_q[y] + extra_q[:, lanes]
            sq = squared[y]
            if step == 0:
                rows = pl.ds(y, CX, stride=CY)
                old_p, old_q = p_before[rows, :], q_before[rows, :]
            else:
                old_p, old_q = p_before[y], q_before[y]
            p_new[y] = 2.0 * p[y] - old_p + sq * lap + source[y] * weight
            new_q = 2.0 * q[y] - old_q + sq * lap_adj
            if step < 3:
                q_new[y] = new_q
            if step < 2:
                lap_out[y] = lap
            if step == 2:
                gathered[y] = q[y] * lap + new_q * old_lap[y]
            if step == 3:
                total = gathered[y] + older_q[y] * lap + new_q * old_lap[y]
                image[y] = 2.0 * sigma[y] * total
    if step == 0 or step == 1:
        far_out_used = None
    else:
        far_out_used = far_out
    edge_rows(p_new, core, near_out, far_out_used, 0)
    if step < 3:
        edge_rows(q_new, core, near_out, far_out_used, 1)
    if step == 1:
        size = CY * OV
        for pair in range(CY // 2):
            for field in range(2):
                extra = halo_part(sent, sent, field, cross, pair)
                for side in range(2):
                    spot = (2 * pair + side) * OV
                    known = far[(2 + field) * size + spot : (2 + field) * size + spot + OV]
                    far_out[field * size + spot : field * size + spot + OV] = (
                        known
                        + beyond[spot : spot + OV] * extra[:OV, side * CZ : side * CZ + CZ]
                    )


def early(
    near, p, p_before, q, q_before, lap_p, lap_q, squared, source, amounts, near_x, out,
):
    core = lax.axis_index("core")
    row = pl.multiple_of(core * (CX - OV), OV)
    weight = amounts[1, :1, :]
    columns = near_x[core]
    size = CY * OV
    for pair in range(CY // 2):
        extra_p = halo_part(near, near, 0, columns, pair)
        extra_q = halo_part(near, near, 1, columns, pair)
        for side in range(2):
            y = 2 * pair + side
            rows = pl.ds(row, OV)
            lanes = slice(side * CZ, side * CZ + CZ)
            sq = squared[y, rows, :]
            lap = lap_p[y, rows, :] + extra_p[:OV, lanes]
            lap_adj = lap_q[y, rows, :] + extra_q[:OV, lanes]
            edge_p, edge_q = p[y, rows, :], q[y, rows, :]
            spot = y * OV
            out[spot : spot + OV] = edge_p
            out[size + spot : size + spot + OV] = edge_q
            out[2 * size + spot : 2 * size + spot + OV] = (
                2.0 * edge_p - p_before[y, rows, :] + sq * lap + source[y, rows, :] * weight
            )
            out[3 * size + spot : 3 * size + spot + OV] = (
                2.0 * edge_q - q_before[y, rows, :] + sq * lap_adj
            )


def inside(p, q, own_x, own_z, lap_p, lap_q):
    interior(p, own_x, own_z, lap_p)
    interior(q, own_x, own_z, lap_q)


def inside_one(p, own_x, own_z, lap_p):
    interior(p, own_x, own_z, lap_p)


def shrink(image, near_in, far_in, shrink_x, shrink_z, own, near, far):
    core = lax.axis_index("core")
    rows_x = shrink_x[core]
    narrow = [None] * CYC
    weights = taps()
    for pair in range(CY // 2):
        high, low = split(cat([image[2 * pair], image[2 * pair + 1]], 1))
        both = dot(rows_x, cat([high, low], 0))
        for side in range(2):
            part = both[:, side * CZ : side * CZ + CZ]
            for j, w in weights[2 * pair + side]:
                term = part * w
                narrow[j] = term if narrow[j] is None else narrow[j] + term
    pieces = []
    for pair in range(CYC // 2):
        parts = []
        for j in (2 * pair, 2 * pair + 1):
            parts += list(split(narrow[j]))
        pieces.append(dot(cat(parts, 1), shrink_z[...]) * UNIT)
    own[...] = cat(pieces, 1)
    field = CY * OV
    near[:field] = near_in[...]
    far[:field] = far_in[...]
    for row in range(4):
        for part in range(4):
            lanes = slice(part * 128, part * 128 + 128)
            spot = field + row * 4 + part
            near[spot : spot + 1] = own[CXC + row : CXC + row + 1, lanes]
            far[spot : spot + 1] = own[CXC + 4 + row : CXC + 5 + row, lanes]


def merge(own, near, far, out):
    out[...] = own[...]
    field = CY * OV
    for row in range(4):
        for part in range(4):
            lanes = slice(part * 128, part * 128 + 128)
            spot = field + row * 4 + part
            a, b = CXC + row, CXC + 4 + row
            out[a : a + 1, lanes] = own[a : a + 1, lanes] + near[spot : spot + 1]
            out[b : b + 1, lanes] = own[b : b + 1, lanes] + far[spot : spot + 1]


def squares(a, b, total, squared):
    core = lax.axis_index("core")
    total[...] = a[...] + b[...]
    first, last = grid_ends()
    total[CXC + 4 : CXC + 6] = jnp.where(first, 0.0, total[CXC + 4 : CXC + 6])
    total[CXC + 6 : CXC + 8] = jnp.where(last, 0.0, total[CXC + 6 : CXC + 8])
    total[0:2] = jnp.where(core == 0, total[CXC + 6 : CXC + 8], total[CXC + 2 : CXC + 4])
    total[CXC - 2 : CXC] = jnp.where(core == 0, total[CXC : CXC + 2], total[CXC + 4 : CXC + 6])
    value = total[:CXC]
    value = value * value
    rows = value[0:8]
    for r in range(1, CXC // 8):
        rows = rows + value[8 * r : 8 * r + 8]
    folded = rows[:, :128]
    for c in range(1, 4):
        folded = folded + rows[:, 128 * c : 128 * c + 128]
    squared[...] = folded


def last_fields(near, far, p, p_before, lap_p, source, amounts, halo_x, lap_out, base):
    core = lax.axis_index("core")
    columns = halo_x[core]
    weight = amounts[STEPS, :1, :]
    for pair in range(CY // 2):
        extra = halo_part(near, far, 0, columns, pair)
        for side in range(2):
            y = 2 * pair + side
            lap_out[y] = lap_p[y] + extra[:, side * CZ : side * CZ + CZ]
            base[y] = 2.0 * p[y] - p_before[y] + source[y] * weight


def add_four(own, one, two, three, out):
    out[...] = (own[...] + one[...]) + (two[...] + three[...])


def spread(total, sigma, lap, base, grow_z, grow_new, zeroth, first, second):
    core = lax.axis_index("core")

    def write(y, fine):
        change = fine * UNIT
        old, curve = sigma[y], lap[y]
        scaled = change * curve
        zeroth[y] = base[y] + old * old * curve
        first[y] = -2.0 * old * scaled
        second[y] = change * scaled

    grow(total[...], grow_z, grow_new[core], write)


def widen(a, b, out):
    value = a[...] + b[...]
    for k in range(out.shape[0]):
        out[k] = value


def finish(count, parts, total, zeroth, first, second, direction, p_last):
    value = parts[0]
    for k in range(1, parts.shape[0]):
        value = value + parts[k]
    value = jnp.sum(jnp.sum(value, axis=0, keepdims=True), axis=1, keepdims=True)
    scale = jnp.sqrt(value * (1.0 / count) + EPSILON)
    inverse = 1.0 / scale
    direction[...] = total[:CXC] * inverse
    rate = LEARN * inverse
    for y in range(CY):
        value = zeroth[y] + rate * (first[y] + rate * second[y])
        p_last[pl.ds(y, CX, stride=CY), :] = value


VM = pl.BlockSpec(memory_space=pltpu.VMEM)
SM = pl.BlockSpec(memory_space=pltpu.SMEM)
FIELD = jax.ShapeDtypeStruct((CY, CX, CZ), F32)
PARAMS = pltpu.CompilerParams(vmem_limit_bytes=4 * 2**20)


def rows_of(count, lanes=128):
    return jax.ShapeDtypeStruct((count, lanes), F32)


def call(body, outs, *args, smem=0, scratch=(), flops=0, name=None, held=()):
    size = sum(int(np.prod(a.shape)) * a.dtype.itemsize for a in args)
    count = len(args)

    def run(*refs):
        body(*refs[:count], *refs[count + len(held) :])

    return pl.pallas_call(
        run,
        out_shape=outs,
        in_specs=[SM] * smem
        + [VM] * (count - smem)
        + [pl.BlockSpec(memory_space=pl.ANY)] * len(held),
        out_specs=jax.tree.map(lambda _: VM, outs),
        scratch_shapes=list(scratch),
        compiler_params=PARAMS,
        cost_estimate=pl.CostEstimate(flops=flops, bytes_accessed=size, transcendentals=0),
        name=name,
    )(*args, *held)


def xor_swap(x, axis, mask):
    count = lax.axis_size(axis)
    if mask >= count:
        return jnp.zeros_like(x)
    return lax.ppermute(x, axis, [(i, i ^ mask) for i in range(count)])


def far_swap(x):
    count = lax.axis_size(TILE)
    pairs = [(i, i + 1) for i in range(1, count - 1, 2)]
    return lax.ppermute(x, TILE, pairs + [(b, a) for a, b in pairs])


def exchange(near, far):
    far = far_swap(far)
    near = xor_swap(near, "core", 1)
    return near, far


def on_device(p_now, p_prev, adj_now, adj_next, coef_old, signs, elem_index, wavelet):
    const = {name: jnp.asarray(value) for name, value in constants().items()}
    own_x, own_z, halo_x = const["own_x"], const["own_z"], const["halo_x"]
    flat = lambda a: a.reshape(CX * CY, CZ)
    p_now, p_prev, adj_now, adj_next = map(flat, (p_now, p_prev, adj_now, adj_next))

    edge = rows_of(2 * CY * OV)
    with_two, with_six = rows_of(2 * CY * OV + 8), rows_of(2 * CY * OV + 24)
    block = pltpu.VMEM((OV * CY, CZ), F32)
    few = pltpu.VMEM((8, CYC * CZC), F32)
    near, far = pl.pallas_call(
        first_edges,
        out_shape=(with_two, with_six),
        in_specs=[pl.BlockSpec(memory_space=pltpu.HBM)] * 3,
        out_specs=(VM, VM),
        scratch_shapes=[block] * 4 + [few] * 2 + [pltpu.SemaphoreType.DMA((6,))],
        compiler_params=PARAMS,
        name="first_edges",
    )(*(pltpu.with_memory_space_constraint(a, pltpu.HBM) for a in (p_now, adj_now, coef_old)))
    near, far = exchange(near, far)

    p, q, lap_p, lap_q, source, amounts = call(
        prepare,
        (FIELD,) * 5 + (jax.ShapeDtypeStruct((STEPS + 1, 8, CZ), F32),),
        signs[0], elem_index, wavelet, p_now, adj_now, own_x, own_z,
        smem=3, flops=10**9, name="prepare",
    )
    sigma, squared, beyond = call(
        speed, (FIELD, FIELD, rows_of(CY * OV)), coef_old, near, far, const["grow_z"], const["grow_old"],
        scratch=[pltpu.VMEM((ROWS, CYC * CZC), F32)], flops=10**8, name="speed",
    )

    p_before, q_before = p_prev, adj_next
    laps, qs = [], [q]
    gathered = None
    for step in range(STEPS):
        args = [near, far, p, p_before, q, q_before, lap_p, lap_q, squared, source, amounts, halo_x]
        body = functools.partial(advance, step)
        name = f"advance_{step}"
        if step == 0:
            outs = (FIELD, FIELD, edge, FIELD)
        elif step == 1:
            args += [sent, beyond, const["cross_x"]]
            outs = (FIELD, FIELD, edge, edge, FIELD)
        elif step == 2:
            args.append(laps[1])
            outs = (FIELD, FIELD, edge, edge, FIELD)
        else:
            args += [laps[0], qs[1], gathered, sigma]
            outs = (FIELD, rows_of(CY * OV), rows_of(CY * OV), FIELD)
        result = call(body, outs, *args, flops=10**8, name=name)
        if step == 3:
            p_new, near, far, image = result
            p, p_before = p_new, p
            continue
        p_new, q_new, *edges, other = result
        if step < 2:
            laps.append(other)
        else:
            gathered = other
        p, p_before = p_new, p
        q, q_before = q_new, q
        qs.append(q)
        if step == 2:
            near, far = exchange(*edges)
        else:
            near = xor_swap(edges[0], "core", 1)
        lap_p, lap_q = call(
            inside, (FIELD, FIELD), p, q, own_x, own_z, flops=10**9, name=f"inside_{step}"
        )
        if step == 0:
            sent = call(
                early, rows_of(4 * CY * OV), near, p, p_before, q, q_before, lap_p, lap_q,
                squared, source, amounts, const["near_x"], flops=10**7, name="early",
            )
            far = far_swap(sent)
        elif step == 1:
            far = edges[1]

    ends = rows_of(CY * OV + 16)
    own, near, far = call(
        shrink,
        (rows_of(ROWS, CYC * CZC), ends, ends),
        image, near, far, const["shrink_x"], const["shrink_z"], flops=10**8, name="shrink",
    )
    near, far = exchange(near, far)
    lap_p = call(inside_one, FIELD, p, own_x, own_z, flops=5 * 10**8, name="inside_last")
    partial = call(merge, rows_of(ROWS, CYC * CZC), own, near, far, name="merge")

    two, one, three = (xor_swap(partial, "y", m) for m in (2, 1, 3))
    lap_p, base = call(
        last_fields, (FIELD, FIELD), near, far, p, p_before, lap_p, source, amounts, halo_x,
        flops=10**8, name="last_fields",
    )
    held = (lap_p, base)
    partial = call(
        add_four, rows_of(ROWS, CYC * CZC), partial, one, two, three, name="add_four", held=held
    )
    other = xor_swap(partial, "xl", 1)
    total, squared_sum = call(
        squares, (rows_of(ROWS, CYC * CZC), rows_of(8)), partial, other, name="squares",
        held=held,
    )
    squared_sum = squared_sum + xor_swap(squared_sum, "core", 1)
    terms = call(
        spread, (FIELD,) * 3, total, sigma, lap_p, base, const["grow_z"], const["grow_new"],
        flops=10**8, name="spread",
    )
    deep = lax.axis_size("z")
    copies = call(
        widen, jax.ShapeDtypeStruct((deep, 8, 128), F32),
        squared_sum, xor_swap(squared_sum, "xh", 1), name="widen", held=terms,
    )
    parts = lax.all_to_all(copies, "z", split_axis=0, concat_axis=0, tiled=True)
    count = float(lax.axis_size(TILE) * CXC * CYC * CZC)
    direction, p_last = call(
        functools.partial(finish, count),
        (rows_of(CXC, CYC * CZC), rows_of(CX * CY)),
        parts, total, *terms, name="finish",
    )
    return direction, p_last.reshape(1, CX, CY, CZ)


def solution(mesh):
    shots, tiles = mesh.shape["shot"], mesh.shape["tile"]
    fine = Mesh(
        mesh.devices.reshape(shots // 2, 2, 2, tiles // 4, 2), ("y", "xl", "xh", "z", "core")
    )
    placed = (
        P(SHOT, TILE, None, None),
        P(SHOT, TILE, None, None),
        P(SHOT, TILE, None, None),
        P(SHOT, TILE, None, None),
        P(TILE, None),
        P(SHOT, TILE),
        P(TILE),
        P(),
    )
    return jax.shard_map(
        on_device,
        mesh=fine,
        in_specs=placed,
        out_specs=(P(TILE, None), P(SHOT, TILE, None, None)),
        check_vma=False,
    )
```

```python
import functools

import jax
import jax.numpy as jnp
import ml_dtypes
import numpy as np
from jax import lax
from jax.experimental import pallas as pl
from jax.experimental.pallas import tpu as pltpu
from jax.sharding import Mesh
from jax.sharding import PartitionSpec as P

CX = 128
CZ = 128
CY = 16
OV = 8
STEPS = 4
ELEMS = 64
CXC = 64
CYC = 8
CZC = 64
ROWS = 72
LEARN = 0.02
EPSILON = 1e-06
BF = jnp.bfloat16
F32 = jnp.float32
SHOT = ("y", "xl")
TILE = ("xh", "z", "core")


def spectral_second(length):
    index = np.arange(length)
    number = np.minimum(index, length - index) * (2.0 * np.pi / length)
    phase = (index[:, None, None] - index[None, :, None]) * index[None, None, :] % length
    return -np.sum(number**2 * np.cos(2.0 * np.pi / length * phase), axis=2) / length


def spline_units(offset):
    mag = np.abs(offset)
    inner = 2.0 / 3.0 - mag**2 + 0.5 * mag**3
    outer = (2.0 - mag) ** 3 / 6.0
    return np.round(384.0 * np.where(mag < 1.0, inner, np.where(mag < 2.0, outer, 0.0)))


def halves(matrix):
    high = matrix.astype(np.float32).astype(ml_dtypes.bfloat16)
    low = (matrix - high.astype(np.float64)).astype(np.float32).astype(ml_dtypes.bfloat16)
    return high, low


def narrow_band(matrix):
    high, low = halves(np.pad(matrix, ((0, OV), (0, OV))))
    return np.concatenate([high, high, low], axis=1)


@functools.cache
def constants():
    out = {}
    second_x = spectral_second(CX + 2 * OV)[OV : OV + CX]
    ramp = np.sin(0.5 * np.pi * (np.arange(OV) + 0.5) / OV) ** 2
    left = second_x[:, :OV] * ramp[None, :]
    right = second_x[:, OV + CX :] * ramp[None, ::-1]
    high, low = halves(second_x[:, OV : OV + CX])
    out["own_x"] = np.block([[high, high], [low, np.zeros_like(low)]])
    sides = []
    for pair in ((right, left), (left, right)):
        high, low = halves(np.concatenate(pair, axis=1))
        sides.append(np.concatenate([high, high, low], axis=1))
    out["halo_x"] = np.stack(sides)
    near_part, cross_part = [], []
    for core in range(2):
        rows = slice(0, OV) if core == 0 else slice(CX - OV, CX)
        near_part.append(narrow_band((right if core == 0 else left)[rows]))
        rows = slice(CX - OV, CX) if core == 0 else slice(0, OV)
        cross_part.append(narrow_band((right if core == 0 else left)[rows]))
    out["near_x"] = np.stack(near_part)
    out["cross_x"] = np.stack(cross_part)
    high, low = halves(spectral_second(CZ) - 2.0 * np.eye(CZ))
    out["own_z"] = np.block([[high, low], [high, np.zeros_like(low)]])

    fine_z = np.arange(CZ)[:, None]
    coarse_z = np.arange(CZC)[None, :]
    weight_z = sum(
        spline_units((fine_z - 2 * coarse_z + image * CZ - 0.5) * 0.5) for image in range(-2, 3)
    )
    zero = np.zeros_like(weight_z.T)
    pair = np.block([[weight_z.T, zero], [zero, weight_z.T]])
    out["grow_z"] = np.concatenate([pair, pair], axis=0)
    zero = np.zeros_like(weight_z)
    out["shrink_z"] = np.block(
        [[weight_z, zero], [weight_z, zero], [zero, weight_z], [zero, weight_z]]
    )

    def column(coarse, start=0, count=CX):
        return spline_units((np.arange(start, start + count) - 2 * coarse - 0.5) * 0.5)

    own = np.stack([column(j) for j in range(CXC)], axis=1)
    lower = {j: column(j) for j in (-2, -1, 0, 1)}
    upper = {j: column(j) for j in (62, 63, 64, 65)}
    stack = lambda d: np.stack([d[j] for j in sorted(d)], axis=1)
    grow_old, grow_new, shrink, shrink_far = [], [], [], []
    blank = np.zeros((CX, 2))
    for core in range(2):
        near = upper if core == 0 else lower
        near_two, far_six = ((64, 65), range(-6, 0)) if core == 0 else ((-2, -1), range(64, 70))
        far_two = (-2, -1) if core == 0 else (64, 65)
        beyond = -OV if core == 0 else CX
        old = np.stack(
            [
                np.concatenate([column(j), column(j, beyond, OV)])
                for j in (*range(CXC), *near_two, *far_six)
            ],
            axis=1,
        )
        inner = own.copy()
        inner[:, [62, 63] if core == 0 else [0, 1]] = 0.0
        outer = np.stack([column(j) for j in far_two], axis=1)
        new = np.concatenate([inner, stack(near), outer, blank], axis=1)
        every = np.concatenate([own, stack(near), outer, blank], axis=1).T
        past = np.zeros((ROWS, OV))
        for row, j in (*enumerate(range(CXC)), *zip((CXC + 4, CXC + 5), far_two)):
            past[row] = column(j, beyond, OV)
        grow_old.append(np.concatenate([old, old], axis=1))
        grow_new.append(np.concatenate([new, new], axis=1))
        shrink.append(np.concatenate([every, every], axis=1))
        shrink_far.append(np.concatenate([past, past], axis=1))
    out["shrink_far"] = np.stack(shrink_far)
    out["grow_old"] = np.stack(grow_old)
    out["grow_new"] = np.stack(grow_new)
    out["shrink_x"] = np.stack(shrink)
    return {name: np.asarray(value).astype(ml_dtypes.bfloat16) for name, value in out.items()}


def taps():
    return [
        [
            (j, float(w))
            for j in range(CYC)
            for w in [
                sum(
                    spline_units(np.float64((i - 2 * j + image * CY - 0.5) * 0.5))
                    for image in range(-2, 3)
                )
            ]
            if w
        ]
        for i in range(CY)
    ]


def split(value):
    high = value.astype(BF)
    return high, (value - high.astype(F32)).astype(BF)


def dot(left, right):
    return jnp.dot(left, right, preferred_element_type=F32)


def cat(parts, axis):
    return jnp.concatenate(parts, axis=axis)


def interior(v, own_x, own_z, out):
    for j in range(CY // 2):
        one, two = 2 * j, 2 * j + 1
        high1, low1 = split(v[one])
        high2, low2 = split(v[two])
        x = dot(own_x[...], cat([cat([high1, high2], 1), cat([low1, low2], 1)], 0))
        z = dot(cat([cat([high1, low1], 1), cat([high2, low2], 1)], 0), own_z[...])
        x = x[:CX] + x[CX:]
        z = z[:, :CZ] + z[:, CZ:]
        beside = v[(one - 1) % CY] + v[two]
        out[one] = x[:, :CZ] + z[:CX] + beside
        beside = v[one] + v[(two + 1) % CY]
        out[two] = x[:, CZ:] + z[CX:] + beside


def halo_part(near, far, field, halo_x, pair):
    parts = []
    for y in (2 * pair, 2 * pair + 1):
        start = (field * CY + y) * OV
        high, low = split(cat([near[start : start + OV], far[start : start + OV]], 0))
        parts.append(cat([high, low, high], 0))
    return dot(halo_x, cat(parts, 1))


def edge_rows(v, core, near, field):
    row = pl.multiple_of((1 - core) * (CX - OV), OV)
    for y in range(CY):
        start = (field * CY + y) * OV
        near[start : start + OV] = v[y, pl.ds(row, OV), :]


def first_edges(p, q, coef, near, far, p_lo, p_hi, q_lo, q_hi, c_lo, c_hi, sems):
    core = lax.axis_index("core")
    block = OV * CY
    copies = [
        pltpu.make_async_copy(source.at[pl.ds(start, size)], target, sems.at[k])
        for k, (source, start, size, target) in enumerate(
            (
                (p, 0, block, p_lo),
                (p, CX * CY - block, block, p_hi),
                (q, 0, block, q_lo),
                (q, CX * CY - block, block, q_hi),
                (coef, 0, 8, c_lo),
                (coef, CXC - 8, 8, c_hi),
            )
        )
    ]
    for copy in copies:
        copy.start()

    def fill(low, high, field):
        for y in range(CY):
            start = (field * CY + y) * OV
            rows = pl.ds(y, OV, stride=CY)
            first, last = low[rows, :], high[rows, :]
            near[start : start + OV] = jnp.where(core == 0, last, first)
            far[start : start + OV] = jnp.where(core == 0, first, last)

    copies[0].wait()
    copies[1].wait()
    fill(p_lo, p_hi, 0)
    copies[2].wait()
    copies[3].wait()
    fill(q_lo, q_hi, 1)
    copies[4].wait()
    copies[5].wait()
    base = 2 * CY * OV
    for row in range(6):
        for part in range(4):
            lanes = slice(part * 128, part * 128 + 128)
            spot = base + row * 4 + part
            if row < 2:
                first = c_lo[row : row + 1, lanes]
                last = c_hi[6 + row : 7 + row, lanes]
                near[spot : spot + 1] = jnp.where(core == 0, last, first)
            first = c_lo[row : row + 1, lanes]
            last = c_hi[2 + row : 3 + row, lanes]
            far[spot : spot + 1] = jnp.where(core == 0, first, last)


def reorder(source, target):
    for y in range(CY):
        target[y] = source[pl.ds(y, CX, stride=CY), :]


def prepare(
    signs, index, wavelet, p_now, q_now, own_x, own_z,
    p0, q0, lap_p, lap_q, source, amounts,
):
    reorder(p_now, p0)
    reorder(q_now, q0)
    interior(p0, own_x, own_z, lap_p)
    interior(q0, own_x, own_z, lap_q)
    source[...] = jnp.zeros_like(source)
    lane = lax.broadcasted_iota(jnp.int32, (1, CZ), 1)

    def add(e, carry):
        spot = index[e]
        x, rest = spot // (CY * CZ), spot % (CY * CZ)
        y, z = rest // CZ, rest % CZ
        amount = (2 * signs[e] - 1).astype(F32)
        row = source[y, pl.ds(x, 1), :]
        source[y, pl.ds(x, 1), :] = row + jnp.where(lane == z, amount, 0.0)
        return carry

    lax.fori_loop(0, ELEMS, add, 0)
    for step in range(STEPS + 1):
        amounts[step] = jnp.full((8, CZ), wavelet[step], F32)


def grow(coef, grow_z, grow_x, write):
    wide = []
    for pair in range(CYC // 2):
        high, low = split(coef[:, pair * 128 : pair * 128 + 128])
        both = dot(cat([high, low], 1), grow_z[...])
        wide += [both[:, :CZ], both[:, CZ:]]
    weights = taps()
    for pair in range(CY // 2):
        parts = []
        for y in (2 * pair, 2 * pair + 1):
            mixed = None
            for j, w in weights[y]:
                term = wide[j] * w
                mixed = term if mixed is None else mixed + term
            parts.append(mixed)
        high, low = split(cat(parts, 1))
        fine = dot(grow_x, cat([high, low], 0))
        write(2 * pair, fine[:, :CZ])
        write(2 * pair + 1, fine[:, CZ:])


UNIT = 1.0 / 384.0**3


def grid_ends():
    core = lax.axis_index("core")
    chip = lax.axis_index("xh") * lax.axis_size("z") + lax.axis_index("z")
    chips = lax.axis_size("xh") * lax.axis_size("z")
    return (core == 0) & (chip == 0), (core == 1) & (chip == chips - 1)


def speed(coef, near, far, grow_z, grow_old, sigma, squared, beyond, held):
    core = lax.axis_index("core")
    held[:CXC] = coef[...]
    base = 2 * CY * OV
    for row in range(6):
        for part in range(4):
            lanes = slice(part * 128, part * 128 + 128)
            spot = base + row * 4 + part
            if row < 2:
                held[CXC + row : CXC + row + 1, lanes] = near[spot : spot + 1]
            held[CXC + 2 + row : CXC + 3 + row, lanes] = far[spot : spot + 1]
    first, last = grid_ends()

    def write(y, fine):
        fine = fine * UNIT
        square = fine * fine
        sigma[y] = fine[:CX]
        squared[y] = square[:CX]
        beyond[y * OV : y * OV + OV] = jnp.where(first | last, 0.0, fine[CX:])

    grow(held[...], grow_z, grow_old[core], write)


def squared_at(beyond, spot):
    value = beyond[spot : spot + OV]
    return value * value


def advance(step, *refs):
    (near, far, p, p_before, q, q_before, lap_p, lap_q, squared, source, amounts, halo_x) = refs[:12]
    refs = refs[12:]
    core = lax.axis_index("core")
    columns = halo_x[core]
    weight = amounts[step, :1, :]
    if step in (1, 3):
        (sent, beyond, cross_x), refs = refs[:3], refs[3:]
        cross = cross_x[core]
    if step == 2:
        old_lap, refs = refs[0], refs[1:]
    if step == 3:
        (old_lap, older_q, gathered, sigma, older_far), refs = refs[:5], refs[5:]
    if step in (0, 2):
        (p_new, q_new, near_out), refs = refs[:3], refs[3:]
    elif step == 1:
        (p_new, q_new, near_out, far_out), refs = refs[:4], refs[4:]
    else:
        p_new, near_out, far_out, image, image_far = refs[:5]
    if step < 2:
        lap_out = refs[0]
    if step == 2:
        gathered = refs[0]
    for pair in range(CY // 2):
        extra_p = halo_part(near, far, 0, columns, pair)
        extra_q = halo_part(near, far, 1, columns, pair)
        for side in range(2):
            y = 2 * pair + side
            lanes = slice(side * CZ, side * CZ + CZ)
            lap = lap_p[y] + extra_p[:, lanes]
            lap_adj = lap_q[y] + extra_q[:, lanes]
            sq = squared[y]
            if step == 0:
                rows = pl.ds(y, CX, stride=CY)
                old_p, old_q = p_before[rows, :], q_before[rows, :]
            else:
                old_p, old_q = p_before[y], q_before[y]
            p_new[y] = 2.0 * p[y] - old_p + sq * lap + source[y] * weight
            new_q = 2.0 * q[y] - old_q + sq * lap_adj
            if step < 3:
                q_new[y] = new_q
            if step < 2:
                lap_out[y] = lap
            if step == 2:
                gathered[y] = q[y] * lap + new_q * old_lap[y]
            if step == 3:
                total = gathered[y] + older_q[y] * lap + new_q * old_lap[y]
                image[y] = 2.0 * sigma[y] * total
    edge_rows(p_new, core, near_out, 0)
    if step < 3:
        edge_rows(q_new, core, near_out, 1)
    if step == 1:
        size = CY * OV
        for pair in range(CY // 2):
            for field in range(2):
                extra = halo_part(sent, sent, field, cross, pair)
                for side in range(2):
                    spot = (2 * pair + side) * OV
                    known = far[(2 + field) * size + spot : (2 + field) * size + spot + OV]
                    far_out[field * size + spot : field * size + spot + OV] = (
                        known
                        + squared_at(beyond, spot) * extra[:OV, side * CZ : side * CZ + CZ]
                    )
    if step == 3:
        size = CY * OV
        for pair in range(CY // 2):
            extra_p = halo_part(sent, sent, 0, cross, pair)
            extra_q = halo_part(sent, sent, 1, cross, pair)
            for side in range(2):
                spot = (2 * pair + side) * OV
                lanes = slice(side * CZ, side * CZ + CZ)
                part_p, part_q = extra_p[:OV, lanes], extra_q[:OV, lanes]
                rows = lambda k: far[k * size + spot : k * size + spot + OV]
                far_out[spot : spot + OV] = rows(2) + squared_at(beyond, spot) * part_p
                near_q = older_far[size + spot : size + spot + OV]
                image_far[spot : spot + OV] = (
                    rows(3) + 2.0 * beyond[spot : spot + OV] * near_q * part_p + rows(4) * part_q
                )


def early(step, *refs):
    (near, p, p_before, q, q_before, lap_p, lap_q, squared, source, amounts, near_x) = refs[:11]
    if step == 3:
        older_q, old_lap, gathered, sigma = refs[11:15]
    out = refs[-1]
    core = lax.axis_index("core")
    rows = pl.ds(pl.multiple_of(core * (CX - OV), OV), OV)
    weight = amounts[step, :1, :]
    columns = near_x[core]
    for pair in range(CY // 2):
        extra_p = halo_part(near, near, 0, columns, pair)
        extra_q = halo_part(near, near, 1, columns, pair)
        for side in range(2):
            y = 2 * pair + side
            lanes = slice(side * CZ, side * CZ + CZ)
            sq = squared[y, rows, :]
            lap = lap_p[y, rows, :] + extra_p[:OV, lanes]
            lap_adj = lap_q[y, rows, :] + extra_q[:OV, lanes]
            edge_p, edge_q = p[y, rows, :], q[y, rows, :]
            next_p = 2.0 * edge_p - p_before[y, rows, :] + sq * lap + source[y, rows, :] * weight
            next_q = 2.0 * edge_q - q_before[y, rows, :] + sq * lap_adj
            if step == 1:
                sets = (edge_p, edge_q, next_p, next_q)
            else:
                twice = 2.0 * sigma[y, rows, :]
                old = old_lap[y, rows, :]
                known = gathered[y, rows, :] + older_q[y, rows, :] * lap + next_q * old
                sets = (edge_p, edge_q, next_p, twice * known, twice * sq * old)
            for k, value in enumerate(sets):
                spot = (k * CY + y) * OV
                out[spot : spot + OV] = value


def inside(p, q, own_x, own_z, lap_p, lap_q):
    interior(p, own_x, own_z, lap_p)
    interior(q, own_x, own_z, lap_q)


def inside_one(p, own_x, own_z, lap_p):
    interior(p, own_x, own_z, lap_p)


def shrink(image, image_far, near_in, shrink_x, shrink_far, shrink_z, own, near):
    core = lax.axis_index("core")
    rows_x = shrink_x[core]
    rows_far = shrink_far[core]
    narrow = [None] * CYC
    weights = taps()
    for pair in range(CY // 2):
        high, low = split(cat([image[2 * pair], image[2 * pair + 1]], 1))
        both = dot(rows_x, cat([high, low], 0))
        spots = [slice(y * OV, y * OV + OV) for y in (2 * pair, 2 * pair + 1)]
        high, low = split(cat([image_far[spots[0]], image_far[spots[1]]], 1))
        both = both + dot(rows_far, cat([high, low], 0))
        for side in range(2):
            part = both[:, side * CZ : side * CZ + CZ]
            for j, w in weights[2 * pair + side]:
                term = part * w
                narrow[j] = term if narrow[j] is None else narrow[j] + term
    pieces = []
    for pair in range(CYC // 2):
        parts = []
        for j in (2 * pair, 2 * pair + 1):
            parts += list(split(narrow[j]))
        pieces.append(dot(cat(parts, 1), shrink_z[...]) * UNIT)
    own[...] = cat(pieces, 1)
    field = CY * OV
    near[:field] = near_in[...]
    for row in range(4):
        for part in range(4):
            lanes = slice(part * 128, part * 128 + 128)
            spot = field + row * 4 + part
            near[spot : spot + 1] = own[CXC + row : CXC + row + 1, lanes]


def merge(own, near, out):
    out[...] = own[...]
    field = CY * OV
    for row in range(4):
        for part in range(4):
            lanes = slice(part * 128, part * 128 + 128)
            spot = field + row * 4 + part
            at = slice(CXC + row, CXC + row + 1)
            out[at, lanes] = own[at, lanes] + near[spot : spot + 1]


def squares(a, b, total, squared):
    core = lax.axis_index("core")
    total[...] = a[...] + b[...]
    first, last = grid_ends()
    total[CXC + 4 : CXC + 6] = jnp.where(first | last, 0.0, total[CXC + 4 : CXC + 6])
    total[0:2] = jnp.where(core == 0, total[0:2], total[CXC + 2 : CXC + 4])
    total[CXC - 2 : CXC] = jnp.where(core == 0, total[CXC : CXC + 2], total[CXC - 2 : CXC])
    value = total[:CXC]
    value = value * value
    rows = value[0:8]
    for r in range(1, CXC // 8):
        rows = rows + value[8 * r : 8 * r + 8]
    folded = rows[:, :128]
    for c in range(1, 4):
        folded = folded + rows[:, 128 * c : 128 * c + 128]
    squared[...] = folded


def last_fields(near, far, p, p_before, lap_p, source, amounts, halo_x, lap_out, base):
    core = lax.axis_index("core")
    columns = halo_x[core]
    weight = amounts[STEPS, :1, :]
    for pair in range(CY // 2):
        extra = halo_part(near, far, 0, columns, pair)
        for side in range(2):
            y = 2 * pair + side
            lap_out[y] = lap_p[y] + extra[:, side * CZ : side * CZ + CZ]
            base[y] = 2.0 * p[y] - p_before[y] + source[y] * weight


def add_four(own, one, two, three, out):
    out[...] = (own[...] + one[...]) + (two[...] + three[...])


def spread(total, sigma, lap, base, grow_z, grow_new, zeroth, first, second):
    core = lax.axis_index("core")

    def write(y, fine):
        change = fine * UNIT
        old, curve = sigma[y], lap[y]
        scaled = change * curve
        zeroth[y] = base[y] + old * old * curve
        first[y] = -2.0 * old * scaled
        second[y] = change * scaled

    grow(total[...], grow_z, grow_new[core], write)


def widen(a, b, out):
    value = a[...] + b[...]
    for k in range(out.shape[0]):
        out[k] = value


def finish(count, parts, total, zeroth, first, second, direction, p_last):
    value = parts[0]
    for k in range(1, parts.shape[0]):
        value = value + parts[k]
    value = jnp.sum(jnp.sum(value, axis=0, keepdims=True), axis=1, keepdims=True)
    scale = jnp.sqrt(value * (1.0 / count) + EPSILON)
    inverse = 1.0 / scale
    direction[...] = total[:CXC] * inverse
    rate = LEARN * inverse
    for y in range(CY):
        value = zeroth[y] + rate * (first[y] + rate * second[y])
        p_last[pl.ds(y, CX, stride=CY), :] = value


VM = pl.BlockSpec(memory_space=pltpu.VMEM)
SM = pl.BlockSpec(memory_space=pltpu.SMEM)
FIELD = jax.ShapeDtypeStruct((CY, CX, CZ), F32)
PARAMS = pltpu.CompilerParams(vmem_limit_bytes=4 * 2**20)


def rows_of(count, lanes=128):
    return jax.ShapeDtypeStruct((count, lanes), F32)


def call(body, outs, *args, smem=0, scratch=(), flops=0, name=None, held=()):
    size = sum(int(np.prod(a.shape)) * a.dtype.itemsize for a in args)
    count = len(args)

    def run(*refs):
        body(*refs[:count], *refs[count + len(held) :])

    return pl.pallas_call(
        run,
        out_shape=outs,
        in_specs=[SM] * smem
        + [VM] * (count - smem)
        + [pl.BlockSpec(memory_space=pl.ANY)] * len(held),
        out_specs=jax.tree.map(lambda _: VM, outs),
        scratch_shapes=list(scratch),
        compiler_params=PARAMS,
        cost_estimate=pl.CostEstimate(flops=flops, bytes_accessed=size, transcendentals=0),
        name=name,
    )(*args, *held)


def xor_swap(x, axis, mask):
    count = lax.axis_size(axis)
    if mask >= count:
        return jnp.zeros_like(x)
    return lax.ppermute(x, axis, [(i, i ^ mask) for i in range(count)])


def far_swap(x):
    count = lax.axis_size(TILE)
    pairs = [(i, i + 1) for i in range(1, count - 1, 2)]
    return lax.ppermute(x, TILE, pairs + [(b, a) for a, b in pairs])


def exchange(near, far):
    far = far_swap(far)
    near = xor_swap(near, "core", 1)
    return near, far


def on_device(p_now, p_prev, adj_now, adj_next, coef_old, signs, elem_index, wavelet):
    const = {name: jnp.asarray(value) for name, value in constants().items()}
    own_x, own_z, halo_x = const["own_x"], const["own_z"], const["halo_x"]
    flat = lambda a: a.reshape(CX * CY, CZ)
    p_now, p_prev, adj_now, adj_next = map(flat, (p_now, p_prev, adj_now, adj_next))

    half, edge = rows_of(CY * OV), rows_of(2 * CY * OV)
    with_two, with_six = rows_of(2 * CY * OV + 8), rows_of(2 * CY * OV + 24)
    block = pltpu.VMEM((OV * CY, CZ), F32)
    few = pltpu.VMEM((8, CYC * CZC), F32)
    near, far = pl.pallas_call(
        first_edges,
        out_shape=(with_two, with_six),
        in_specs=[pl.BlockSpec(memory_space=pltpu.HBM)] * 3,
        out_specs=(VM, VM),
        scratch_shapes=[block] * 4 + [few] * 2 + [pltpu.SemaphoreType.DMA((6,))],
        compiler_params=PARAMS,
        name="first_edges",
    )(*(pltpu.with_memory_space_constraint(a, pltpu.HBM) for a in (p_now, adj_now, coef_old)))
    near, far = exchange(near, far)

    p, q, lap_p, lap_q, source, amounts = call(
        prepare,
        (FIELD,) * 5 + (jax.ShapeDtypeStruct((STEPS + 1, 8, CZ), F32),),
        signs[0], elem_index, wavelet, p_now, adj_now, own_x, own_z,
        smem=3, flops=10**9, name="prepare",
    )
    sigma, squared, beyond = call(
        speed, (FIELD, FIELD, rows_of(CY * OV)), coef_old, near, far, const["grow_z"], const["grow_old"],
        scratch=[pltpu.VMEM((ROWS, CYC * CZC), F32)], flops=10**8, name="speed",
    )

    p_before, q_before = p_prev, adj_next
    laps, qs = [], [q]
    gathered = None
    for step in range(STEPS):
        args = [near, far, p, p_before, q, q_before, lap_p, lap_q, squared, source, amounts, halo_x]
        body = functools.partial(advance, step)
        name = f"advance_{step}"
        if step == 0:
            outs = (FIELD, FIELD, edge, FIELD)
        elif step == 1:
            args += [sent, beyond, const["cross_x"]]
            outs = (FIELD, FIELD, edge, edge, FIELD)
            older_far = far
        elif step == 2:
            args.append(laps[1])
            outs = (FIELD, FIELD, edge, FIELD)
        else:
            args += [sent, beyond, const["cross_x"], laps[0], qs[1], gathered, sigma, older_far]
            outs = (FIELD, half, half, FIELD, half)
        result = call(body, outs, *args, flops=10**8, name=name)
        if step == 3:
            p_new, near, far, image, image_far = result
            p, p_before = p_new, p
            continue
        p_new, q_new, *edges, other = result
        if step < 2:
            laps.append(other)
        else:
            gathered = other
        p, p_before = p_new, p
        q, q_before = q_new, q
        qs.append(q)
        near = xor_swap(edges[0], "core", 1)
        lap_p, lap_q = call(
            inside, (FIELD, FIELD), p, q, own_x, own_z, flops=10**9, name=f"inside_{step}"
        )
        if step == 1:
            far = edges[1]
            continue
        args = [near, p, p_before, q, q_before, lap_p, lap_q, squared, source, amounts]
        args.append(const["near_x"])
        if step == 2:
            args += [qs[1], laps[0], gathered, sigma]
        sent = call(
            functools.partial(early, step + 1), rows_of((4 if step == 0 else 5) * CY * OV),
            *args, flops=10**7, name=f"early_{step + 1}",
        )
        far = far_swap(sent)

    own, near = call(
        shrink,
        (rows_of(ROWS, CYC * CZC), rows_of(CY * OV + 16)),
        image, image_far, near, const["shrink_x"], const["shrink_far"], const["shrink_z"],
        flops=10**8, name="shrink",
    )
    near = xor_swap(near, "core", 1)
    lap_p = call(inside_one, FIELD, p, own_x, own_z, flops=5 * 10**8, name="inside_last")
    partial = call(merge, rows_of(ROWS, CYC * CZC), own, near, name="merge")

    two, one, three = (xor_swap(partial, "y", m) for m in (2, 1, 3))
    lap_p, base = call(
        last_fields, (FIELD, FIELD), near, far, p, p_before, lap_p, source, amounts, halo_x,
        flops=10**8, name="last_fields",
    )
    held = (lap_p, base)
    partial = call(
        add_four, rows_of(ROWS, CYC * CZC), partial, one, two, three, name="add_four", held=held
    )
    other = xor_swap(partial, "xl", 1)
    total, squared_sum = call(
        squares, (rows_of(ROWS, CYC * CZC), rows_of(8)), partial, other, name="squares",
        held=held,
    )
    squared_sum = squared_sum + xor_swap(squared_sum, "core", 1)
    terms = call(
        spread, (FIELD,) * 3, total, sigma, lap_p, base, const["grow_z"], const["grow_new"],
        flops=10**8, name="spread",
    )
    deep = lax.axis_size("z")
    copies = call(
        widen, jax.ShapeDtypeStruct((deep, 8, 128), F32),
        squared_sum, xor_swap(squared_sum, "xh", 1), name="widen", held=terms,
    )
    parts = lax.all_to_all(copies, "z", split_axis=0, concat_axis=0, tiled=True)
    count = float(lax.axis_size(TILE) * CXC * CYC * CZC)
    direction, p_last = call(
        functools.partial(finish, count),
        (rows_of(CXC, CYC * CZC), rows_of(CX * CY)),
        parts, total, *terms, name="finish",
    )
    return direction, p_last.reshape(1, CX, CY, CZ)


def solution(mesh):
    shots, tiles = mesh.shape["shot"], mesh.shape["tile"]
    fine = Mesh(
        mesh.devices.reshape(shots // 2, 2, 2, tiles // 4, 2), ("y", "xl", "xh", "z", "core")
    )
    placed = (
        P(SHOT, TILE, None, None),
        P(SHOT, TILE, None, None),
        P(SHOT, TILE, None, None),
        P(SHOT, TILE, None, None),
        P(TILE, None),
        P(SHOT, TILE),
        P(TILE),
        P(),
    )
    return jax.shard_map(
        on_device,
        mesh=fine,
        in_specs=placed,
        out_specs=(P(TILE, None), P(SHOT, TILE, None, None)),
        check_vma=False,
    )
```

```python
import functools

import jax
import jax.numpy as jnp
import ml_dtypes
import numpy as np
from jax import lax
from jax.experimental import pallas as pl
from jax.experimental.pallas import tpu as pltpu
from jax.sharding import Mesh
from jax.sharding import PartitionSpec as P

CX = 128
CZ = 128
CY = 16
OV = 8
STEPS = 4
ELEMS = 64
CXC = 64
CYC = 8
CZC = 64
ROWS = 72
LEARN = 0.02
EPSILON = 1e-06
BF = jnp.bfloat16
F32 = jnp.float32
SHOT = ("y", "xl")
TILE = ("xh", "z", "core")


def spectral_second(length):
    index = np.arange(length)
    number = np.minimum(index, length - index) * (2.0 * np.pi / length)
    phase = (index[:, None, None] - index[None, :, None]) * index[None, None, :] % length
    return -np.sum(number**2 * np.cos(2.0 * np.pi / length * phase), axis=2) / length


def spline_units(offset):
    mag = np.abs(offset)
    inner = 2.0 / 3.0 - mag**2 + 0.5 * mag**3
    outer = (2.0 - mag) ** 3 / 6.0
    return np.round(384.0 * np.where(mag < 1.0, inner, np.where(mag < 2.0, outer, 0.0)))


def halves(matrix):
    high = matrix.astype(np.float32).astype(ml_dtypes.bfloat16)
    low = (matrix - high.astype(np.float64)).astype(np.float32).astype(ml_dtypes.bfloat16)
    return high, low


def narrow_band(matrix):
    high, low = halves(np.pad(matrix, ((0, OV), (0, OV))))
    return np.concatenate([high, high, low], axis=1)


@functools.cache
def constants():
    out = {}
    second_x = spectral_second(CX + 2 * OV)[OV : OV + CX]
    ramp = np.sin(0.5 * np.pi * (np.arange(OV) + 0.5) / OV) ** 2
    left = second_x[:, :OV] * ramp[None, :]
    right = second_x[:, OV + CX :] * ramp[None, ::-1]
    high, low = halves(second_x[:, OV : OV + CX])
    out["own_x"] = np.block([[high, high], [low, np.zeros_like(low)]])
    sides = []
    for pair in ((right, left), (left, right)):
        high, low = halves(np.concatenate(pair, axis=1))
        sides.append(np.concatenate([high, high, low], axis=1))
    out["halo_x"] = np.stack(sides)
    near_part, cross_part = [], []
    for core in range(2):
        rows = slice(0, OV) if core == 0 else slice(CX - OV, CX)
        near_part.append(narrow_band((right if core == 0 else left)[rows]))
        rows = slice(CX - OV, CX) if core == 0 else slice(0, OV)
        cross_part.append(narrow_band((right if core == 0 else left)[rows]))
    out["near_x"] = np.stack(near_part)
    out["cross_x"] = np.stack(cross_part)
    high, low = halves(spectral_second(CZ) - 2.0 * np.eye(CZ))
    out["own_z"] = np.block([[high, low], [high, np.zeros_like(low)]])

    fine_z = np.arange(CZ)[:, None]
    coarse_z = np.arange(CZC)[None, :]
    weight_z = sum(
        spline_units((fine_z - 2 * coarse_z + image * CZ - 0.5) * 0.5) for image in range(-2, 3)
    )
    zero = np.zeros_like(weight_z.T)
    pair = np.block([[weight_z.T, zero], [zero, weight_z.T]])
    out["grow_z"] = np.concatenate([pair, pair], axis=0)
    zero = np.zeros_like(weight_z)
    out["shrink_z"] = np.block(
        [[weight_z, zero], [weight_z, zero], [zero, weight_z], [zero, weight_z]]
    )

    def column(coarse, start=0, count=CX):
        return spline_units((np.arange(start, start + count) - 2 * coarse - 0.5) * 0.5)

    own = np.stack([column(j) for j in range(CXC)], axis=1)
    lower = {j: column(j) for j in (-2, -1, 0, 1)}
    upper = {j: column(j) for j in (62, 63, 64, 65)}
    stack = lambda d: np.stack([d[j] for j in sorted(d)], axis=1)
    grow_old, grow_new, shrink, shrink_far = [], [], [], []
    blank = np.zeros((CX, 2))
    for core in range(2):
        near = upper if core == 0 else lower
        near_two, far_six = ((64, 65), range(-6, 0)) if core == 0 else ((-2, -1), range(64, 70))
        far_two = (-2, -1) if core == 0 else (64, 65)
        beyond = -OV if core == 0 else CX
        old = np.stack(
            [
                np.concatenate([column(j), column(j, beyond, OV)])
                for j in (*range(CXC), *near_two, *far_six)
            ],
            axis=1,
        )
        inner = own.copy()
        inner[:, [62, 63] if core == 0 else [0, 1]] = 0.0
        outer = np.stack([column(j) for j in far_two], axis=1)
        new = np.concatenate([inner, stack(near), outer, blank], axis=1)
        every = np.concatenate([own, stack(near), outer, blank], axis=1).T
        past = np.zeros((ROWS, OV))
        for row, j in (*enumerate(range(CXC)), *zip((CXC + 4, CXC + 5), far_two)):
            past[row] = column(j, beyond, OV)
        grow_old.append(np.concatenate([old, old], axis=1))
        grow_new.append(np.concatenate([new, new], axis=1))
        shrink.append(np.concatenate([every, every], axis=1))
        shrink_far.append(np.concatenate([past, past], axis=1))
    out["shrink_far"] = np.stack(shrink_far)
    out["grow_old"] = np.stack(grow_old)
    out["grow_new"] = np.stack(grow_new)
    out["shrink_x"] = np.stack(shrink)
    return {name: np.asarray(value).astype(ml_dtypes.bfloat16) for name, value in out.items()}


def taps():
    return [
        [
            (j, float(w))
            for j in range(CYC)
            for w in [
                sum(
                    spline_units(np.float64((i - 2 * j + image * CY - 0.5) * 0.5))
                    for image in range(-2, 3)
                )
            ]
            if w
        ]
        for i in range(CY)
    ]


def split(value):
    high = value.astype(BF)
    return high, (value - high.astype(F32)).astype(BF)


def dot(left, right):
    return jnp.dot(left, right, preferred_element_type=F32)


def cat(parts, axis):
    return jnp.concatenate(parts, axis=axis)


def interior(v, own_x, own_z, out):
    for j in range(CY // 2):
        one, two = 2 * j, 2 * j + 1
        high1, low1 = split(v[one])
        high2, low2 = split(v[two])
        x = dot(own_x[...], cat([cat([high1, high2], 1), cat([low1, low2], 1)], 0))
        z = dot(cat([cat([high1, low1], 1), cat([high2, low2], 1)], 0), own_z[...])
        x = x[:CX] + x[CX:]
        z = z[:, :CZ] + z[:, CZ:]
        beside = v[(one - 1) % CY] + v[two]
        out[one] = x[:, :CZ] + z[:CX] + beside
        beside = v[one] + v[(two + 1) % CY]
        out[two] = x[:, CZ:] + z[CX:] + beside


def halo_part(near, far, field, halo_x, pair):
    parts = []
    for y in (2 * pair, 2 * pair + 1):
        start = (field * CY + y) * OV
        high, low = split(cat([near[start : start + OV], far[start : start + OV]], 0))
        parts.append(cat([high, low, high], 0))
    return dot(halo_x, cat(parts, 1))


def edge_rows(v, core, near, field):
    row = pl.multiple_of((1 - core) * (CX - OV), OV)
    for y in range(CY):
        start = (field * CY + y) * OV
        near[start : start + OV] = v[y, pl.ds(row, OV), :]


def first_edges(p, q, coef, near, far, p_lo, p_hi, q_lo, q_hi, c_lo, c_hi, sems):
    core = lax.axis_index("core")
    block = OV * CY
    copies = [
        pltpu.make_async_copy(source.at[pl.ds(start, size)], target, sems.at[k])
        for k, (source, start, size, target) in enumerate(
            (
                (p, 0, block, p_lo),
                (p, CX * CY - block, block, p_hi),
                (q, 0, block, q_lo),
                (q, CX * CY - block, block, q_hi),
                (coef, 0, 8, c_lo),
                (coef, CXC - 8, 8, c_hi),
            )
        )
    ]
    for copy in copies:
        copy.start()

    def fill(low, high, field):
        for y in range(CY):
            start = (field * CY + y) * OV
            rows = pl.ds(y, OV, stride=CY)
            first, last = low[rows, :], high[rows, :]
            near[start : start + OV] = jnp.where(core == 0, last, first)
            far[start : start + OV] = jnp.where(core == 0, first, last)

    copies[0].wait()
    copies[1].wait()
    fill(p_lo, p_hi, 0)
    copies[2].wait()
    copies[3].wait()
    fill(q_lo, q_hi, 1)
    copies[4].wait()
    copies[5].wait()
    base = 2 * CY * OV
    for row in range(6):
        for part in range(4):
            lanes = slice(part * 128, part * 128 + 128)
            spot = base + row * 4 + part
            if row < 2:
                first = c_lo[row : row + 1, lanes]
                last = c_hi[6 + row : 7 + row, lanes]
                near[spot : spot + 1] = jnp.where(core == 0, last, first)
            first = c_lo[row : row + 1, lanes]
            last = c_hi[2 + row : 3 + row, lanes]
            far[spot : spot + 1] = jnp.where(core == 0, first, last)


def reorder(source, target):
    for y in range(CY):
        target[y] = source[pl.ds(y, CX, stride=CY), :]


def prepare(
    signs, index, wavelet, p_now, q_now, own_x, own_z,
    p0, q0, lap_p, lap_q, source, amounts,
):
    reorder(p_now, p0)
    reorder(q_now, q0)
    interior(p0, own_x, own_z, lap_p)
    interior(q0, own_x, own_z, lap_q)
    source[...] = jnp.zeros_like(source)
    lane = lax.broadcasted_iota(jnp.int32, (1, CZ), 1)

    def add(e, carry):
        spot = index[e]
        x, rest = spot // (CY * CZ), spot % (CY * CZ)
        y, z = rest // CZ, rest % CZ
        amount = (2 * signs[e] - 1).astype(F32)
        row = source[y, pl.ds(x, 1), :]
        source[y, pl.ds(x, 1), :] = row + jnp.where(lane == z, amount, 0.0)
        return carry

    lax.fori_loop(0, ELEMS, add, 0)
    for step in range(STEPS + 1):
        amounts[step] = jnp.full((8, CZ), wavelet[step], F32)


def grow(coef, grow_z, grow_x, write):
    wide = []
    for pair in range(CYC // 2):
        high, low = split(coef[:, pair * 128 : pair * 128 + 128])
        both = dot(cat([high, low], 1), grow_z[...])
        wide += [both[:, :CZ], both[:, CZ:]]
    weights = taps()
    for pair in range(CY // 2):
        parts = []
        for y in (2 * pair, 2 * pair + 1):
            mixed = None
            for j, w in weights[y]:
                term = wide[j] * w
                mixed = term if mixed is None else mixed + term
            parts.append(mixed)
        high, low = split(cat(parts, 1))
        fine = dot(grow_x, cat([high, low], 0))
        write(2 * pair, fine[:, :CZ])
        write(2 * pair + 1, fine[:, CZ:])


UNIT = 1.0 / 384.0**3


def grid_ends():
    core = lax.axis_index("core")
    chip = lax.axis_index("xh") * lax.axis_size("z") + lax.axis_index("z")
    chips = lax.axis_size("xh") * lax.axis_size("z")
    return (core == 0) & (chip == 0), (core == 1) & (chip == chips - 1)


def speed(coef, near, far, grow_z, grow_old, sigma, squared, beyond, held):
    core = lax.axis_index("core")
    held[:CXC] = coef[...]
    base = 2 * CY * OV
    for row in range(6):
        for part in range(4):
            lanes = slice(part * 128, part * 128 + 128)
            spot = base + row * 4 + part
            if row < 2:
                held[CXC + row : CXC + row + 1, lanes] = near[spot : spot + 1]
            held[CXC + 2 + row : CXC + 3 + row, lanes] = far[spot : spot + 1]
    first, last = grid_ends()

    def write(y, fine):
        fine = fine * UNIT
        square = fine * fine
        sigma[y] = fine[:CX]
        squared[y] = square[:CX]
        beyond[y * OV : y * OV + OV] = jnp.where(first | last, 0.0, fine[CX:])

    grow(held[...], grow_z, grow_old[core], write)


def squared_at(beyond, spot):
    value = beyond[spot : spot + OV]
    return value * value


def advance(step, *refs):
    (near, far, p, p_before, q, q_before, lap_p, lap_q, squared, source, amounts, halo_x) = refs[:12]
    refs = refs[12:]
    core = lax.axis_index("core")
    columns = halo_x[core]
    weight = amounts[step, :1, :]
    if step in (1, 3):
        (sent, beyond, cross_x), refs = refs[:3], refs[3:]
        cross = cross_x[core]
    if step == 2:
        old_lap, refs = refs[0], refs[1:]
    if step == 3:
        (old_lap, older_q, gathered, sigma, older_far), refs = refs[:5], refs[5:]
    if step in (0, 2):
        (p_new, q_new, near_out), refs = refs[:3], refs[3:]
    elif step == 1:
        (p_new, q_new, near_out, far_out), refs = refs[:4], refs[4:]
    else:
        p_new, near_out, far_out, image, image_far = refs[:5]
    if step < 2:
        lap_out = refs[0]
    if step == 2:
        gathered = refs[0]
    for pair in range(CY // 2):
        extra_p = halo_part(near, far, 0, columns, pair)
        extra_q = halo_part(near, far, 1, columns, pair)
        for side in range(2):
            y = 2 * pair + side
            lanes = slice(side * CZ, side * CZ + CZ)
            lap = lap_p[y] + extra_p[:, lanes]
            lap_adj = lap_q[y] + extra_q[:, lanes]
            sq = squared[y]
            if step == 0:
                rows = pl.ds(y, CX, stride=CY)
                old_p, old_q = p_before[rows, :], q_before[rows, :]
            else:
                old_p, old_q = p_before[y], q_before[y]
            p_new[y] = 2.0 * p[y] - old_p + sq * lap + source[y] * weight
            new_q = 2.0 * q[y] - old_q + sq * lap_adj
            if step < 3:
                q_new[y] = new_q
            if step < 2:
                lap_out[y] = lap
            if step == 2:
                gathered[y] = q[y] * lap + new_q * old_lap[y]
            if step == 3:
                total = gathered[y] + older_q[y] * lap + new_q * old_lap[y]
                image[y] = 2.0 * sigma[y] * total
    edge_rows(p_new, core, near_out, 0)
    if step < 3:
        edge_rows(q_new, core, near_out, 1)
    if step == 1:
        size = CY * OV
        for pair in range(CY // 2):
            for field in range(2):
                extra = halo_part(sent, sent, field, cross, pair)
                for side in range(2):
                    spot = (2 * pair + side) * OV
                    known = far[(2 + field) * size + spot : (2 + field) * size + spot + OV]
                    far_out[field * size + spot : field * size + spot + OV] = (
                        known
                        + squared_at(beyond, spot) * extra[:OV, side * CZ : side * CZ + CZ]
                    )
    if step == 3:
        size = CY * OV
        for pair in range(CY // 2):
            extra_p = halo_part(sent, sent, 0, cross, pair)
            extra_q = halo_part(sent, sent, 1, cross, pair)
            for side in range(2):
                spot = (2 * pair + side) * OV
                lanes = slice(side * CZ, side * CZ + CZ)
                part_p, part_q = extra_p[:OV, lanes], extra_q[:OV, lanes]
                rows = lambda k: far[k * size + spot : k * size + spot + OV]
                far_out[spot : spot + OV] = rows(2) + squared_at(beyond, spot) * part_p
                near_q = older_far[size + spot : size + spot + OV]
                image_far[spot : spot + OV] = (
                    rows(3) + 2.0 * beyond[spot : spot + OV] * near_q * part_p + rows(4) * part_q
                )


def early(step, *refs):
    (near, p, p_before, q, q_before, lap_p, lap_q, squared, source, amounts, near_x) = refs[:11]
    if step == 3:
        older_q, old_lap, gathered, sigma = refs[11:15]
    out = refs[-1]
    core = lax.axis_index("core")
    rows = pl.ds(pl.multiple_of(core * (CX - OV), OV), OV)
    weight = amounts[step, :1, :]
    columns = near_x[core]
    for pair in range(CY // 2):
        extra_p = halo_part(near, near, 0, columns, pair)
        extra_q = halo_part(near, near, 1, columns, pair)
        for side in range(2):
            y = 2 * pair + side
            lanes = slice(side * CZ, side * CZ + CZ)
            sq = squared[y, rows, :]
            lap = lap_p[y, rows, :] + extra_p[:OV, lanes]
            lap_adj = lap_q[y, rows, :] + extra_q[:OV, lanes]
            edge_p, edge_q = p[y, rows, :], q[y, rows, :]
            next_p = 2.0 * edge_p - p_before[y, rows, :] + sq * lap + source[y, rows, :] * weight
            next_q = 2.0 * edge_q - q_before[y, rows, :] + sq * lap_adj
            if step == 1:
                sets = (edge_p, edge_q, next_p, next_q)
            else:
                twice = 2.0 * sigma[y, rows, :]
                old = old_lap[y, rows, :]
                known = gathered[y, rows, :] + older_q[y, rows, :] * lap + next_q * old
                sets = (edge_p, edge_q, next_p, twice * known, twice * sq * old)
            for k, value in enumerate(sets):
                spot = (k * CY + y) * OV
                out[spot : spot + OV] = value


def inside(p, q, own_x, own_z, lap_p, lap_q):
    interior(p, own_x, own_z, lap_p)
    interior(q, own_x, own_z, lap_q)


def inside_one(p, own_x, own_z, lap_p):
    interior(p, own_x, own_z, lap_p)


def shrink(image, image_far, shrink_x, shrink_far, shrink_z, own):
    core = lax.axis_index("core")
    rows_x = shrink_x[core]
    rows_far = shrink_far[core]
    narrow = [None] * CYC
    weights = taps()
    for pair in range(CY // 2):
        high, low = split(cat([image[2 * pair], image[2 * pair + 1]], 1))
        both = dot(rows_x, cat([high, low], 0))
        spots = [slice(y * OV, y * OV + OV) for y in (2 * pair, 2 * pair + 1)]
        high, low = split(cat([image_far[spots[0]], image_far[spots[1]]], 1))
        both = both + dot(rows_far, cat([high, low], 0))
        for side in range(2):
            part = both[:, side * CZ : side * CZ + CZ]
            for j, w in weights[2 * pair + side]:
                term = part * w
                narrow[j] = term if narrow[j] is None else narrow[j] + term
    pieces = []
    for pair in range(CYC // 2):
        parts = []
        for j in (2 * pair, 2 * pair + 1):
            parts += list(split(narrow[j]))
        pieces.append(dot(cat(parts, 1), shrink_z[...]) * UNIT)
    own[...] = cat(pieces, 1)


def fold(value):
    rows = value[0:8]
    for r in range(1, value.shape[0] // 8):
        rows = rows + value[8 * r : 8 * r + 8]
    folded = rows[:, :128]
    for c in range(1, 4):
        folded = folded + rows[:, 128 * c : 128 * c + 128]
    return folded


def squares(a, b, total, near):
    core = lax.axis_index("core")
    total[...] = a[...] + b[...]
    first, last = grid_ends()
    total[CXC + 4 : CXC + 6] = jnp.where(first | last, 0.0, total[CXC + 4 : CXC + 6])
    row = lax.broadcasted_iota(jnp.int32, (CXC, CYC * CZC), 0)
    start = (1 - core) * (CXC - 2)
    value = jnp.where((row >= start) & (row < start + 2), 0.0, total[:CXC])
    for r in range(4):
        for part in range(4):
            lanes = slice(part * 128, part * 128 + 128)
            spot = r * 4 + part
            near[spot : spot + 1] = total[CXC + r : CXC + r + 1, lanes]
    near[16:24] = fold(value * value)


def pair_up(total, mine, other, out, squared):
    core = lax.axis_index("core")
    out[...] = total[...]
    edge = mine[0:16] + other[0:16]
    for r in range(4):
        for part in range(4):
            lanes = slice(part * 128, part * 128 + 128)
            spot = r * 4 + part
            out[CXC + r : CXC + r + 1, lanes] = edge[spot : spot + 1]
    out[0:2] = jnp.where(core == 0, out[0:2], out[CXC + 2 : CXC + 4])
    out[CXC - 2 : CXC] = jnp.where(core == 0, out[CXC : CXC + 2], out[CXC - 2 : CXC])
    edge = edge * edge
    squared[...] = (mine[16:24] + other[16:24]) + (edge[0:8] + edge[8:16])


def last_fields(near, far, p, p_before, lap_p, source, amounts, halo_x, lap_out, base):
    core = lax.axis_index("core")
    columns = halo_x[core]
    weight = amounts[STEPS, :1, :]
    for pair in range(CY // 2):
        extra = halo_part(near, far, 0, columns, pair)
        for side in range(2):
            y = 2 * pair + side
            lap_out[y] = lap_p[y] + extra[:, side * CZ : side * CZ + CZ]
            base[y] = 2.0 * p[y] - p_before[y] + source[y] * weight


def add_two(a, b, out):
    out[...] = a[...] + b[...]


def spread(total, sigma, lap, base, grow_z, grow_new, zeroth, first, second):
    core = lax.axis_index("core")

    def write(y, fine):
        change = fine * UNIT
        old, curve = sigma[y], lap[y]
        scaled = change * curve
        zeroth[y] = base[y] + old * old * curve
        first[y] = -2.0 * old * scaled
        second[y] = change * scaled

    grow(total[...], grow_z, grow_new[core], write)


def widen(a, b, out):
    value = a[...] + b[...]
    for k in range(out.shape[0]):
        out[k] = value


def finish(count, parts, total, zeroth, first, second, direction, p_last, held, sems):
    value = parts[0]
    for k in range(1, parts.shape[0]):
        value = value + parts[k]
    value = jnp.sum(jnp.sum(value, axis=0, keepdims=True), axis=1, keepdims=True)
    inverse = 1.0 / jnp.sqrt(value * (1.0 / count) + EPSILON)
    rate = LEARN * inverse
    chunks = sems.shape[0]
    step = CX // chunks
    copies = []
    for c in range(chunks):
        rows = slice(c * step, c * step + step)
        for y in range(CY):
            value = zeroth[y, rows] + rate * (first[y, rows] + rate * second[y, rows])
            held[pl.ds(c * step * CY + y, step, stride=CY), :] = value
        block = pl.ds(c * step * CY, step * CY)
        copies.append(pltpu.make_async_copy(held.at[block], p_last.at[block], sems.at[c]))
        copies[-1].start()
    direction[...] = total[:CXC] * inverse
    for copy in copies:
        copy.wait()


VM = pl.BlockSpec(memory_space=pltpu.VMEM)
SM = pl.BlockSpec(memory_space=pltpu.SMEM)
FIELD = jax.ShapeDtypeStruct((CY, CX, CZ), F32)
PARAMS = pltpu.CompilerParams(vmem_limit_bytes=4 * 2**20)


def rows_of(count, lanes=128):
    return jax.ShapeDtypeStruct((count, lanes), F32)


def call(body, outs, *args, smem=0, scratch=(), flops=0, name=None, held=(), out_specs=None):
    size = sum(int(np.prod(a.shape)) * a.dtype.itemsize for a in args)
    count = len(args)

    def run(*refs):
        body(*refs[:count], *refs[count + len(held) :])

    return pl.pallas_call(
        run,
        out_shape=outs,
        in_specs=[SM] * smem
        + [VM] * (count - smem)
        + [pl.BlockSpec(memory_space=pl.ANY)] * len(held),
        out_specs=jax.tree.map(lambda _: VM, outs) if out_specs is None else out_specs,
        scratch_shapes=list(scratch),
        compiler_params=PARAMS,
        cost_estimate=pl.CostEstimate(flops=flops, bytes_accessed=size, transcendentals=0),
        name=name,
    )(*args, *held)


def xor_swap(x, axis, mask):
    count = lax.axis_size(axis)
    if mask >= count:
        return jnp.zeros_like(x)
    return lax.ppermute(x, axis, [(i, i ^ mask) for i in range(count)])


def far_swap(x):
    count = lax.axis_size(TILE)
    pairs = [(i, i + 1) for i in range(1, count - 1, 2)]
    return lax.ppermute(x, TILE, pairs + [(b, a) for a, b in pairs])


def exchange(near, far):
    far = far_swap(far)
    near = xor_swap(near, "core", 1)
    return near, far


def on_device(p_now, p_prev, adj_now, adj_next, coef_old, signs, elem_index, wavelet):
    const = {name: jnp.asarray(value) for name, value in constants().items()}
    own_x, own_z, halo_x = const["own_x"], const["own_z"], const["halo_x"]
    flat = lambda a: a.reshape(CX * CY, CZ)
    p_now, p_prev, adj_now, adj_next = map(flat, (p_now, p_prev, adj_now, adj_next))

    half, edge = rows_of(CY * OV), rows_of(2 * CY * OV)
    with_two, with_six = rows_of(2 * CY * OV + 8), rows_of(2 * CY * OV + 24)
    block = pltpu.VMEM((OV * CY, CZ), F32)
    few = pltpu.VMEM((8, CYC * CZC), F32)
    near, far = pl.pallas_call(
        first_edges,
        out_shape=(with_two, with_six),
        in_specs=[pl.BlockSpec(memory_space=pltpu.HBM)] * 3,
        out_specs=(VM, VM),
        scratch_shapes=[block] * 4 + [few] * 2 + [pltpu.SemaphoreType.DMA((6,))],
        compiler_params=PARAMS,
        name="first_edges",
    )(*(pltpu.with_memory_space_constraint(a, pltpu.HBM) for a in (p_now, adj_now, coef_old)))
    near, far = exchange(near, far)

    p, q, lap_p, lap_q, source, amounts = call(
        prepare,
        (FIELD,) * 5 + (jax.ShapeDtypeStruct((STEPS + 1, 8, CZ), F32),),
        signs[0], elem_index, wavelet, p_now, adj_now, own_x, own_z,
        smem=3, flops=10**9, name="prepare",
    )
    sigma, squared, beyond = call(
        speed, (FIELD, FIELD, rows_of(CY * OV)), coef_old, near, far, const["grow_z"], const["grow_old"],
        scratch=[pltpu.VMEM((ROWS, CYC * CZC), F32)], flops=10**8, name="speed",
    )

    p_before, q_before = p_prev, adj_next
    laps, qs = [], [q]
    gathered = None
    for step in range(STEPS):
        args = [near, far, p, p_before, q, q_before, lap_p, lap_q, squared, source, amounts, halo_x]
        body = functools.partial(advance, step)
        name = f"advance_{step}"
        if step == 0:
            outs = (FIELD, FIELD, edge, FIELD)
        elif step == 1:
            args += [sent, beyond, const["cross_x"]]
            outs = (FIELD, FIELD, edge, edge, FIELD)
            older_far = far
        elif step == 2:
            args.append(laps[1])
            outs = (FIELD, FIELD, edge, FIELD)
        else:
            args += [sent, beyond, const["cross_x"], laps[0], qs[1], gathered, sigma, older_far]
            outs = (FIELD, half, half, FIELD, half)
        result = call(body, outs, *args, flops=10**8, name=name)
        if step == 3:
            p_new, near, far, image, image_far = result
            p, p_before = p_new, p
            continue
        p_new, q_new, *edges, other = result
        if step < 2:
            laps.append(other)
        else:
            gathered = other
        p, p_before = p_new, p
        q, q_before = q_new, q
        qs.append(q)
        near = xor_swap(edges[0], "core", 1)
        lap_p, lap_q = call(
            inside, (FIELD, FIELD), p, q, own_x, own_z, flops=10**9, name=f"inside_{step}"
        )
        if step == 1:
            far = edges[1]
            continue
        args = [near, p, p_before, q, q_before, lap_p, lap_q, squared, source, amounts]
        args.append(const["near_x"])
        if step == 2:
            args += [qs[1], laps[0], gathered, sigma]
        sent = call(
            functools.partial(early, step + 1), rows_of((4 if step == 0 else 5) * CY * OV),
            *args, flops=10**7, name=f"early_{step + 1}",
        )
        far = far_swap(sent)

    partial = call(
        shrink, rows_of(ROWS, CYC * CZC),
        image, image_far, const["shrink_x"], const["shrink_far"], const["shrink_z"],
        flops=10**8, name="shrink",
    )
    other = xor_swap(partial, "y", 1)
    near = xor_swap(near, "core", 1)
    lap_p = call(inside_one, FIELD, p, own_x, own_z, flops=5 * 10**8, name="inside_last")
    lap_p, base = call(
        last_fields, (FIELD, FIELD), near, far, p, p_before, lap_p, source, amounts, halo_x,
        flops=10**8, name="last_fields",
    )
    held = (lap_p, base)
    partial = call(
        add_two, rows_of(ROWS, CYC * CZC), partial, other, name="add_y1", held=held
    )
    partial = call(
        add_two, rows_of(ROWS, CYC * CZC), partial, xor_swap(partial, "y", 3), name="add_y3",
        held=held,
    )
    total, mine = call(
        squares, (rows_of(ROWS, CYC * CZC), rows_of(24)), partial, xor_swap(partial, "xl", 1),
        name="squares", held=held,
    )
    total, squared_sum = call(
        pair_up, (rows_of(ROWS, CYC * CZC), rows_of(8)), total, mine, xor_swap(mine, "core", 1),
        name="pair_up", held=held,
    )
    terms = call(
        spread, (FIELD,) * 3, total, sigma, lap_p, base, const["grow_z"], const["grow_new"],
        flops=10**8, name="spread",
    )
    deep = lax.axis_size("z")
    copies = call(
        widen, jax.ShapeDtypeStruct((deep, 8, 128), F32),
        squared_sum, xor_swap(squared_sum, "xh", 1), name="widen", held=terms,
    )
    parts = lax.all_to_all(copies, "z", split_axis=0, concat_axis=0, tiled=True)
    count = float(lax.axis_size(TILE) * CXC * CYC * CZC)
    direction, p_last = call(
        functools.partial(finish, count),
        (rows_of(CXC, CYC * CZC), pltpu.HBM((CX * CY, CZ), F32)),
        parts, total, *terms, name="finish",
        scratch=[pltpu.VMEM((CX * CY, CZ), F32), pltpu.SemaphoreType.DMA((4,))],
        out_specs=(VM, pl.BlockSpec(memory_space=pltpu.HBM)),
    )
    return direction, p_last.reshape(1, CX, CY, CZ)


def solution(mesh):
    shots, tiles = mesh.shape["shot"], mesh.shape["tile"]
    fine = Mesh(
        mesh.devices.reshape(shots // 2, 2, 2, tiles // 4, 2), ("y", "xl", "xh", "z", "core")
    )
    placed = (
        P(SHOT, TILE, None, None),
        P(SHOT, TILE, None, None),
        P(SHOT, TILE, None, None),
        P(SHOT, TILE, None, None),
        P(TILE, None),
        P(SHOT, TILE),
        P(TILE),
        P(),
    )
    return jax.shard_map(
        on_device,
        mesh=fine,
        in_specs=placed,
        out_specs=(P(TILE, None), P(SHOT, TILE, None, None)),
        check_vma=False,
    )
```

```python
import functools

import jax
import jax.numpy as jnp
import ml_dtypes
import numpy as np
from jax import lax
from jax.experimental import pallas as pl
from jax.experimental.pallas import tpu as pltpu
from jax.sharding import Mesh
from jax.sharding import PartitionSpec as P

CX = 128
CZ = 128
CY = 16
OV = 8
STEPS = 4
ELEMS = 64
CXC = 64
CYC = 8
CZC = 64
ROWS = 72
THIRD = 24
LEARN = 0.02
EPSILON = 1e-06
BF = jnp.bfloat16
F32 = jnp.float32
SHOT = ("y", "xl")
TILE = ("xh", "z", "core")


def spectral_second(length):
    index = np.arange(length)
    number = np.minimum(index, length - index) * (2.0 * np.pi / length)
    phase = (index[:, None, None] - index[None, :, None]) * index[None, None, :] % length
    return -np.sum(number**2 * np.cos(2.0 * np.pi / length * phase), axis=2) / length


def spline_units(offset):
    mag = np.abs(offset)
    inner = 2.0 / 3.0 - mag**2 + 0.5 * mag**3
    outer = (2.0 - mag) ** 3 / 6.0
    return np.round(384.0 * np.where(mag < 1.0, inner, np.where(mag < 2.0, outer, 0.0)))


def halves(matrix):
    high = matrix.astype(np.float32).astype(ml_dtypes.bfloat16)
    low = (matrix - high.astype(np.float64)).astype(np.float32).astype(ml_dtypes.bfloat16)
    return high, low


def narrow_band(matrix):
    high, low = halves(np.pad(matrix, ((0, OV), (0, OV))))
    return np.concatenate([high, high, low], axis=1)


@functools.cache
def constants():
    out = {}
    second_x = spectral_second(CX + 2 * OV)[OV : OV + CX]
    ramp = np.sin(0.5 * np.pi * (np.arange(OV) + 0.5) / OV) ** 2
    left = second_x[:, :OV] * ramp[None, :]
    right = second_x[:, OV + CX :] * ramp[None, ::-1]
    high, low = halves(second_x[:, OV : OV + CX])
    out["own_x"] = np.block([[high, high], [low, low]])
    sides = []
    for pair in ((right, left), (left, right)):
        high, low = halves(np.concatenate(pair, axis=1))
        sides.append(np.concatenate([high, high, low], axis=1))
    out["halo_x"] = np.stack(sides)
    near_part, cross_part = [], []
    for core in range(2):
        rows = slice(0, OV) if core == 0 else slice(CX - OV, CX)
        near_part.append(narrow_band((right if core == 0 else left)[rows]))
        rows = slice(CX - OV, CX) if core == 0 else slice(0, OV)
        cross_part.append(narrow_band((right if core == 0 else left)[rows]))
    out["near_x"] = np.stack(near_part)
    out["cross_x"] = np.stack(cross_part)
    high, low = halves(spectral_second(CZ) - 2.0 * np.eye(CZ))
    out["own_z"] = np.block([[high, low], [high, low]])

    fine_z = np.arange(CZ)[:, None]
    coarse_z = np.arange(CZC)[None, :]
    weight_z = sum(
        spline_units((fine_z - 2 * coarse_z + image * CZ - 0.5) * 0.5) for image in range(-2, 3)
    )
    zero = np.zeros_like(weight_z.T)
    pair = np.block([[weight_z.T, zero], [zero, weight_z.T]])
    out["grow_z"] = np.concatenate([pair, pair], axis=0)
    zero = np.zeros_like(weight_z)
    out["shrink_z"] = np.block(
        [[weight_z, zero], [weight_z, zero], [zero, weight_z], [zero, weight_z]]
    )

    def column(coarse, start=0, count=CX):
        return spline_units((np.arange(start, start + count) - 2 * coarse - 0.5) * 0.5)

    own = np.stack([column(j) for j in range(CXC)], axis=1)
    lower = {j: column(j) for j in (-2, -1, 0, 1)}
    upper = {j: column(j) for j in (62, 63, 64, 65)}
    stack = lambda d: np.stack([d[j] for j in sorted(d)], axis=1)
    grow_old, grow_new, shrink, shrink_far = [], [], [], []
    blank = np.zeros((CX, 2))
    for core in range(2):
        near = upper if core == 0 else lower
        near_two, far_six = ((64, 65), range(-6, 0)) if core == 0 else ((-2, -1), range(64, 70))
        far_two = (-2, -1) if core == 0 else (64, 65)
        beyond = -OV if core == 0 else CX
        old = np.stack(
            [
                np.concatenate([column(j), column(j, beyond, OV)])
                for j in (*range(CXC), *near_two, *far_six)
            ],
            axis=1,
        )
        inner = own.copy()
        inner[:, [62, 63] if core == 0 else [0, 1]] = 0.0
        outer = np.stack([column(j) for j in far_two], axis=1)
        new = np.concatenate([inner, stack(near), outer, blank], axis=1)
        every = np.concatenate([own, stack(near), outer, blank], axis=1).T
        past = np.zeros((ROWS, OV))
        for row, j in (*enumerate(range(CXC)), *zip((CXC + 4, CXC + 5), far_two)):
            past[row] = column(j, beyond, OV)
        grow_old.append(np.concatenate([old, old], axis=1))
        grow_new.append(np.concatenate([new, new], axis=1))
        shrink.append(np.concatenate([every, every], axis=1))
        shrink_far.append(np.concatenate([past, past], axis=1))
    out["shrink_far"] = np.stack(shrink_far)
    out["grow_old"] = np.stack(grow_old)
    out["grow_new"] = np.stack(grow_new)
    out["shrink_x"] = np.stack(shrink)
    return {name: np.asarray(value).astype(ml_dtypes.bfloat16) for name, value in out.items()}


def taps():
    return [
        [
            (j, float(w))
            for j in range(CYC)
            for w in [
                sum(
                    spline_units(np.float64((i - 2 * j + image * CY - 0.5) * 0.5))
                    for image in range(-2, 3)
                )
            ]
            if w
        ]
        for i in range(CY)
    ]


def split(value):
    high = value.astype(BF)
    return high, (value - high.astype(F32)).astype(BF)


def dot(left, right):
    return jnp.dot(left, right, preferred_element_type=F32)


def cat(parts, axis):
    return jnp.concatenate(parts, axis=axis)


def interior(v, own_x, own_z, out):
    for j in range(CY // 2):
        one, two = 2 * j, 2 * j + 1
        high1, low1 = split(v[one])
        high2, low2 = split(v[two])
        x = dot(own_x[...], cat([cat([high1, high2], 1), cat([low1, low2], 1)], 0))
        z = dot(cat([cat([high1, low1], 1), cat([high2, low2], 1)], 0), own_z[...])
        x = x[:CX] + x[CX:]
        z = z[:, :CZ] + z[:, CZ:]
        beside = v[(one - 1) % CY] + v[two]
        out[one] = x[:, :CZ] + z[:CX] + beside
        beside = v[one] + v[(two + 1) % CY]
        out[two] = x[:, CZ:] + z[CX:] + beside


def halo_part(near, far, field, halo_x, pair):
    parts = []
    for y in (2 * pair, 2 * pair + 1):
        start = (field * CY + y) * OV
        high, low = split(cat([near[start : start + OV], far[start : start + OV]], 0))
        parts.append(cat([high, low, high], 0))
    return dot(halo_x, cat(parts, 1))


def edge_rows(v, core, near, field):
    row = pl.multiple_of((1 - core) * (CX - OV), OV)
    for y in range(CY):
        start = (field * CY + y) * OV
        near[start : start + OV] = v[y, pl.ds(row, OV), :]


def first_edges(p, q, coef, near, far, p_lo, p_hi, q_lo, q_hi, c_lo, c_hi, sems):
    core = lax.axis_index("core")
    block = OV * CY
    copies = [
        pltpu.make_async_copy(source.at[pl.ds(start, size)], target, sems.at[k])
        for k, (source, start, size, target) in enumerate(
            (
                (p, 0, block, p_lo),
                (p, CX * CY - block, block, p_hi),
                (q, 0, block, q_lo),
                (q, CX * CY - block, block, q_hi),
                (coef, 0, 8, c_lo),
                (coef, CXC - 8, 8, c_hi),
            )
        )
    ]
    for copy in copies:
        copy.start()

    def fill(low, high, field):
        for y in range(CY):
            start = (field * CY + y) * OV
            rows = pl.ds(y, OV, stride=CY)
            first, last = low[rows, :], high[rows, :]
            near[start : start + OV] = jnp.where(core == 0, last, first)
            far[start : start + OV] = jnp.where(core == 0, first, last)

    copies[0].wait()
    copies[1].wait()
    fill(p_lo, p_hi, 0)
    copies[2].wait()
    copies[3].wait()
    fill(q_lo, q_hi, 1)
    copies[4].wait()
    copies[5].wait()
    base = 2 * CY * OV
    for row in range(6):
        for part in range(4):
            lanes = slice(part * 128, part * 128 + 128)
            spot = base + row * 4 + part
            if row < 2:
                first = c_lo[row : row + 1, lanes]
                last = c_hi[6 + row : 7 + row, lanes]
                near[spot : spot + 1] = jnp.where(core == 0, last, first)
            first = c_lo[row : row + 1, lanes]
            last = c_hi[2 + row : 3 + row, lanes]
            far[spot : spot + 1] = jnp.where(core == 0, first, last)


def reorder(source, target):
    for y in range(CY):
        target[y] = source[pl.ds(y, CX, stride=CY), :]


def prepare(
    signs, index, wavelet, p_now, q_now, own_x, own_z,
    p0, q0, lap_p, lap_q, source, amounts,
):
    reorder(p_now, p0)
    reorder(q_now, q0)
    interior(p0, own_x, own_z, lap_p)
    interior(q0, own_x, own_z, lap_q)
    source[...] = jnp.zeros_like(source)
    lane = lax.broadcasted_iota(jnp.int32, (1, CZ), 1)

    def add(e, carry):
        spot = index[e]
        x, rest = spot // (CY * CZ), spot % (CY * CZ)
        y, z = rest // CZ, rest % CZ
        amount = (2 * signs[e] - 1).astype(F32)
        row = source[y, pl.ds(x, 1), :]
        source[y, pl.ds(x, 1), :] = row + jnp.where(lane == z, amount, 0.0)
        return carry

    lax.fori_loop(0, ELEMS, add, 0)
    for step in range(STEPS + 1):
        amounts[step] = jnp.full((8, CZ), wavelet[step], F32)


def grow(coef, grow_z, grow_x, write):
    wide = []
    for pair in range(CYC // 2):
        high, low = split(coef[:, pair * 128 : pair * 128 + 128])
        both = dot(cat([high, low], 1), grow_z[...])
        wide += [both[:, :CZ], both[:, CZ:]]
    weights = taps()
    for pair in range(CY // 2):
        parts = []
        for y in (2 * pair, 2 * pair + 1):
            mixed = None
            for j, w in weights[y]:
                term = wide[j] * w
                mixed = term if mixed is None else mixed + term
            parts.append(mixed)
        high, low = split(cat(parts, 1))
        fine = dot(grow_x, cat([high, low], 0))
        write(2 * pair, fine[:, :CZ])
        write(2 * pair + 1, fine[:, CZ:])


UNIT = 1.0 / 384.0**3


def grid_ends():
    core = lax.axis_index("core")
    chip = lax.axis_index("xh") * lax.axis_size("z") + lax.axis_index("z")
    chips = lax.axis_size("xh") * lax.axis_size("z")
    return (core == 0) & (chip == 0), (core == 1) & (chip == chips - 1)


def speed(coef, near, far, grow_z, grow_old, sigma, squared, beyond, held):
    core = lax.axis_index("core")
    held[:CXC] = coef[...]
    base = 2 * CY * OV
    for row in range(6):
        for part in range(4):
            lanes = slice(part * 128, part * 128 + 128)
            spot = base + row * 4 + part
            if row < 2:
                held[CXC + row : CXC + row + 1, lanes] = near[spot : spot + 1]
            held[CXC + 2 + row : CXC + 3 + row, lanes] = far[spot : spot + 1]
    first, last = grid_ends()

    def write(y, fine):
        fine = fine * UNIT
        square = fine * fine
        sigma[y] = fine[:CX]
        squared[y] = square[:CX]
        beyond[y * OV : y * OV + OV] = jnp.where(first | last, 0.0, fine[CX:])

    grow(held[...], grow_z, grow_old[core], write)


def squared_at(beyond, spot):
    value = beyond[spot : spot + OV]
    return value * value


def advance(step, *refs):
    (near, far, p, p_before, q, q_before, lap_p, lap_q, squared, source, amounts, halo_x) = refs[:12]
    refs = refs[12:]
    core = lax.axis_index("core")
    columns = halo_x[core]
    weight = amounts[step, :1, :]
    if step in (1, 3):
        (sent, beyond, cross_x), refs = refs[:3], refs[3:]
        cross = cross_x[core]
    if step == 2:
        old_lap, refs = refs[0], refs[1:]
    if step == 3:
        (old_lap, older_q, gathered, sigma, older_far), refs = refs[:5], refs[5:]
    if step in (0, 2):
        (p_new, q_new, near_out), refs = refs[:3], refs[3:]
    elif step == 1:
        (p_new, q_new, near_out, far_out), refs = refs[:4], refs[4:]
    else:
        p_new, near_out, far_out, image, image_far = refs[:5]
    if step < 2:
        lap_out = refs[0]
    if step == 2:
        gathered = refs[0]
    for pair in range(CY // 2):
        extra_p = halo_part(near, far, 0, columns, pair)
        extra_q = halo_part(near, far, 1, columns, pair)
        for side in range(2):
            y = 2 * pair + side
            lanes = slice(side * CZ, side * CZ + CZ)
            lap = lap_p[y] + extra_p[:, lanes]
            lap_adj = lap_q[y] + extra_q[:, lanes]
            sq = squared[y]
            if step == 0:
                rows = pl.ds(y, CX, stride=CY)
                old_p, old_q = p_before[rows, :], q_before[rows, :]
            else:
                old_p, old_q = p_before[y], q_before[y]
            p_new[y] = 2.0 * p[y] - old_p + sq * lap + source[y] * weight
            new_q = 2.0 * q[y] - old_q + sq * lap_adj
            if step < 3:
                q_new[y] = new_q
            if step < 2:
                lap_out[y] = lap
            if step == 2:
                gathered[y] = q[y] * lap + new_q * old_lap[y]
            if step == 3:
                total = gathered[y] + older_q[y] * lap + new_q * old_lap[y]
                image[y] = 2.0 * sigma[y] * total
    edge_rows(p_new, core, near_out, 0)
    if step < 3:
        edge_rows(q_new, core, near_out, 1)
    if step == 1:
        size = CY * OV
        for pair in range(CY // 2):
            for field in range(2):
                extra = halo_part(sent, sent, field, cross, pair)
                for side in range(2):
                    spot = (2 * pair + side) * OV
                    known = far[(2 + field) * size + spot : (2 + field) * size + spot + OV]
                    far_out[field * size + spot : field * size + spot + OV] = (
                        known
                        + squared_at(beyond, spot) * extra[:OV, side * CZ : side * CZ + CZ]
                    )
    if step == 3:
        size = CY * OV
        for pair in range(CY // 2):
            extra_p = halo_part(sent, sent, 0, cross, pair)
            extra_q = halo_part(sent, sent, 1, cross, pair)
            for side in range(2):
                spot = (2 * pair + side) * OV
                lanes = slice(side * CZ, side * CZ + CZ)
                part_p, part_q = extra_p[:OV, lanes], extra_q[:OV, lanes]
                rows = lambda k: far[k * size + spot : k * size + spot + OV]
                far_out[spot : spot + OV] = rows(2) + squared_at(beyond, spot) * part_p
                near_q = older_far[size + spot : size + spot + OV]
                image_far[spot : spot + OV] = (
                    rows(3) + 2.0 * beyond[spot : spot + OV] * near_q * part_p + rows(4) * part_q
                )


def early(step, *refs):
    (near, p, p_before, q, q_before, lap_p, lap_q, squared, source, amounts, near_x) = refs[:11]
    if step == 3:
        older_q, old_lap, gathered, sigma = refs[11:15]
    out = refs[-1]
    core = lax.axis_index("core")
    rows = pl.ds(pl.multiple_of(core * (CX - OV), OV), OV)
    weight = amounts[step, :1, :]
    columns = near_x[core]
    for pair in range(CY // 2):
        extra_p = halo_part(near, near, 0, columns, pair)
        extra_q = halo_part(near, near, 1, columns, pair)
        for side in range(2):
            y = 2 * pair + side
            lanes = slice(side * CZ, side * CZ + CZ)
            sq = squared[y, rows, :]
            lap = lap_p[y, rows, :] + extra_p[:OV, lanes]
            lap_adj = lap_q[y, rows, :] + extra_q[:OV, lanes]
            edge_p, edge_q = p[y, rows, :], q[y, rows, :]
            next_p = 2.0 * edge_p - p_before[y, rows, :] + sq * lap + source[y, rows, :] * weight
            next_q = 2.0 * edge_q - q_before[y, rows, :] + sq * lap_adj
            if step == 1:
                sets = (edge_p, edge_q, next_p, next_q)
            else:
                twice = 2.0 * sigma[y, rows, :]
                old = old_lap[y, rows, :]
                known = gathered[y, rows, :] + older_q[y, rows, :] * lap + next_q * old
                sets = (edge_p, edge_q, next_p, twice * known, twice * sq * old)
            for k, value in enumerate(sets):
                spot = (k * CY + y) * OV
                out[spot : spot + OV] = value


def inside(p, q, own_x, own_z, lap_p, lap_q):
    interior(p, own_x, own_z, lap_p)
    interior(q, own_x, own_z, lap_q)


def inside_one(p, own_x, own_z, lap_p):
    interior(p, own_x, own_z, lap_p)


def shrink(image, image_far, shrink_x, shrink_far, shrink_z, *thirds):
    core = lax.axis_index("core")
    rows_x = shrink_x[core]
    rows_far = shrink_far[core]
    narrow = [None] * CYC
    weights = taps()
    for pair in range(CY // 2):
        high, low = split(cat([image[2 * pair], image[2 * pair + 1]], 1))
        both = dot(rows_x, cat([high, low], 0))
        spots = [slice(y * OV, y * OV + OV) for y in (2 * pair, 2 * pair + 1)]
        high, low = split(cat([image_far[spots[0]], image_far[spots[1]]], 1))
        both = both + dot(rows_far, cat([high, low], 0))
        for side in range(2):
            part = both[:, side * CZ : side * CZ + CZ]
            for j, w in weights[2 * pair + side]:
                term = part * w
                narrow[j] = term if narrow[j] is None else narrow[j] + term
    pieces = []
    for pair in range(CYC // 2):
        parts = []
        for j in (2 * pair, 2 * pair + 1):
            parts += list(split(narrow[j]))
        pieces.append(dot(cat(parts, 1), shrink_z[...]) * UNIT)
    whole = cat(pieces, 1)
    for k, third in enumerate(thirds):
        third[...] = whole[k * THIRD : k * THIRD + THIRD]


def fold(value):
    rows = value[0:8]
    for r in range(1, value.shape[0] // 8):
        rows = rows + value[8 * r : 8 * r + 8]
    folded = rows[:, :128]
    for c in range(1, 4):
        folded = folded + rows[:, 128 * c : 128 * c + 128]
    return folded


def squares(*refs):
    core = lax.axis_index("core")
    total, near = refs[6:]
    for k in range(3):
        total[k * THIRD : k * THIRD + THIRD] = refs[k][...] + refs[3 + k][...]
    first, last = grid_ends()
    total[CXC + 4 : CXC + 6] = jnp.where(first | last, 0.0, total[CXC + 4 : CXC + 6])
    row = lax.broadcasted_iota(jnp.int32, (CXC, CYC * CZC), 0)
    start = (1 - core) * (CXC - 2)
    value = jnp.where((row >= start) & (row < start + 2), 0.0, total[:CXC])
    for r in range(4):
        for part in range(4):
            lanes = slice(part * 128, part * 128 + 128)
            spot = r * 4 + part
            near[spot : spot + 1] = total[CXC + r : CXC + r + 1, lanes]
    near[16:24] = fold(value * value)


def pair_up(total, mine, other, out, squared):
    core = lax.axis_index("core")
    out[...] = total[...]
    edge = mine[0:16] + other[0:16]
    for r in range(4):
        for part in range(4):
            lanes = slice(part * 128, part * 128 + 128)
            spot = r * 4 + part
            out[CXC + r : CXC + r + 1, lanes] = edge[spot : spot + 1]
    out[0:2] = jnp.where(core == 0, out[0:2], out[CXC + 2 : CXC + 4])
    out[CXC - 2 : CXC] = jnp.where(core == 0, out[CXC : CXC + 2], out[CXC - 2 : CXC])
    edge = edge * edge
    squared[...] = (mine[16:24] + other[16:24]) + (edge[0:8] + edge[8:16])


def last_fields(near, far, p, p_before, lap_p, source, amounts, halo_x, lap_out, base):
    core = lax.axis_index("core")
    columns = halo_x[core]
    weight = amounts[STEPS, :1, :]
    for pair in range(CY // 2):
        extra = halo_part(near, far, 0, columns, pair)
        for side in range(2):
            y = 2 * pair + side
            lap_out[y] = lap_p[y] + extra[:, side * CZ : side * CZ + CZ]
            base[y] = 2.0 * p[y] - p_before[y] + source[y] * weight


def add_thirds(*refs):
    for mine, other, out in zip(refs[:3], refs[3:6], refs[6:]):
        out[...] = mine[...] + other[...]


def spread(total, sigma, lap, base, grow_z, grow_new, zeroth, first, second):
    core = lax.axis_index("core")

    def write(y, fine):
        change = fine * UNIT
        old, curve = sigma[y], lap[y]
        scaled = change * curve
        zeroth[y] = base[y] + old * old * curve
        first[y] = -2.0 * old * scaled
        second[y] = change * scaled

    grow(total[...], grow_z, grow_new[core], write)


def widen(a, b, out):
    value = a[...] + b[...]
    for k in range(out.shape[0]):
        out[k] = value


def finish(count, parts, total, zeroth, first, second, direction, p_last):
    value = parts[0]
    for k in range(1, parts.shape[0]):
        value = value + parts[k]
    value = jnp.sum(jnp.sum(value, axis=0, keepdims=True), axis=1, keepdims=True)
    inverse = 1.0 / jnp.sqrt(value * (1.0 / count) + EPSILON)
    rate = LEARN * inverse
    for y in range(CY):
        value = zeroth[y] + rate * (first[y] + rate * second[y])
        p_last[pl.ds(y, CX, stride=CY), :] = value
    direction[...] = total[:CXC] * inverse


VM = pl.BlockSpec(memory_space=pltpu.VMEM)
SM = pl.BlockSpec(memory_space=pltpu.SMEM)
FIELD = jax.ShapeDtypeStruct((CY, CX, CZ), F32)
PARAMS = pltpu.CompilerParams(vmem_limit_bytes=4 * 2**20)


def rows_of(count, lanes=128):
    return jax.ShapeDtypeStruct((count, lanes), F32)


def call(body, outs, *args, smem=0, scratch=(), flops=0, name=None, held=(), out_specs=None):
    size = sum(int(np.prod(a.shape)) * a.dtype.itemsize for a in args)
    count = len(args)

    def run(*refs):
        body(*refs[:count], *refs[count + len(held) :])

    return pl.pallas_call(
        run,
        out_shape=outs,
        in_specs=[SM] * smem
        + [VM] * (count - smem)
        + [pl.BlockSpec(memory_space=pl.ANY)] * len(held),
        out_specs=jax.tree.map(lambda _: VM, outs) if out_specs is None else out_specs,
        scratch_shapes=list(scratch),
        compiler_params=PARAMS,
        cost_estimate=pl.CostEstimate(flops=flops, bytes_accessed=size, transcendentals=0),
        name=name,
    )(*args, *held)


def xor_swap(x, axis, mask):
    count = lax.axis_size(axis)
    if mask >= count:
        return jnp.zeros_like(x)
    return lax.ppermute(x, axis, [(i, i ^ mask) for i in range(count)])


def far_swap(x):
    count = lax.axis_size(TILE)
    pairs = [(i, i + 1) for i in range(1, count - 1, 2)]
    return lax.ppermute(x, TILE, pairs + [(b, a) for a, b in pairs])


def exchange(near, far):
    far = far_swap(far)
    near = xor_swap(near, "core", 1)
    return near, far


def on_device(p_now, p_prev, adj_now, adj_next, coef_old, signs, elem_index, wavelet):
    const = {name: jnp.asarray(value) for name, value in constants().items()}
    own_x, own_z, halo_x = const["own_x"], const["own_z"], const["halo_x"]
    flat = lambda a: a.reshape(CX * CY, CZ)
    p_now, p_prev, adj_now, adj_next = map(flat, (p_now, p_prev, adj_now, adj_next))

    half, edge = rows_of(CY * OV), rows_of(2 * CY * OV)
    with_two, with_six = rows_of(2 * CY * OV + 8), rows_of(2 * CY * OV + 24)
    block = pltpu.VMEM((OV * CY, CZ), F32)
    few = pltpu.VMEM((8, CYC * CZC), F32)
    near, far = pl.pallas_call(
        first_edges,
        out_shape=(with_two, with_six),
        in_specs=[pl.BlockSpec(memory_space=pltpu.HBM)] * 3,
        out_specs=(VM, VM),
        scratch_shapes=[block] * 4 + [few] * 2 + [pltpu.SemaphoreType.DMA((6,))],
        compiler_params=PARAMS,
        name="first_edges",
    )(*(pltpu.with_memory_space_constraint(a, pltpu.HBM) for a in (p_now, adj_now, coef_old)))
    near, far = exchange(near, far)

    p, q, lap_p, lap_q, source, amounts = call(
        prepare,
        (FIELD,) * 5 + (jax.ShapeDtypeStruct((STEPS + 1, 8, CZ), F32),),
        signs[0], elem_index, wavelet, p_now, adj_now, own_x, own_z,
        smem=3, flops=10**9, name="prepare",
    )
    sigma, squared, beyond = call(
        speed, (FIELD, FIELD, rows_of(CY * OV)), coef_old, near, far, const["grow_z"], const["grow_old"],
        scratch=[pltpu.VMEM((ROWS, CYC * CZC), F32)], flops=10**8, name="speed",
    )

    p_before, q_before = p_prev, adj_next
    laps, qs = [], [q]
    gathered = None
    for step in range(STEPS):
        args = [near, far, p, p_before, q, q_before, lap_p, lap_q, squared, source, amounts, halo_x]
        body = functools.partial(advance, step)
        name = f"advance_{step}"
        if step == 0:
            outs = (FIELD, FIELD, edge, FIELD)
        elif step == 1:
            args += [sent, beyond, const["cross_x"]]
            outs = (FIELD, FIELD, edge, edge, FIELD)
            older_far = far
        elif step == 2:
            args.append(laps[1])
            outs = (FIELD, FIELD, edge, FIELD)
        else:
            args += [sent, beyond, const["cross_x"], laps[0], qs[1], gathered, sigma, older_far]
            outs = (FIELD, half, half, FIELD, half)
        result = call(body, outs, *args, flops=10**8, name=name)
        if step == 3:
            p_new, near, far, image, image_far = result
            p, p_before = p_new, p
            continue
        p_new, q_new, *edges, other = result
        if step < 2:
            laps.append(other)
        else:
            gathered = other
        p, p_before = p_new, p
        q, q_before = q_new, q
        qs.append(q)
        near = xor_swap(edges[0], "core", 1)
        lap_p, lap_q = call(
            inside, (FIELD, FIELD), p, q, own_x, own_z, flops=10**9, name=f"inside_{step}"
        )
        if step == 1:
            far = edges[1]
            continue
        args = [near, p, p_before, q, q_before, lap_p, lap_q, squared, source, amounts]
        args.append(const["near_x"])
        if step == 2:
            args += [qs[1], laps[0], gathered, sigma]
        sent = call(
            functools.partial(early, step + 1), rows_of((4 if step == 0 else 5) * CY * OV),
            *args, flops=10**7, name=f"early_{step + 1}",
        )
        far = far_swap(sent)

    thirds = (rows_of(THIRD, CYC * CZC),) * 3
    partial = call(
        shrink, thirds,
        image, image_far, const["shrink_x"], const["shrink_far"], const["shrink_z"],
        flops=10**8, name="shrink",
    )
    ways = (("xl", 1), ("y", 1), ("y", 3))

    def swapped(stage):
        return [xor_swap(x, *ways[(k + stage) % 3]) for k, x in enumerate(partial)]

    other = swapped(0)
    near = xor_swap(near, "core", 1)
    lap_p = call(inside_one, FIELD, p, own_x, own_z, flops=5 * 10**8, name="inside_last")
    lap_p, base = call(
        last_fields, (FIELD, FIELD), near, far, p, p_before, lap_p, source, amounts, halo_x,
        flops=10**8, name="last_fields",
    )
    held = (lap_p, base)
    partial = call(add_thirds, thirds, *partial, *other, name="add_1", held=held)
    partial = call(add_thirds, thirds, *partial, *swapped(1), name="add_2", held=held)
    total, mine = call(
        squares, (rows_of(ROWS, CYC * CZC), rows_of(24)), *partial, *swapped(2),
        name="squares", held=held,
    )
    total, squared_sum = call(
        pair_up, (rows_of(ROWS, CYC * CZC), rows_of(8)), total, mine, xor_swap(mine, "core", 1),
        name="pair_up", held=held,
    )
    terms = call(
        spread, (FIELD,) * 3, total, sigma, lap_p, base, const["grow_z"], const["grow_new"],
        flops=10**8, name="spread",
    )
    deep = lax.axis_size("z")
    copies = call(
        widen, jax.ShapeDtypeStruct((deep, 8, 128), F32),
        squared_sum, xor_swap(squared_sum, "xh", 1), name="widen", held=terms,
    )
    parts = lax.all_to_all(copies, "z", split_axis=0, concat_axis=0, tiled=True)
    count = float(lax.axis_size(TILE) * CXC * CYC * CZC)
    direction, p_last = call(
        functools.partial(finish, count),
        (rows_of(CXC, CYC * CZC), rows_of(CX * CY)),
        parts, total, *terms, name="finish",
    )
    return direction, p_last.reshape(1, CX, CY, CZ)


def solution(mesh):
    shots, tiles = mesh.shape["shot"], mesh.shape["tile"]
    fine = Mesh(
        mesh.devices.reshape(shots // 2, 2, 2, tiles // 4, 2), ("y", "xl", "xh", "z", "core")
    )
    placed = (
        P(SHOT, TILE, None, None),
        P(SHOT, TILE, None, None),
        P(SHOT, TILE, None, None),
        P(SHOT, TILE, None, None),
        P(TILE, None),
        P(SHOT, TILE),
        P(TILE),
        P(),
    )
    return jax.shard_map(
        on_device,
        mesh=fine,
        in_specs=placed,
        out_specs=(P(TILE, None), P(SHOT, TILE, None, None)),
        check_vma=False,
    )
```

```python
import functools

import jax
import jax.numpy as jnp
import ml_dtypes
import numpy as np
from jax import lax
from jax.experimental import pallas as pl
from jax.experimental.pallas import tpu as pltpu
from jax.sharding import Mesh
from jax.sharding import PartitionSpec as P

CX = 128
CZ = 128
CY = 16
OV = 8
STEPS = 4
ELEMS = 64
CXC = 64
CYC = 8
CZC = 64
ROWS = 72
LEARN = 0.02
EPSILON = 1e-06
BF = jnp.bfloat16
F32 = jnp.float32
SHOT = ("y", "xl")
TILE = ("xh", "z", "core")


def spectral_second(length):
    index = np.arange(length)
    number = np.minimum(index, length - index) * (2.0 * np.pi / length)
    phase = (index[:, None, None] - index[None, :, None]) * index[None, None, :] % length
    return -np.sum(number**2 * np.cos(2.0 * np.pi / length * phase), axis=2) / length


def spline_units(offset):
    mag = np.abs(offset)
    inner = 2.0 / 3.0 - mag**2 + 0.5 * mag**3
    outer = (2.0 - mag) ** 3 / 6.0
    return np.round(384.0 * np.where(mag < 1.0, inner, np.where(mag < 2.0, outer, 0.0)))


def halves(matrix):
    high = matrix.astype(np.float32).astype(ml_dtypes.bfloat16)
    low = (matrix - high.astype(np.float64)).astype(np.float32).astype(ml_dtypes.bfloat16)
    return high, low


def narrow_band(matrix):
    high, low = halves(np.pad(matrix, ((0, OV), (0, OV))))
    return np.concatenate([high, high, low], axis=1)


@functools.cache
def constants():
    out = {}
    second_x = spectral_second(CX + 2 * OV)[OV : OV + CX]
    ramp = np.sin(0.5 * np.pi * (np.arange(OV) + 0.5) / OV) ** 2
    left = second_x[:, :OV] * ramp[None, :]
    right = second_x[:, OV + CX :] * ramp[None, ::-1]
    high, low = halves(second_x[:, OV : OV + CX])
    out["own_x"] = np.block([[high, high], [low, low]])
    sides = []
    for pair in ((right, left), (left, right)):
        high, low = halves(np.concatenate(pair, axis=1))
        sides.append(np.concatenate([high, high, low], axis=1))
    out["halo_x"] = np.stack(sides)
    near_part, cross_part = [], []
    for core in range(2):
        rows = slice(0, OV) if core == 0 else slice(CX - OV, CX)
        near_part.append(narrow_band((right if core == 0 else left)[rows]))
        rows = slice(CX - OV, CX) if core == 0 else slice(0, OV)
        cross_part.append(narrow_band((right if core == 0 else left)[rows]))
    out["near_x"] = np.stack(near_part)
    out["cross_x"] = np.stack(cross_part)
    high, low = halves(spectral_second(CZ) - 2.0 * np.eye(CZ))
    out["own_z"] = np.block([[high, low], [high, low]])

    fine_z = np.arange(CZ)[:, None]
    coarse_z = np.arange(CZC)[None, :]
    weight_z = sum(
        spline_units((fine_z - 2 * coarse_z + image * CZ - 0.5) * 0.5) for image in range(-2, 3)
    )
    zero = np.zeros_like(weight_z.T)
    pair = np.block([[weight_z.T, zero], [zero, weight_z.T]])
    out["grow_z"] = np.concatenate([pair, pair], axis=0)
    zero = np.zeros_like(weight_z)
    out["shrink_z"] = np.block(
        [[weight_z, zero], [weight_z, zero], [zero, weight_z], [zero, weight_z]]
    )

    def column(coarse, start=0, count=CX):
        return spline_units((np.arange(start, start + count) - 2 * coarse - 0.5) * 0.5)

    own = np.stack([column(j) for j in range(CXC)], axis=1)
    lower = {j: column(j) for j in (-2, -1, 0, 1)}
    upper = {j: column(j) for j in (62, 63, 64, 65)}
    stack = lambda d: np.stack([d[j] for j in sorted(d)], axis=1)
    grow_own, grow_rest, grow_new, shrink, shrink_far = [], [], [], [], []
    blank = np.zeros((CX, 2))
    for core in range(2):
        near = upper if core == 0 else lower
        near_two, far_six = ((64, 65), range(-6, 0)) if core == 0 else ((-2, -1), range(64, 70))
        far_two = (-2, -1) if core == 0 else (64, 65)
        beyond = -OV if core == 0 else CX
        both = lambda j: np.concatenate([column(j), column(j, beyond, OV)])
        mine = np.stack([both(j) for j in range(CXC)], axis=1)
        rest = np.stack([both(j) for j in (*near_two, *far_six)], axis=1)
        inner = own.copy()
        inner[:, [62, 63] if core == 0 else [0, 1]] = 0.0
        outer = np.stack([column(j) for j in far_two], axis=1)
        new = np.concatenate([inner, stack(near), outer, blank], axis=1)
        every = np.concatenate([own, stack(near), outer, blank], axis=1).T
        past = np.zeros((ROWS, OV))
        for row, j in (*enumerate(range(CXC)), *zip((CXC + 4, CXC + 5), far_two)):
            past[row] = column(j, beyond, OV)
        grow_own.append(np.concatenate([mine, mine], axis=1))
        grow_rest.append(np.concatenate([rest, rest], axis=1))
        grow_new.append(np.concatenate([new, new], axis=1))
        shrink.append(np.concatenate([every, every], axis=1))
        shrink_far.append(np.concatenate([past, past], axis=1))
    out["shrink_far"] = np.stack(shrink_far)
    out["grow_own"] = np.stack(grow_own)
    out["grow_rest"] = np.stack(grow_rest)
    out["grow_new"] = np.stack(grow_new)
    out["shrink_x"] = np.stack(shrink)
    return {name: np.asarray(value).astype(ml_dtypes.bfloat16) for name, value in out.items()}


def taps():
    return [
        [
            (j, float(w))
            for j in range(CYC)
            for w in [
                sum(
                    spline_units(np.float64((i - 2 * j + image * CY - 0.5) * 0.5))
                    for image in range(-2, 3)
                )
            ]
            if w
        ]
        for i in range(CY)
    ]


def split(value):
    high = value.astype(BF)
    return high, (value - high.astype(F32)).astype(BF)


def dot(left, right):
    return jnp.dot(left, right, preferred_element_type=F32)


def cat(parts, axis):
    return jnp.concatenate(parts, axis=axis)


def interior(v, own_x, own_z, out):
    for j in range(CY // 2):
        one, two = 2 * j, 2 * j + 1
        high1, low1 = split(v[one])
        high2, low2 = split(v[two])
        x = dot(own_x[...], cat([cat([high1, high2], 1), cat([low1, low2], 1)], 0))
        z = dot(cat([cat([high1, low1], 1), cat([high2, low2], 1)], 0), own_z[...])
        x = x[:CX] + x[CX:]
        z = z[:, :CZ] + z[:, CZ:]
        beside = v[(one - 1) % CY] + v[two]
        out[one] = x[:, :CZ] + z[:CX] + beside
        beside = v[one] + v[(two + 1) % CY]
        out[two] = x[:, CZ:] + z[CX:] + beside


def halo_part(near, far, field, halo_x, pair):
    parts = []
    for y in (2 * pair, 2 * pair + 1):
        start = (field * CY + y) * OV
        high, low = split(cat([near[start : start + OV], far[start : start + OV]], 0))
        parts.append(cat([high, low, high], 0))
    return dot(halo_x, cat(parts, 1))


def edge_rows(v, core, near, field):
    row = pl.multiple_of((1 - core) * (CX - OV), OV)
    for y in range(CY):
        start = (field * CY + y) * OV
        near[start : start + OV] = v[y, pl.ds(row, OV), :]


def first_edges(p, q, coef, near, far, p_lo, p_hi, q_lo, q_hi, c_lo, c_hi, sems):
    core = lax.axis_index("core")
    block = OV * CY
    copies = [
        pltpu.make_async_copy(source.at[pl.ds(start, size)], target, sems.at[k])
        for k, (source, start, size, target) in enumerate(
            (
                (p, 0, block, p_lo),
                (p, CX * CY - block, block, p_hi),
                (q, 0, block, q_lo),
                (q, CX * CY - block, block, q_hi),
                (coef, 0, 8, c_lo),
                (coef, CXC - 8, 8, c_hi),
            )
        )
    ]
    for copy in copies:
        copy.start()

    def fill(low, high, field):
        for y in range(CY):
            start = (field * CY + y) * OV
            rows = pl.ds(y, OV, stride=CY)
            first, last = low[rows, :], high[rows, :]
            near[start : start + OV] = jnp.where(core == 0, last, first)
            far[start : start + OV] = jnp.where(core == 0, first, last)

    copies[0].wait()
    copies[1].wait()
    fill(p_lo, p_hi, 0)
    copies[2].wait()
    copies[3].wait()
    fill(q_lo, q_hi, 1)
    copies[4].wait()
    copies[5].wait()
    base = 2 * CY * OV
    for row in range(6):
        for part in range(4):
            lanes = slice(part * 128, part * 128 + 128)
            spot = base + row * 4 + part
            if row < 2:
                first = c_lo[row : row + 1, lanes]
                last = c_hi[6 + row : 7 + row, lanes]
                near[spot : spot + 1] = jnp.where(core == 0, last, first)
            first = c_lo[row : row + 1, lanes]
            last = c_hi[2 + row : 3 + row, lanes]
            far[spot : spot + 1] = jnp.where(core == 0, first, last)


def reorder(source, target):
    for y in range(CY):
        target[y] = source[pl.ds(y, CX, stride=CY), :]


def prepare(
    signs, index, wavelet, p_now, q_now, grow_z, own_x_in, own_z_in, p_prev_in, q_prev_in, coef_in, grow_own_in,
    p0, q0, p1, q1, lap_p, lap_q, source, amounts, sigma_own,
    own_x, own_z, p_prev, q_prev, coef, grow_own, sems,
):
    copies = [
        pltpu.make_async_copy(far, near, sems.at[k])
        for k, (far, near) in enumerate(
            (
                (own_x_in, own_x),
                (own_z_in, own_z),
                (p_prev_in, p_prev),
                (q_prev_in, q_prev),
                (coef_in, coef),
                (grow_own_in, grow_own),
            )
        )
    ]
    for copy in copies:
        copy.start()
    reorder(p_now, p0)
    reorder(q_now, q0)
    source[...] = jnp.zeros_like(source)
    lane = lax.broadcasted_iota(jnp.int32, (1, CZ), 1)

    def add(e, carry):
        spot = index[e]
        x, rest = spot // (CY * CZ), spot % (CY * CZ)
        y, z = rest // CZ, rest % CZ
        amount = (2 * signs[e] - 1).astype(F32)
        row = source[y, pl.ds(x, 1), :]
        source[y, pl.ds(x, 1), :] = row + jnp.where(lane == z, amount, 0.0)
        return carry

    lax.fori_loop(0, ELEMS, add, 0)
    for step in range(STEPS + 1):
        amounts[step] = jnp.full((8, CZ), wavelet[step], F32)
    copies[0].wait()
    copies[1].wait()
    interior(p0, own_x, own_z, lap_p)
    interior(q0, own_x, own_z, lap_q)
    copies[2].wait()
    reorder(p_prev, p1)
    copies[3].wait()
    reorder(q_prev, q1)
    copies[4].wait()
    copies[5].wait()

    def write(y, fine):
        sigma_own[y] = fine

    grow(coef[...], grow_z, grow_own[lax.axis_index("core")], write)


def grow(coef, grow_z, grow_x, write):
    wide = []
    for pair in range(CYC // 2):
        high, low = split(coef[:, pair * 128 : pair * 128 + 128])
        both = dot(cat([high, low], 1), grow_z[...])
        wide += [both[:, :CZ], both[:, CZ:]]
    weights = taps()
    for pair in range(CY // 2):
        parts = []
        for y in (2 * pair, 2 * pair + 1):
            mixed = None
            for j, w in weights[y]:
                term = wide[j] * w
                mixed = term if mixed is None else mixed + term
            parts.append(mixed)
        high, low = split(cat(parts, 1))
        fine = dot(grow_x, cat([high, low], 0))
        write(2 * pair, fine[:, :CZ])
        write(2 * pair + 1, fine[:, CZ:])


UNIT = 1.0 / 384.0**3


def grid_ends():
    core = lax.axis_index("core")
    chip = lax.axis_index("xh") * lax.axis_size("z") + lax.axis_index("z")
    chips = lax.axis_size("xh") * lax.axis_size("z")
    return (core == 0) & (chip == 0), (core == 1) & (chip == chips - 1)


def speed(sigma_own, near, far, grow_z, grow_rest, sigma, squared, beyond, held):
    core = lax.axis_index("core")
    base = 2 * CY * OV
    for row in range(6):
        for part in range(4):
            lanes = slice(part * 128, part * 128 + 128)
            spot = base + row * 4 + part
            if row < 2:
                held[row : row + 1, lanes] = near[spot : spot + 1]
            held[2 + row : 3 + row, lanes] = far[spot : spot + 1]
    first, last = grid_ends()

    def write(y, fine):
        fine = (sigma_own[y] + fine) * UNIT
        sigma[y] = fine[:CX]
        squared[y] = fine[:CX] * fine[:CX]
        beyond[y * OV : y * OV + OV] = jnp.where(first | last, 0.0, fine[CX:])

    grow(held[...], grow_z, grow_rest[core], write)


def squared_at(beyond, spot):
    value = beyond[spot : spot + OV]
    return value * value


def advance(step, *refs):
    (near, far, p, p_before, q, q_before, lap_p, lap_q, squared, source, amounts, halo_x) = refs[:12]
    refs = refs[12:]
    core = lax.axis_index("core")
    columns = halo_x[core]
    weight = amounts[step, :1, :]
    if step in (1, 3):
        (sent, beyond, cross_x), refs = refs[:3], refs[3:]
        cross = cross_x[core]
    if step == 2:
        old_lap, refs = refs[0], refs[1:]
    if step == 3:
        (old_lap, older_q, gathered, sigma, older_far), refs = refs[:5], refs[5:]
    if step in (0, 2):
        (p_new, q_new, near_out), refs = refs[:3], refs[3:]
    elif step == 1:
        (p_new, q_new, near_out, far_out), refs = refs[:4], refs[4:]
    else:
        p_new, near_out, far_out, image, image_far = refs[:5]
    if step < 2:
        lap_out = refs[0]
    if step == 2:
        gathered = refs[0]
    for pair in range(CY // 2):
        extra_p = halo_part(near, far, 0, columns, pair)
        extra_q = halo_part(near, far, 1, columns, pair)
        for side in range(2):
            y = 2 * pair + side
            lanes = slice(side * CZ, side * CZ + CZ)
            lap = lap_p[y] + extra_p[:, lanes]
            lap_adj = lap_q[y] + extra_q[:, lanes]
            sq = squared[y]
            p_new[y] = 2.0 * p[y] - p_before[y] + sq * lap + source[y] * weight
            new_q = 2.0 * q[y] - q_before[y] + sq * lap_adj
            if step < 3:
                q_new[y] = new_q
            if step < 2:
                lap_out[y] = lap
            if step == 2:
                gathered[y] = q[y] * lap + new_q * old_lap[y]
            if step == 3:
                total = gathered[y] + older_q[y] * lap + new_q * old_lap[y]
                image[y] = 2.0 * sigma[y] * total
    edge_rows(p_new, core, near_out, 0)
    if step < 3:
        edge_rows(q_new, core, near_out, 1)
    if step == 1:
        size = CY * OV
        for pair in range(CY // 2):
            for field in range(2):
                extra = halo_part(sent, sent, field, cross, pair)
                for side in range(2):
                    spot = (2 * pair + side) * OV
                    known = far[(2 + field) * size + spot : (2 + field) * size + spot + OV]
                    far_out[field * size + spot : field * size + spot + OV] = (
                        known
                        + squared_at(beyond, spot) * extra[:OV, side * CZ : side * CZ + CZ]
                    )
    if step == 3:
        size = CY * OV
        for pair in range(CY // 2):
            extra_p = halo_part(sent, sent, 0, cross, pair)
            extra_q = halo_part(sent, sent, 1, cross, pair)
            for side in range(2):
                spot = (2 * pair + side) * OV
                lanes = slice(side * CZ, side * CZ + CZ)
                part_p, part_q = extra_p[:OV, lanes], extra_q[:OV, lanes]
                rows = lambda k: far[k * size + spot : k * size + spot + OV]
                far_out[spot : spot + OV] = rows(2) + squared_at(beyond, spot) * part_p
                near_q = older_far[size + spot : size + spot + OV]
                image_far[spot : spot + OV] = (
                    rows(3) + 2.0 * beyond[spot : spot + OV] * near_q * part_p + rows(4) * part_q
                )


def early(step, *refs):
    (near, p, p_before, q, q_before, lap_p, lap_q, squared, source, amounts, near_x) = refs[:11]
    if step == 3:
        older_q, old_lap, gathered, sigma = refs[11:15]
    out = refs[-1]
    core = lax.axis_index("core")
    rows = pl.ds(pl.multiple_of(core * (CX - OV), OV), OV)
    weight = amounts[step, :1, :]
    columns = near_x[core]
    for pair in range(CY // 2):
        extra_p = halo_part(near, near, 0, columns, pair)
        extra_q = halo_part(near, near, 1, columns, pair)
        for side in range(2):
            y = 2 * pair + side
            lanes = slice(side * CZ, side * CZ + CZ)
            sq = squared[y, rows, :]
            lap = lap_p[y, rows, :] + extra_p[:OV, lanes]
            lap_adj = lap_q[y, rows, :] + extra_q[:OV, lanes]
            edge_p, edge_q = p[y, rows, :], q[y, rows, :]
            next_p = 2.0 * edge_p - p_before[y, rows, :] + sq * lap + source[y, rows, :] * weight
            next_q = 2.0 * edge_q - q_before[y, rows, :] + sq * lap_adj
            if step == 1:
                sets = (edge_p, edge_q, next_p, next_q)
            else:
                twice = 2.0 * sigma[y, rows, :]
                old = old_lap[y, rows, :]
                known = gathered[y, rows, :] + older_q[y, rows, :] * lap + next_q * old
                sets = (edge_p, edge_q, next_p, twice * known, twice * sq * old)
            for k, value in enumerate(sets):
                spot = (k * CY + y) * OV
                out[spot : spot + OV] = value


def inside(p, q, own_x, own_z, lap_p, lap_q):
    interior(p, own_x, own_z, lap_p)
    interior(q, own_x, own_z, lap_q)


def inside_one(p, own_x, own_z, lap_p):
    interior(p, own_x, own_z, lap_p)


def shrink(image, image_far, shrink_x, shrink_far, shrink_z, own):
    core = lax.axis_index("core")
    rows_x = shrink_x[core]
    rows_far = shrink_far[core]
    narrow = [None] * CYC
    weights = taps()
    for pair in range(CY // 2):
        high, low = split(cat([image[2 * pair], image[2 * pair + 1]], 1))
        both = dot(rows_x, cat([high, low], 0))
        spots = [slice(y * OV, y * OV + OV) for y in (2 * pair, 2 * pair + 1)]
        high, low = split(cat([image_far[spots[0]], image_far[spots[1]]], 1))
        both = both + dot(rows_far, cat([high, low], 0))
        for side in range(2):
            part = both[:, side * CZ : side * CZ + CZ]
            for j, w in weights[2 * pair + side]:
                term = part * w
                narrow[j] = term if narrow[j] is None else narrow[j] + term
    pieces = []
    for pair in range(CYC // 2):
        parts = []
        for j in (2 * pair, 2 * pair + 1):
            parts += list(split(narrow[j]))
        pieces.append(dot(cat(parts, 1), shrink_z[...]) * UNIT)
    own[...] = cat(pieces, 1)


def fold(value):
    rows = value[0:8]
    for r in range(1, value.shape[0] // 8):
        rows = rows + value[8 * r : 8 * r + 8]
    folded = rows[:, :128]
    for c in range(1, 4):
        folded = folded + rows[:, 128 * c : 128 * c + 128]
    return folded


def squares(a, b, total, near):
    core = lax.axis_index("core")
    total[...] = a[...] + b[...]
    first, last = grid_ends()
    total[CXC + 4 : CXC + 6] = jnp.where(first | last, 0.0, total[CXC + 4 : CXC + 6])
    row = lax.broadcasted_iota(jnp.int32, (CXC, CYC * CZC), 0)
    start = (1 - core) * (CXC - 2)
    value = jnp.where((row >= start) & (row < start + 2), 0.0, total[:CXC])
    for r in range(4):
        for part in range(4):
            lanes = slice(part * 128, part * 128 + 128)
            spot = r * 4 + part
            near[spot : spot + 1] = total[CXC + r : CXC + r + 1, lanes]
    near[16:24] = fold(value * value)


def pair_up(total, mine, other, out, squared):
    core = lax.axis_index("core")
    out[...] = total[...]
    edge = mine[0:16] + other[0:16]
    for r in range(4):
        for part in range(4):
            lanes = slice(part * 128, part * 128 + 128)
            spot = r * 4 + part
            out[CXC + r : CXC + r + 1, lanes] = edge[spot : spot + 1]
    out[0:2] = jnp.where(core == 0, out[0:2], out[CXC + 2 : CXC + 4])
    out[CXC - 2 : CXC] = jnp.where(core == 0, out[CXC : CXC + 2], out[CXC - 2 : CXC])
    edge = edge * edge
    squared[...] = (mine[16:24] + other[16:24]) + (edge[0:8] + edge[8:16])


def last_fields(near, far, p, p_before, lap_p, source, amounts, halo_x, lap_out, base):
    core = lax.axis_index("core")
    columns = halo_x[core]
    weight = amounts[STEPS, :1, :]
    for pair in range(CY // 2):
        extra = halo_part(near, far, 0, columns, pair)
        for side in range(2):
            y = 2 * pair + side
            lap_out[y] = lap_p[y] + extra[:, side * CZ : side * CZ + CZ]
            base[y] = 2.0 * p[y] - p_before[y] + source[y] * weight


def add_four(own, one, two, three, out):
    out[...] = (own[...] + one[...]) + (two[...] + three[...])


def spread(total, sigma, lap, base, grow_z, grow_new, zeroth, first, second):
    core = lax.axis_index("core")

    def write(y, fine):
        change = fine * UNIT
        old, curve = sigma[y], lap[y]
        scaled = change * curve
        rows = pl.ds(y, CX, stride=CY)
        zeroth[rows, :] = base[y] + old * old * curve
        first[rows, :] = -2.0 * old * scaled
        second[rows, :] = change * scaled

    grow(total[...], grow_z, grow_new[core], write)


def widen(a, b, out):
    value = a[...] + b[...]
    for k in range(out.shape[0]):
        out[k] = value


def finish(count, parts, total, zeroth, first, second, direction, p_last, held, sems):
    value = parts[0]
    for k in range(1, parts.shape[0]):
        value = value + parts[k]
    value = jnp.sum(jnp.sum(value, axis=0, keepdims=True), axis=1, keepdims=True)
    inverse = 1.0 / jnp.sqrt(value * (1.0 / count) + EPSILON)
    rate = LEARN * inverse
    size = CX * CY // sems.shape[0]
    copies = []
    for c in range(sems.shape[0]):
        rows = slice(c * size, c * size + size)
        held[rows] = zeroth[rows] + rate * (first[rows] + rate * second[rows])
        copies.append(pltpu.make_async_copy(held.at[rows], p_last.at[rows], sems.at[c]))
        copies[-1].start()
    direction[...] = total[:CXC] * inverse
    for copy in copies:
        copy.wait()


VM = pl.BlockSpec(memory_space=pltpu.VMEM)
SM = pl.BlockSpec(memory_space=pltpu.SMEM)
FIELD = jax.ShapeDtypeStruct((CY, CX, CZ), F32)
PARAMS = pltpu.CompilerParams(vmem_limit_bytes=6 * 2**20)


def rows_of(count, lanes=128):
    return jax.ShapeDtypeStruct((count, lanes), F32)


def call(body, outs, *args, smem=0, scratch=(), flops=0, name=None, held=(), in_specs=None, out_specs=None):
    size = sum(int(np.prod(a.shape)) * a.dtype.itemsize for a in args)
    count = len(args)

    def run(*refs):
        body(*refs[:count], *refs[count + len(held) :])

    return pl.pallas_call(
        run,
        out_shape=outs,
        in_specs=([SM] * smem + [VM] * (count - smem) if in_specs is None else in_specs)
        + [pl.BlockSpec(memory_space=pl.ANY)] * len(held),
        out_specs=jax.tree.map(lambda _: VM, outs) if out_specs is None else out_specs,
        scratch_shapes=list(scratch),
        compiler_params=PARAMS,
        cost_estimate=pl.CostEstimate(flops=flops, bytes_accessed=size, transcendentals=0),
        name=name,
    )(*args, *held)


def xor_swap(x, axis, mask):
    count = lax.axis_size(axis)
    if mask >= count:
        return jnp.zeros_like(x)
    return lax.ppermute(x, axis, [(i, i ^ mask) for i in range(count)])


def far_swap(x):
    count = lax.axis_size(TILE)
    pairs = [(i, i + 1) for i in range(1, count - 1, 2)]
    return lax.ppermute(x, TILE, pairs + [(b, a) for a, b in pairs])


def exchange(near, far):
    far = far_swap(far)
    near = xor_swap(near, "core", 1)
    return near, far


def on_device(p_now, p_prev, adj_now, adj_next, coef_old, signs, elem_index, wavelet):
    const = {name: jnp.asarray(value) for name, value in constants().items()}
    own_x, own_z, halo_x = const["own_x"], const["own_z"], const["halo_x"]
    flat = lambda a: a.reshape(CX * CY, CZ)
    p_now, p_prev, adj_now, adj_next = map(flat, (p_now, p_prev, adj_now, adj_next))

    half, edge = rows_of(CY * OV), rows_of(2 * CY * OV)
    with_two, with_six = rows_of(2 * CY * OV + 8), rows_of(2 * CY * OV + 24)
    block = pltpu.VMEM((OV * CY, CZ), F32)
    few = pltpu.VMEM((8, CYC * CZC), F32)
    near, far = pl.pallas_call(
        first_edges,
        out_shape=(with_two, with_six),
        in_specs=[pl.BlockSpec(memory_space=pltpu.HBM)] * 3,
        out_specs=(VM, VM),
        scratch_shapes=[block] * 4 + [few] * 2 + [pltpu.SemaphoreType.DMA((6,))],
        compiler_params=PARAMS,
        name="first_edges",
    )(*(pltpu.with_memory_space_constraint(a, pltpu.HBM) for a in (p_now, adj_now, coef_old)))
    near, far = exchange(near, far)

    wide = jax.ShapeDtypeStruct((CY, CX + OV, CZ), F32)
    later = [own_x, own_z, p_prev, adj_next, coef_old, const["grow_own"]]
    p, q, p_before, q_before, lap_p, lap_q, source, amounts, sigma_own = call(
        prepare,
        (FIELD,) * 7 + (jax.ShapeDtypeStruct((STEPS + 1, 8, CZ), F32), wide),
        signs[0], elem_index, wavelet, p_now, adj_now, const["grow_z"],
        *(pltpu.with_memory_space_constraint(a, pltpu.HBM) for a in later),
        flops=10**9, name="prepare",
        in_specs=[SM] * 3 + [VM] * 3 + [pl.BlockSpec(memory_space=pltpu.HBM)] * len(later),
        scratch=[pltpu.VMEM(a.shape, a.dtype) for a in later]
        + [pltpu.SemaphoreType.DMA((len(later),))],
    )
    sigma, squared, beyond = call(
        speed, (FIELD, FIELD, half), sigma_own, near, far, const["grow_z"], const["grow_rest"],
        scratch=[pltpu.VMEM((8, CYC * CZC), F32)], flops=10**8, name="speed",
    )

    laps, qs = [], [q]
    gathered = None
    for step in range(STEPS):
        args = [near, far, p, p_before, q, q_before, lap_p, lap_q, squared, source, amounts, halo_x]
        body = functools.partial(advance, step)
        name = f"advance_{step}"
        if step == 0:
            outs = (FIELD, FIELD, edge, FIELD)
        elif step == 1:
            args += [sent, beyond, const["cross_x"]]
            outs = (FIELD, FIELD, edge, edge, FIELD)
            older_far = far
        elif step == 2:
            args.append(laps[1])
            outs = (FIELD, FIELD, edge, FIELD)
        else:
            args += [sent, beyond, const["cross_x"], laps[0], qs[1], gathered, sigma, older_far]
            outs = (FIELD, half, half, FIELD, half)
        result = call(body, outs, *args, flops=10**8, name=name)
        if step == 3:
            p_new, near, far, image, image_far = result
            p, p_before = p_new, p
            continue
        p_new, q_new, *edges, other = result
        if step < 2:
            laps.append(other)
        else:
            gathered = other
        p, p_before = p_new, p
        q, q_before = q_new, q
        qs.append(q)
        near = xor_swap(edges[0], "core", 1)
        lap_p, lap_q = call(
            inside, (FIELD, FIELD), p, q, own_x, own_z, flops=10**9, name=f"inside_{step}"
        )
        if step == 1:
            far = edges[1]
            continue
        args = [near, p, p_before, q, q_before, lap_p, lap_q, squared, source, amounts]
        args.append(const["near_x"])
        if step == 2:
            args += [qs[1], laps[0], gathered, sigma]
        sent = call(
            functools.partial(early, step + 1), rows_of((4 if step == 0 else 5) * CY * OV),
            *args, flops=10**7, name=f"early_{step + 1}",
        )
        far = far_swap(sent)

    partial = call(
        shrink, rows_of(ROWS, CYC * CZC),
        image, image_far, const["shrink_x"], const["shrink_far"], const["shrink_z"],
        flops=10**8, name="shrink",
    )
    two, three, one = (xor_swap(partial, "y", m) for m in (2, 3, 1))
    near = xor_swap(near, "core", 1)
    lap_p = call(inside_one, FIELD, p, own_x, own_z, flops=5 * 10**8, name="inside_last")
    lap_p, base = call(
        last_fields, (FIELD, FIELD), near, far, p, p_before, lap_p, source, amounts, halo_x,
        flops=10**8, name="last_fields",
    )
    held = (lap_p, base)
    partial = call(
        add_four, rows_of(ROWS, CYC * CZC), partial, one, two, three, name="add_four", held=held
    )
    total, mine = call(
        squares, (rows_of(ROWS, CYC * CZC), rows_of(24)), partial, xor_swap(partial, "xl", 1),
        name="squares", held=held,
    )
    total, squared_sum = call(
        pair_up, (rows_of(ROWS, CYC * CZC), rows_of(8)), total, mine, xor_swap(mine, "core", 1),
        name="pair_up", held=held,
    )
    terms = call(
        spread, (rows_of(CX * CY),) * 3, total, sigma, lap_p, base, const["grow_z"], const["grow_new"],
        flops=10**8, name="spread",
    )
    deep = lax.axis_size("z")
    copies = call(
        widen, jax.ShapeDtypeStruct((deep, 8, 128), F32),
        squared_sum, xor_swap(squared_sum, "xh", 1), name="widen", held=terms,
    )
    parts = lax.all_to_all(copies, "z", split_axis=0, concat_axis=0, tiled=True)
    count = float(lax.axis_size(TILE) * CXC * CYC * CZC)
    direction, p_last = call(
        functools.partial(finish, count),
        (rows_of(CXC, CYC * CZC), pltpu.HBM((CX * CY, CZ), F32)),
        parts, total, *terms, name="finish",
        scratch=[pltpu.VMEM((CX * CY, CZ), F32), pltpu.SemaphoreType.DMA((4,))],
        out_specs=(VM, pl.BlockSpec(memory_space=pltpu.HBM)),
    )
    return direction, p_last.reshape(1, CX, CY, CZ)


def solution(mesh):
    shots, tiles = mesh.shape["shot"], mesh.shape["tile"]
    fine = Mesh(
        mesh.devices.reshape(shots // 2, 2, 2, tiles // 4, 2), ("y", "xl", "xh", "z", "core")
    )
    placed = (
        P(SHOT, TILE, None, None),
        P(SHOT, TILE, None, None),
        P(SHOT, TILE, None, None),
        P(SHOT, TILE, None, None),
        P(TILE, None),
        P(SHOT, TILE),
        P(TILE),
        P(),
    )
    return jax.shard_map(
        on_device,
        mesh=fine,
        in_specs=placed,
        out_specs=(P(TILE, None), P(SHOT, TILE, None, None)),
        check_vma=False,
    )
```

```python
import functools

import jax
import jax.numpy as jnp
import ml_dtypes
import numpy as np
from jax import lax
from jax.experimental import pallas as pl
from jax.experimental.pallas import tpu as pltpu
from jax.sharding import Mesh
from jax.sharding import PartitionSpec as P

CX = 128
CZ = 128
CY = 16
OV = 8
STEPS = 4
ELEMS = 64
CXC = 64
CYC = 8
CZC = 64
ROWS = 72
LEARN = 0.02
EPSILON = 1e-06
BF = jnp.bfloat16
F32 = jnp.float32
SHOT = ("y", "xl")
TILE = ("xh", "z", "core")


def spectral_second(length):
    index = np.arange(length)
    number = np.minimum(index, length - index) * (2.0 * np.pi / length)
    phase = (index[:, None, None] - index[None, :, None]) * index[None, None, :] % length
    return -np.sum(number**2 * np.cos(2.0 * np.pi / length * phase), axis=2) / length


def spline_units(offset):
    mag = np.abs(offset)
    inner = 2.0 / 3.0 - mag**2 + 0.5 * mag**3
    outer = (2.0 - mag) ** 3 / 6.0
    return np.round(384.0 * np.where(mag < 1.0, inner, np.where(mag < 2.0, outer, 0.0)))


def halves(matrix):
    high = matrix.astype(np.float32).astype(ml_dtypes.bfloat16)
    low = (matrix - high.astype(np.float64)).astype(np.float32).astype(ml_dtypes.bfloat16)
    return high, low


def narrow_band(matrix):
    high, low = halves(np.pad(matrix, ((0, OV), (0, OV))))
    return np.concatenate([high, high, low], axis=1)


@functools.cache
def constants():
    out = {}
    second_x = spectral_second(CX + 2 * OV)[OV : OV + CX]
    ramp = np.sin(0.5 * np.pi * (np.arange(OV) + 0.5) / OV) ** 2
    left = second_x[:, :OV] * ramp[None, :]
    right = second_x[:, OV + CX :] * ramp[None, ::-1]
    high, low = halves(second_x[:, OV : OV + CX])
    out["own_x"] = np.block([[high, high], [low, low]])
    sides = []
    for pair in ((right, left), (left, right)):
        high, low = halves(np.concatenate(pair, axis=1))
        sides.append(np.concatenate([high, high, low], axis=1))
    out["halo_x"] = np.stack(sides)
    edge = []
    for rows in (slice(0, OV), slice(CX - OV, CX)):
        high, low = halves(second_x[rows, OV : OV + CX])
        edge.append(np.block([[high, high], [low, low]]))
    out["edge_x"] = np.stack(edge)
    near_part, cross_part = [], []
    for core in range(2):
        rows = slice(0, OV) if core == 0 else slice(CX - OV, CX)
        near_part.append(narrow_band((right if core == 0 else left)[rows]))
        rows = slice(CX - OV, CX) if core == 0 else slice(0, OV)
        cross_part.append(narrow_band((right if core == 0 else left)[rows]))
    out["near_x"] = np.stack(near_part)
    out["cross_x"] = np.stack(cross_part)
    high, low = halves(spectral_second(CZ) - 2.0 * np.eye(CZ))
    out["own_z"] = np.block([[high, low], [high, low]])

    fine_z = np.arange(CZ)[:, None]
    coarse_z = np.arange(CZC)[None, :]
    weight_z = sum(
        spline_units((fine_z - 2 * coarse_z + image * CZ - 0.5) * 0.5) for image in range(-2, 3)
    )
    zero = np.zeros_like(weight_z.T)
    pair = np.block([[weight_z.T, zero], [zero, weight_z.T]])
    out["grow_z"] = np.concatenate([pair, pair], axis=0)
    zero = np.zeros_like(weight_z)
    out["shrink_z"] = np.block(
        [[weight_z, zero], [weight_z, zero], [zero, weight_z], [zero, weight_z]]
    )

    def column(coarse, start=0, count=CX):
        return spline_units((np.arange(start, start + count) - 2 * coarse - 0.5) * 0.5)

    own = np.stack([column(j) for j in range(CXC)], axis=1)
    lower = {j: column(j) for j in (-2, -1, 0, 1)}
    upper = {j: column(j) for j in (62, 63, 64, 65)}
    stack = lambda d: np.stack([d[j] for j in sorted(d)], axis=1)
    grow_own, grow_rest, grow_new, shrink, shrink_far = [], [], [], [], []
    blank = np.zeros((CX, 2))
    for core in range(2):
        near = upper if core == 0 else lower
        near_two, far_six = ((64, 65), range(-6, 0)) if core == 0 else ((-2, -1), range(64, 70))
        far_two = (-2, -1) if core == 0 else (64, 65)
        beyond = -OV if core == 0 else CX
        both = lambda j: np.concatenate([column(j), column(j, beyond, OV)])
        mine = np.stack([both(j) for j in range(CXC)], axis=1)
        rest = np.stack([both(j) for j in (*near_two, *far_six)], axis=1)
        inner = own.copy()
        inner[:, [62, 63] if core == 0 else [0, 1]] = 0.0
        outer = np.stack([column(j) for j in far_two], axis=1)
        new = np.concatenate([inner, stack(near), outer, blank], axis=1)
        every = np.concatenate([own, stack(near), outer, blank], axis=1).T
        past = np.zeros((ROWS, OV))
        for row, j in (*enumerate(range(CXC)), *zip((CXC + 4, CXC + 5), far_two)):
            past[row] = column(j, beyond, OV)
        grow_own.append(np.concatenate([mine, mine], axis=1))
        grow_rest.append(np.concatenate([rest, rest], axis=1))
        grow_new.append(np.concatenate([new, new], axis=1))
        shrink.append(np.concatenate([every, every], axis=1))
        shrink_far.append(np.concatenate([past, past], axis=1))
    out["shrink_far"] = np.stack(shrink_far)
    out["grow_own"] = np.stack(grow_own)
    out["grow_rest"] = np.stack(grow_rest)
    out["grow_new"] = np.stack(grow_new)
    out["shrink_x"] = np.stack(shrink)
    return {name: np.asarray(value).astype(ml_dtypes.bfloat16) for name, value in out.items()}


def taps():
    return [
        [
            (j, float(w))
            for j in range(CYC)
            for w in [
                sum(
                    spline_units(np.float64((i - 2 * j + image * CY - 0.5) * 0.5))
                    for image in range(-2, 3)
                )
            ]
            if w
        ]
        for i in range(CY)
    ]


def split(value):
    high = value.astype(BF)
    return high, (value - high.astype(F32)).astype(BF)


def dot(left, right):
    return jnp.dot(left, right, preferred_element_type=F32)


def cat(parts, axis):
    return jnp.concatenate(parts, axis=axis)


def interior(v, own_x, own_z, out):
    for j in range(CY // 2):
        one, two = 2 * j, 2 * j + 1
        high1, low1 = split(v[one])
        high2, low2 = split(v[two])
        x = dot(own_x[...], cat([cat([high1, high2], 1), cat([low1, low2], 1)], 0))
        z = dot(cat([cat([high1, low1], 1), cat([high2, low2], 1)], 0), own_z[...])
        x = x[:CX] + x[CX:]
        z = z[:, :CZ] + z[:, CZ:]
        beside = v[(one - 1) % CY] + v[two]
        out[one] = x[:, :CZ] + z[:CX] + beside
        beside = v[one] + v[(two + 1) % CY]
        out[two] = x[:, CZ:] + z[CX:] + beside


def halo_part(near, far, field, halo_x, pair):
    parts = []
    for y in (2 * pair, 2 * pair + 1):
        start = (field * CY + y) * OV
        high, low = split(cat([near[start : start + OV], far[start : start + OV]], 0))
        parts.append(cat([high, low, high], 0))
    return dot(halo_x, cat(parts, 1))


def edge_rows(v, core, near, field):
    row = pl.multiple_of((1 - core) * (CX - OV), OV)
    for y in range(CY):
        start = (field * CY + y) * OV
        near[start : start + OV] = v[y, pl.ds(row, OV), :]


def first_edges(p, q, coef, near, far, p_lo, p_hi, q_lo, q_hi, c_lo, c_hi, sems):
    core = lax.axis_index("core")
    block = OV * CY
    copies = [
        pltpu.make_async_copy(source.at[pl.ds(start, size)], target, sems.at[k])
        for k, (source, start, size, target) in enumerate(
            (
                (p, 0, block, p_lo),
                (p, CX * CY - block, block, p_hi),
                (q, 0, block, q_lo),
                (q, CX * CY - block, block, q_hi),
                (coef, 0, 8, c_lo),
                (coef, CXC - 8, 8, c_hi),
            )
        )
    ]
    for copy in copies:
        copy.start()

    def fill(low, high, field):
        for y in range(CY):
            start = (field * CY + y) * OV
            rows = pl.ds(y, OV, stride=CY)
            first, last = low[rows, :], high[rows, :]
            near[start : start + OV] = jnp.where(core == 0, last, first)
            far[start : start + OV] = jnp.where(core == 0, first, last)

    copies[0].wait()
    copies[1].wait()
    fill(p_lo, p_hi, 0)
    copies[2].wait()
    copies[3].wait()
    fill(q_lo, q_hi, 1)
    copies[4].wait()
    copies[5].wait()
    base = 2 * CY * OV
    for row in range(6):
        for part in range(4):
            lanes = slice(part * 128, part * 128 + 128)
            spot = base + row * 4 + part
            if row < 2:
                first = c_lo[row : row + 1, lanes]
                last = c_hi[6 + row : 7 + row, lanes]
                near[spot : spot + 1] = jnp.where(core == 0, last, first)
            first = c_lo[row : row + 1, lanes]
            last = c_hi[2 + row : 3 + row, lanes]
            far[spot : spot + 1] = jnp.where(core == 0, first, last)


def reorder(source, target):
    for y in range(CY):
        target[y] = source[pl.ds(y, CX, stride=CY), :]


def prepare(
    signs, index, wavelet, p_now, q_now, grow_z, own_x_in, own_z_in, p_prev_in, q_prev_in, coef_in, grow_own_in,
    p0, q0, p1, q1, lap_p, lap_q, source, amounts, sigma_own,
    own_x, own_z, p_prev, q_prev, coef, grow_own, sems,
):
    copies = [
        pltpu.make_async_copy(far, near, sems.at[k])
        for k, (far, near) in enumerate(
            (
                (own_x_in, own_x),
                (own_z_in, own_z),
                (p_prev_in, p_prev),
                (q_prev_in, q_prev),
                (coef_in, coef),
                (grow_own_in, grow_own),
            )
        )
    ]
    for copy in copies:
        copy.start()
    reorder(p_now, p0)
    reorder(q_now, q0)
    source[...] = jnp.zeros_like(source)
    lane = lax.broadcasted_iota(jnp.int32, (1, CZ), 1)

    def add(e, carry):
        spot = index[e]
        x, rest = spot // (CY * CZ), spot % (CY * CZ)
        y, z = rest // CZ, rest % CZ
        amount = (2 * signs[e] - 1).astype(F32)
        row = source[y, pl.ds(x, 1), :]
        source[y, pl.ds(x, 1), :] = row + jnp.where(lane == z, amount, 0.0)
        return carry

    lax.fori_loop(0, ELEMS, add, 0)
    for step in range(STEPS + 1):
        amounts[step] = jnp.full((8, CZ), wavelet[step], F32)
    copies[0].wait()
    copies[1].wait()
    interior(p0, own_x, own_z, lap_p)
    interior(q0, own_x, own_z, lap_q)
    copies[2].wait()
    reorder(p_prev, p1)
    copies[3].wait()
    reorder(q_prev, q1)
    copies[4].wait()
    copies[5].wait()

    def write(y, fine):
        sigma_own[y] = fine

    grow(coef[...], grow_z, grow_own[lax.axis_index("core")], write)


def grow(coef, grow_z, grow_x, write):
    wide = []
    for pair in range(CYC // 2):
        high, low = split(coef[:, pair * 128 : pair * 128 + 128])
        both = dot(cat([high, low], 1), grow_z[...])
        wide += [both[:, :CZ], both[:, CZ:]]
    weights = taps()
    for pair in range(CY // 2):
        parts = []
        for y in (2 * pair, 2 * pair + 1):
            mixed = None
            for j, w in weights[y]:
                term = wide[j] * w
                mixed = term if mixed is None else mixed + term
            parts.append(mixed)
        high, low = split(cat(parts, 1))
        fine = dot(grow_x, cat([high, low], 0))
        write(2 * pair, fine[:, :CZ])
        write(2 * pair + 1, fine[:, CZ:])


UNIT = 1.0 / 384.0**3


def grid_ends():
    core = lax.axis_index("core")
    chip = lax.axis_index("xh") * lax.axis_size("z") + lax.axis_index("z")
    chips = lax.axis_size("xh") * lax.axis_size("z")
    return (core == 0) & (chip == 0), (core == 1) & (chip == chips - 1)


def speed(sigma_own, near, far, grow_z, grow_rest, sigma, squared, beyond, held):
    core = lax.axis_index("core")
    base = 2 * CY * OV
    for row in range(6):
        for part in range(4):
            lanes = slice(part * 128, part * 128 + 128)
            spot = base + row * 4 + part
            if row < 2:
                held[row : row + 1, lanes] = near[spot : spot + 1]
            held[2 + row : 3 + row, lanes] = far[spot : spot + 1]
    first, last = grid_ends()

    def write(y, fine):
        fine = (sigma_own[y] + fine) * UNIT
        sigma[y] = fine[:CX]
        squared[y] = fine[:CX] * fine[:CX]
        beyond[y * OV : y * OV + OV] = jnp.where(first | last, 0.0, fine[CX:])

    grow(held[...], grow_z, grow_rest[core], write)


def squared_at(beyond, spot):
    value = beyond[spot : spot + OV]
    return value * value


def advance(step, *refs):
    (near, far, p, p_before, q, q_before, lap_p, lap_q, squared, source, amounts, halo_x) = refs[:12]
    refs = refs[12:]
    core = lax.axis_index("core")
    columns = halo_x[core]
    weight = amounts[step, :1, :]
    if step in (1, 3):
        (sent, beyond, cross_x), refs = refs[:3], refs[3:]
        cross = cross_x[core]
    if step == 2:
        old_lap, refs = refs[0], refs[1:]
    if step == 3:
        (old_lap, older_q, gathered, sigma, older_far), refs = refs[:5], refs[5:]
    if step in (0, 2):
        (p_new, q_new, near_out), refs = refs[:3], refs[3:]
    elif step == 1:
        (p_new, q_new, near_out, far_out), refs = refs[:4], refs[4:]
    else:
        p_new, near_out, far_out, image, image_far = refs[:5]
    if step < 2:
        lap_out = refs[0]
    if step == 2:
        gathered = refs[0]
    for pair in range(CY // 2):
        extra_p = halo_part(near, far, 0, columns, pair)
        extra_q = halo_part(near, far, 1, columns, pair)
        for side in range(2):
            y = 2 * pair + side
            lanes = slice(side * CZ, side * CZ + CZ)
            lap = lap_p[y] + extra_p[:, lanes]
            lap_adj = lap_q[y] + extra_q[:, lanes]
            sq = squared[y]
            p_new[y] = 2.0 * p[y] - p_before[y] + sq * lap + source[y] * weight
            new_q = 2.0 * q[y] - q_before[y] + sq * lap_adj
            if step < 3:
                q_new[y] = new_q
            if step < 2:
                lap_out[y] = lap
            if step == 2:
                gathered[y] = q[y] * lap + new_q * old_lap[y]
            if step == 3:
                total = gathered[y] + older_q[y] * lap + new_q * old_lap[y]
                image[y] = 2.0 * sigma[y] * total
    edge_rows(p_new, core, near_out, 0)
    if step < 3:
        edge_rows(q_new, core, near_out, 1)
    if step == 1:
        size = CY * OV
        for pair in range(CY // 2):
            for field in range(2):
                extra = halo_part(sent, sent, field, cross, pair)
                for side in range(2):
                    spot = (2 * pair + side) * OV
                    known = far[(2 + field) * size + spot : (2 + field) * size + spot + OV]
                    far_out[field * size + spot : field * size + spot + OV] = (
                        known
                        + squared_at(beyond, spot) * extra[:OV, side * CZ : side * CZ + CZ]
                    )
    if step == 3:
        size = CY * OV
        for pair in range(CY // 2):
            extra_p = halo_part(sent, sent, 0, cross, pair)
            extra_q = halo_part(sent, sent, 1, cross, pair)
            for side in range(2):
                spot = (2 * pair + side) * OV
                lanes = slice(side * CZ, side * CZ + CZ)
                part_p, part_q = extra_p[:OV, lanes], extra_q[:OV, lanes]
                rows = lambda k: far[k * size + spot : k * size + spot + OV]
                far_out[spot : spot + OV] = rows(2) + squared_at(beyond, spot) * part_p
                near_q = older_far[size + spot : size + spot + OV]
                image_far[spot : spot + OV] = (
                    rows(3) + 2.0 * beyond[spot : spot + OV] * near_q * part_p + rows(4) * part_q
                )


def early(step, *refs):
    (near, p, p_before, q, q_before, laps, squared, source, amounts, near_x) = refs[:10]
    if step == 3:
        older_q, old_lap, gathered, sigma = refs[10:14]
    out = refs[-1]
    core = lax.axis_index("core")
    rows = pl.ds(pl.multiple_of(core * (CX - OV), OV), OV)
    weight = amounts[step, :1, :]
    columns = near_x[core]
    for pair in range(CY // 2):
        extra_p = halo_part(near, near, 0, columns, pair)
        extra_q = halo_part(near, near, 1, columns, pair)
        for side in range(2):
            y = 2 * pair + side
            lanes = slice(side * CZ, side * CZ + CZ)
            sq = squared[y, rows, :]
            spot = y * OV
            lap = laps[spot : spot + OV] + extra_p[:OV, lanes]
            spot += CY * OV
            lap_adj = laps[spot : spot + OV] + extra_q[:OV, lanes]
            edge_p, edge_q = p[y, rows, :], q[y, rows, :]
            next_p = 2.0 * edge_p - p_before[y, rows, :] + sq * lap + source[y, rows, :] * weight
            next_q = 2.0 * edge_q - q_before[y, rows, :] + sq * lap_adj
            if step == 1:
                sets = (edge_p, edge_q, next_p, next_q)
            else:
                twice = 2.0 * sigma[y, rows, :]
                old = old_lap[y, rows, :]
                known = gathered[y, rows, :] + older_q[y, rows, :] * lap + next_q * old
                sets = (edge_p, edge_q, next_p, twice * known, twice * sq * old)
            for k, value in enumerate(sets):
                spot = (k * CY + y) * OV
                out[spot : spot + OV] = value


def edge_interior(v, edge_x, own_z, first, out, field):
    strips = []
    for j in range(CY // 2):
        one, two = 2 * j, 2 * j + 1
        high1, low1 = split(v[one])
        high2, low2 = split(v[two])
        x = dot(edge_x, cat([cat([high1, high2], 1), cat([low1, low2], 1)], 0))
        x = x[:OV] + x[OV:]
        strips += [x[:, :CZ], x[:, CZ:]]
    rows = pl.ds(first, OV)
    edge = [v[y, rows, :] for y in range(CY)]
    high, low = split(cat(edge, 0))
    z = dot(cat([high, low], 1), own_z[...])
    z = z[:, :CZ] + z[:, CZ:]
    for y in range(CY):
        beside = edge[(y - 1) % CY] + edge[(y + 1) % CY]
        spot = (field * CY + y) * OV
        out[spot : spot + OV] = strips[y] + z[y * OV : y * OV + OV] + beside


def edge_inside(p, q, edge_x, own_z, out):
    core = lax.axis_index("core")
    first = pl.multiple_of(core * (CX - OV), OV)
    edge_interior(p, edge_x[core], own_z, first, out, 0)
    edge_interior(q, edge_x[core], own_z, first, out, 1)


def inside(p, q, own_x, own_z, lap_p, lap_q):
    interior(p, own_x, own_z, lap_p)
    interior(q, own_x, own_z, lap_q)


def inside_one(p, own_x, own_z, lap_p):
    interior(p, own_x, own_z, lap_p)


def shrink(image, image_far, shrink_x, shrink_far, shrink_z, own):
    core = lax.axis_index("core")
    rows_x = shrink_x[core]
    rows_far = shrink_far[core]
    narrow = [None] * CYC
    weights = taps()
    for pair in range(CY // 2):
        high, low = split(cat([image[2 * pair], image[2 * pair + 1]], 1))
        both = dot(rows_x, cat([high, low], 0))
        spots = [slice(y * OV, y * OV + OV) for y in (2 * pair, 2 * pair + 1)]
        high, low = split(cat([image_far[spots[0]], image_far[spots[1]]], 1))
        both = both + dot(rows_far, cat([high, low], 0))
        for side in range(2):
            part = both[:, side * CZ : side * CZ + CZ]
            for j, w in weights[2 * pair + side]:
                term = part * w
                narrow[j] = term if narrow[j] is None else narrow[j] + term
    pieces = []
    for pair in range(CYC // 2):
        parts = []
        for j in (2 * pair, 2 * pair + 1):
            parts += list(split(narrow[j]))
        pieces.append(dot(cat(parts, 1), shrink_z[...]) * UNIT)
    own[...] = cat(pieces, 1)


def fold(value):
    rows = value[0:8]
    for r in range(1, value.shape[0] // 8):
        rows = rows + value[8 * r : 8 * r + 8]
    folded = rows[:, :128]
    for c in range(1, 4):
        folded = folded + rows[:, 128 * c : 128 * c + 128]
    return folded


def squares(a, b, total, near):
    core = lax.axis_index("core")
    total[...] = a[...] + b[...]
    first, last = grid_ends()
    total[CXC + 4 : CXC + 6] = jnp.where(first | last, 0.0, total[CXC + 4 : CXC + 6])
    row = lax.broadcasted_iota(jnp.int32, (CXC, CYC * CZC), 0)
    start = (1 - core) * (CXC - 2)
    value = jnp.where((row >= start) & (row < start + 2), 0.0, total[:CXC])
    for r in range(4):
        for part in range(4):
            lanes = slice(part * 128, part * 128 + 128)
            spot = r * 4 + part
            near[spot : spot + 1] = total[CXC + r : CXC + r + 1, lanes]
    near[16:24] = fold(value * value)


def pair_up(total, mine, other, out, squared):
    core = lax.axis_index("core")
    out[...] = total[...]
    edge = mine[0:16] + other[0:16]
    for r in range(4):
        for part in range(4):
            lanes = slice(part * 128, part * 128 + 128)
            spot = r * 4 + part
            out[CXC + r : CXC + r + 1, lanes] = edge[spot : spot + 1]
    out[0:2] = jnp.where(core == 0, out[0:2], out[CXC + 2 : CXC + 4])
    out[CXC - 2 : CXC] = jnp.where(core == 0, out[CXC : CXC + 2], out[CXC - 2 : CXC])
    edge = edge * edge
    squared[...] = (mine[16:24] + other[16:24]) + (edge[0:8] + edge[8:16])


def last_fields(near, far, p, p_before, lap_p, source, amounts, halo_x, lap_out, base):
    core = lax.axis_index("core")
    columns = halo_x[core]
    weight = amounts[STEPS, :1, :]
    for pair in range(CY // 2):
        extra = halo_part(near, far, 0, columns, pair)
        for side in range(2):
            y = 2 * pair + side
            lap_out[y] = lap_p[y] + extra[:, side * CZ : side * CZ + CZ]
            base[y] = 2.0 * p[y] - p_before[y] + source[y] * weight


def add_four(own, one, two, three, out):
    out[...] = (own[...] + one[...]) + (two[...] + three[...])


def spread(total, sigma, lap, base, grow_z, grow_new, zeroth, first, second):
    core = lax.axis_index("core")

    def write(y, fine):
        change = fine * UNIT
        old, curve = sigma[y], lap[y]
        scaled = change * curve
        rows = pl.ds(y, CX, stride=CY)
        zeroth[rows, :] = base[y] + old * old * curve
        first[rows, :] = -2.0 * old * scaled
        second[rows, :] = change * scaled

    grow(total[...], grow_z, grow_new[core], write)


def widen(a, b, out):
    value = a[...] + b[...]
    for k in range(out.shape[0]):
        out[k] = value


def finish(count, parts, total, zeroth, first, second, direction, p_last, held, sems):
    value = parts[0]
    for k in range(1, parts.shape[0]):
        value = value + parts[k]
    value = jnp.sum(jnp.sum(value, axis=0, keepdims=True), axis=1, keepdims=True)
    inverse = 1.0 / jnp.sqrt(value * (1.0 / count) + EPSILON)
    rate = LEARN * inverse
    size = CX * CY // sems.shape[0]
    copies = []
    for c in range(sems.shape[0]):
        rows = slice(c * size, c * size + size)
        held[rows] = zeroth[rows] + rate * (first[rows] + rate * second[rows])
        copies.append(pltpu.make_async_copy(held.at[rows], p_last.at[rows], sems.at[c]))
        copies[-1].start()
    direction[...] = total[:CXC] * inverse
    for copy in copies:
        copy.wait()


VM = pl.BlockSpec(memory_space=pltpu.VMEM)
SM = pl.BlockSpec(memory_space=pltpu.SMEM)
FIELD = jax.ShapeDtypeStruct((CY, CX, CZ), F32)
PARAMS = pltpu.CompilerParams(vmem_limit_bytes=6 * 2**20)


def rows_of(count, lanes=128):
    return jax.ShapeDtypeStruct((count, lanes), F32)


def call(body, outs, *args, smem=0, scratch=(), flops=0, name=None, held=(), in_specs=None, out_specs=None):
    size = sum(int(np.prod(a.shape)) * a.dtype.itemsize for a in args)
    count = len(args)

    def run(*refs):
        body(*refs[:count], *refs[count + len(held) :])

    return pl.pallas_call(
        run,
        out_shape=outs,
        in_specs=([SM] * smem + [VM] * (count - smem) if in_specs is None else in_specs)
        + [pl.BlockSpec(memory_space=pl.ANY)] * len(held),
        out_specs=jax.tree.map(lambda _: VM, outs) if out_specs is None else out_specs,
        scratch_shapes=list(scratch),
        compiler_params=PARAMS,
        cost_estimate=pl.CostEstimate(flops=flops, bytes_accessed=size, transcendentals=0),
        name=name,
    )(*args, *held)


def xor_swap(x, axis, mask):
    count = lax.axis_size(axis)
    if mask >= count:
        return jnp.zeros_like(x)
    return lax.ppermute(x, axis, [(i, i ^ mask) for i in range(count)])


def far_swap(x):
    count = lax.axis_size(TILE)
    pairs = [(i, i + 1) for i in range(1, count - 1, 2)]
    return lax.ppermute(x, TILE, pairs + [(b, a) for a, b in pairs])


def exchange(near, far):
    far = far_swap(far)
    near = xor_swap(near, "core", 1)
    return near, far


def on_device(p_now, p_prev, adj_now, adj_next, coef_old, signs, elem_index, wavelet):
    const = {name: jnp.asarray(value) for name, value in constants().items()}
    own_x, own_z, halo_x = const["own_x"], const["own_z"], const["halo_x"]
    flat = lambda a: a.reshape(CX * CY, CZ)
    p_now, p_prev, adj_now, adj_next = map(flat, (p_now, p_prev, adj_now, adj_next))

    half, edge = rows_of(CY * OV), rows_of(2 * CY * OV)
    with_two, with_six = rows_of(2 * CY * OV + 8), rows_of(2 * CY * OV + 24)
    block = pltpu.VMEM((OV * CY, CZ), F32)
    few = pltpu.VMEM((8, CYC * CZC), F32)
    near, far = pl.pallas_call(
        first_edges,
        out_shape=(with_two, with_six),
        in_specs=[pl.BlockSpec(memory_space=pltpu.HBM)] * 3,
        out_specs=(VM, VM),
        scratch_shapes=[block] * 4 + [few] * 2 + [pltpu.SemaphoreType.DMA((6,))],
        compiler_params=PARAMS,
        name="first_edges",
    )(*(pltpu.with_memory_space_constraint(a, pltpu.HBM) for a in (p_now, adj_now, coef_old)))
    near, far = exchange(near, far)

    wide = jax.ShapeDtypeStruct((CY, CX + OV, CZ), F32)
    later = [own_x, own_z, p_prev, adj_next, coef_old, const["grow_own"]]
    p, q, p_before, q_before, lap_p, lap_q, source, amounts, sigma_own = call(
        prepare,
        (FIELD,) * 7 + (jax.ShapeDtypeStruct((STEPS + 1, 8, CZ), F32), wide),
        signs[0], elem_index, wavelet, p_now, adj_now, const["grow_z"],
        *(pltpu.with_memory_space_constraint(a, pltpu.HBM) for a in later),
        flops=10**9, name="prepare", held=(halo_x,),
        in_specs=[SM] * 3 + [VM] * 3 + [pl.BlockSpec(memory_space=pltpu.HBM)] * len(later),
        scratch=[pltpu.VMEM(a.shape, a.dtype) for a in later]
        + [pltpu.SemaphoreType.DMA((len(later),))],
    )
    sigma, squared, beyond = call(
        speed, (FIELD, FIELD, half), sigma_own, near, far, const["grow_z"], const["grow_rest"],
        scratch=[pltpu.VMEM((8, CYC * CZC), F32)], flops=10**8, name="speed",
    )

    laps, qs = [], [q]
    gathered = None
    for step in range(STEPS):
        args = [near, far, p, p_before, q, q_before, lap_p, lap_q, squared, source, amounts, halo_x]
        body = functools.partial(advance, step)
        name = f"advance_{step}"
        if step == 0:
            outs = (FIELD, FIELD, edge, FIELD)
        elif step == 1:
            args += [sent, beyond, const["cross_x"]]
            outs = (FIELD, FIELD, edge, edge, FIELD)
            older_far = far
        elif step == 2:
            args.append(laps[1])
            outs = (FIELD, FIELD, edge, FIELD)
        else:
            args += [sent, beyond, const["cross_x"], laps[0], qs[1], gathered, sigma, older_far]
            outs = (FIELD, half, half, FIELD, half)
        result = call(body, outs, *args, flops=10**8, name=name)
        if step == 3:
            p_new, near, far, image, image_far = result
            p, p_before = p_new, p
            continue
        p_new, q_new, *edges, other = result
        if step < 2:
            laps.append(other)
        else:
            gathered = other
        p, p_before = p_new, p
        q, q_before = q_new, q
        qs.append(q)
        near = xor_swap(edges[0], "core", 1)
        if step == 1:
            lap_p, lap_q = call(
                inside, (FIELD, FIELD), p, q, own_x, own_z, flops=10**9, name="inside_1"
            )
            far = edges[1]
            continue
        edge_laps = call(
            edge_inside, edge, p, q, const["edge_x"], own_z, flops=10**8, name=f"edge_inside_{step}"
        )
        args = [near, p, p_before, q, q_before, edge_laps, squared, source, amounts]
        args.append(const["near_x"])
        if step == 2:
            args += [qs[1], laps[0], gathered, sigma]
        sent = call(
            functools.partial(early, step + 1), rows_of((4 if step == 0 else 5) * CY * OV),
            *args, flops=10**7, name=f"early_{step + 1}",
        )
        far = far_swap(sent)
        lap_p, lap_q = call(
            inside, (FIELD, FIELD), p, q, own_x, own_z, flops=10**9, name=f"inside_{step}",
            held=(sent,),
        )

    partial = call(
        shrink, rows_of(ROWS, CYC * CZC),
        image, image_far, const["shrink_x"], const["shrink_far"], const["shrink_z"],
        flops=10**8, name="shrink",
    )
    two, three, one = (xor_swap(partial, "y", m) for m in (2, 3, 1))
    near = xor_swap(near, "core", 1)
    lap_p = call(inside_one, FIELD, p, own_x, own_z, flops=5 * 10**8, name="inside_last")
    lap_p, base = call(
        last_fields, (FIELD, FIELD), near, far, p, p_before, lap_p, source, amounts, halo_x,
        flops=10**8, name="last_fields",
    )
    held = (lap_p, base)
    partial = call(
        add_four, rows_of(ROWS, CYC * CZC), partial, one, two, three, name="add_four", held=held
    )
    total, mine = call(
        squares, (rows_of(ROWS, CYC * CZC), rows_of(24)), partial, xor_swap(partial, "xl", 1),
        name="squares", held=held,
    )
    total, squared_sum = call(
        pair_up, (rows_of(ROWS, CYC * CZC), rows_of(8)), total, mine, xor_swap(mine, "core", 1),
        name="pair_up", held=held,
    )
    terms = call(
        spread, (rows_of(CX * CY),) * 3, total, sigma, lap_p, base, const["grow_z"], const["grow_new"],
        flops=10**8, name="spread",
    )
    deep = lax.axis_size("z")
    copies = call(
        widen, jax.ShapeDtypeStruct((deep, 8, 128), F32),
        squared_sum, xor_swap(squared_sum, "xh", 1), name="widen", held=terms,
    )
    parts = lax.all_to_all(copies, "z", split_axis=0, concat_axis=0, tiled=True)
    count = float(lax.axis_size(TILE) * CXC * CYC * CZC)
    direction, p_last = call(
        functools.partial(finish, count),
        (rows_of(CXC, CYC * CZC), pltpu.HBM((CX * CY, CZ), F32)),
        parts, total, *terms, name="finish",
        scratch=[pltpu.VMEM((CX * CY, CZ), F32), pltpu.SemaphoreType.DMA((4,))],
        out_specs=(VM, pl.BlockSpec(memory_space=pltpu.HBM)),
    )
    return direction, p_last.reshape(1, CX, CY, CZ)


def solution(mesh):
    shots, tiles = mesh.shape["shot"], mesh.shape["tile"]
    fine = Mesh(
        mesh.devices.reshape(shots // 2, 2, 2, tiles // 4, 2), ("y", "xl", "xh", "z", "core")
    )
    placed = (
        P(SHOT, TILE, None, None),
        P(SHOT, TILE, None, None),
        P(SHOT, TILE, None, None),
        P(SHOT, TILE, None, None),
        P(TILE, None),
        P(SHOT, TILE),
        P(TILE),
        P(),
    )
    return jax.shard_map(
        on_device,
        mesh=fine,
        in_specs=placed,
        out_specs=(P(TILE, None), P(SHOT, TILE, None, None)),
        check_vma=False,
    )
```

```python
import functools

import jax
import jax.numpy as jnp
import ml_dtypes
import numpy as np
from jax import lax
from jax.experimental import pallas as pl
from jax.experimental.pallas import tpu as pltpu
from jax.sharding import Mesh
from jax.sharding import PartitionSpec as P

CX = 128
CZ = 128
CY = 16
OV = 8
STEPS = 4
ELEMS = 64
CXC = 64
CYC = 8
CZC = 64
ROWS = 72
LEARN = 0.02
EPSILON = 1e-06
BF = jnp.bfloat16
F32 = jnp.float32
SHOT = ("y", "xl")
TILE = ("xh", "z", "core")


def spectral_second(length):
    index = np.arange(length)
    number = np.minimum(index, length - index) * (2.0 * np.pi / length)
    phase = (index[:, None, None] - index[None, :, None]) * index[None, None, :] % length
    return -np.sum(number**2 * np.cos(2.0 * np.pi / length * phase), axis=2) / length


def spline_units(offset):
    mag = np.abs(offset)
    inner = 2.0 / 3.0 - mag**2 + 0.5 * mag**3
    outer = (2.0 - mag) ** 3 / 6.0
    return np.round(384.0 * np.where(mag < 1.0, inner, np.where(mag < 2.0, outer, 0.0)))


def halves(matrix):
    high = matrix.astype(np.float32).astype(ml_dtypes.bfloat16)
    low = (matrix - high.astype(np.float64)).astype(np.float32).astype(ml_dtypes.bfloat16)
    return high, low


def narrow_band(matrix):
    high, low = halves(np.pad(matrix, ((0, OV), (0, OV))))
    return np.concatenate([high, high, low], axis=1)


@functools.cache
def constants():
    out = {}
    second_x = spectral_second(CX + 2 * OV)[OV : OV + CX]
    ramp = np.sin(0.5 * np.pi * (np.arange(OV) + 0.5) / OV) ** 2
    left = second_x[:, :OV] * ramp[None, :]
    right = second_x[:, OV + CX :] * ramp[None, ::-1]
    high, low = halves(second_x[:, OV : OV + CX])
    out["own_x"] = np.block([[high, high], [low, low]])
    sides = []
    for pair in ((right, left), (left, right)):
        high, low = halves(np.concatenate(pair, axis=1))
        sides.append(np.concatenate([high, high, low], axis=1))
    out["halo_x"] = np.stack(sides)
    edge = []
    for rows in (slice(0, OV), slice(CX - OV, CX)):
        high, low = halves(second_x[rows, OV : OV + CX])
        edge.append(np.block([[high, high], [low, low]]))
    out["edge_x"] = np.stack(edge)
    near_part, cross_part = [], []
    for core in range(2):
        rows = slice(0, OV) if core == 0 else slice(CX - OV, CX)
        near_part.append(narrow_band((right if core == 0 else left)[rows]))
        rows = slice(CX - OV, CX) if core == 0 else slice(0, OV)
        cross_part.append(narrow_band((right if core == 0 else left)[rows]))
    out["near_x"] = np.stack(near_part)
    out["cross_x"] = np.stack(cross_part)
    high, low = halves(spectral_second(CZ) - 2.0 * np.eye(CZ))
    out["own_z"] = np.block([[high, low], [high, low]])

    fine_z = np.arange(CZ)[:, None]
    coarse_z = np.arange(CZC)[None, :]
    weight_z = sum(
        spline_units((fine_z - 2 * coarse_z + image * CZ - 0.5) * 0.5) for image in range(-2, 3)
    )
    zero = np.zeros_like(weight_z.T)
    pair = np.block([[weight_z.T, zero], [zero, weight_z.T]])
    out["grow_z"] = np.concatenate([pair, pair], axis=0)
    zero = np.zeros_like(weight_z)
    out["shrink_z"] = np.block(
        [[weight_z, zero], [weight_z, zero], [zero, weight_z], [zero, weight_z]]
    )

    def column(coarse, start=0, count=CX):
        return spline_units((np.arange(start, start + count) - 2 * coarse - 0.5) * 0.5)

    own = np.stack([column(j) for j in range(CXC)], axis=1)
    lower = {j: column(j) for j in (-2, -1, 0, 1)}
    upper = {j: column(j) for j in (62, 63, 64, 65)}
    stack = lambda d: np.stack([d[j] for j in sorted(d)], axis=1)
    grow_own, grow_rest, grow_new, shrink, shrink_far = [], [], [], [], []
    blank = np.zeros((CX, 2))
    for core in range(2):
        near = upper if core == 0 else lower
        near_two, far_six = ((64, 65), range(-6, 0)) if core == 0 else ((-2, -1), range(64, 70))
        far_two = (-2, -1) if core == 0 else (64, 65)
        beyond = -OV if core == 0 else CX
        both = lambda j: np.concatenate([column(j), column(j, beyond, OV)])
        mine = np.stack([both(j) for j in range(CXC)], axis=1)
        rest = np.stack([both(j) for j in (*near_two, *far_six)], axis=1)
        inner = own.copy()
        inner[:, [62, 63] if core == 0 else [0, 1]] = 0.0
        outer = np.stack([column(j) for j in far_two], axis=1)
        new = np.concatenate([inner, stack(near), outer, blank], axis=1)
        every = np.concatenate([own, stack(near), outer, blank], axis=1).T
        past = np.zeros((ROWS, OV))
        for row, j in (*enumerate(range(CXC)), *zip((CXC + 4, CXC + 5), far_two)):
            past[row] = column(j, beyond, OV)
        grow_own.append(np.concatenate([mine, mine], axis=1))
        grow_rest.append(np.concatenate([rest, rest], axis=1))
        grow_new.append(np.concatenate([new, new], axis=1))
        shrink.append(np.concatenate([every, every], axis=1))
        shrink_far.append(np.concatenate([past, past], axis=1))
    out["shrink_far"] = np.stack(shrink_far)
    out["grow_own"] = np.stack(grow_own)
    out["grow_rest"] = np.stack(grow_rest)
    out["grow_new"] = np.stack(grow_new)
    out["shrink_x"] = np.stack(shrink)
    return {name: np.asarray(value).astype(ml_dtypes.bfloat16) for name, value in out.items()}


def taps():
    return [
        [
            (j, float(w))
            for j in range(CYC)
            for w in [
                sum(
                    spline_units(np.float64((i - 2 * j + image * CY - 0.5) * 0.5))
                    for image in range(-2, 3)
                )
            ]
            if w
        ]
        for i in range(CY)
    ]


def split(value):
    high = value.astype(BF)
    return high, (value - high.astype(F32)).astype(BF)


def dot(left, right):
    return jnp.dot(left, right, preferred_element_type=F32)


def cat(parts, axis):
    return jnp.concatenate(parts, axis=axis)


def interior(v, own_x, own_z, out):
    for j in range(CY // 2):
        one, two = 2 * j, 2 * j + 1
        high1, low1 = split(v[one])
        high2, low2 = split(v[two])
        x = dot(own_x[...], cat([cat([high1, high2], 1), cat([low1, low2], 1)], 0))
        z = dot(cat([cat([high1, low1], 1), cat([high2, low2], 1)], 0), own_z[...])
        x = x[:CX] + x[CX:]
        z = z[:, :CZ] + z[:, CZ:]
        beside = v[(one - 1) % CY] + v[two]
        out[one] = x[:, :CZ] + z[:CX] + beside
        beside = v[one] + v[(two + 1) % CY]
        out[two] = x[:, CZ:] + z[CX:] + beside


def halo_part(near, far, field, halo_x, pair):
    parts = []
    for y in (2 * pair, 2 * pair + 1):
        start = (field * CY + y) * OV
        high, low = split(cat([near[start : start + OV], far[start : start + OV]], 0))
        parts.append(cat([high, low, high], 0))
    return dot(halo_x, cat(parts, 1))


def edge_rows(v, core, near, field):
    row = pl.multiple_of((1 - core) * (CX - OV), OV)
    for y in range(CY):
        start = (field * CY + y) * OV
        near[start : start + OV] = v[y, pl.ds(row, OV), :]


def first_edge(far_side, p, q, coef, out, p_rows, q_rows, c_rows, sems):
    core = lax.axis_index("core")
    end = core if far_side else 1 - core
    block = OV * CY
    copies = [
        pltpu.make_async_copy(source.at[pl.ds(pl.multiple_of(start, 8), size)], target, sems.at[k])
        for k, (source, start, size, target) in enumerate(
            (
                (p, end * (CX * CY - block), block, p_rows),
                (q, end * (CX * CY - block), block, q_rows),
                (coef, end * (CXC - 8), 8, c_rows),
            )
        )
    ]
    for copy in copies:
        copy.start()
    for field, rows in enumerate((p_rows, q_rows)):
        copies[field].wait()
        for y in range(CY):
            start = (field * CY + y) * OV
            out[start : start + OV] = rows[pl.ds(y, OV, stride=CY), :]
    copies[2].wait()
    base = 2 * CY * OV
    count = 6 if far_side else 2
    for row in range(count):
        for part in range(4):
            lanes = slice(part * 128, part * 128 + 128)
            spot = base + row * 4 + part
            last = 8 - count + row
            out[spot : spot + 1] = jnp.where(
                end == 0, c_rows[row : row + 1, lanes], c_rows[last : last + 1, lanes]
            )


def reorder(source, target):
    for y in range(CY):
        target[y] = source[pl.ds(y, CX, stride=CY), :]


def prepare(
    signs, index, wavelet, p_now, q_now,
    own_x_in, own_z_in, p_prev_in, q_prev_in, coef_in, grow_own_in, grow_z_in,
    p0, q0, p1, q1, lap_p, lap_q, source, amounts, sigma_own,
    own_x, own_z, p_prev, q_prev, coef, grow_own, grow_z, sems,
):
    copies = [
        pltpu.make_async_copy(far, near, sems.at[k])
        for k, (far, near) in enumerate(
            (
                (own_x_in, own_x),
                (own_z_in, own_z),
                (p_prev_in, p_prev),
                (q_prev_in, q_prev),
                (coef_in, coef),
                (grow_own_in, grow_own),
                (grow_z_in, grow_z),
            )
        )
    ]
    for copy in copies:
        copy.start()
    reorder(p_now, p0)
    reorder(q_now, q0)
    source[...] = jnp.zeros_like(source)
    lane = lax.broadcasted_iota(jnp.int32, (1, CZ), 1)

    def add(e, carry):
        spot = index[e]
        x, rest = spot // (CY * CZ), spot % (CY * CZ)
        y, z = rest // CZ, rest % CZ
        amount = (2 * signs[e] - 1).astype(F32)
        row = source[y, pl.ds(x, 1), :]
        source[y, pl.ds(x, 1), :] = row + jnp.where(lane == z, amount, 0.0)
        return carry

    lax.fori_loop(0, ELEMS, add, 0)
    for step in range(STEPS + 1):
        amounts[step] = jnp.full((8, CZ), wavelet[step], F32)
    copies[0].wait()
    copies[1].wait()
    interior(p0, own_x, own_z, lap_p)
    interior(q0, own_x, own_z, lap_q)
    copies[2].wait()
    reorder(p_prev, p1)
    copies[3].wait()
    reorder(q_prev, q1)
    for copy in copies[4:]:
        copy.wait()

    def write(y, fine):
        sigma_own[y] = fine

    grow(coef[...], grow_z, grow_own[lax.axis_index("core")], write)


def grow(coef, grow_z, grow_x, write):
    wide = []
    for pair in range(CYC // 2):
        high, low = split(coef[:, pair * 128 : pair * 128 + 128])
        both = dot(cat([high, low], 1), grow_z[...])
        wide += [both[:, :CZ], both[:, CZ:]]
    weights = taps()
    for pair in range(CY // 2):
        parts = []
        for y in (2 * pair, 2 * pair + 1):
            mixed = None
            for j, w in weights[y]:
                term = wide[j] * w
                mixed = term if mixed is None else mixed + term
            parts.append(mixed)
        high, low = split(cat(parts, 1))
        fine = dot(grow_x, cat([high, low], 0))
        write(2 * pair, fine[:, :CZ])
        write(2 * pair + 1, fine[:, CZ:])


UNIT = 1.0 / 384.0**3


def grid_ends():
    core = lax.axis_index("core")
    chip = lax.axis_index("xh") * lax.axis_size("z") + lax.axis_index("z")
    chips = lax.axis_size("xh") * lax.axis_size("z")
    return (core == 0) & (chip == 0), (core == 1) & (chip == chips - 1)


def speed(sigma_own, near, far, grow_z, grow_rest, sigma, squared, beyond, held):
    core = lax.axis_index("core")
    base = 2 * CY * OV
    for row in range(6):
        for part in range(4):
            lanes = slice(part * 128, part * 128 + 128)
            spot = base + row * 4 + part
            if row < 2:
                held[row : row + 1, lanes] = near[spot : spot + 1]
            held[2 + row : 3 + row, lanes] = far[spot : spot + 1]
    first, last = grid_ends()

    def write(y, fine):
        fine = (sigma_own[y] + fine) * UNIT
        sigma[y] = fine[:CX]
        squared[y] = fine[:CX] * fine[:CX]
        beyond[y * OV : y * OV + OV] = jnp.where(first | last, 0.0, fine[CX:])

    grow(held[...], grow_z, grow_rest[core], write)


def squared_at(beyond, spot):
    value = beyond[spot : spot + OV]
    return value * value


def advance(step, *refs):
    (near, far, p, p_before, q, q_before, lap_p, lap_q, squared, source, amounts, halo_x) = refs[:12]
    refs = refs[12:]
    core = lax.axis_index("core")
    columns = halo_x[core]
    weight = amounts[step, :1, :]
    if step in (1, 3):
        (sent, beyond, cross_x), refs = refs[:3], refs[3:]
        cross = cross_x[core]
    if step == 2:
        old_lap, refs = refs[0], refs[1:]
    if step == 3:
        (old_lap, older_q, gathered, sigma, older_far), refs = refs[:5], refs[5:]
    if step in (0, 2):
        (p_new, q_new, near_out), refs = refs[:3], refs[3:]
    elif step == 1:
        (p_new, q_new, near_out, far_out), refs = refs[:4], refs[4:]
    else:
        p_new, near_out, far_out, image, image_far = refs[:5]
    if step < 2:
        lap_out = refs[0]
    if step == 2:
        gathered = refs[0]
    for pair in range(CY // 2):
        extra_p = halo_part(near, far, 0, columns, pair)
        extra_q = halo_part(near, far, 1, columns, pair)
        for side in range(2):
            y = 2 * pair + side
            lanes = slice(side * CZ, side * CZ + CZ)
            lap = lap_p[y] + extra_p[:, lanes]
            lap_adj = lap_q[y] + extra_q[:, lanes]
            sq = squared[y]
            p_new[y] = 2.0 * p[y] - p_before[y] + sq * lap + source[y] * weight
            new_q = 2.0 * q[y] - q_before[y] + sq * lap_adj
            if step < 3:
                q_new[y] = new_q
            if step < 2:
                lap_out[y] = lap
            if step == 2:
                gathered[y] = q[y] * lap + new_q * old_lap[y]
            if step == 3:
                total = gathered[y] + older_q[y] * lap + new_q * old_lap[y]
                image[y] = 2.0 * sigma[y] * total
    edge_rows(p_new, core, near_out, 0)
    if step < 3:
        edge_rows(q_new, core, near_out, 1)
    if step == 1:
        size = CY * OV
        for pair in range(CY // 2):
            for field in range(2):
                extra = halo_part(sent, sent, field, cross, pair)
                for side in range(2):
                    spot = (2 * pair + side) * OV
                    known = far[(2 + field) * size + spot : (2 + field) * size + spot + OV]
                    far_out[field * size + spot : field * size + spot + OV] = (
                        known
                        + squared_at(beyond, spot) * extra[:OV, side * CZ : side * CZ + CZ]
                    )
    if step == 3:
        size = CY * OV
        for pair in range(CY // 2):
            extra_p = halo_part(sent, sent, 0, cross, pair)
            extra_q = halo_part(sent, sent, 1, cross, pair)
            for side in range(2):
                spot = (2 * pair + side) * OV
                lanes = slice(side * CZ, side * CZ + CZ)
                part_p, part_q = extra_p[:OV, lanes], extra_q[:OV, lanes]
                rows = lambda k: far[k * size + spot : k * size + spot + OV]
                far_out[spot : spot + OV] = rows(2) + squared_at(beyond, spot) * part_p
                near_q = older_far[size + spot : size + spot + OV]
                image_far[spot : spot + OV] = (
                    rows(3) + 2.0 * beyond[spot : spot + OV] * near_q * part_p + rows(4) * part_q
                )


def early(step, *refs):
    (near, p, p_before, q, q_before, laps, squared, source, amounts, near_x) = refs[:10]
    if step == 3:
        older_q, old_lap, gathered, sigma = refs[10:14]
    out = refs[-1]
    core = lax.axis_index("core")
    rows = pl.ds(pl.multiple_of(core * (CX - OV), OV), OV)
    weight = amounts[step, :1, :]
    columns = near_x[core]
    for pair in range(CY // 2):
        extra_p = halo_part(near, near, 0, columns, pair)
        extra_q = halo_part(near, near, 1, columns, pair)
        for side in range(2):
            y = 2 * pair + side
            lanes = slice(side * CZ, side * CZ + CZ)
            sq = squared[y, rows, :]
            spot = y * OV
            lap = laps[spot : spot + OV] + extra_p[:OV, lanes]
            spot += CY * OV
            lap_adj = laps[spot : spot + OV] + extra_q[:OV, lanes]
            edge_p, edge_q = p[y, rows, :], q[y, rows, :]
            next_p = 2.0 * edge_p - p_before[y, rows, :] + sq * lap + source[y, rows, :] * weight
            next_q = 2.0 * edge_q - q_before[y, rows, :] + sq * lap_adj
            if step == 1:
                sets = (edge_p, edge_q, next_p, next_q)
            else:
                twice = 2.0 * sigma[y, rows, :]
                old = old_lap[y, rows, :]
                known = gathered[y, rows, :] + older_q[y, rows, :] * lap + next_q * old
                sets = (edge_p, edge_q, next_p, twice * known, twice * sq * old)
            for k, value in enumerate(sets):
                spot = (k * CY + y) * OV
                out[spot : spot + OV] = value


def edge_interior(v, edge_x, own_z, first, out, field):
    strips = []
    for j in range(CY // 2):
        one, two = 2 * j, 2 * j + 1
        high1, low1 = split(v[one])
        high2, low2 = split(v[two])
        x = dot(edge_x, cat([cat([high1, high2], 1), cat([low1, low2], 1)], 0))
        x = x[:OV] + x[OV:]
        strips += [x[:, :CZ], x[:, CZ:]]
    rows = pl.ds(first, OV)
    edge = [v[y, rows, :] for y in range(CY)]
    high, low = split(cat(edge, 0))
    z = dot(cat([high, low], 1), own_z[...])
    z = z[:, :CZ] + z[:, CZ:]
    for y in range(CY):
        beside = edge[(y - 1) % CY] + edge[(y + 1) % CY]
        spot = (field * CY + y) * OV
        out[spot : spot + OV] = strips[y] + z[y * OV : y * OV + OV] + beside


def edge_inside(p, q, edge_x, own_z, out):
    core = lax.axis_index("core")
    first = pl.multiple_of(core * (CX - OV), OV)
    edge_interior(p, edge_x[core], own_z, first, out, 0)
    edge_interior(q, edge_x[core], own_z, first, out, 1)


def inside(p, q, own_x, own_z, lap_p, lap_q):
    interior(p, own_x, own_z, lap_p)
    interior(q, own_x, own_z, lap_q)


def inside_one(p, own_x, own_z, lap_p):
    interior(p, own_x, own_z, lap_p)


def shrink(image, image_far, shrink_x, shrink_far, shrink_z, own):
    core = lax.axis_index("core")
    rows_x = shrink_x[core]
    rows_far = shrink_far[core]
    narrow = [None] * CYC
    weights = taps()
    for pair in range(CY // 2):
        high, low = split(cat([image[2 * pair], image[2 * pair + 1]], 1))
        both = dot(rows_x, cat([high, low], 0))
        spots = [slice(y * OV, y * OV + OV) for y in (2 * pair, 2 * pair + 1)]
        high, low = split(cat([image_far[spots[0]], image_far[spots[1]]], 1))
        both = both + dot(rows_far, cat([high, low], 0))
        for side in range(2):
            part = both[:, side * CZ : side * CZ + CZ]
            for j, w in weights[2 * pair + side]:
                term = part * w
                narrow[j] = term if narrow[j] is None else narrow[j] + term
    pieces = []
    for pair in range(CYC // 2):
        parts = []
        for j in (2 * pair, 2 * pair + 1):
            parts += list(split(narrow[j]))
        pieces.append(dot(cat(parts, 1), shrink_z[...]) * UNIT)
    own[...] = cat(pieces, 1)


def fold(value):
    rows = value[0:8]
    for r in range(1, value.shape[0] // 8):
        rows = rows + value[8 * r : 8 * r + 8]
    folded = rows[:, :128]
    for c in range(1, 4):
        folded = folded + rows[:, 128 * c : 128 * c + 128]
    return folded


def squares(a, b, total, near):
    core = lax.axis_index("core")
    total[...] = a[...] + b[...]
    first, last = grid_ends()
    total[CXC + 4 : CXC + 6] = jnp.where(first | last, 0.0, total[CXC + 4 : CXC + 6])
    row = lax.broadcasted_iota(jnp.int32, (CXC, CYC * CZC), 0)
    start = (1 - core) * (CXC - 2)
    value = jnp.where((row >= start) & (row < start + 2), 0.0, total[:CXC])
    for r in range(4):
        for part in range(4):
            lanes = slice(part * 128, part * 128 + 128)
            spot = r * 4 + part
            near[spot : spot + 1] = total[CXC + r : CXC + r + 1, lanes]
    near[16:24] = fold(value * value)


def pair_up(total, mine, other, out, squared):
    core = lax.axis_index("core")
    out[...] = total[...]
    edge = mine[0:16] + other[0:16]
    for r in range(4):
        for part in range(4):
            lanes = slice(part * 128, part * 128 + 128)
            spot = r * 4 + part
            out[CXC + r : CXC + r + 1, lanes] = edge[spot : spot + 1]
    out[0:2] = jnp.where(core == 0, out[0:2], out[CXC + 2 : CXC + 4])
    out[CXC - 2 : CXC] = jnp.where(core == 0, out[CXC : CXC + 2], out[CXC - 2 : CXC])
    edge = edge * edge
    squared[...] = (mine[16:24] + other[16:24]) + (edge[0:8] + edge[8:16])


def last_fields(near, far, p, p_before, lap_p, source, amounts, halo_x, lap_out, base):
    core = lax.axis_index("core")
    columns = halo_x[core]
    weight = amounts[STEPS, :1, :]
    for pair in range(CY // 2):
        extra = halo_part(near, far, 0, columns, pair)
        for side in range(2):
            y = 2 * pair + side
            lap_out[y] = lap_p[y] + extra[:, side * CZ : side * CZ + CZ]
            base[y] = 2.0 * p[y] - p_before[y] + source[y] * weight


def add_four(own, two, three, one, out):
    out[...] = (own[...] + one[...]) + (two[...] + three[...])


def spread(total, sigma, lap, base, grow_z, grow_new, zeroth, first, second):
    core = lax.axis_index("core")

    def write(y, fine):
        change = fine * UNIT
        old, curve = sigma[y], lap[y]
        scaled = change * curve
        rows = pl.ds(y, CX, stride=CY)
        zeroth[rows, :] = base[y] + old * old * curve
        first[rows, :] = -2.0 * old * scaled
        second[rows, :] = change * scaled

    grow(total[...], grow_z, grow_new[core], write)


def widen(a, b, out):
    value = a[...] + b[...]
    for k in range(out.shape[0]):
        out[k] = value


def finish(count, parts, total, zeroth, first, second, direction, p_last, held, sems):
    value = parts[0]
    for k in range(1, parts.shape[0]):
        value = value + parts[k]
    value = jnp.sum(jnp.sum(value, axis=0, keepdims=True), axis=1, keepdims=True)
    inverse = 1.0 / jnp.sqrt(value * (1.0 / count) + EPSILON)
    rate = LEARN * inverse
    size = CX * CY // sems.shape[0]
    copies = []
    for c in range(sems.shape[0]):
        rows = slice(c * size, c * size + size)
        held[rows] = zeroth[rows] + rate * (first[rows] + rate * second[rows])
        copies.append(pltpu.make_async_copy(held.at[rows], p_last.at[rows], sems.at[c]))
        copies[-1].start()
    direction[...] = total[:CXC] * inverse
    for copy in copies:
        copy.wait()


VM = pl.BlockSpec(memory_space=pltpu.VMEM)
SM = pl.BlockSpec(memory_space=pltpu.SMEM)
FIELD = jax.ShapeDtypeStruct((CY, CX, CZ), F32)
PARAMS = pltpu.CompilerParams(vmem_limit_bytes=6 * 2**20)


def rows_of(count, lanes=128):
    return jax.ShapeDtypeStruct((count, lanes), F32)


def call(body, outs, *args, smem=0, scratch=(), flops=0, name=None, held=(), in_specs=None, out_specs=None):
    size = sum(int(np.prod(a.shape)) * a.dtype.itemsize for a in args)
    count = len(args)

    def run(*refs):
        body(*refs[:count], *refs[count + len(held) :])

    return pl.pallas_call(
        run,
        out_shape=outs,
        in_specs=([SM] * smem + [VM] * (count - smem) if in_specs is None else in_specs)
        + [pl.BlockSpec(memory_space=pl.ANY)] * len(held),
        out_specs=jax.tree.map(lambda _: VM, outs) if out_specs is None else out_specs,
        scratch_shapes=list(scratch),
        compiler_params=PARAMS,
        cost_estimate=pl.CostEstimate(flops=flops, bytes_accessed=size, transcendentals=0),
        name=name,
    )(*args, *held)


def xor_swap(x, axis, mask):
    count = lax.axis_size(axis)
    if mask >= count:
        return jnp.zeros_like(x)
    return lax.ppermute(x, axis, [(i, i ^ mask) for i in range(count)])


def far_swap(x):
    count = lax.axis_size(TILE)
    pairs = [(i, i + 1) for i in range(1, count - 1, 2)]
    return lax.ppermute(x, TILE, pairs + [(b, a) for a, b in pairs])


def on_device(p_now, p_prev, adj_now, adj_next, coef_old, signs, elem_index, wavelet):
    const = {name: jnp.asarray(value) for name, value in constants().items()}
    own_x, own_z, halo_x = const["own_x"], const["own_z"], const["halo_x"]
    flat = lambda a: a.reshape(CX * CY, CZ)
    p_now, p_prev, adj_now, adj_next = map(flat, (p_now, p_prev, adj_now, adj_next))

    half, edge = rows_of(CY * OV), rows_of(2 * CY * OV)
    sources = [pltpu.with_memory_space_constraint(a, pltpu.HBM) for a in (p_now, adj_now, coef_old)]

    def first(far_side, *held):
        return call(
            functools.partial(first_edge, far_side),
            rows_of(2 * CY * OV + (24 if far_side else 8)),
            *sources,
            in_specs=[pl.BlockSpec(memory_space=pltpu.HBM)] * 3,
            scratch=[pltpu.VMEM((OV * CY, CZ), F32)] * 2
            + [pltpu.VMEM((8, CYC * CZC), F32), pltpu.SemaphoreType.DMA((3,))],
            name="far_edge" if far_side else "near_edge",
            held=held,
        )

    far = first(True)
    near = xor_swap(first(False, far), "core", 1)
    far = far_swap(far)

    wide = jax.ShapeDtypeStruct((CY, CX + OV, CZ), F32)
    later = [own_x, own_z, p_prev, adj_next, coef_old, const["grow_own"]]
    later.append(const["grow_z"])
    p, q, p_before, q_before, lap_p, lap_q, source, amounts, sigma_own = call(
        prepare,
        (FIELD,) * 7 + (jax.ShapeDtypeStruct((STEPS + 1, 8, CZ), F32), wide),
        signs[0], elem_index, wavelet, p_now, adj_now,
        *(pltpu.with_memory_space_constraint(a, pltpu.HBM) for a in later),
        flops=10**9, name="prepare", held=(halo_x,),
        in_specs=[SM] * 3 + [VM] * 2 + [pl.BlockSpec(memory_space=pltpu.HBM)] * len(later),
        scratch=[pltpu.VMEM(a.shape, a.dtype) for a in later]
        + [pltpu.SemaphoreType.DMA((len(later),))],
    )
    sigma, squared, beyond = call(
        speed, (FIELD, FIELD, half), sigma_own, near, far, const["grow_z"], const["grow_rest"],
        scratch=[pltpu.VMEM((8, CYC * CZC), F32)], flops=10**8, name="speed",
    )

    laps, qs = [], [q]
    gathered = None
    for step in range(STEPS):
        args = [near, far, p, p_before, q, q_before, lap_p, lap_q, squared, source, amounts, halo_x]
        body = functools.partial(advance, step)
        name = f"advance_{step}"
        if step == 0:
            outs = (FIELD, FIELD, edge, FIELD)
        elif step == 1:
            args += [sent, beyond, const["cross_x"]]
            outs = (FIELD, FIELD, edge, edge, FIELD)
            older_far = far
        elif step == 2:
            args.append(laps[1])
            outs = (FIELD, FIELD, edge, FIELD)
        else:
            args += [sent, beyond, const["cross_x"], laps[0], qs[1], gathered, sigma, older_far]
            outs = (FIELD, half, half, FIELD, half)
        result = call(body, outs, *args, flops=10**8, name=name)
        if step == 3:
            p_new, near, far, image, image_far = result
            p, p_before = p_new, p
            continue
        p_new, q_new, *edges, other = result
        if step < 2:
            laps.append(other)
        else:
            gathered = other
        p, p_before = p_new, p
        q, q_before = q_new, q
        qs.append(q)
        near = xor_swap(edges[0], "core", 1)
        if step == 1:
            lap_p, lap_q = call(
                inside, (FIELD, FIELD), p, q, own_x, own_z, flops=10**9, name="inside_1"
            )
            far = edges[1]
            continue
        edge_laps = call(
            edge_inside, edge, p, q, const["edge_x"], own_z, flops=10**8, name=f"edge_inside_{step}"
        )
        args = [near, p, p_before, q, q_before, edge_laps, squared, source, amounts]
        args.append(const["near_x"])
        if step == 2:
            args += [qs[1], laps[0], gathered, sigma]
        sent = call(
            functools.partial(early, step + 1), rows_of((4 if step == 0 else 5) * CY * OV),
            *args, flops=10**7, name=f"early_{step + 1}",
        )
        far = far_swap(sent)
        lap_p, lap_q = call(
            inside, (FIELD, FIELD), p, q, own_x, own_z, flops=10**9, name=f"inside_{step}",
            held=(sent,),
        )

    partial = call(
        shrink, rows_of(ROWS, CYC * CZC),
        image, image_far, const["shrink_x"], const["shrink_far"], const["shrink_z"],
        flops=10**8, name="shrink",
    )
    two, three, one = (xor_swap(partial, "y", m) for m in (2, 3, 1))
    near = xor_swap(near, "core", 1)
    lap_p = call(inside_one, FIELD, p, own_x, own_z, flops=5 * 10**8, name="inside_last")
    lap_p, base = call(
        last_fields, (FIELD, FIELD), near, far, p, p_before, lap_p, source, amounts, halo_x,
        flops=10**8, name="last_fields",
    )
    held = (lap_p, base)
    partial = call(
        add_four, rows_of(ROWS, CYC * CZC), partial, two, three, one, name="add_four", held=held
    )
    total, mine = call(
        squares, (rows_of(ROWS, CYC * CZC), rows_of(24)), partial, xor_swap(partial, "xl", 1),
        name="squares", held=held,
    )
    total, squared_sum = call(
        pair_up, (rows_of(ROWS, CYC * CZC), rows_of(8)), total, mine, xor_swap(mine, "core", 1),
        name="pair_up", held=held,
    )
    terms = call(
        spread, (rows_of(CX * CY),) * 3, total, sigma, lap_p, base, const["grow_z"], const["grow_new"],
        flops=10**8, name="spread",
    )
    deep = lax.axis_size("z")
    copies = call(
        widen, jax.ShapeDtypeStruct((deep, 8, 128), F32),
        squared_sum, xor_swap(squared_sum, "xh", 1), name="widen", held=terms,
    )
    parts = lax.all_to_all(copies, "z", split_axis=0, concat_axis=0, tiled=True)
    count = float(lax.axis_size(TILE) * CXC * CYC * CZC)
    direction, p_last = call(
        functools.partial(finish, count),
        (rows_of(CXC, CYC * CZC), pltpu.HBM((CX * CY, CZ), F32)),
        parts, total, *terms, name="finish",
        scratch=[pltpu.VMEM((CX * CY, CZ), F32), pltpu.SemaphoreType.DMA((4,))],
        out_specs=(VM, pl.BlockSpec(memory_space=pltpu.HBM)),
    )
    return direction, p_last.reshape(1, CX, CY, CZ)


def solution(mesh):
    shots, tiles = mesh.shape["shot"], mesh.shape["tile"]
    fine = Mesh(
        mesh.devices.reshape(shots // 2, 2, 2, tiles // 4, 2), ("y", "xl", "xh", "z", "core")
    )
    placed = (
        P(SHOT, TILE, None, None),
        P(SHOT, TILE, None, None),
        P(SHOT, TILE, None, None),
        P(SHOT, TILE, None, None),
        P(TILE, None),
        P(SHOT, TILE),
        P(TILE),
        P(),
    )
    return jax.shard_map(
        on_device,
        mesh=fine,
        in_specs=placed,
        out_specs=(P(TILE, None), P(SHOT, TILE, None, None)),
        check_vma=False,
    )
```

```python
import functools

import jax
import jax.numpy as jnp
import ml_dtypes
import numpy as np
from jax import lax
from jax.experimental import pallas as pl
from jax.experimental.pallas import tpu as pltpu
from jax.sharding import Mesh
from jax.sharding import PartitionSpec as P

CX = 128
CZ = 128
CY = 16
OV = 8
STEPS = 4
ELEMS = 64
CXC = 64
CYC = 8
CZC = 64
ROWS = 72
LEARN = 0.02
EPSILON = 1e-06
BF = jnp.bfloat16
F32 = jnp.float32
SHOT = ("y", "xl")
TILE = ("xh", "z", "core")


def spectral_second(length):
    index = np.arange(length)
    number = np.minimum(index, length - index) * (2.0 * np.pi / length)
    phase = (index[:, None, None] - index[None, :, None]) * index[None, None, :] % length
    return -np.sum(number**2 * np.cos(2.0 * np.pi / length * phase), axis=2) / length


def spline_units(offset):
    mag = np.abs(offset)
    inner = 2.0 / 3.0 - mag**2 + 0.5 * mag**3
    outer = (2.0 - mag) ** 3 / 6.0
    return np.round(384.0 * np.where(mag < 1.0, inner, np.where(mag < 2.0, outer, 0.0)))


def halves(matrix):
    high = matrix.astype(np.float32).astype(ml_dtypes.bfloat16)
    low = (matrix - high.astype(np.float64)).astype(np.float32).astype(ml_dtypes.bfloat16)
    return high, low


def narrow_band(matrix):
    high, low = halves(np.pad(matrix, ((0, OV), (0, OV))))
    return np.concatenate([high, high, low], axis=1)


@functools.cache
def constants():
    out = {}
    second_x = spectral_second(CX + 2 * OV)[OV : OV + CX]
    ramp = np.sin(0.5 * np.pi * (np.arange(OV) + 0.5) / OV) ** 2
    left = second_x[:, :OV] * ramp[None, :]
    right = second_x[:, OV + CX :] * ramp[None, ::-1]
    high, low = halves(second_x[:, OV : OV + CX])
    out["own_x"] = np.block([[high, high], [low, low]])
    sides = []
    for pair in ((right, left), (left, right)):
        high, low = halves(np.concatenate(pair, axis=1))
        sides.append(np.concatenate([high, high, low], axis=1))
    out["halo_x"] = np.stack(sides)
    edge = []
    for rows in (slice(0, OV), slice(CX - OV, CX)):
        high, low = halves(second_x[rows, OV : OV + CX])
        edge.append(np.block([[high, high], [low, low]]))
    out["edge_x"] = np.stack(edge)
    near_part, cross_part = [], []
    for core in range(2):
        rows = slice(0, OV) if core == 0 else slice(CX - OV, CX)
        near_part.append(narrow_band((right if core == 0 else left)[rows]))
        rows = slice(CX - OV, CX) if core == 0 else slice(0, OV)
        cross_part.append(narrow_band((right if core == 0 else left)[rows]))
    out["near_x"] = np.stack(near_part)
    out["cross_x"] = np.stack(cross_part)
    high, low = halves(spectral_second(CZ) - 2.0 * np.eye(CZ))
    out["own_z"] = np.block([[high, low], [high, low]])

    fine_z = np.arange(CZ)[:, None]
    coarse_z = np.arange(CZC)[None, :]
    weight_z = sum(
        spline_units((fine_z - 2 * coarse_z + image * CZ - 0.5) * 0.5) for image in range(-2, 3)
    )
    zero = np.zeros_like(weight_z.T)
    pair = np.block([[weight_z.T, zero], [zero, weight_z.T]])
    out["grow_z"] = np.concatenate([pair, pair], axis=0)
    zero = np.zeros_like(weight_z)
    out["shrink_z"] = np.block(
        [[weight_z, zero], [weight_z, zero], [zero, weight_z], [zero, weight_z]]
    )

    def column(coarse, start=0, count=CX):
        return spline_units((np.arange(start, start + count) - 2 * coarse - 0.5) * 0.5)

    own = np.stack([column(j) for j in range(CXC)], axis=1)
    lower = {j: column(j) for j in (-2, -1, 0, 1)}
    upper = {j: column(j) for j in (62, 63, 64, 65)}
    stack = lambda d: np.stack([d[j] for j in sorted(d)], axis=1)
    grow_own, grow_rest, grow_new, shrink, shrink_far = [], [], [], [], []
    blank = np.zeros((CX, 2))
    for core in range(2):
        near = upper if core == 0 else lower
        near_two, far_six = ((64, 65), range(-6, 0)) if core == 0 else ((-2, -1), range(64, 70))
        far_two = (-2, -1) if core == 0 else (64, 65)
        beyond = -OV if core == 0 else CX
        both = lambda j: np.concatenate([column(j), column(j, beyond, OV)])
        mine = np.stack([both(j) for j in range(CXC)], axis=1)
        rest = np.stack([both(j) for j in (*near_two, *far_six)], axis=1)
        inner = own.copy()
        inner[:, [62, 63] if core == 0 else [0, 1]] = 0.0
        outer = np.stack([column(j) for j in far_two], axis=1)
        new = np.concatenate([inner, stack(near), outer, blank], axis=1)
        every = np.concatenate([own, stack(near), outer, blank], axis=1).T
        past = np.zeros((ROWS, OV))
        for row, j in (*enumerate(range(CXC)), *zip((CXC + 4, CXC + 5), far_two)):
            past[row] = column(j, beyond, OV)
        grow_own.append(np.concatenate([mine, mine], axis=1))
        grow_rest.append(np.concatenate([rest, rest], axis=1))
        grow_new.append(np.concatenate([new, new], axis=1))
        shrink.append(np.concatenate([every, every], axis=1))
        shrink_far.append(np.concatenate([past, past], axis=1))
    out["shrink_far"] = np.stack(shrink_far)
    out["grow_own"] = np.stack(grow_own)
    out["grow_rest"] = np.stack(grow_rest)
    out["grow_new"] = np.stack(grow_new)
    out["shrink_x"] = np.stack(shrink)
    return {name: np.asarray(value).astype(ml_dtypes.bfloat16) for name, value in out.items()}


def taps():
    return [
        [
            (j, float(w))
            for j in range(CYC)
            for w in [
                sum(
                    spline_units(np.float64((i - 2 * j + image * CY - 0.5) * 0.5))
                    for image in range(-2, 3)
                )
            ]
            if w
        ]
        for i in range(CY)
    ]


def split(value):
    high = value.astype(BF)
    return high, (value - high.astype(F32)).astype(BF)


def dot(left, right):
    return jnp.dot(left, right, preferred_element_type=F32)


def cat(parts, axis):
    return jnp.concatenate(parts, axis=axis)


def interior(v, own_x, own_z, out):
    for j in range(CY // 2):
        one, two = 2 * j, 2 * j + 1
        high1, low1 = split(v[one])
        high2, low2 = split(v[two])
        x = dot(own_x[...], cat([cat([high1, high2], 1), cat([low1, low2], 1)], 0))
        z = dot(cat([cat([high1, low1], 1), cat([high2, low2], 1)], 0), own_z[...])
        x = x[:CX] + x[CX:]
        z = z[:, :CZ] + z[:, CZ:]
        beside = v[(one - 1) % CY] + v[two]
        out[one] = x[:, :CZ] + z[:CX] + beside
        beside = v[one] + v[(two + 1) % CY]
        out[two] = x[:, CZ:] + z[CX:] + beside


def halo_part(near, far, field, halo_x, pair):
    parts = []
    for y in (2 * pair, 2 * pair + 1):
        start = (field * CY + y) * OV
        high, low = split(cat([near[start : start + OV], far[start : start + OV]], 0))
        parts.append(cat([high, low, high], 0))
    return dot(halo_x, cat(parts, 1))


def edge_rows(v, core, near, field):
    row = pl.multiple_of((1 - core) * (CX - OV), OV)
    for y in range(CY):
        start = (field * CY + y) * OV
        near[start : start + OV] = v[y, pl.ds(row, OV), :]


def first_edges(p, q, coef, far, near, *scratch):
    core = lax.axis_index("core")
    sems = scratch[6]
    block = OV * CY
    ends, copies = (core, 1 - core), []
    for side, end in enumerate(ends):
        for k, (source, whole, size) in enumerate(
            ((p, CX * CY, block), (q, CX * CY, block), (coef, CXC, 8))
        ):
            start = pl.multiple_of(end * (whole - size), 8)
            at = 3 * side + k
            copies.append(
                pltpu.make_async_copy(source.at[pl.ds(start, size)], scratch[at], sems.at[at])
            )
    for copy in copies:
        copy.start()
    for side, (end, out, count) in enumerate(zip(ends, (far, near), (6, 2))):
        for field in range(2):
            copies[3 * side + field].wait()
            rows = scratch[3 * side + field]
            for y in range(CY):
                start = (field * CY + y) * OV
                out[start : start + OV] = rows[pl.ds(y, OV, stride=CY), :]
        copies[3 * side + 2].wait()
        rows = scratch[3 * side + 2]
        base = 2 * CY * OV
        for row in range(count):
            for part in range(4):
                lanes = slice(part * 128, part * 128 + 128)
                spot = base + row * 4 + part
                last = 8 - count + row
                out[spot : spot + 1] = jnp.where(
                    end == 0, rows[row : row + 1, lanes], rows[last : last + 1, lanes]
                )


def reorder(source, target):
    for y in range(CY):
        target[y] = source[pl.ds(y, CX, stride=CY), :]


def prepare(
    signs, index, wavelet, p_now, q_now,
    own_x_in, own_z_in, p_prev_in, q_prev_in, coef_in, grow_own_in, grow_z_in,
    p0, q0, p1, q1, lap_p, lap_q, source, amounts, sigma_own,
    own_x, own_z, p_prev, q_prev, coef, grow_own, grow_z, sems,
):
    copies = [
        pltpu.make_async_copy(far, near, sems.at[k])
        for k, (far, near) in enumerate(
            (
                (own_x_in, own_x),
                (own_z_in, own_z),
                (p_prev_in, p_prev),
                (q_prev_in, q_prev),
                (coef_in, coef),
                (grow_own_in, grow_own),
                (grow_z_in, grow_z),
            )
        )
    ]
    for copy in copies:
        copy.start()
    reorder(p_now, p0)
    reorder(q_now, q0)
    source[...] = jnp.zeros_like(source)
    lane = lax.broadcasted_iota(jnp.int32, (1, CZ), 1)

    def add(e, carry):
        spot = index[e]
        x, rest = spot // (CY * CZ), spot % (CY * CZ)
        y, z = rest // CZ, rest % CZ
        amount = (2 * signs[e] - 1).astype(F32)
        row = source[y, pl.ds(x, 1), :]
        source[y, pl.ds(x, 1), :] = row + jnp.where(lane == z, amount, 0.0)
        return carry

    lax.fori_loop(0, ELEMS, add, 0)
    for step in range(STEPS + 1):
        amounts[step] = jnp.full((8, CZ), wavelet[step], F32)
    copies[0].wait()
    copies[1].wait()
    interior(p0, own_x, own_z, lap_p)
    interior(q0, own_x, own_z, lap_q)
    copies[2].wait()
    reorder(p_prev, p1)
    copies[3].wait()
    reorder(q_prev, q1)
    for copy in copies[4:]:
        copy.wait()

    def write(y, fine):
        sigma_own[y] = fine

    grow(coef[...], grow_z, grow_own[lax.axis_index("core")], write)


def grow(coef, grow_z, grow_x, write):
    wide = []
    for pair in range(CYC // 2):
        high, low = split(coef[:, pair * 128 : pair * 128 + 128])
        both = dot(cat([high, low], 1), grow_z[...])
        wide += [both[:, :CZ], both[:, CZ:]]
    weights = taps()
    for pair in range(CY // 2):
        parts = []
        for y in (2 * pair, 2 * pair + 1):
            mixed = None
            for j, w in weights[y]:
                term = wide[j] * w
                mixed = term if mixed is None else mixed + term
            parts.append(mixed)
        high, low = split(cat(parts, 1))
        fine = dot(grow_x, cat([high, low], 0))
        write(2 * pair, fine[:, :CZ])
        write(2 * pair + 1, fine[:, CZ:])


UNIT = 1.0 / 384.0**3


def grid_ends():
    core = lax.axis_index("core")
    chip = lax.axis_index("xh") * lax.axis_size("z") + lax.axis_index("z")
    chips = lax.axis_size("xh") * lax.axis_size("z")
    return (core == 0) & (chip == 0), (core == 1) & (chip == chips - 1)


def speed(sigma_own, near, far, grow_z, grow_rest, sigma, squared, beyond, held):
    core = lax.axis_index("core")
    base = 2 * CY * OV
    for row in range(6):
        for part in range(4):
            lanes = slice(part * 128, part * 128 + 128)
            spot = base + row * 4 + part
            if row < 2:
                held[row : row + 1, lanes] = near[spot : spot + 1]
            held[2 + row : 3 + row, lanes] = far[spot : spot + 1]
    first, last = grid_ends()

    def write(y, fine):
        fine = (sigma_own[y] + fine) * UNIT
        sigma[y] = fine[:CX]
        squared[y] = fine[:CX] * fine[:CX]
        beyond[y * OV : y * OV + OV] = jnp.where(first | last, 0.0, fine[CX:])

    grow(held[...], grow_z, grow_rest[core], write)


def squared_at(beyond, spot):
    value = beyond[spot : spot + OV]
    return value * value


def advance(step, *refs):
    (near, far, p, p_before, q, q_before, lap_p, lap_q, squared, source, amounts, halo_x) = refs[:12]
    refs = refs[12:]
    core = lax.axis_index("core")
    columns = halo_x[core]
    weight = amounts[step, :1, :]
    if step in (1, 3):
        (sent, beyond, cross_x), refs = refs[:3], refs[3:]
        cross = cross_x[core]
    if step == 2:
        old_lap, refs = refs[0], refs[1:]
    if step == 3:
        (old_lap, older_q, gathered, sigma, older_far), refs = refs[:5], refs[5:]
    if step in (0, 2):
        (p_new, q_new, near_out), refs = refs[:3], refs[3:]
    elif step == 1:
        (p_new, q_new, near_out, far_out), refs = refs[:4], refs[4:]
    else:
        p_new, near_out, far_out, image, image_far = refs[:5]
    if step < 2:
        lap_out = refs[0]
    if step == 2:
        gathered = refs[0]
    for pair in range(CY // 2):
        extra_p = halo_part(near, far, 0, columns, pair)
        extra_q = halo_part(near, far, 1, columns, pair)
        for side in range(2):
            y = 2 * pair + side
            lanes = slice(side * CZ, side * CZ + CZ)
            lap = lap_p[y] + extra_p[:, lanes]
            lap_adj = lap_q[y] + extra_q[:, lanes]
            sq = squared[y]
            p_new[y] = 2.0 * p[y] - p_before[y] + sq * lap + source[y] * weight
            new_q = 2.0 * q[y] - q_before[y] + sq * lap_adj
            if step < 3:
                q_new[y] = new_q
            if step < 2:
                lap_out[y] = lap
            if step == 2:
                gathered[y] = q[y] * lap + new_q * old_lap[y]
            if step == 3:
                total = gathered[y] + older_q[y] * lap + new_q * old_lap[y]
                image[y] = 2.0 * sigma[y] * total
    edge_rows(p_new, core, near_out, 0)
    if step < 3:
        edge_rows(q_new, core, near_out, 1)
    if step == 1:
        size = CY * OV
        for pair in range(CY // 2):
            for field in range(2):
                extra = halo_part(sent, sent, field, cross, pair)
                for side in range(2):
                    spot = (2 * pair + side) * OV
                    known = far[(2 + field) * size + spot : (2 + field) * size + spot + OV]
                    far_out[field * size + spot : field * size + spot + OV] = (
                        known
                        + squared_at(beyond, spot) * extra[:OV, side * CZ : side * CZ + CZ]
                    )
    if step == 3:
        size = CY * OV
        for pair in range(CY // 2):
            extra_p = halo_part(sent, sent, 0, cross, pair)
            extra_q = halo_part(sent, sent, 1, cross, pair)
            for side in range(2):
                spot = (2 * pair + side) * OV
                lanes = slice(side * CZ, side * CZ + CZ)
                part_p, part_q = extra_p[:OV, lanes], extra_q[:OV, lanes]
                rows = lambda k: far[k * size + spot : k * size + spot + OV]
                far_out[spot : spot + OV] = rows(2) + squared_at(beyond, spot) * part_p
                near_q = older_far[size + spot : size + spot + OV]
                image_far[spot : spot + OV] = (
                    rows(3) + 2.0 * beyond[spot : spot + OV] * near_q * part_p + rows(4) * part_q
                )


def early(step, *refs):
    (near, p, p_before, q, q_before, laps, squared, source, amounts, near_x) = refs[:10]
    if step == 3:
        older_q, old_lap, gathered, sigma = refs[10:14]
    out = refs[-1]
    core = lax.axis_index("core")
    rows = pl.ds(pl.multiple_of(core * (CX - OV), OV), OV)
    weight = amounts[step, :1, :]
    columns = near_x[core]
    for pair in range(CY // 2):
        extra_p = halo_part(near, near, 0, columns, pair)
        extra_q = halo_part(near, near, 1, columns, pair)
        for side in range(2):
            y = 2 * pair + side
            lanes = slice(side * CZ, side * CZ + CZ)
            sq = squared[y, rows, :]
            spot = y * OV
            lap = laps[spot : spot + OV] + extra_p[:OV, lanes]
            spot += CY * OV
            lap_adj = laps[spot : spot + OV] + extra_q[:OV, lanes]
            edge_p, edge_q = p[y, rows, :], q[y, rows, :]
            next_p = 2.0 * edge_p - p_before[y, rows, :] + sq * lap + source[y, rows, :] * weight
            next_q = 2.0 * edge_q - q_before[y, rows, :] + sq * lap_adj
            if step == 1:
                sets = (edge_p, edge_q, next_p, next_q)
            else:
                twice = 2.0 * sigma[y, rows, :]
                old = old_lap[y, rows, :]
                known = gathered[y, rows, :] + older_q[y, rows, :] * lap + next_q * old
                sets = (edge_p, edge_q, next_p, twice * known, twice * sq * old)
            for k, value in enumerate(sets):
                spot = (k * CY + y) * OV
                out[spot : spot + OV] = value


def edge_interior(v, edge_x, own_z, first, out, field):
    strips = []
    for j in range(CY // 2):
        one, two = 2 * j, 2 * j + 1
        high1, low1 = split(v[one])
        high2, low2 = split(v[two])
        x = dot(edge_x, cat([cat([high1, high2], 1), cat([low1, low2], 1)], 0))
        x = x[:OV] + x[OV:]
        strips += [x[:, :CZ], x[:, CZ:]]
    rows = pl.ds(first, OV)
    edge = [v[y, rows, :] for y in range(CY)]
    high, low = split(cat(edge, 0))
    z = dot(cat([high, low], 1), own_z[...])
    z = z[:, :CZ] + z[:, CZ:]
    for y in range(CY):
        beside = edge[(y - 1) % CY] + edge[(y + 1) % CY]
        spot = (field * CY + y) * OV
        out[spot : spot + OV] = strips[y] + z[y * OV : y * OV + OV] + beside


def edge_inside(p, q, edge_x, own_z, out):
    core = lax.axis_index("core")
    first = pl.multiple_of(core * (CX - OV), OV)
    edge_interior(p, edge_x[core], own_z, first, out, 0)
    edge_interior(q, edge_x[core], own_z, first, out, 1)


def inside(p, q, own_x, own_z, lap_p, lap_q):
    interior(p, own_x, own_z, lap_p)
    interior(q, own_x, own_z, lap_q)


def inside_one(p, own_x, own_z, lap_p):
    interior(p, own_x, own_z, lap_p)


def shrink(image, image_far, shrink_x, shrink_far, shrink_z, own):
    core = lax.axis_index("core")
    rows_x = shrink_x[core]
    rows_far = shrink_far[core]
    narrow = [None] * CYC
    weights = taps()
    for pair in range(CY // 2):
        high, low = split(cat([image[2 * pair], image[2 * pair + 1]], 1))
        both = dot(rows_x, cat([high, low], 0))
        spots = [slice(y * OV, y * OV + OV) for y in (2 * pair, 2 * pair + 1)]
        high, low = split(cat([image_far[spots[0]], image_far[spots[1]]], 1))
        both = both + dot(rows_far, cat([high, low], 0))
        for side in range(2):
            part = both[:, side * CZ : side * CZ + CZ]
            for j, w in weights[2 * pair + side]:
                term = part * w
                narrow[j] = term if narrow[j] is None else narrow[j] + term
    pieces = []
    for pair in range(CYC // 2):
        parts = []
        for j in (2 * pair, 2 * pair + 1):
            parts += list(split(narrow[j]))
        pieces.append(dot(cat(parts, 1), shrink_z[...]) * UNIT)
    own[...] = cat(pieces, 1)


def fold(value):
    rows = value[0:8]
    for r in range(1, value.shape[0] // 8):
        rows = rows + value[8 * r : 8 * r + 8]
    folded = rows[:, :128]
    for c in range(1, 4):
        folded = folded + rows[:, 128 * c : 128 * c + 128]
    return folded


def squares(a, b, total, near):
    core = lax.axis_index("core")
    total[...] = a[...] + b[...]
    first, last = grid_ends()
    total[CXC + 4 : CXC + 6] = jnp.where(first | last, 0.0, total[CXC + 4 : CXC + 6])
    row = lax.broadcasted_iota(jnp.int32, (CXC, CYC * CZC), 0)
    start = (1 - core) * (CXC - 2)
    value = jnp.where((row >= start) & (row < start + 2), 0.0, total[:CXC])
    for r in range(4):
        for part in range(4):
            lanes = slice(part * 128, part * 128 + 128)
            spot = r * 4 + part
            near[spot : spot + 1] = total[CXC + r : CXC + r + 1, lanes]
    near[16:24] = fold(value * value)


def pair_up(total, mine, other, out, squared):
    core = lax.axis_index("core")
    out[...] = total[...]
    edge = mine[0:16] + other[0:16]
    for r in range(4):
        for part in range(4):
            lanes = slice(part * 128, part * 128 + 128)
            spot = r * 4 + part
            out[CXC + r : CXC + r + 1, lanes] = edge[spot : spot + 1]
    out[0:2] = jnp.where(core == 0, out[0:2], out[CXC + 2 : CXC + 4])
    out[CXC - 2 : CXC] = jnp.where(core == 0, out[CXC : CXC + 2], out[CXC - 2 : CXC])
    edge = edge * edge
    squared[...] = (mine[16:24] + other[16:24]) + (edge[0:8] + edge[8:16])


def last_fields(near, far, p, p_before, lap_p, source, amounts, halo_x, lap_out, base):
    core = lax.axis_index("core")
    columns = halo_x[core]
    weight = amounts[STEPS, :1, :]
    for pair in range(CY // 2):
        extra = halo_part(near, far, 0, columns, pair)
        for side in range(2):
            y = 2 * pair + side
            lap_out[y] = lap_p[y] + extra[:, side * CZ : side * CZ + CZ]
            base[y] = 2.0 * p[y] - p_before[y] + source[y] * weight


def add_four(own, one, two, three, out):
    out[...] = (own[...] + one[...]) + (two[...] + three[...])


def spread(total, sigma, lap, base, grow_z, grow_new, zeroth, first, second):
    core = lax.axis_index("core")

    def write(y, fine):
        change = fine * UNIT
        old, curve = sigma[y], lap[y]
        scaled = change * curve
        rows = pl.ds(y, CX, stride=CY)
        zeroth[rows, :] = base[y] + old * old * curve
        first[rows, :] = -2.0 * old * scaled
        second[rows, :] = change * scaled

    grow(total[...], grow_z, grow_new[core], write)


def widen(a, b, out):
    value = a[...] + b[...]
    for k in range(out.shape[0]):
        out[k] = value


def finish(count, parts, total, zeroth, first, second, direction, p_last, held, sems):
    value = parts[0]
    for k in range(1, parts.shape[0]):
        value = value + parts[k]
    value = jnp.sum(jnp.sum(value, axis=0, keepdims=True), axis=1, keepdims=True)
    inverse = 1.0 / jnp.sqrt(value * (1.0 / count) + EPSILON)
    rate = LEARN * inverse
    size = CX * CY // sems.shape[0]
    copies = []
    for c in range(sems.shape[0]):
        rows = slice(c * size, c * size + size)
        held[rows] = zeroth[rows] + rate * (first[rows] + rate * second[rows])
        copies.append(pltpu.make_async_copy(held.at[rows], p_last.at[rows], sems.at[c]))
        copies[-1].start(priority=c % 2)
    direction[...] = total[:CXC] * inverse
    for copy in copies:
        copy.wait()


VM = pl.BlockSpec(memory_space=pltpu.VMEM)
SM = pl.BlockSpec(memory_space=pltpu.SMEM)
FIELD = jax.ShapeDtypeStruct((CY, CX, CZ), F32)
PARAMS = pltpu.CompilerParams(vmem_limit_bytes=6 * 2**20)


def rows_of(count, lanes=128):
    return jax.ShapeDtypeStruct((count, lanes), F32)


def call(body, outs, *args, smem=0, scratch=(), flops=0, name=None, held=(), in_specs=None, out_specs=None):
    size = sum(int(np.prod(a.shape)) * a.dtype.itemsize for a in args)
    count = len(args)

    def run(*refs):
        body(*refs[:count], *refs[count + len(held) :])

    return pl.pallas_call(
        run,
        out_shape=outs,
        in_specs=([SM] * smem + [VM] * (count - smem) if in_specs is None else in_specs)
        + [pl.BlockSpec(memory_space=pl.ANY)] * len(held),
        out_specs=jax.tree.map(lambda _: VM, outs) if out_specs is None else out_specs,
        scratch_shapes=list(scratch),
        compiler_params=PARAMS,
        cost_estimate=pl.CostEstimate(flops=flops, bytes_accessed=size, transcendentals=0),
        name=name,
    )(*args, *held)


def xor_swap(x, axis, mask):
    count = lax.axis_size(axis)
    if mask >= count:
        return jnp.zeros_like(x)
    return lax.ppermute(x, axis, [(i, i ^ mask) for i in range(count)])


def far_swap(x):
    count = lax.axis_size(TILE)
    pairs = [(i, i + 1) for i in range(1, count - 1, 2)]
    return lax.ppermute(x, TILE, pairs + [(b, a) for a, b in pairs])


def on_device(p_now, p_prev, adj_now, adj_next, coef_old, signs, elem_index, wavelet):
    const = {name: jnp.asarray(value) for name, value in constants().items()}
    own_x, own_z, halo_x = const["own_x"], const["own_z"], const["halo_x"]
    flat = lambda a: a.reshape(CX * CY, CZ)
    p_now, p_prev, adj_now, adj_next = map(flat, (p_now, p_prev, adj_now, adj_next))

    half, edge = rows_of(CY * OV), rows_of(2 * CY * OV)
    sources = [pltpu.with_memory_space_constraint(a, pltpu.HBM) for a in (p_now, adj_now, coef_old)]

    blocks = [pltpu.VMEM((OV * CY, CZ), F32)] * 2 + [pltpu.VMEM((8, CYC * CZC), F32)]
    far, near = call(
        first_edges, (rows_of(2 * CY * OV + 24), rows_of(2 * CY * OV + 8)), *sources,
        in_specs=[pl.BlockSpec(memory_space=pltpu.HBM)] * 3,
        scratch=blocks * 2 + [pltpu.SemaphoreType.DMA((6,))],
        name="first_edges",
    )
    far, near = far_swap(far), xor_swap(near, "core", 1)

    wide = jax.ShapeDtypeStruct((CY, CX + OV, CZ), F32)
    later = [own_x, own_z, p_prev, adj_next, coef_old, const["grow_own"]]
    later.append(const["grow_z"])
    p, q, p_before, q_before, lap_p, lap_q, source, amounts, sigma_own = call(
        prepare,
        (FIELD,) * 7 + (jax.ShapeDtypeStruct((STEPS + 1, 8, CZ), F32), wide),
        signs[0], elem_index, wavelet, p_now, adj_now,
        *(pltpu.with_memory_space_constraint(a, pltpu.HBM) for a in later),
        flops=10**9, name="prepare", held=(halo_x,),
        in_specs=[SM] * 3 + [VM] * 2 + [pl.BlockSpec(memory_space=pltpu.HBM)] * len(later),
        scratch=[pltpu.VMEM(a.shape, a.dtype) for a in later]
        + [pltpu.SemaphoreType.DMA((len(later),))],
    )
    sigma, squared, beyond = call(
        speed, (FIELD, FIELD, half), sigma_own, near, far, const["grow_z"], const["grow_rest"],
        scratch=[pltpu.VMEM((8, CYC * CZC), F32)], flops=10**8, name="speed",
    )

    laps, qs = [], [q]
    gathered = None
    for step in range(STEPS):
        args = [near, far, p, p_before, q, q_before, lap_p, lap_q, squared, source, amounts, halo_x]
        body = functools.partial(advance, step)
        name = f"advance_{step}"
        if step == 0:
            outs = (FIELD, FIELD, edge, FIELD)
        elif step == 1:
            args += [sent, beyond, const["cross_x"]]
            outs = (FIELD, FIELD, edge, edge, FIELD)
            older_far = far
        elif step == 2:
            args.append(laps[1])
            outs = (FIELD, FIELD, edge, FIELD)
        else:
            args += [sent, beyond, const["cross_x"], laps[0], qs[1], gathered, sigma, older_far]
            outs = (FIELD, half, half, FIELD, half)
        result = call(body, outs, *args, flops=10**8, name=name)
        if step == 3:
            p_new, near, far, image, image_far = result
            p, p_before = p_new, p
            continue
        p_new, q_new, *edges, other = result
        if step < 2:
            laps.append(other)
        else:
            gathered = other
        p, p_before = p_new, p
        q, q_before = q_new, q
        qs.append(q)
        near = xor_swap(edges[0], "core", 1)
        if step == 1:
            lap_p, lap_q = call(
                inside, (FIELD, FIELD), p, q, own_x, own_z, flops=10**9, name="inside_1"
            )
            far = edges[1]
            continue
        edge_laps = call(
            edge_inside, edge, p, q, const["edge_x"], own_z, flops=10**8, name=f"edge_inside_{step}"
        )
        args = [near, p, p_before, q, q_before, edge_laps, squared, source, amounts]
        args.append(const["near_x"])
        if step == 2:
            args += [qs[1], laps[0], gathered, sigma]
        sent = call(
            functools.partial(early, step + 1), rows_of((4 if step == 0 else 5) * CY * OV),
            *args, flops=10**7, name=f"early_{step + 1}",
        )
        far = far_swap(sent)
        lap_p, lap_q = call(
            inside, (FIELD, FIELD), p, q, own_x, own_z, flops=10**9, name=f"inside_{step}",
            held=(sent,),
        )

    partial = call(
        shrink, rows_of(ROWS, CYC * CZC),
        image, image_far, const["shrink_x"], const["shrink_far"], const["shrink_z"],
        flops=10**8, name="shrink",
    )
    two, three, one = (xor_swap(partial, "y", m) for m in (2, 3, 1))
    near = xor_swap(near, "core", 1)
    lap_p = call(inside_one, FIELD, p, own_x, own_z, flops=5 * 10**8, name="inside_last")
    lap_p, base = call(
        last_fields, (FIELD, FIELD), near, far, p, p_before, lap_p, source, amounts, halo_x,
        flops=10**8, name="last_fields",
    )
    held = (lap_p, base)
    partial = call(
        add_four, rows_of(ROWS, CYC * CZC), partial, one, two, three, name="add_four", held=held
    )
    total, mine = call(
        squares, (rows_of(ROWS, CYC * CZC), rows_of(24)), partial, xor_swap(partial, "xl", 1),
        name="squares", held=held,
    )
    total, squared_sum = call(
        pair_up, (rows_of(ROWS, CYC * CZC), rows_of(8)), total, mine, xor_swap(mine, "core", 1),
        name="pair_up", held=held,
    )
    terms = call(
        spread, (rows_of(CX * CY),) * 3, total, sigma, lap_p, base, const["grow_z"], const["grow_new"],
        flops=10**8, name="spread",
    )
    deep = lax.axis_size("z")
    copies = call(
        widen, jax.ShapeDtypeStruct((deep, 8, 128), F32),
        squared_sum, xor_swap(squared_sum, "xh", 1), name="widen", held=terms,
    )
    parts = lax.all_to_all(copies, "z", split_axis=0, concat_axis=0, tiled=True)
    count = float(lax.axis_size(TILE) * CXC * CYC * CZC)
    direction, p_last = call(
        functools.partial(finish, count),
        (rows_of(CXC, CYC * CZC), pltpu.HBM((CX * CY, CZ), F32)),
        parts, total, *terms, name="finish",
        scratch=[pltpu.VMEM((CX * CY, CZ), F32), pltpu.SemaphoreType.DMA((4,))],
        out_specs=(VM, pl.BlockSpec(memory_space=pltpu.HBM)),
    )
    return direction, p_last.reshape(1, CX, CY, CZ)


def solution(mesh):
    shots, tiles = mesh.shape["shot"], mesh.shape["tile"]
    fine = Mesh(
        mesh.devices.reshape(shots // 2, 2, 2, tiles // 4, 2), ("y", "xl", "xh", "z", "core")
    )
    placed = (
        P(SHOT, TILE, None, None),
        P(SHOT, TILE, None, None),
        P(SHOT, TILE, None, None),
        P(SHOT, TILE, None, None),
        P(TILE, None),
        P(SHOT, TILE),
        P(TILE),
        P(),
    )
    return jax.shard_map(
        on_device,
        mesh=fine,
        in_specs=placed,
        out_specs=(P(TILE, None), P(SHOT, TILE, None, None)),
        check_vma=False,
    )
```

```python
import functools

import jax
import jax.numpy as jnp
import ml_dtypes
import numpy as np
from jax import lax
from jax.experimental import pallas as pl
from jax.experimental.pallas import tpu as pltpu
from jax.sharding import Mesh
from jax.sharding import PartitionSpec as P

CX = 128
CZ = 128
CY = 16
OV = 8
STEPS = 4
ELEMS = 64
CXC = 64
CYC = 8
CZC = 64
ROWS = 72
LEARN = 0.02
EPSILON = 1e-06
BF = jnp.bfloat16
F32 = jnp.float32
SHOT = ("y", "xl")
TILE = ("xh", "z", "core")


def spectral_second(length):
    index = np.arange(length)
    number = np.minimum(index, length - index) * (2.0 * np.pi / length)
    phase = (index[:, None, None] - index[None, :, None]) * index[None, None, :] % length
    return -np.sum(number**2 * np.cos(2.0 * np.pi / length * phase), axis=2) / length


def spline_units(offset):
    mag = np.abs(offset)
    inner = 2.0 / 3.0 - mag**2 + 0.5 * mag**3
    outer = (2.0 - mag) ** 3 / 6.0
    return np.round(384.0 * np.where(mag < 1.0, inner, np.where(mag < 2.0, outer, 0.0)))


def halves(matrix):
    high = matrix.astype(np.float32).astype(ml_dtypes.bfloat16)
    low = (matrix - high.astype(np.float64)).astype(np.float32).astype(ml_dtypes.bfloat16)
    return high, low


def narrow_band(matrix):
    high, low = halves(np.pad(matrix, ((0, OV), (0, OV))))
    return np.concatenate([high, high, low], axis=1)


@functools.cache
def constants():
    out = {}
    second_x = spectral_second(CX + 2 * OV)[OV : OV + CX]
    ramp = np.sin(0.5 * np.pi * (np.arange(OV) + 0.5) / OV) ** 2
    left = second_x[:, :OV] * ramp[None, :]
    right = second_x[:, OV + CX :] * ramp[None, ::-1]
    high, low = halves(second_x[:, OV : OV + CX])
    out["own_x"] = np.block([[high, high], [low, low]])
    sides = []
    for pair in ((right, left), (left, right)):
        high, low = halves(np.concatenate(pair, axis=1))
        sides.append(np.concatenate([high, high, low], axis=1))
    out["halo_x"] = np.stack(sides)
    edge = []
    for rows in (slice(0, OV), slice(CX - OV, CX)):
        high, low = halves(second_x[rows, OV : OV + CX])
        edge.append(np.block([[high, high], [low, low]]))
    out["edge_x"] = np.stack(edge)
    near_part, cross_part = [], []
    for core in range(2):
        rows = slice(0, OV) if core == 0 else slice(CX - OV, CX)
        near_part.append(narrow_band((right if core == 0 else left)[rows]))
        rows = slice(CX - OV, CX) if core == 0 else slice(0, OV)
        cross_part.append(narrow_band((right if core == 0 else left)[rows]))
    out["near_x"] = np.stack(near_part)
    out["cross_x"] = np.stack(cross_part)
    high, low = halves(spectral_second(CZ) - 2.0 * np.eye(CZ))
    out["own_z"] = np.block([[high, low], [high, low]])

    fine_z = np.arange(CZ)[:, None]
    coarse_z = np.arange(CZC)[None, :]
    weight_z = sum(
        spline_units((fine_z - 2 * coarse_z + image * CZ - 0.5) * 0.5) for image in range(-2, 3)
    )
    zero = np.zeros_like(weight_z.T)
    pair = np.block([[weight_z.T, zero], [zero, weight_z.T]])
    out["grow_z"] = np.concatenate([pair, pair], axis=0)
    zero = np.zeros_like(weight_z)
    out["shrink_z"] = np.block(
        [[weight_z, zero], [weight_z, zero], [zero, weight_z], [zero, weight_z]]
    )

    def column(coarse, start=0, count=CX):
        return spline_units((np.arange(start, start + count) - 2 * coarse - 0.5) * 0.5)

    own = np.stack([column(j) for j in range(CXC)], axis=1)
    lower = {j: column(j) for j in (-2, -1, 0, 1)}
    upper = {j: column(j) for j in (62, 63, 64, 65)}
    stack = lambda d: np.stack([d[j] for j in sorted(d)], axis=1)
    grow_own, grow_rest, grow_new, shrink, shrink_far = [], [], [], [], []
    blank = np.zeros((CX, 2))
    for core in range(2):
        near = upper if core == 0 else lower
        near_two, far_six = ((64, 65), range(-6, 0)) if core == 0 else ((-2, -1), range(64, 70))
        far_two = (-2, -1) if core == 0 else (64, 65)
        beyond = -OV if core == 0 else CX
        both = lambda j: np.concatenate([column(j), column(j, beyond, OV)])
        mine = np.stack([both(j) for j in range(CXC)], axis=1)
        rest = np.stack([both(j) for j in (*near_two, *far_six)], axis=1)
        inner = own.copy()
        inner[:, [62, 63] if core == 0 else [0, 1]] = 0.0
        outer = np.stack([column(j) for j in far_two], axis=1)
        new = np.concatenate([inner, stack(near), outer, blank], axis=1)
        every = np.concatenate([own, stack(near), outer, blank], axis=1).T
        past = np.zeros((ROWS, OV))
        for row, j in (*enumerate(range(CXC)), *zip((CXC + 4, CXC + 5), far_two)):
            past[row] = column(j, beyond, OV)
        grow_own.append(np.concatenate([mine, mine], axis=1))
        grow_rest.append(np.concatenate([rest, rest], axis=1))
        grow_new.append(np.concatenate([new, new], axis=1))
        shrink.append(np.concatenate([every, every], axis=1))
        shrink_far.append(np.concatenate([past, past], axis=1))
    out["shrink_far"] = np.stack(shrink_far)
    out["grow_own"] = np.stack(grow_own)
    out["grow_rest"] = np.stack(grow_rest)
    out["grow_new"] = np.stack(grow_new)
    out["shrink_x"] = np.stack(shrink)
    return {name: np.asarray(value).astype(ml_dtypes.bfloat16) for name, value in out.items()}


def taps():
    return [
        [
            (j, float(w))
            for j in range(CYC)
            for w in [
                sum(
                    spline_units(np.float64((i - 2 * j + image * CY - 0.5) * 0.5))
                    for image in range(-2, 3)
                )
            ]
            if w
        ]
        for i in range(CY)
    ]


def split(value):
    high = value.astype(BF)
    return high, (value - high.astype(F32)).astype(BF)


def dot(left, right):
    return jnp.dot(left, right, preferred_element_type=F32)


def cat(parts, axis):
    return jnp.concatenate(parts, axis=axis)


def interior(v, own_x, own_z, out):
    for j in range(CY // 2):
        one, two = 2 * j, 2 * j + 1
        high1, low1 = split(v[one])
        high2, low2 = split(v[two])
        x = dot(own_x[...], cat([cat([high1, high2], 1), cat([low1, low2], 1)], 0))
        z = dot(cat([cat([high1, low1], 1), cat([high2, low2], 1)], 0), own_z[...])
        x = x[:CX] + x[CX:]
        z = z[:, :CZ] + z[:, CZ:]
        beside = v[(one - 1) % CY] + v[two]
        out[one] = x[:, :CZ] + z[:CX] + beside
        beside = v[one] + v[(two + 1) % CY]
        out[two] = x[:, CZ:] + z[CX:] + beside


def halo_part(near, far, field, halo_x, pair):
    parts = []
    for y in (2 * pair, 2 * pair + 1):
        start = (field * CY + y) * OV
        high, low = split(cat([near[start : start + OV], far[start : start + OV]], 0))
        parts.append(cat([high, low, high], 0))
    return dot(halo_x, cat(parts, 1))


def edge_rows(v, core, near, field):
    row = pl.multiple_of((1 - core) * (CX - OV), OV)
    for y in range(CY):
        start = (field * CY + y) * OV
        near[start : start + OV] = v[y, pl.ds(row, OV), :]


def first_edges(p, q, coef, far, near, *scratch):
    core = lax.axis_index("core")
    sems = scratch[6]
    block = OV * CY
    ends, copies = (core, 1 - core), []
    for side, end in enumerate(ends):
        for k, (source, whole, size) in enumerate(
            ((p, CX * CY, block), (q, CX * CY, block), (coef, CXC, 8))
        ):
            start = pl.multiple_of(end * (whole - size), 8)
            at = 3 * side + k
            copies.append(
                pltpu.make_async_copy(source.at[pl.ds(start, size)], scratch[at], sems.at[at])
            )
    for copy in copies:
        copy.start()
    for side, (end, out, count) in enumerate(zip(ends, (far, near), (6, 2))):
        for field in range(2):
            copies[3 * side + field].wait()
            rows = scratch[3 * side + field]
            for y in range(CY):
                start = (field * CY + y) * OV
                out[start : start + OV] = rows[pl.ds(y, OV, stride=CY), :]
        copies[3 * side + 2].wait()
        rows = scratch[3 * side + 2]
        base = 2 * CY * OV
        for row in range(count):
            for part in range(4):
                lanes = slice(part * 128, part * 128 + 128)
                spot = base + row * 4 + part
                last = 8 - count + row
                out[spot : spot + 1] = jnp.where(
                    end == 0, rows[row : row + 1, lanes], rows[last : last + 1, lanes]
                )


def reorder(source, target):
    for y in range(CY):
        target[y] = source[pl.ds(y, CX, stride=CY), :]


def prepare(
    signs, index, wavelet, p_now, q_now,
    own_x_in, own_z_in, p_prev_in, q_prev_in, coef_in, grow_own_in, grow_z_in,
    p0, q0, p1, q1, lap_p, lap_q, source, amounts, sigma_own,
    own_x, own_z, p_prev, q_prev, coef, grow_own, grow_z, sems,
):
    copies = [
        pltpu.make_async_copy(far, near, sems.at[k])
        for k, (far, near) in enumerate(
            (
                (own_x_in, own_x),
                (own_z_in, own_z),
                (p_prev_in, p_prev),
                (q_prev_in, q_prev),
                (coef_in, coef),
                (grow_own_in, grow_own),
                (grow_z_in, grow_z),
            )
        )
    ]
    for copy in copies:
        copy.start()
    reorder(p_now, p0)
    reorder(q_now, q0)
    source[...] = jnp.zeros_like(source)
    lane = lax.broadcasted_iota(jnp.int32, (1, CZ), 1)

    def add(e, carry):
        spot = index[e]
        x, rest = spot // (CY * CZ), spot % (CY * CZ)
        y, z = rest // CZ, rest % CZ
        amount = (2 * signs[e] - 1).astype(F32)
        row = source[y, pl.ds(x, 1), :]
        source[y, pl.ds(x, 1), :] = row + jnp.where(lane == z, amount, 0.0)
        return carry

    lax.fori_loop(0, ELEMS, add, 0)
    for step in range(STEPS + 1):
        amounts[step] = jnp.full((8, CZ), wavelet[step], F32)
    copies[0].wait()
    copies[1].wait()
    interior(p0, own_x, own_z, lap_p)
    interior(q0, own_x, own_z, lap_q)
    copies[2].wait()
    reorder(p_prev, p1)
    copies[3].wait()
    reorder(q_prev, q1)
    for copy in copies[4:]:
        copy.wait()

    def write(y, fine):
        sigma_own[y] = fine

    grow(coef[...], grow_z, grow_own[lax.axis_index("core")], write)


def grow(coef, grow_z, grow_x, write):
    wide = []
    for pair in range(CYC // 2):
        high, low = split(coef[:, pair * 128 : pair * 128 + 128])
        both = dot(cat([high, low], 1), grow_z[...])
        wide += [both[:, :CZ], both[:, CZ:]]
    weights = taps()
    for pair in range(CY // 2):
        parts = []
        for y in (2 * pair, 2 * pair + 1):
            mixed = None
            for j, w in weights[y]:
                term = wide[j] * w
                mixed = term if mixed is None else mixed + term
            parts.append(mixed)
        high, low = split(cat(parts, 1))
        fine = dot(grow_x, cat([high, low], 0))
        write(2 * pair, fine[:, :CZ])
        write(2 * pair + 1, fine[:, CZ:])


UNIT = 1.0 / 384.0**3


def grid_ends():
    core = lax.axis_index("core")
    chip = lax.axis_index("xh") * lax.axis_size("z") + lax.axis_index("z")
    chips = lax.axis_size("xh") * lax.axis_size("z")
    return (core == 0) & (chip == 0), (core == 1) & (chip == chips - 1)


def speed(sigma_own, near, far, grow_z, grow_rest, sigma, squared, beyond, held):
    core = lax.axis_index("core")
    base = 2 * CY * OV
    for row in range(6):
        for part in range(4):
            lanes = slice(part * 128, part * 128 + 128)
            spot = base + row * 4 + part
            if row < 2:
                held[row : row + 1, lanes] = near[spot : spot + 1]
            held[2 + row : 3 + row, lanes] = far[spot : spot + 1]
    first, last = grid_ends()

    def write(y, fine):
        fine = (sigma_own[y] + fine) * UNIT
        sigma[y] = fine[:CX]
        squared[y] = fine[:CX] * fine[:CX]
        beyond[y * OV : y * OV + OV] = jnp.where(first | last, 0.0, fine[CX:])

    grow(held[...], grow_z, grow_rest[core], write)


def squared_at(beyond, spot):
    value = beyond[spot : spot + OV]
    return value * value


def advance(step, *refs):
    (near, far, p, p_before, q, q_before, lap_p, lap_q, squared, source, amounts, halo_x) = refs[:12]
    refs = refs[12:]
    core = lax.axis_index("core")
    columns = halo_x[core]
    weight = amounts[step, :1, :]
    if step in (1, 3):
        (sent, beyond, cross_x), refs = refs[:3], refs[3:]
        cross = cross_x[core]
    if step == 2:
        old_lap, refs = refs[0], refs[1:]
    if step == 3:
        (old_lap, older_q, gathered, sigma, older_far), refs = refs[:5], refs[5:]
    if step in (0, 2):
        (p_new, q_new, near_out), refs = refs[:3], refs[3:]
    elif step == 1:
        (p_new, q_new, near_out, far_out), refs = refs[:4], refs[4:]
    else:
        p_new, near_out, far_out, image, image_far = refs[:5]
    if step < 2:
        lap_out = refs[0]
    if step == 2:
        gathered = refs[0]
    for pair in range(CY // 2):
        extra_p = halo_part(near, far, 0, columns, pair)
        extra_q = halo_part(near, far, 1, columns, pair)
        for side in range(2):
            y = 2 * pair + side
            lanes = slice(side * CZ, side * CZ + CZ)
            lap = lap_p[y] + extra_p[:, lanes]
            lap_adj = lap_q[y] + extra_q[:, lanes]
            sq = squared[y]
            p_new[y] = 2.0 * p[y] - p_before[y] + sq * lap + source[y] * weight
            new_q = 2.0 * q[y] - q_before[y] + sq * lap_adj
            if step < 3:
                q_new[y] = new_q
            if step < 2:
                lap_out[y] = lap
            if step == 2:
                gathered[y] = q[y] * lap + new_q * old_lap[y]
            if step == 3:
                total = gathered[y] + older_q[y] * lap + new_q * old_lap[y]
                image[y] = 2.0 * sigma[y] * total
    edge_rows(p_new, core, near_out, 0)
    if step < 3:
        edge_rows(q_new, core, near_out, 1)
    if step == 1:
        size = CY * OV
        for pair in range(CY // 2):
            for field in range(2):
                extra = halo_part(sent, sent, field, cross, pair)
                for side in range(2):
                    spot = (2 * pair + side) * OV
                    known = far[(2 + field) * size + spot : (2 + field) * size + spot + OV]
                    far_out[field * size + spot : field * size + spot + OV] = (
                        known
                        + squared_at(beyond, spot) * extra[:OV, side * CZ : side * CZ + CZ]
                    )
    if step == 3:
        size = CY * OV
        for pair in range(CY // 2):
            extra_p = halo_part(sent, sent, 0, cross, pair)
            extra_q = halo_part(sent, sent, 1, cross, pair)
            for side in range(2):
                spot = (2 * pair + side) * OV
                lanes = slice(side * CZ, side * CZ + CZ)
                part_p, part_q = extra_p[:OV, lanes], extra_q[:OV, lanes]
                rows = lambda k: far[k * size + spot : k * size + spot + OV]
                far_out[spot : spot + OV] = rows(2) + squared_at(beyond, spot) * part_p
                near_q = older_far[size + spot : size + spot + OV]
                image_far[spot : spot + OV] = (
                    rows(3) + 2.0 * beyond[spot : spot + OV] * near_q * part_p + rows(4) * part_q
                )


def early(step, *refs):
    (near, p, p_before, q, q_before, laps, squared, source, amounts, near_x) = refs[:10]
    if step == 3:
        older_q, old_lap, gathered, sigma = refs[10:14]
    out = refs[-1]
    core = lax.axis_index("core")
    rows = pl.ds(pl.multiple_of(core * (CX - OV), OV), OV)
    weight = amounts[step, :1, :]
    columns = near_x[core]
    for pair in range(CY // 2):
        extra_p = halo_part(near, near, 0, columns, pair)
        extra_q = halo_part(near, near, 1, columns, pair)
        for side in range(2):
            y = 2 * pair + side
            lanes = slice(side * CZ, side * CZ + CZ)
            sq = squared[y, rows, :]
            spot = y * OV
            lap = laps[spot : spot + OV] + extra_p[:OV, lanes]
            spot += CY * OV
            lap_adj = laps[spot : spot + OV] + extra_q[:OV, lanes]
            edge_p, edge_q = p[y, rows, :], q[y, rows, :]
            next_p = 2.0 * edge_p - p_before[y, rows, :] + sq * lap + source[y, rows, :] * weight
            next_q = 2.0 * edge_q - q_before[y, rows, :] + sq * lap_adj
            if step == 1:
                sets = (edge_p, edge_q, next_p, next_q)
            else:
                twice = 2.0 * sigma[y, rows, :]
                old = old_lap[y, rows, :]
                known = gathered[y, rows, :] + older_q[y, rows, :] * lap + next_q * old
                sets = (edge_p, edge_q, next_p, twice * known, twice * sq * old)
            for k, value in enumerate(sets):
                spot = (k * CY + y) * OV
                out[spot : spot + OV] = value


def edge_interior(v, edge_x, own_z, first, out, field):
    strips = []
    for j in range(CY // 2):
        one, two = 2 * j, 2 * j + 1
        high1, low1 = split(v[one])
        high2, low2 = split(v[two])
        x = dot(edge_x, cat([cat([high1, high2], 1), cat([low1, low2], 1)], 0))
        x = x[:OV] + x[OV:]
        strips += [x[:, :CZ], x[:, CZ:]]
    rows = pl.ds(first, OV)
    edge = [v[y, rows, :] for y in range(CY)]
    high, low = split(cat(edge, 0))
    z = dot(cat([high, low], 1), own_z[...])
    z = z[:, :CZ] + z[:, CZ:]
    for y in range(CY):
        beside = edge[(y - 1) % CY] + edge[(y + 1) % CY]
        spot = (field * CY + y) * OV
        out[spot : spot + OV] = strips[y] + z[y * OV : y * OV + OV] + beside


def edge_inside(p, q, edge_x, own_z, out):
    core = lax.axis_index("core")
    first = pl.multiple_of(core * (CX - OV), OV)
    edge_interior(p, edge_x[core], own_z, first, out, 0)
    edge_interior(q, edge_x[core], own_z, first, out, 1)


def inside(p, q, own_x, own_z, lap_p, lap_q):
    interior(p, own_x, own_z, lap_p)
    interior(q, own_x, own_z, lap_q)


def inside_one(p, own_x, own_z, lap_p):
    interior(p, own_x, own_z, lap_p)


def shrink(image, image_far, shrink_x, shrink_far, shrink_z, own):
    core = lax.axis_index("core")
    rows_x = shrink_x[core]
    rows_far = shrink_far[core]
    narrow = [None] * CYC
    weights = taps()
    for pair in range(CY // 2):
        high, low = split(cat([image[2 * pair], image[2 * pair + 1]], 1))
        both = dot(rows_x, cat([high, low], 0))
        spots = [slice(y * OV, y * OV + OV) for y in (2 * pair, 2 * pair + 1)]
        high, low = split(cat([image_far[spots[0]], image_far[spots[1]]], 1))
        both = both + dot(rows_far, cat([high, low], 0))
        for side in range(2):
            part = both[:, side * CZ : side * CZ + CZ]
            for j, w in weights[2 * pair + side]:
                term = part * w
                narrow[j] = term if narrow[j] is None else narrow[j] + term
    pieces = []
    for pair in range(CYC // 2):
        parts = []
        for j in (2 * pair, 2 * pair + 1):
            parts += list(split(narrow[j]))
        pieces.append(dot(cat(parts, 1), shrink_z[...]) * UNIT)
    own[...] = cat(pieces, 1)


def fold(value):
    rows = value[0:8]
    for r in range(1, value.shape[0] // 8):
        rows = rows + value[8 * r : 8 * r + 8]
    folded = rows[:, :128]
    for c in range(1, 4):
        folded = folded + rows[:, 128 * c : 128 * c + 128]
    return folded


def squares(a, b, total, near):
    core = lax.axis_index("core")
    total[...] = a[...] + b[...]
    first, last = grid_ends()
    total[CXC + 4 : CXC + 6] = jnp.where(first | last, 0.0, total[CXC + 4 : CXC + 6])
    row = lax.broadcasted_iota(jnp.int32, (CXC, CYC * CZC), 0)
    start = (1 - core) * (CXC - 2)
    value = jnp.where((row >= start) & (row < start + 2), 0.0, total[:CXC])
    for r in range(4):
        for part in range(4):
            lanes = slice(part * 128, part * 128 + 128)
            spot = r * 4 + part
            near[spot : spot + 1] = total[CXC + r : CXC + r + 1, lanes]
    near[16:24] = fold(value * value)


def pair_up(total, mine, other, out, squared):
    core = lax.axis_index("core")
    out[...] = total[...]
    edge = mine[0:16] + other[0:16]
    for r in range(4):
        for part in range(4):
            lanes = slice(part * 128, part * 128 + 128)
            spot = r * 4 + part
            out[CXC + r : CXC + r + 1, lanes] = edge[spot : spot + 1]
    out[0:2] = jnp.where(core == 0, out[0:2], out[CXC + 2 : CXC + 4])
    out[CXC - 2 : CXC] = jnp.where(core == 0, out[CXC : CXC + 2], out[CXC - 2 : CXC])
    edge = edge * edge
    squared[...] = (mine[16:24] + other[16:24]) + (edge[0:8] + edge[8:16])


def last_fields(near, far, p, p_before, lap_p, source, amounts, halo_x, lap_out, base):
    core = lax.axis_index("core")
    columns = halo_x[core]
    weight = amounts[STEPS, :1, :]
    for pair in range(CY // 2):
        extra = halo_part(near, far, 0, columns, pair)
        for side in range(2):
            y = 2 * pair + side
            lap_out[y] = lap_p[y] + extra[:, side * CZ : side * CZ + CZ]
            base[y] = 2.0 * p[y] - p_before[y] + source[y] * weight


def add_four(own, one, three, two, out):
    out[...] = (own[...] + one[...]) + (two[...] + three[...])


def spread(total, sigma, lap, base, grow_z, grow_new, zeroth, first, second):
    core = lax.axis_index("core")

    def write(y, fine):
        change = fine * UNIT
        old, curve = sigma[y], lap[y]
        scaled = change * curve
        rows = pl.ds(y, CX, stride=CY)
        zeroth[rows, :] = base[y] + old * old * curve
        first[rows, :] = -2.0 * old * scaled
        second[rows, :] = change * scaled

    grow(total[...], grow_z, grow_new[core], write)


def widen(a, b, out):
    value = jnp.sum(a[...] + b[...], axis=0, keepdims=True)
    out[...] = jnp.broadcast_to(value, out.shape)


def finish(count, parts, total, zeroth, first, second, direction, p_last, held, sems):
    value = jnp.sum(jnp.sum(parts[...], axis=0, keepdims=True), axis=1, keepdims=True)
    inverse = 1.0 / jnp.sqrt(value * (1.0 / count) + EPSILON)
    rate = LEARN * inverse
    size = CX * CY // sems.shape[0]
    copies = []
    for c in range(sems.shape[0]):
        rows = slice(c * size, c * size + size)
        held[rows] = zeroth[rows] + rate * (first[rows] + rate * second[rows])
        copies.append(pltpu.make_async_copy(held.at[rows], p_last.at[rows], sems.at[c]))
        copies[-1].start(priority=c % 2)
    direction[...] = total[:CXC] * inverse
    for copy in copies:
        copy.wait()


VM = pl.BlockSpec(memory_space=pltpu.VMEM)
SM = pl.BlockSpec(memory_space=pltpu.SMEM)
FIELD = jax.ShapeDtypeStruct((CY, CX, CZ), F32)
PARAMS = pltpu.CompilerParams(vmem_limit_bytes=6 * 2**20)


def rows_of(count, lanes=128):
    return jax.ShapeDtypeStruct((count, lanes), F32)


def call(body, outs, *args, smem=0, scratch=(), flops=0, name=None, held=(), in_specs=None, out_specs=None):
    size = sum(int(np.prod(a.shape)) * a.dtype.itemsize for a in args)
    count = len(args)

    def run(*refs):
        body(*refs[:count], *refs[count + len(held) :])

    return pl.pallas_call(
        run,
        out_shape=outs,
        in_specs=([SM] * smem + [VM] * (count - smem) if in_specs is None else in_specs)
        + [pl.BlockSpec(memory_space=pl.ANY)] * len(held),
        out_specs=jax.tree.map(lambda _: VM, outs) if out_specs is None else out_specs,
        scratch_shapes=list(scratch),
        compiler_params=PARAMS,
        cost_estimate=pl.CostEstimate(flops=flops, bytes_accessed=size, transcendentals=0),
        name=name,
    )(*args, *held)


def xor_swap(x, axis, mask):
    count = lax.axis_size(axis)
    if mask >= count:
        return jnp.zeros_like(x)
    return lax.ppermute(x, axis, [(i, i ^ mask) for i in range(count)])


def far_swap(x):
    count = lax.axis_size(TILE)
    pairs = [(i, i + 1) for i in range(1, count - 1, 2)]
    return lax.ppermute(x, TILE, pairs + [(b, a) for a, b in pairs])


def on_device(p_now, p_prev, adj_now, adj_next, coef_old, signs, elem_index, wavelet):
    const = {name: jnp.asarray(value) for name, value in constants().items()}
    own_x, own_z, halo_x = const["own_x"], const["own_z"], const["halo_x"]
    flat = lambda a: a.reshape(CX * CY, CZ)
    p_now, p_prev, adj_now, adj_next = map(flat, (p_now, p_prev, adj_now, adj_next))

    half, edge = rows_of(CY * OV), rows_of(2 * CY * OV)
    sources = [pltpu.with_memory_space_constraint(a, pltpu.HBM) for a in (p_now, adj_now, coef_old)]

    blocks = [pltpu.VMEM((OV * CY, CZ), F32)] * 2 + [pltpu.VMEM((8, CYC * CZC), F32)]
    far, near = call(
        first_edges, (rows_of(2 * CY * OV + 24), rows_of(2 * CY * OV + 8)), *sources,
        in_specs=[pl.BlockSpec(memory_space=pltpu.HBM)] * 3,
        scratch=blocks * 2 + [pltpu.SemaphoreType.DMA((6,))],
        name="first_edges",
    )
    far, near = far_swap(far), xor_swap(near, "core", 1)

    wide = jax.ShapeDtypeStruct((CY, CX + OV, CZ), F32)
    later = [own_x, own_z, p_prev, adj_next, coef_old, const["grow_own"]]
    later.append(const["grow_z"])
    p, q, p_before, q_before, lap_p, lap_q, source, amounts, sigma_own = call(
        prepare,
        (FIELD,) * 7 + (jax.ShapeDtypeStruct((STEPS + 1, 8, CZ), F32), wide),
        signs[0], elem_index, wavelet, p_now, adj_now,
        *(pltpu.with_memory_space_constraint(a, pltpu.HBM) for a in later),
        flops=10**9, name="prepare", held=(halo_x,),
        in_specs=[SM] * 3 + [VM] * 2 + [pl.BlockSpec(memory_space=pltpu.HBM)] * len(later),
        scratch=[pltpu.VMEM(a.shape, a.dtype) for a in later]
        + [pltpu.SemaphoreType.DMA((len(later),))],
    )
    sigma, squared, beyond = call(
        speed, (FIELD, FIELD, half), sigma_own, near, far, const["grow_z"], const["grow_rest"],
        scratch=[pltpu.VMEM((8, CYC * CZC), F32)], flops=10**8, name="speed",
    )

    laps, qs = [], [q]
    gathered = None
    for step in range(STEPS):
        args = [near, far, p, p_before, q, q_before, lap_p, lap_q, squared, source, amounts, halo_x]
        body = functools.partial(advance, step)
        name = f"advance_{step}"
        if step == 0:
            outs = (FIELD, FIELD, edge, FIELD)
        elif step == 1:
            args += [sent, beyond, const["cross_x"]]
            outs = (FIELD, FIELD, edge, edge, FIELD)
            older_far = far
        elif step == 2:
            args.append(laps[1])
            outs = (FIELD, FIELD, edge, FIELD)
        else:
            args += [sent, beyond, const["cross_x"], laps[0], qs[1], gathered, sigma, older_far]
            outs = (FIELD, half, half, FIELD, half)
        result = call(body, outs, *args, flops=10**8, name=name)
        if step == 3:
            p_new, near, far, image, image_far = result
            p, p_before = p_new, p
            continue
        p_new, q_new, *edges, other = result
        if step < 2:
            laps.append(other)
        else:
            gathered = other
        p, p_before = p_new, p
        q, q_before = q_new, q
        qs.append(q)
        near = xor_swap(edges[0], "core", 1)
        if step == 1:
            lap_p, lap_q = call(
                inside, (FIELD, FIELD), p, q, own_x, own_z, flops=10**9, name="inside_1"
            )
            far = edges[1]
            continue
        edge_laps = call(
            edge_inside, edge, p, q, const["edge_x"], own_z, flops=10**8, name=f"edge_inside_{step}"
        )
        args = [near, p, p_before, q, q_before, edge_laps, squared, source, amounts]
        args.append(const["near_x"])
        if step == 2:
            args += [qs[1], laps[0], gathered, sigma]
        sent = call(
            functools.partial(early, step + 1), rows_of((4 if step == 0 else 5) * CY * OV),
            *args, flops=10**7, name=f"early_{step + 1}",
        )
        far = far_swap(sent)
        lap_p, lap_q = call(
            inside, (FIELD, FIELD), p, q, own_x, own_z, flops=10**9, name=f"inside_{step}",
            held=(sent,),
        )

    partial = call(
        shrink, rows_of(ROWS, CYC * CZC),
        image, image_far, const["shrink_x"], const["shrink_far"], const["shrink_z"],
        flops=10**8, name="shrink",
    )
    two, three, one = (xor_swap(partial, "y", m) for m in (2, 3, 1))
    near = xor_swap(near, "core", 1)
    lap_p = call(inside_one, FIELD, p, own_x, own_z, flops=5 * 10**8, name="inside_last")
    lap_p, base = call(
        last_fields, (FIELD, FIELD), near, far, p, p_before, lap_p, source, amounts, halo_x,
        flops=10**8, name="last_fields",
    )
    held = (lap_p, base)
    partial = call(
        add_four, rows_of(ROWS, CYC * CZC), partial, one, three, two, name="add_four", held=held
    )
    total, mine = call(
        squares, (rows_of(ROWS, CYC * CZC), rows_of(24)), partial, xor_swap(partial, "xl", 1),
        name="squares", held=held,
    )
    total, squared_sum = call(
        pair_up, (rows_of(ROWS, CYC * CZC), rows_of(8)), total, mine, xor_swap(mine, "core", 1),
        name="pair_up", held=held,
    )
    terms = call(
        spread, (rows_of(CX * CY),) * 3, total, sigma, lap_p, base, const["grow_z"], const["grow_new"],
        flops=10**8, name="spread",
    )
    deep = lax.axis_size("z")
    copies = call(
        widen, rows_of(deep),
        squared_sum, xor_swap(squared_sum, "xh", 1), name="widen", held=terms,
    )
    parts = lax.all_to_all(copies, "z", split_axis=0, concat_axis=0, tiled=True)
    count = float(lax.axis_size(TILE) * CXC * CYC * CZC)
    direction, p_last = call(
        functools.partial(finish, count),
        (rows_of(CXC, CYC * CZC), pltpu.HBM((CX * CY, CZ), F32)),
        parts, total, *terms, name="finish",
        scratch=[pltpu.VMEM((CX * CY, CZ), F32), pltpu.SemaphoreType.DMA((4,))],
        out_specs=(VM, pl.BlockSpec(memory_space=pltpu.HBM)),
    )
    return direction, p_last.reshape(1, CX, CY, CZ)


def solution(mesh):
    shots, tiles = mesh.shape["shot"], mesh.shape["tile"]
    fine = Mesh(
        mesh.devices.reshape(shots // 2, 2, 2, tiles // 4, 2), ("y", "xl", "xh", "z", "core")
    )
    placed = (
        P(SHOT, TILE, None, None),
        P(SHOT, TILE, None, None),
        P(SHOT, TILE, None, None),
        P(SHOT, TILE, None, None),
        P(TILE, None),
        P(SHOT, TILE),
        P(TILE),
        P(),
    )
    return jax.shard_map(
        on_device,
        mesh=fine,
        in_specs=placed,
        out_specs=(P(TILE, None), P(SHOT, TILE, None, None)),
        check_vma=False,
    )
```

```python
import functools

import jax
import jax.numpy as jnp
import ml_dtypes
import numpy as np
from jax import lax
from jax.experimental import pallas as pl
from jax.experimental.pallas import tpu as pltpu
from jax.sharding import Mesh
from jax.sharding import PartitionSpec as P

CX = 128
CZ = 128
CY = 16
OV = 8
STEPS = 4
ELEMS = 64
CXC = 64
CYC = 8
CZC = 64
ROWS = 72
LEARN = 0.02
EPSILON = 1e-06
BF = jnp.bfloat16
F32 = jnp.float32
SHOT = ("y", "xl")
TILE = ("xh", "z", "core")


def spectral_second(length):
    index = np.arange(length)
    number = np.minimum(index, length - index) * (2.0 * np.pi / length)
    phase = (index[:, None, None] - index[None, :, None]) * index[None, None, :] % length
    return -np.sum(number**2 * np.cos(2.0 * np.pi / length * phase), axis=2) / length


def spline_units(offset):
    mag = np.abs(offset)
    inner = 2.0 / 3.0 - mag**2 + 0.5 * mag**3
    outer = (2.0 - mag) ** 3 / 6.0
    return np.round(384.0 * np.where(mag < 1.0, inner, np.where(mag < 2.0, outer, 0.0)))


def halves(matrix):
    high = matrix.astype(np.float32).astype(ml_dtypes.bfloat16)
    low = (matrix - high.astype(np.float64)).astype(np.float32).astype(ml_dtypes.bfloat16)
    return high, low


def narrow_band(matrix):
    high, low = halves(np.pad(matrix, ((0, OV), (0, OV))))
    return np.concatenate([high, high, low], axis=1)


@functools.cache
def constants():
    out = {}
    second_x = spectral_second(CX + 2 * OV)[OV : OV + CX]
    ramp = np.sin(0.5 * np.pi * (np.arange(OV) + 0.5) / OV) ** 2
    left = second_x[:, :OV] * ramp[None, :]
    right = second_x[:, OV + CX :] * ramp[None, ::-1]
    high, low = halves(second_x[:, OV : OV + CX])
    out["own_x"] = np.block([[high, high], [low, low]])
    sides = []
    for pair in ((right, left), (left, right)):
        high, low = halves(np.concatenate(pair, axis=1))
        sides.append(np.concatenate([high, high, low], axis=1))
    out["halo_x"] = np.stack(sides)
    edge = []
    for rows in (slice(0, OV), slice(CX - OV, CX)):
        high, low = halves(second_x[rows, OV : OV + CX])
        edge.append(np.block([[high, high], [low, low]]))
    out["edge_x"] = np.stack(edge)
    near_part, cross_part = [], []
    for core in range(2):
        rows = slice(0, OV) if core == 0 else slice(CX - OV, CX)
        near_part.append(narrow_band((right if core == 0 else left)[rows]))
        rows = slice(CX - OV, CX) if core == 0 else slice(0, OV)
        cross_part.append(narrow_band((right if core == 0 else left)[rows]))
    out["near_x"] = np.stack(near_part)
    out["cross_x"] = np.stack(cross_part)
    high, low = halves(spectral_second(CZ) - 2.0 * np.eye(CZ))
    out["own_z"] = np.block([[high, low], [high, low]])

    fine_z = np.arange(CZ)[:, None]
    coarse_z = np.arange(CZC)[None, :]
    weight_z = sum(
        spline_units((fine_z - 2 * coarse_z + image * CZ - 0.5) * 0.5) for image in range(-2, 3)
    )
    zero = np.zeros_like(weight_z.T)
    pair = np.block([[weight_z.T, zero], [zero, weight_z.T]])
    out["grow_z"] = np.concatenate([pair, pair], axis=0)
    zero = np.zeros_like(weight_z)
    out["shrink_z"] = np.block(
        [[weight_z, zero], [weight_z, zero], [zero, weight_z], [zero, weight_z]]
    )

    def column(coarse, start=0, count=CX):
        return spline_units((np.arange(start, start + count) - 2 * coarse - 0.5) * 0.5)

    own = np.stack([column(j) for j in range(CXC)], axis=1)
    lower = {j: column(j) for j in (-2, -1, 0, 1)}
    upper = {j: column(j) for j in (62, 63, 64, 65)}
    stack = lambda d: np.stack([d[j] for j in sorted(d)], axis=1)
    grow_own, grow_rest, grow_new, shrink, shrink_far = [], [], [], [], []
    blank = np.zeros((CX, 2))
    for core in range(2):
        near = upper if core == 0 else lower
        near_two, far_six = ((64, 65), range(-6, 0)) if core == 0 else ((-2, -1), range(64, 70))
        far_two = (-2, -1) if core == 0 else (64, 65)
        beyond = -OV if core == 0 else CX
        both = lambda j: np.concatenate([column(j), column(j, beyond, OV)])
        mine = np.stack([both(j) for j in range(CXC)], axis=1)
        rest = np.stack([both(j) for j in (*near_two, *far_six)], axis=1)
        inner = own.copy()
        inner[:, [62, 63] if core == 0 else [0, 1]] = 0.0
        outer = np.stack([column(j) for j in far_two], axis=1)
        new = np.concatenate([inner, stack(near), outer, blank], axis=1)
        every = np.concatenate([own, stack(near), outer, blank], axis=1).T
        past = np.zeros((ROWS, OV))
        for row, j in (*enumerate(range(CXC)), *zip((CXC + 4, CXC + 5), far_two)):
            past[row] = column(j, beyond, OV)
        grow_own.append(np.concatenate([mine, mine], axis=1))
        grow_rest.append(np.concatenate([rest, rest], axis=1))
        grow_new.append(np.concatenate([new, new], axis=1))
        shrink.append(np.concatenate([every, every], axis=1))
        shrink_far.append(np.concatenate([past, past], axis=1))
    out["shrink_far"] = np.stack(shrink_far)
    out["grow_own"] = np.stack(grow_own)
    out["grow_rest"] = np.stack(grow_rest)
    out["grow_new"] = np.stack(grow_new)
    out["shrink_x"] = np.stack(shrink)
    return {name: np.asarray(value).astype(ml_dtypes.bfloat16) for name, value in out.items()}


def taps():
    return [
        [
            (j, float(w))
            for j in range(CYC)
            for w in [
                sum(
                    spline_units(np.float64((i - 2 * j + image * CY - 0.5) * 0.5))
                    for image in range(-2, 3)
                )
            ]
            if w
        ]
        for i in range(CY)
    ]


def split(value):
    high = value.astype(BF)
    return high, (value - high.astype(F32)).astype(BF)


def dot(left, right):
    return jnp.dot(left, right, preferred_element_type=F32)


def cat(parts, axis):
    return jnp.concatenate(parts, axis=axis)


def interior(v, own_x, own_z, out):
    for j in range(CY // 2):
        one, two = 2 * j, 2 * j + 1
        high1, low1 = split(v[one])
        high2, low2 = split(v[two])
        x = dot(own_x[...], cat([cat([high1, high2], 1), cat([low1, low2], 1)], 0))
        z = dot(cat([cat([high1, low1], 1), cat([high2, low2], 1)], 0), own_z[...])
        x = x[:CX] + x[CX:]
        z = z[:, :CZ] + z[:, CZ:]
        beside = v[(one - 1) % CY] + v[two]
        out[one] = x[:, :CZ] + z[:CX] + beside
        beside = v[one] + v[(two + 1) % CY]
        out[two] = x[:, CZ:] + z[CX:] + beside


def halo_part(near, far, field, halo_x, pair):
    parts = []
    for y in (2 * pair, 2 * pair + 1):
        start = (field * CY + y) * OV
        high, low = split(cat([near[start : start + OV], far[start : start + OV]], 0))
        parts.append(cat([high, low, high], 0))
    return dot(halo_x, cat(parts, 1))


def edge_rows(v, core, near, field):
    row = pl.multiple_of((1 - core) * (CX - OV), OV)
    for y in range(CY):
        start = (field * CY + y) * OV
        near[start : start + OV] = v[y, pl.ds(row, OV), :]


def first_edges(p, q, coef, far, near, *scratch):
    core = lax.axis_index("core")
    sems = scratch[6]
    block = OV * CY
    ends, copies = (core, 1 - core), []
    for side, end in enumerate(ends):
        for k, (source, whole, size) in enumerate(
            ((p, CX * CY, block), (q, CX * CY, block), (coef, CXC, 8))
        ):
            start = pl.multiple_of(end * (whole - size), 8)
            at = 3 * side + k
            copies.append(
                pltpu.make_async_copy(source.at[pl.ds(start, size)], scratch[at], sems.at[at])
            )
    for copy in copies:
        copy.start()
    for side, (end, out, count) in enumerate(zip(ends, (far, near), (6, 2))):
        for field in range(2):
            copies[3 * side + field].wait()
            rows = scratch[3 * side + field]
            for y in range(CY):
                start = (field * CY + y) * OV
                out[start : start + OV] = rows[pl.ds(y, OV, stride=CY), :]
        copies[3 * side + 2].wait()
        rows = scratch[3 * side + 2]
        base = 2 * CY * OV
        for row in range(count):
            for part in range(4):
                lanes = slice(part * 128, part * 128 + 128)
                spot = base + row * 4 + part
                last = 8 - count + row
                out[spot : spot + 1] = jnp.where(
                    end == 0, rows[row : row + 1, lanes], rows[last : last + 1, lanes]
                )


def reorder(source, target):
    for y in range(CY):
        target[y] = source[pl.ds(y, CX, stride=CY), :]


def prepare(
    signs, index, wavelet, p_now, q_now,
    own_x_in, own_z_in, p_prev_in, q_prev_in, coef_in, grow_own_in, grow_z_in,
    p0, q0, p1, q1, lap_p, lap_q, source, amounts, sigma_own,
    own_x, own_z, p_prev, q_prev, coef, grow_own, grow_z, sems,
):
    copies = [
        pltpu.make_async_copy(far, near, sems.at[k])
        for k, (far, near) in enumerate(
            (
                (own_x_in, own_x),
                (own_z_in, own_z),
                (p_prev_in, p_prev),
                (q_prev_in, q_prev),
                (coef_in, coef),
                (grow_own_in, grow_own),
                (grow_z_in, grow_z),
            )
        )
    ]
    for copy in copies:
        copy.start()
    reorder(p_now, p0)
    reorder(q_now, q0)
    source[...] = jnp.zeros_like(source)
    lane = lax.broadcasted_iota(jnp.int32, (1, CZ), 1)

    def add(e, carry):
        spot = index[e]
        x, rest = spot // (CY * CZ), spot % (CY * CZ)
        y, z = rest // CZ, rest % CZ
        amount = (2 * signs[e] - 1).astype(F32)
        row = source[y, pl.ds(x, 1), :]
        source[y, pl.ds(x, 1), :] = row + jnp.where(lane == z, amount, 0.0)
        return carry

    lax.fori_loop(0, ELEMS, add, 0)
    for step in range(STEPS + 1):
        amounts[step] = jnp.full((8, CZ), wavelet[step], F32)
    copies[0].wait()
    copies[1].wait()
    interior(p0, own_x, own_z, lap_p)
    interior(q0, own_x, own_z, lap_q)
    copies[2].wait()
    reorder(p_prev, p1)
    copies[3].wait()
    reorder(q_prev, q1)
    for copy in copies[4:]:
        copy.wait()

    def write(y, fine):
        sigma_own[y] = fine

    grow(coef[...], grow_z, grow_own[lax.axis_index("core")], write)


def grow(coef, grow_z, grow_x, write):
    wide = []
    for pair in range(CYC // 2):
        high, low = split(coef[:, pair * 128 : pair * 128 + 128])
        both = dot(cat([high, low], 1), grow_z[...])
        wide += [both[:, :CZ], both[:, CZ:]]
    weights = taps()
    for pair in range(CY // 2):
        parts = []
        for y in (2 * pair, 2 * pair + 1):
            mixed = None
            for j, w in weights[y]:
                term = wide[j] * w
                mixed = term if mixed is None else mixed + term
            parts.append(mixed)
        high, low = split(cat(parts, 1))
        fine = dot(grow_x, cat([high, low], 0))
        write(2 * pair, fine[:, :CZ])
        write(2 * pair + 1, fine[:, CZ:])


UNIT = 1.0 / 384.0**3


def grid_ends():
    core = lax.axis_index("core")
    chip = lax.axis_index("xh") * lax.axis_size("z") + lax.axis_index("z")
    chips = lax.axis_size("xh") * lax.axis_size("z")
    return (core == 0) & (chip == 0), (core == 1) & (chip == chips - 1)


def speed(sigma_own, near, far, grow_z, grow_rest, sigma, squared, beyond, held):
    core = lax.axis_index("core")
    base = 2 * CY * OV
    for row in range(6):
        for part in range(4):
            lanes = slice(part * 128, part * 128 + 128)
            spot = base + row * 4 + part
            if row < 2:
                held[row : row + 1, lanes] = near[spot : spot + 1]
            held[2 + row : 3 + row, lanes] = far[spot : spot + 1]
    first, last = grid_ends()

    def write(y, fine):
        fine = (sigma_own[y] + fine) * UNIT
        sigma[y] = fine[:CX]
        squared[y] = fine[:CX] * fine[:CX]
        beyond[y * OV : y * OV + OV] = jnp.where(first | last, 0.0, fine[CX:])

    grow(held[...], grow_z, grow_rest[core], write)


def squared_at(beyond, spot):
    value = beyond[spot : spot + OV]
    return value * value


def advance(step, *refs):
    (near, far, p, p_before, q, q_before, lap_p, lap_q, squared, source, amounts, halo_x) = refs[:12]
    refs = refs[12:]
    core = lax.axis_index("core")
    columns = halo_x[core]
    weight = amounts[step, :1, :]
    if step in (1, 3):
        (sent, beyond, cross_x), refs = refs[:3], refs[3:]
        cross = cross_x[core]
    if step == 2:
        old_lap, refs = refs[0], refs[1:]
    if step == 3:
        (old_lap, older_q, gathered, sigma, older_far), refs = refs[:5], refs[5:]
    if step in (0, 2):
        (p_new, q_new, near_out), refs = refs[:3], refs[3:]
    elif step == 1:
        (p_new, q_new, near_out, far_out), refs = refs[:4], refs[4:]
    else:
        p_new, near_out, far_out, image, image_far = refs[:5]
    if step < 2:
        lap_out = refs[0]
    if step == 2:
        gathered = refs[0]
    for pair in range(CY // 2):
        extra_p = halo_part(near, far, 0, columns, pair)
        extra_q = halo_part(near, far, 1, columns, pair)
        for side in range(2):
            y = 2 * pair + side
            lanes = slice(side * CZ, side * CZ + CZ)
            lap = lap_p[y] + extra_p[:, lanes]
            lap_adj = lap_q[y] + extra_q[:, lanes]
            sq = squared[y]
            p_new[y] = 2.0 * p[y] - p_before[y] + sq * lap + source[y] * weight
            new_q = 2.0 * q[y] - q_before[y] + sq * lap_adj
            if step < 3:
                q_new[y] = new_q
            if step < 2:
                lap_out[y] = lap
            if step == 2:
                gathered[y] = q[y] * lap + new_q * old_lap[y]
            if step == 3:
                total = gathered[y] + older_q[y] * lap + new_q * old_lap[y]
                image[y] = 2.0 * sigma[y] * total
    edge_rows(p_new, core, near_out, 0)
    if step < 3:
        edge_rows(q_new, core, near_out, 1)
    if step == 1:
        size = CY * OV
        for pair in range(CY // 2):
            for field in range(2):
                extra = halo_part(sent, sent, field, cross, pair)
                for side in range(2):
                    spot = (2 * pair + side) * OV
                    known = far[(2 + field) * size + spot : (2 + field) * size + spot + OV]
                    far_out[field * size + spot : field * size + spot + OV] = (
                        known
                        + squared_at(beyond, spot) * extra[:OV, side * CZ : side * CZ + CZ]
                    )
    if step == 3:
        size = CY * OV
        for pair in range(CY // 2):
            extra_p = halo_part(sent, sent, 0, cross, pair)
            extra_q = halo_part(sent, sent, 1, cross, pair)
            for side in range(2):
                spot = (2 * pair + side) * OV
                lanes = slice(side * CZ, side * CZ + CZ)
                part_p, part_q = extra_p[:OV, lanes], extra_q[:OV, lanes]
                rows = lambda k: far[k * size + spot : k * size + spot + OV]
                far_out[spot : spot + OV] = rows(2) + squared_at(beyond, spot) * part_p
                near_q = older_far[size + spot : size + spot + OV]
                image_far[spot : spot + OV] = (
                    rows(3) + 2.0 * beyond[spot : spot + OV] * near_q * part_p + rows(4) * part_q
                )


def early(step, *refs):
    (near, p, p_before, q, q_before, laps, squared, source, amounts, near_x) = refs[:10]
    if step == 3:
        older_q, old_lap, gathered, sigma = refs[10:14]
    out = refs[-1]
    core = lax.axis_index("core")
    rows = pl.ds(pl.multiple_of(core * (CX - OV), OV), OV)
    weight = amounts[step, :1, :]
    columns = near_x[core]
    for pair in range(CY // 2):
        extra_p = halo_part(near, near, 0, columns, pair)
        extra_q = halo_part(near, near, 1, columns, pair)
        for side in range(2):
            y = 2 * pair + side
            lanes = slice(side * CZ, side * CZ + CZ)
            sq = squared[y, rows, :]
            spot = y * OV
            lap = laps[spot : spot + OV] + extra_p[:OV, lanes]
            spot += CY * OV
            lap_adj = laps[spot : spot + OV] + extra_q[:OV, lanes]
            edge_p, edge_q = p[y, rows, :], q[y, rows, :]
            next_p = 2.0 * edge_p - p_before[y, rows, :] + sq * lap + source[y, rows, :] * weight
            next_q = 2.0 * edge_q - q_before[y, rows, :] + sq * lap_adj
            if step == 1:
                sets = (edge_p, edge_q, next_p, next_q)
            else:
                twice = 2.0 * sigma[y, rows, :]
                old = old_lap[y, rows, :]
                known = gathered[y, rows, :] + older_q[y, rows, :] * lap + next_q * old
                sets = (edge_p, edge_q, next_p, twice * known, twice * sq * old)
            for k, value in enumerate(sets):
                spot = (k * CY + y) * OV
                out[spot : spot + OV] = value


def edge_interior(v, edge_x, own_z, first, out, field):
    strips = []
    for j in range(CY // 2):
        one, two = 2 * j, 2 * j + 1
        high1, low1 = split(v[one])
        high2, low2 = split(v[two])
        x = dot(edge_x, cat([cat([high1, high2], 1), cat([low1, low2], 1)], 0))
        x = x[:OV] + x[OV:]
        strips += [x[:, :CZ], x[:, CZ:]]
    rows = pl.ds(first, OV)
    edge = [v[y, rows, :] for y in range(CY)]
    high, low = split(cat(edge, 0))
    z = dot(cat([high, low], 1), own_z[...])
    z = z[:, :CZ] + z[:, CZ:]
    for y in range(CY):
        beside = edge[(y - 1) % CY] + edge[(y + 1) % CY]
        spot = (field * CY + y) * OV
        out[spot : spot + OV] = strips[y] + z[y * OV : y * OV + OV] + beside


def edge_inside(p, q, edge_x, own_z, out):
    core = lax.axis_index("core")
    first = pl.multiple_of(core * (CX - OV), OV)
    edge_interior(p, edge_x[core], own_z, first, out, 0)
    edge_interior(q, edge_x[core], own_z, first, out, 1)


def inside(p, q, own_x, own_z, lap_p, lap_q):
    interior(p, own_x, own_z, lap_p)
    interior(q, own_x, own_z, lap_q)


def inside_one(p, own_x, own_z, lap_p):
    interior(p, own_x, own_z, lap_p)


def shrink(image, image_far, shrink_x, shrink_far, shrink_z, own):
    core = lax.axis_index("core")
    rows_x = shrink_x[core]
    rows_far = shrink_far[core]
    narrow = [None] * CYC
    weights = taps()
    for pair in range(CY // 2):
        high, low = split(cat([image[2 * pair], image[2 * pair + 1]], 1))
        both = dot(rows_x, cat([high, low], 0))
        spots = [slice(y * OV, y * OV + OV) for y in (2 * pair, 2 * pair + 1)]
        high, low = split(cat([image_far[spots[0]], image_far[spots[1]]], 1))
        both = both + dot(rows_far, cat([high, low], 0))
        for side in range(2):
            part = both[:, side * CZ : side * CZ + CZ]
            for j, w in weights[2 * pair + side]:
                term = part * w
                narrow[j] = term if narrow[j] is None else narrow[j] + term
    pieces = []
    for pair in range(CYC // 2):
        parts = []
        for j in (2 * pair, 2 * pair + 1):
            parts += list(split(narrow[j]))
        pieces.append(dot(cat(parts, 1), shrink_z[...]) * UNIT)
    own[...] = cat(pieces, 1)


def fold(value):
    rows = value[0:8]
    for r in range(1, value.shape[0] // 8):
        rows = rows + value[8 * r : 8 * r + 8]
    folded = rows[:, :128]
    for c in range(1, 4):
        folded = folded + rows[:, 128 * c : 128 * c + 128]
    return folded


def squares(a, b, total, near):
    core = lax.axis_index("core")
    total[...] = a[...] + b[...]
    first, last = grid_ends()
    total[CXC + 4 : CXC + 6] = jnp.where(first | last, 0.0, total[CXC + 4 : CXC + 6])
    row = lax.broadcasted_iota(jnp.int32, (CXC, CYC * CZC), 0)
    start = (1 - core) * (CXC - 2)
    value = jnp.where((row >= start) & (row < start + 2), 0.0, total[:CXC])
    for r in range(4):
        for part in range(4):
            lanes = slice(part * 128, part * 128 + 128)
            spot = r * 4 + part
            near[spot : spot + 1] = total[CXC + r : CXC + r + 1, lanes]
    near[16:24] = fold(value * value)


def pair_up(total, mine, other, out, squared):
    core = lax.axis_index("core")
    out[...] = total[...]
    edge = mine[0:16] + other[0:16]
    for r in range(4):
        for part in range(4):
            lanes = slice(part * 128, part * 128 + 128)
            spot = r * 4 + part
            out[CXC + r : CXC + r + 1, lanes] = edge[spot : spot + 1]
    out[0:2] = jnp.where(core == 0, out[0:2], out[CXC + 2 : CXC + 4])
    out[CXC - 2 : CXC] = jnp.where(core == 0, out[CXC : CXC + 2], out[CXC - 2 : CXC])
    edge = edge * edge
    squared[...] = (mine[16:24] + other[16:24]) + (edge[0:8] + edge[8:16])


def last_fields(near, far, p, p_before, lap_p, source, amounts, halo_x, lap_out, base):
    core = lax.axis_index("core")
    columns = halo_x[core]
    weight = amounts[STEPS, :1, :]
    for pair in range(CY // 2):
        extra = halo_part(near, far, 0, columns, pair)
        for side in range(2):
            y = 2 * pair + side
            lap_out[y] = lap_p[y] + extra[:, side * CZ : side * CZ + CZ]
            base[y] = 2.0 * p[y] - p_before[y] + source[y] * weight


def add_four(own, one, three, two, out):
    out[...] = (own[...] + one[...]) + (two[...] + three[...])


def spread(total, sigma, lap, base, grow_z, grow_new, zeroth, first, second):
    core = lax.axis_index("core")

    def write(y, fine):
        change = fine * UNIT
        old, curve = sigma[y], lap[y]
        scaled = change * curve
        rows = pl.ds(y, CX, stride=CY)
        zeroth[rows, :] = base[y] + old * old * curve
        first[rows, :] = -2.0 * old * scaled
        second[rows, :] = change * scaled

    grow(total[...], grow_z, grow_new[core], write)


def widen(a, b, out):
    value = jnp.sum(a[...] + b[...], axis=0, keepdims=True)
    out[...] = jnp.broadcast_to(value, out.shape)


def finish(count, parts, total, zeroth, first, second, direction, p_last):
    value = jnp.sum(jnp.sum(parts[...], axis=0, keepdims=True), axis=1, keepdims=True)
    inverse = 1.0 / jnp.sqrt(value * (1.0 / count) + EPSILON)
    rate = LEARN * inverse
    p_last[...] = zeroth[...] + rate * (first[...] + rate * second[...])
    direction[...] = total[:CXC] * inverse


VM = pl.BlockSpec(memory_space=pltpu.VMEM)
SM = pl.BlockSpec(memory_space=pltpu.SMEM)
FIELD = jax.ShapeDtypeStruct((CY, CX, CZ), F32)
PARAMS = pltpu.CompilerParams(vmem_limit_bytes=6 * 2**20)


def rows_of(count, lanes=128):
    return jax.ShapeDtypeStruct((count, lanes), F32)


def call(body, outs, *args, smem=0, scratch=(), flops=0, name=None, held=(), in_specs=None, out_specs=None):
    size = sum(int(np.prod(a.shape)) * a.dtype.itemsize for a in args)
    count = len(args)

    def run(*refs):
        body(*refs[:count], *refs[count + len(held) :])

    return pl.pallas_call(
        run,
        out_shape=outs,
        in_specs=([SM] * smem + [VM] * (count - smem) if in_specs is None else in_specs)
        + [pl.BlockSpec(memory_space=pl.ANY)] * len(held),
        out_specs=jax.tree.map(lambda _: VM, outs) if out_specs is None else out_specs,
        scratch_shapes=list(scratch),
        compiler_params=PARAMS,
        cost_estimate=pl.CostEstimate(flops=flops, bytes_accessed=size, transcendentals=0),
        name=name,
    )(*args, *held)


def xor_swap(x, axis, mask):
    count = lax.axis_size(axis)
    if mask >= count:
        return jnp.zeros_like(x)
    return lax.ppermute(x, axis, [(i, i ^ mask) for i in range(count)])


def far_swap(x):
    count = lax.axis_size(TILE)
    pairs = [(i, i + 1) for i in range(1, count - 1, 2)]
    return lax.ppermute(x, TILE, pairs + [(b, a) for a, b in pairs])


def on_device(p_now, p_prev, adj_now, adj_next, coef_old, signs, elem_index, wavelet):
    const = {name: jnp.asarray(value) for name, value in constants().items()}
    own_x, own_z, halo_x = const["own_x"], const["own_z"], const["halo_x"]
    flat = lambda a: a.reshape(CX * CY, CZ)
    p_now, p_prev, adj_now, adj_next = map(flat, (p_now, p_prev, adj_now, adj_next))

    half, edge = rows_of(CY * OV), rows_of(2 * CY * OV)
    sources = [pltpu.with_memory_space_constraint(a, pltpu.HBM) for a in (p_now, adj_now, coef_old)]

    blocks = [pltpu.VMEM((OV * CY, CZ), F32)] * 2 + [pltpu.VMEM((8, CYC * CZC), F32)]
    far, near = call(
        first_edges, (rows_of(2 * CY * OV + 24), rows_of(2 * CY * OV + 8)), *sources,
        in_specs=[pl.BlockSpec(memory_space=pltpu.HBM)] * 3,
        scratch=blocks * 2 + [pltpu.SemaphoreType.DMA((6,))],
        name="first_edges",
    )
    far, near = far_swap(far), xor_swap(near, "core", 1)

    wide = jax.ShapeDtypeStruct((CY, CX + OV, CZ), F32)
    later = [own_x, own_z, p_prev, adj_next, coef_old, const["grow_own"]]
    later.append(const["grow_z"])
    p, q, p_before, q_before, lap_p, lap_q, source, amounts, sigma_own = call(
        prepare,
        (FIELD,) * 7 + (jax.ShapeDtypeStruct((STEPS + 1, 8, CZ), F32), wide),
        signs[0], elem_index, wavelet, p_now, adj_now,
        *(pltpu.with_memory_space_constraint(a, pltpu.HBM) for a in later),
        flops=10**9, name="prepare", held=(halo_x,),
        in_specs=[SM] * 3 + [VM] * 2 + [pl.BlockSpec(memory_space=pltpu.HBM)] * len(later),
        scratch=[pltpu.VMEM(a.shape, a.dtype) for a in later]
        + [pltpu.SemaphoreType.DMA((len(later),))],
    )
    sigma, squared, beyond = call(
        speed, (FIELD, FIELD, half), sigma_own, near, far, const["grow_z"], const["grow_rest"],
        scratch=[pltpu.VMEM((8, CYC * CZC), F32)], flops=10**8, name="speed",
    )

    laps, qs = [], [q]
    gathered = None
    for step in range(STEPS):
        args = [near, far, p, p_before, q, q_before, lap_p, lap_q, squared, source, amounts, halo_x]
        body = functools.partial(advance, step)
        name = f"advance_{step}"
        if step == 0:
            outs = (FIELD, FIELD, edge, FIELD)
        elif step == 1:
            args += [sent, beyond, const["cross_x"]]
            outs = (FIELD, FIELD, edge, edge, FIELD)
            older_far = far
        elif step == 2:
            args.append(laps[1])
            outs = (FIELD, FIELD, edge, FIELD)
        else:
            args += [sent, beyond, const["cross_x"], laps[0], qs[1], gathered, sigma, older_far]
            outs = (FIELD, half, half, FIELD, half)
        result = call(body, outs, *args, flops=10**8, name=name)
        if step == 3:
            p_new, near, far, image, image_far = result
            p, p_before = p_new, p
            continue
        p_new, q_new, *edges, other = result
        if step < 2:
            laps.append(other)
        else:
            gathered = other
        p, p_before = p_new, p
        q, q_before = q_new, q
        qs.append(q)
        near = xor_swap(edges[0], "core", 1)
        if step == 1:
            lap_p, lap_q = call(
                inside, (FIELD, FIELD), p, q, own_x, own_z, flops=10**9, name="inside_1"
            )
            far = edges[1]
            continue
        edge_laps = call(
            edge_inside, edge, p, q, const["edge_x"], own_z, flops=10**8, name=f"edge_inside_{step}"
        )
        args = [near, p, p_before, q, q_before, edge_laps, squared, source, amounts]
        args.append(const["near_x"])
        if step == 2:
            args += [qs[1], laps[0], gathered, sigma]
        sent = call(
            functools.partial(early, step + 1), rows_of((4 if step == 0 else 5) * CY * OV),
            *args, flops=10**7, name=f"early_{step + 1}",
        )
        far = far_swap(sent)
        lap_p, lap_q = call(
            inside, (FIELD, FIELD), p, q, own_x, own_z, flops=10**9, name=f"inside_{step}",
            held=(sent,),
        )

    partial = call(
        shrink, rows_of(ROWS, CYC * CZC),
        image, image_far, const["shrink_x"], const["shrink_far"], const["shrink_z"],
        flops=10**8, name="shrink",
    )
    two, three, one = (xor_swap(partial, "y", m) for m in (2, 3, 1))
    near = xor_swap(near, "core", 1)
    lap_p = call(inside_one, FIELD, p, own_x, own_z, flops=5 * 10**8, name="inside_last")
    lap_p, base = call(
        last_fields, (FIELD, FIELD), near, far, p, p_before, lap_p, source, amounts, halo_x,
        flops=10**8, name="last_fields",
    )
    held = (lap_p, base)
    partial = call(
        add_four, rows_of(ROWS, CYC * CZC), partial, one, three, two, name="add_four", held=held
    )
    total, mine = call(
        squares, (rows_of(ROWS, CYC * CZC), rows_of(24)), partial, xor_swap(partial, "xl", 1),
        name="squares", held=held,
    )
    total, squared_sum = call(
        pair_up, (rows_of(ROWS, CYC * CZC), rows_of(8)), total, mine, xor_swap(mine, "core", 1),
        name="pair_up", held=held,
    )
    terms = call(
        spread, (rows_of(CX * CY),) * 3, total, sigma, lap_p, base, const["grow_z"], const["grow_new"],
        flops=10**8, name="spread",
    )
    deep = lax.axis_size("z")
    copies = call(
        widen, rows_of(deep),
        squared_sum, xor_swap(squared_sum, "xh", 1), name="widen", held=terms,
    )
    parts = lax.all_to_all(copies, "z", split_axis=0, concat_axis=0, tiled=True)
    count = float(lax.axis_size(TILE) * CXC * CYC * CZC)
    direction, p_last = call(
        functools.partial(finish, count),
        (rows_of(CXC, CYC * CZC), rows_of(CX * CY)),
        parts, total, *terms, name="finish",
    )
    return direction, p_last.reshape(1, CX, CY, CZ)


def solution(mesh):
    shots, tiles = mesh.shape["shot"], mesh.shape["tile"]
    fine = Mesh(
        mesh.devices.reshape(shots // 2, 2, 2, tiles // 4, 2), ("y", "xl", "xh", "z", "core")
    )
    placed = (
        P(SHOT, TILE, None, None),
        P(SHOT, TILE, None, None),
        P(SHOT, TILE, None, None),
        P(SHOT, TILE, None, None),
        P(TILE, None),
        P(SHOT, TILE),
        P(TILE),
        P(),
    )
    return jax.shard_map(
        on_device,
        mesh=fine,
        in_specs=placed,
        out_specs=(P(TILE, None), P(SHOT, TILE, None, None)),
        check_vma=False,
    )
```

```python
import functools

import jax
import jax.numpy as jnp
import ml_dtypes
import numpy as np
from jax import lax
from jax.experimental import pallas as pl
from jax.experimental.pallas import tpu as pltpu
from jax.sharding import Mesh
from jax.sharding import PartitionSpec as P

CX = 128
CZ = 128
CY = 16
OV = 8
STEPS = 4
ELEMS = 64
CXC = 64
CYC = 8
CZC = 64
ROWS = 72
LEARN = 0.02
EPSILON = 1e-06
BF = jnp.bfloat16
F32 = jnp.float32
SHOT = ("y", "xl")
TILE = ("xh", "z", "core")


def spectral_second(length):
    index = np.arange(length)
    number = np.minimum(index, length - index) * (2.0 * np.pi / length)
    phase = (index[:, None, None] - index[None, :, None]) * index[None, None, :] % length
    return -np.sum(number**2 * np.cos(2.0 * np.pi / length * phase), axis=2) / length


def spline_units(offset):
    mag = np.abs(offset)
    inner = 2.0 / 3.0 - mag**2 + 0.5 * mag**3
    outer = (2.0 - mag) ** 3 / 6.0
    return np.round(384.0 * np.where(mag < 1.0, inner, np.where(mag < 2.0, outer, 0.0)))


def halves(matrix):
    high = matrix.astype(np.float32).astype(ml_dtypes.bfloat16)
    low = (matrix - high.astype(np.float64)).astype(np.float32).astype(ml_dtypes.bfloat16)
    return high, low


def narrow_band(matrix):
    high, low = halves(np.pad(matrix, ((0, OV), (0, OV))))
    return np.concatenate([high, high, low], axis=1)


@functools.cache
def constants():
    out = {}
    second_x = spectral_second(CX + 2 * OV)[OV : OV + CX]
    ramp = np.sin(0.5 * np.pi * (np.arange(OV) + 0.5) / OV) ** 2
    left = second_x[:, :OV] * ramp[None, :]
    right = second_x[:, OV + CX :] * ramp[None, ::-1]
    high, low = halves(second_x[:, OV : OV + CX])
    out["own_x"] = np.block([[high, high], [low, low]])
    sides = []
    for pair in ((right, left), (left, right)):
        high, low = halves(np.concatenate(pair, axis=1))
        sides.append(np.concatenate([high, high, low], axis=1))
    out["halo_x"] = np.stack(sides)
    edge = []
    for rows in (slice(0, OV), slice(CX - OV, CX)):
        high, low = halves(second_x[rows, OV : OV + CX])
        edge.append(np.block([[high, high], [low, low]]))
    out["edge_x"] = np.stack(edge)
    near_part, cross_part = [], []
    for core in range(2):
        rows = slice(0, OV) if core == 0 else slice(CX - OV, CX)
        near_part.append(narrow_band((right if core == 0 else left)[rows]))
        rows = slice(CX - OV, CX) if core == 0 else slice(0, OV)
        cross_part.append(narrow_band((right if core == 0 else left)[rows]))
    out["near_x"] = np.stack(near_part)
    out["cross_x"] = np.stack(cross_part)
    high, low = halves(spectral_second(CZ) - 2.0 * np.eye(CZ))
    out["own_z"] = np.block([[high, low], [high, low]])

    fine_z = np.arange(CZ)[:, None]
    coarse_z = np.arange(CZC)[None, :]
    weight_z = sum(
        spline_units((fine_z - 2 * coarse_z + image * CZ - 0.5) * 0.5) for image in range(-2, 3)
    )
    zero = np.zeros_like(weight_z.T)
    pair = np.block([[weight_z.T, zero], [zero, weight_z.T]])
    out["grow_z"] = np.concatenate([pair, pair], axis=0)
    zero = np.zeros_like(weight_z)
    out["shrink_z"] = np.block(
        [[weight_z, zero], [weight_z, zero], [zero, weight_z], [zero, weight_z]]
    )

    def column(coarse, start=0, count=CX):
        return spline_units((np.arange(start, start + count) - 2 * coarse - 0.5) * 0.5)

    own = np.stack([column(j) for j in range(CXC)], axis=1)
    lower = {j: column(j) for j in (-2, -1, 0, 1)}
    upper = {j: column(j) for j in (62, 63, 64, 65)}
    stack = lambda d: np.stack([d[j] for j in sorted(d)], axis=1)
    grow_own, grow_rest, grow_new, shrink, shrink_far = [], [], [], [], []
    blank = np.zeros((CX, 2))
    for core in range(2):
        near = upper if core == 0 else lower
        near_two, far_six = ((64, 65), range(-6, 0)) if core == 0 else ((-2, -1), range(64, 70))
        far_two = (-2, -1) if core == 0 else (64, 65)
        beyond = -OV if core == 0 else CX
        both = lambda j: np.concatenate([column(j), column(j, beyond, OV)])
        mine = np.stack([both(j) for j in range(CXC)], axis=1)
        rest = np.stack([both(j) for j in (*near_two, *far_six)], axis=1)
        inner = own.copy()
        inner[:, [62, 63] if core == 0 else [0, 1]] = 0.0
        outer = np.stack([column(j) for j in far_two], axis=1)
        new = np.concatenate([inner, stack(near), outer, blank], axis=1)
        every = np.concatenate([own, stack(near), outer, blank], axis=1).T
        past = np.zeros((ROWS, OV))
        for row, j in (*enumerate(range(CXC)), *zip((CXC + 4, CXC + 5), far_two)):
            past[row] = column(j, beyond, OV)
        grow_own.append(np.concatenate([mine, mine], axis=1))
        grow_rest.append(np.concatenate([rest, rest], axis=1))
        grow_new.append(np.concatenate([new, new], axis=1))
        shrink.append(np.concatenate([every, every], axis=1))
        shrink_far.append(np.concatenate([past, past], axis=1))
    out["shrink_far"] = np.stack(shrink_far)
    out["grow_own"] = np.stack(grow_own)
    out["grow_rest"] = np.stack(grow_rest)
    out["grow_new"] = np.stack(grow_new)
    out["shrink_x"] = np.stack(shrink)
    return {name: np.asarray(value).astype(ml_dtypes.bfloat16) for name, value in out.items()}


def taps():
    return [
        [
            (j, float(w))
            for j in range(CYC)
            for w in [
                sum(
                    spline_units(np.float64((i - 2 * j + image * CY - 0.5) * 0.5))
                    for image in range(-2, 3)
                )
            ]
            if w
        ]
        for i in range(CY)
    ]


def split(value):
    high = value.astype(BF)
    return high, (value - high.astype(F32)).astype(BF)


def dot(left, right):
    return jnp.dot(left, right, preferred_element_type=F32)


def cat(parts, axis):
    return jnp.concatenate(parts, axis=axis)


def interior(v, own_x, own_z, out):
    for j in range(CY // 2):
        one, two = 2 * j, 2 * j + 1
        high1, low1 = split(v[one])
        high2, low2 = split(v[two])
        x = dot(own_x[...], cat([cat([high1, high2], 1), cat([low1, low2], 1)], 0))
        z = dot(cat([cat([high1, low1], 1), cat([high2, low2], 1)], 0), own_z[...])
        x = x[:CX] + x[CX:]
        z = z[:, :CZ] + z[:, CZ:]
        beside = v[(one - 1) % CY] + v[two]
        out[one] = x[:, :CZ] + z[:CX] + beside
        beside = v[one] + v[(two + 1) % CY]
        out[two] = x[:, CZ:] + z[CX:] + beside


def halo_part(near, far, field, halo_x, pair):
    parts = []
    for y in (2 * pair, 2 * pair + 1):
        start = (field * CY + y) * OV
        high, low = split(cat([near[start : start + OV], far[start : start + OV]], 0))
        parts.append(cat([high, low, high], 0))
    return dot(halo_x, cat(parts, 1))


def edge_rows(v, core, near, field):
    row = pl.multiple_of((1 - core) * (CX - OV), OV)
    for y in range(CY):
        start = (field * CY + y) * OV
        near[start : start + OV] = v[y, pl.ds(row, OV), :]


def first_edges(p, q, coef, far, near, *scratch):
    core = lax.axis_index("core")
    sems = scratch[6]
    block = OV * CY
    ends, copies = (core, 1 - core), []
    for side, end in enumerate(ends):
        for k, (source, whole, size) in enumerate(
            ((p, CX * CY, block), (q, CX * CY, block), (coef, CXC, 8))
        ):
            start = pl.multiple_of(end * (whole - size), 8)
            at = 3 * side + k
            copies.append(
                pltpu.make_async_copy(source.at[pl.ds(start, size)], scratch[at], sems.at[at])
            )
    for copy in copies:
        copy.start()
    for side, (end, out, count) in enumerate(zip(ends, (far, near), (6, 2))):
        for field in range(2):
            copies[3 * side + field].wait()
            rows = scratch[3 * side + field]
            for y in range(CY):
                start = (field * CY + y) * OV
                out[start : start + OV] = rows[pl.ds(y, OV, stride=CY), :]
        copies[3 * side + 2].wait()
        rows = scratch[3 * side + 2]
        base = 2 * CY * OV
        for row in range(count):
            for part in range(4):
                lanes = slice(part * 128, part * 128 + 128)
                spot = base + row * 4 + part
                last = 8 - count + row
                out[spot : spot + 1] = jnp.where(
                    end == 0, rows[row : row + 1, lanes], rows[last : last + 1, lanes]
                )


def reorder(source, target):
    for y in range(CY):
        target[y] = source[pl.ds(y, CX, stride=CY), :]


def prepare(
    signs, index, wavelet, p_now, q_now,
    own_x_in, own_z_in, p_prev_in, q_prev_in, coef_in, grow_own_in, grow_z_in,
    p0, q0, p1, q1, lap_p, lap_q, source, amounts, sigma_own,
    own_x, own_z, p_prev, q_prev, coef, grow_own, grow_z, sems,
):
    copies = [
        pltpu.make_async_copy(far, near, sems.at[k])
        for k, (far, near) in enumerate(
            (
                (own_x_in, own_x),
                (own_z_in, own_z),
                (p_prev_in, p_prev),
                (q_prev_in, q_prev),
                (coef_in, coef),
                (grow_own_in, grow_own),
                (grow_z_in, grow_z),
            )
        )
    ]
    for copy in copies:
        copy.start()
    reorder(p_now, p0)
    reorder(q_now, q0)
    source[...] = jnp.zeros_like(source)
    lane = lax.broadcasted_iota(jnp.int32, (1, CZ), 1)

    def add(e, carry):
        spot = index[e]
        x, rest = spot // (CY * CZ), spot % (CY * CZ)
        y, z = rest // CZ, rest % CZ
        amount = (2 * signs[e] - 1).astype(F32)
        row = source[y, pl.ds(x, 1), :]
        source[y, pl.ds(x, 1), :] = row + jnp.where(lane == z, amount, 0.0)
        return carry

    lax.fori_loop(0, ELEMS, add, 0)
    for step in range(STEPS + 1):
        amounts[step] = jnp.full((8, CZ), wavelet[step], F32)
    copies[0].wait()
    copies[1].wait()
    interior(p0, own_x, own_z, lap_p)
    interior(q0, own_x, own_z, lap_q)
    copies[2].wait()
    reorder(p_prev, p1)
    copies[3].wait()
    reorder(q_prev, q1)
    for copy in copies[4:]:
        copy.wait()

    def write(y, fine):
        sigma_own[y] = fine

    grow(coef[...], grow_z, grow_own[lax.axis_index("core")], write)


def grow(coef, grow_z, grow_x, write):
    wide = []
    for pair in range(CYC // 2):
        high, low = split(coef[:, pair * 128 : pair * 128 + 128])
        both = dot(cat([high, low], 1), grow_z[...])
        wide += [both[:, :CZ], both[:, CZ:]]
    weights = taps()
    for pair in range(CY // 2):
        parts = []
        for y in (2 * pair, 2 * pair + 1):
            mixed = None
            for j, w in weights[y]:
                term = wide[j] * w
                mixed = term if mixed is None else mixed + term
            parts.append(mixed)
        high, low = split(cat(parts, 1))
        fine = dot(grow_x, cat([high, low], 0))
        write(2 * pair, fine[:, :CZ])
        write(2 * pair + 1, fine[:, CZ:])


UNIT = 1.0 / 384.0**3


def grid_ends():
    core = lax.axis_index("core")
    chip = lax.axis_index("xh") * lax.axis_size("z") + lax.axis_index("z")
    chips = lax.axis_size("xh") * lax.axis_size("z")
    return (core == 0) & (chip == 0), (core == 1) & (chip == chips - 1)


def speed(sigma_own, near, far, grow_z, grow_rest, sigma, squared, beyond, held):
    core = lax.axis_index("core")
    base = 2 * CY * OV
    for row in range(6):
        for part in range(4):
            lanes = slice(part * 128, part * 128 + 128)
            spot = base + row * 4 + part
            if row < 2:
                held[row : row + 1, lanes] = near[spot : spot + 1]
            held[2 + row : 3 + row, lanes] = far[spot : spot + 1]
    first, last = grid_ends()

    def write(y, fine):
        fine = (sigma_own[y] + fine) * UNIT
        sigma[y] = fine[:CX]
        squared[y] = fine[:CX] * fine[:CX]
        beyond[y * OV : y * OV + OV] = jnp.where(first | last, 0.0, fine[CX:])

    grow(held[...], grow_z, grow_rest[core], write)


def squared_at(beyond, spot):
    value = beyond[spot : spot + OV]
    return value * value


def advance(step, *refs):
    (near, far, p, p_before, q, q_before, lap_p, lap_q, squared, source, amounts, halo_x) = refs[:12]
    refs = refs[12:]
    core = lax.axis_index("core")
    columns = halo_x[core]
    weight = amounts[step, :1, :]
    if step in (1, 3):
        (sent, beyond, cross_x), refs = refs[:3], refs[3:]
        cross = cross_x[core]
    if step == 2:
        old_lap, refs = refs[0], refs[1:]
    if step == 3:
        (old_lap, older_q, gathered, sigma, older_far), refs = refs[:5], refs[5:]
    if step in (0, 2):
        (p_new, q_new, near_out), refs = refs[:3], refs[3:]
    elif step == 1:
        (p_new, q_new, near_out, far_out), refs = refs[:4], refs[4:]
    else:
        p_new, near_out, far_out, image, image_far = refs[:5]
    if step < 2:
        lap_out = refs[0]
    if step == 2:
        gathered = refs[0]
    for pair in range(CY // 2):
        extra_p = halo_part(near, far, 0, columns, pair)
        extra_q = halo_part(near, far, 1, columns, pair)
        for side in range(2):
            y = 2 * pair + side
            lanes = slice(side * CZ, side * CZ + CZ)
            lap = lap_p[y] + extra_p[:, lanes]
            lap_adj = lap_q[y] + extra_q[:, lanes]
            sq = squared[y]
            p_new[y] = 2.0 * p[y] - p_before[y] + sq * lap + source[y] * weight
            new_q = 2.0 * q[y] - q_before[y] + sq * lap_adj
            if step < 3:
                q_new[y] = new_q
            if step < 2:
                lap_out[y] = lap
            if step == 2:
                gathered[y] = q[y] * lap + new_q * old_lap[y]
            if step == 3:
                total = gathered[y] + older_q[y] * lap + new_q * old_lap[y]
                image[y] = 2.0 * sigma[y] * total
    edge_rows(p_new, core, near_out, 0)
    if step < 3:
        edge_rows(q_new, core, near_out, 1)
    if step == 1:
        size = CY * OV
        for pair in range(CY // 2):
            for field in range(2):
                extra = halo_part(sent, sent, field, cross, pair)
                for side in range(2):
                    spot = (2 * pair + side) * OV
                    known = far[(2 + field) * size + spot : (2 + field) * size + spot + OV]
                    far_out[field * size + spot : field * size + spot + OV] = (
                        known
                        + squared_at(beyond, spot) * extra[:OV, side * CZ : side * CZ + CZ]
                    )
    if step == 3:
        size = CY * OV
        for pair in range(CY // 2):
            extra_p = halo_part(sent, sent, 0, cross, pair)
            extra_q = halo_part(sent, sent, 1, cross, pair)
            for side in range(2):
                spot = (2 * pair + side) * OV
                lanes = slice(side * CZ, side * CZ + CZ)
                part_p, part_q = extra_p[:OV, lanes], extra_q[:OV, lanes]
                rows = lambda k: far[k * size + spot : k * size + spot + OV]
                far_out[spot : spot + OV] = rows(2) + squared_at(beyond, spot) * part_p
                near_q = older_far[size + spot : size + spot + OV]
                image_far[spot : spot + OV] = (
                    rows(3) + 2.0 * beyond[spot : spot + OV] * near_q * part_p + rows(4) * part_q
                )


def early(step, *refs):
    (near, p, p_before, q, q_before, laps, squared, source, amounts, near_x) = refs[:10]
    if step == 3:
        older_q, old_lap, gathered, sigma = refs[10:14]
    out = refs[-1]
    core = lax.axis_index("core")
    rows = pl.ds(pl.multiple_of(core * (CX - OV), OV), OV)
    weight = amounts[step, :1, :]
    columns = near_x[core]
    for pair in range(CY // 2):
        extra_p = halo_part(near, near, 0, columns, pair)
        extra_q = halo_part(near, near, 1, columns, pair)
        for side in range(2):
            y = 2 * pair + side
            lanes = slice(side * CZ, side * CZ + CZ)
            sq = squared[y, rows, :]
            spot = y * OV
            lap = laps[spot : spot + OV] + extra_p[:OV, lanes]
            spot += CY * OV
            lap_adj = laps[spot : spot + OV] + extra_q[:OV, lanes]
            edge_p, edge_q = p[y, rows, :], q[y, rows, :]
            next_p = 2.0 * edge_p - p_before[y, rows, :] + sq * lap + source[y, rows, :] * weight
            next_q = 2.0 * edge_q - q_before[y, rows, :] + sq * lap_adj
            if step == 1:
                sets = (edge_p, edge_q, next_p, next_q)
            else:
                twice = 2.0 * sigma[y, rows, :]
                old = old_lap[y, rows, :]
                known = gathered[y, rows, :] + older_q[y, rows, :] * lap + next_q * old
                sets = (edge_p, edge_q, next_p, twice * known, twice * sq * old)
            for k, value in enumerate(sets):
                spot = (k * CY + y) * OV
                out[spot : spot + OV] = value


def edge_interior(v, edge_x, own_z, first, out, field):
    strips = []
    for j in range(CY // 2):
        one, two = 2 * j, 2 * j + 1
        high1, low1 = split(v[one])
        high2, low2 = split(v[two])
        x = dot(edge_x, cat([cat([high1, high2], 1), cat([low1, low2], 1)], 0))
        x = x[:OV] + x[OV:]
        strips += [x[:, :CZ], x[:, CZ:]]
    rows = pl.ds(first, OV)
    edge = [v[y, rows, :] for y in range(CY)]
    high, low = split(cat(edge, 0))
    z = dot(cat([high, low], 1), own_z[...])
    z = z[:, :CZ] + z[:, CZ:]
    for y in range(CY):
        beside = edge[(y - 1) % CY] + edge[(y + 1) % CY]
        spot = (field * CY + y) * OV
        out[spot : spot + OV] = strips[y] + z[y * OV : y * OV + OV] + beside


def edge_inside(p, q, edge_x, own_z, out):
    core = lax.axis_index("core")
    first = pl.multiple_of(core * (CX - OV), OV)
    edge_interior(p, edge_x[core], own_z, first, out, 0)
    edge_interior(q, edge_x[core], own_z, first, out, 1)


def inside(p, q, own_x, own_z, lap_p, lap_q):
    interior(p, own_x, own_z, lap_p)
    interior(q, own_x, own_z, lap_q)


def inside_one(p, own_x, own_z, lap_p):
    interior(p, own_x, own_z, lap_p)


def shrink(image, image_far, shrink_x, shrink_far, shrink_z, own):
    core = lax.axis_index("core")
    rows_x = shrink_x[core]
    rows_far = shrink_far[core]
    narrow = [None] * CYC
    weights = taps()
    for pair in range(CY // 2):
        high, low = split(cat([image[2 * pair], image[2 * pair + 1]], 1))
        both = dot(rows_x, cat([high, low], 0))
        spots = [slice(y * OV, y * OV + OV) for y in (2 * pair, 2 * pair + 1)]
        high, low = split(cat([image_far[spots[0]], image_far[spots[1]]], 1))
        both = both + dot(rows_far, cat([high, low], 0))
        for side in range(2):
            part = both[:, side * CZ : side * CZ + CZ]
            for j, w in weights[2 * pair + side]:
                term = part * w
                narrow[j] = term if narrow[j] is None else narrow[j] + term
    pieces = []
    for pair in range(CYC // 2):
        parts = []
        for j in (2 * pair, 2 * pair + 1):
            parts += list(split(narrow[j]))
        pieces.append(dot(cat(parts, 1), shrink_z[...]) * UNIT)
    own[...] = cat(pieces, 1)


def advance_and_shrink(*refs):
    fields, matrices = refs[:20], refs[20:23]
    p_new, near, far, own, image, image_far = refs[23:]
    advance(3, *fields, p_new, near, far, image, image_far)
    shrink(image, image_far, *matrices, own)


def fold(value):
    rows = value[0:8]
    for r in range(1, value.shape[0] // 8):
        rows = rows + value[8 * r : 8 * r + 8]
    folded = rows[:, :128]
    for c in range(1, 4):
        folded = folded + rows[:, 128 * c : 128 * c + 128]
    return folded


def squares(a, b, total, near):
    core = lax.axis_index("core")
    total[...] = a[...] + b[...]
    first, last = grid_ends()
    total[CXC + 4 : CXC + 6] = jnp.where(first | last, 0.0, total[CXC + 4 : CXC + 6])
    row = lax.broadcasted_iota(jnp.int32, (CXC, CYC * CZC), 0)
    start = (1 - core) * (CXC - 2)
    value = jnp.where((row >= start) & (row < start + 2), 0.0, total[:CXC])
    for r in range(4):
        for part in range(4):
            lanes = slice(part * 128, part * 128 + 128)
            spot = r * 4 + part
            near[spot : spot + 1] = total[CXC + r : CXC + r + 1, lanes]
    near[16:24] = fold(value * value)


def pair_up(total, mine, other, out, squared):
    core = lax.axis_index("core")
    out[...] = total[...]
    edge = mine[0:16] + other[0:16]
    for r in range(4):
        for part in range(4):
            lanes = slice(part * 128, part * 128 + 128)
            spot = r * 4 + part
            out[CXC + r : CXC + r + 1, lanes] = edge[spot : spot + 1]
    out[0:2] = jnp.where(core == 0, out[0:2], out[CXC + 2 : CXC + 4])
    out[CXC - 2 : CXC] = jnp.where(core == 0, out[CXC : CXC + 2], out[CXC - 2 : CXC])
    edge = edge * edge
    squared[...] = (mine[16:24] + other[16:24]) + (edge[0:8] + edge[8:16])


def last_fields(near, far, p, p_before, lap_p, source, amounts, halo_x, lap_out, base):
    core = lax.axis_index("core")
    columns = halo_x[core]
    weight = amounts[STEPS, :1, :]
    for pair in range(CY // 2):
        extra = halo_part(near, far, 0, columns, pair)
        for side in range(2):
            y = 2 * pair + side
            lap_out[y] = lap_p[y] + extra[:, side * CZ : side * CZ + CZ]
            base[y] = 2.0 * p[y] - p_before[y] + source[y] * weight


def add_four(own, one, three, two, out):
    out[...] = (own[...] + one[...]) + (two[...] + three[...])


def spread(total, sigma, lap, base, grow_z, grow_new, zeroth, first, second):
    core = lax.axis_index("core")

    def write(y, fine):
        change = fine * UNIT
        old, curve = sigma[y], lap[y]
        scaled = change * curve
        rows = pl.ds(y, CX, stride=CY)
        zeroth[rows, :] = base[y] + old * old * curve
        first[rows, :] = -2.0 * old * scaled
        second[rows, :] = change * scaled

    grow(total[...], grow_z, grow_new[core], write)


def widen(a, b, out):
    value = jnp.sum(a[...] + b[...], axis=0, keepdims=True)
    out[...] = jnp.broadcast_to(value, out.shape)


def finish(count, parts, total, zeroth, first, second, direction, p_last):
    value = jnp.sum(jnp.sum(parts[...], axis=0, keepdims=True), axis=1, keepdims=True)
    inverse = 1.0 / jnp.sqrt(value * (1.0 / count) + EPSILON)
    rate = LEARN * inverse
    p_last[...] = zeroth[...] + rate * (first[...] + rate * second[...])
    direction[...] = total[:CXC] * inverse


VM = pl.BlockSpec(memory_space=pltpu.VMEM)
SM = pl.BlockSpec(memory_space=pltpu.SMEM)
FIELD = jax.ShapeDtypeStruct((CY, CX, CZ), F32)
PARAMS = pltpu.CompilerParams(vmem_limit_bytes=6 * 2**20)


def rows_of(count, lanes=128):
    return jax.ShapeDtypeStruct((count, lanes), F32)


def call(body, outs, *args, smem=0, scratch=(), flops=0, name=None, held=(), in_specs=None, out_specs=None):
    size = sum(int(np.prod(a.shape)) * a.dtype.itemsize for a in args)
    count = len(args)

    def run(*refs):
        body(*refs[:count], *refs[count + len(held) :])

    return pl.pallas_call(
        run,
        out_shape=outs,
        in_specs=([SM] * smem + [VM] * (count - smem) if in_specs is None else in_specs)
        + [pl.BlockSpec(memory_space=pl.ANY)] * len(held),
        out_specs=jax.tree.map(lambda _: VM, outs) if out_specs is None else out_specs,
        scratch_shapes=list(scratch),
        compiler_params=PARAMS,
        cost_estimate=pl.CostEstimate(flops=flops, bytes_accessed=size, transcendentals=0),
        name=name,
    )(*args, *held)


def xor_swap(x, axis, mask):
    count = lax.axis_size(axis)
    if mask >= count:
        return jnp.zeros_like(x)
    return lax.ppermute(x, axis, [(i, i ^ mask) for i in range(count)])


def far_swap(x):
    count = lax.axis_size(TILE)
    pairs = [(i, i + 1) for i in range(1, count - 1, 2)]
    return lax.ppermute(x, TILE, pairs + [(b, a) for a, b in pairs])


def on_device(p_now, p_prev, adj_now, adj_next, coef_old, signs, elem_index, wavelet):
    const = {name: jnp.asarray(value) for name, value in constants().items()}
    own_x, own_z, halo_x = const["own_x"], const["own_z"], const["halo_x"]
    flat = lambda a: a.reshape(CX * CY, CZ)
    p_now, p_prev, adj_now, adj_next = map(flat, (p_now, p_prev, adj_now, adj_next))

    half, edge = rows_of(CY * OV), rows_of(2 * CY * OV)
    sources = [pltpu.with_memory_space_constraint(a, pltpu.HBM) for a in (p_now, adj_now, coef_old)]

    blocks = [pltpu.VMEM((OV * CY, CZ), F32)] * 2 + [pltpu.VMEM((8, CYC * CZC), F32)]
    far, near = call(
        first_edges, (rows_of(2 * CY * OV + 24), rows_of(2 * CY * OV + 8)), *sources,
        in_specs=[pl.BlockSpec(memory_space=pltpu.HBM)] * 3,
        scratch=blocks * 2 + [pltpu.SemaphoreType.DMA((6,))],
        name="first_edges",
    )
    far, near = far_swap(far), xor_swap(near, "core", 1)

    wide = jax.ShapeDtypeStruct((CY, CX + OV, CZ), F32)
    later = [own_x, own_z, p_prev, adj_next, coef_old, const["grow_own"]]
    later.append(const["grow_z"])
    p, q, p_before, q_before, lap_p, lap_q, source, amounts, sigma_own = call(
        prepare,
        (FIELD,) * 7 + (jax.ShapeDtypeStruct((STEPS + 1, 8, CZ), F32), wide),
        signs[0], elem_index, wavelet, p_now, adj_now,
        *(pltpu.with_memory_space_constraint(a, pltpu.HBM) for a in later),
        flops=10**9, name="prepare", held=(halo_x,),
        in_specs=[SM] * 3 + [VM] * 2 + [pl.BlockSpec(memory_space=pltpu.HBM)] * len(later),
        scratch=[pltpu.VMEM(a.shape, a.dtype) for a in later]
        + [pltpu.SemaphoreType.DMA((len(later),))],
    )
    sigma, squared, beyond = call(
        speed, (FIELD, FIELD, half), sigma_own, near, far, const["grow_z"], const["grow_rest"],
        scratch=[pltpu.VMEM((8, CYC * CZC), F32)], flops=10**8, name="speed",
    )

    laps, qs = [], [q]
    gathered = None
    for step in range(STEPS):
        args = [near, far, p, p_before, q, q_before, lap_p, lap_q, squared, source, amounts, halo_x]
        body = functools.partial(advance, step)
        name = f"advance_{step}"
        if step == 0:
            outs = (FIELD, FIELD, edge, FIELD)
        elif step == 1:
            args += [sent, beyond, const["cross_x"]]
            outs = (FIELD, FIELD, edge, edge, FIELD)
            older_far = far
        elif step == 2:
            args.append(laps[1])
            outs = (FIELD, FIELD, edge, FIELD)
        else:
            args += [sent, beyond, const["cross_x"], laps[0], qs[1], gathered, sigma, older_far]
            args += [const["shrink_x"], const["shrink_far"], const["shrink_z"]]
            p_new, near, far, partial = call(
                advance_and_shrink, (FIELD, half, half, rows_of(ROWS, CYC * CZC)), *args,
                scratch=[pltpu.VMEM((CY, CX, CZ), F32), pltpu.VMEM((CY * OV, CZ), F32)],
                flops=2 * 10**8, name="advance_3",
            )
            p, p_before = p_new, p
            continue
        result = call(body, outs, *args, flops=10**8, name=name)
        p_new, q_new, *edges, other = result
        if step < 2:
            laps.append(other)
        else:
            gathered = other
        p, p_before = p_new, p
        q, q_before = q_new, q
        qs.append(q)
        near = xor_swap(edges[0], "core", 1)
        if step == 1:
            lap_p, lap_q = call(
                inside, (FIELD, FIELD), p, q, own_x, own_z, flops=10**9, name="inside_1"
            )
            far = edges[1]
            continue
        edge_laps = call(
            edge_inside, edge, p, q, const["edge_x"], own_z, flops=10**8, name=f"edge_inside_{step}"
        )
        args = [near, p, p_before, q, q_before, edge_laps, squared, source, amounts]
        args.append(const["near_x"])
        if step == 2:
            args += [qs[1], laps[0], gathered, sigma]
        sent = call(
            functools.partial(early, step + 1), rows_of((4 if step == 0 else 5) * CY * OV),
            *args, flops=10**7, name=f"early_{step + 1}",
        )
        far = far_swap(sent)
        lap_p, lap_q = call(
            inside, (FIELD, FIELD), p, q, own_x, own_z, flops=10**9, name=f"inside_{step}",
            held=(sent,),
        )

    two, three, one = (xor_swap(partial, "y", m) for m in (2, 3, 1))
    near = xor_swap(near, "core", 1)
    lap_p = call(inside_one, FIELD, p, own_x, own_z, flops=5 * 10**8, name="inside_last")
    lap_p, base = call(
        last_fields, (FIELD, FIELD), near, far, p, p_before, lap_p, source, amounts, halo_x,
        flops=10**8, name="last_fields",
    )
    held = (lap_p, base)
    partial = call(
        add_four, rows_of(ROWS, CYC * CZC), partial, one, three, two, name="add_four", held=held
    )
    total, mine = call(
        squares, (rows_of(ROWS, CYC * CZC), rows_of(24)), partial, xor_swap(partial, "xl", 1),
        name="squares", held=held,
    )
    total, squared_sum = call(
        pair_up, (rows_of(ROWS, CYC * CZC), rows_of(8)), total, mine, xor_swap(mine, "core", 1),
        name="pair_up", held=held,
    )
    terms = call(
        spread, (rows_of(CX * CY),) * 3, total, sigma, lap_p, base, const["grow_z"], const["grow_new"],
        flops=10**8, name="spread",
    )
    deep = lax.axis_size("z")
    copies = call(
        widen, rows_of(deep),
        squared_sum, xor_swap(squared_sum, "xh", 1), name="widen", held=terms,
    )
    parts = lax.all_to_all(copies, "z", split_axis=0, concat_axis=0, tiled=True)
    count = float(lax.axis_size(TILE) * CXC * CYC * CZC)
    direction, p_last = call(
        functools.partial(finish, count),
        (rows_of(CXC, CYC * CZC), rows_of(CX * CY)),
        parts, total, *terms, name="finish",
    )
    return direction, p_last.reshape(1, CX, CY, CZ)


def solution(mesh):
    shots, tiles = mesh.shape["shot"], mesh.shape["tile"]
    fine = Mesh(
        mesh.devices.reshape(shots // 2, 2, 2, tiles // 4, 2), ("y", "xl", "xh", "z", "core")
    )
    placed = (
        P(SHOT, TILE, None, None),
        P(SHOT, TILE, None, None),
        P(SHOT, TILE, None, None),
        P(SHOT, TILE, None, None),
        P(TILE, None),
        P(SHOT, TILE),
        P(TILE),
        P(),
    )
    return jax.shard_map(
        on_device,
        mesh=fine,
        in_specs=placed,
        out_specs=(P(TILE, None), P(SHOT, TILE, None, None)),
        check_vma=False,
    )
```
